32 devices in a mesh: fsdp: 8 (over z, y), rep: 4 (over x, core).
Axes of the slice: x: 2, y: 2, z: 4, core: 2. Of those that a mesh axis runs over, the one named last changes fastest.
Arguments:
- tokens: bfloat16 [8, 1024, 1152], P('fsdp', 'rep'), may hold values from -6 to 6
- conditions: bfloat16 [8, 4, 1152], P('fsdp'), may hold values from -6 to 6
- lengths: int32 [8, 4], P('fsdp'), may hold values from 0 to 1024, as said below
- segments: int32 [8, 1024], P('fsdp', 'rep'), may hold values from 0 to 3, as said below
- condition_weight: bfloat16 [1152, 6, 1152], P('fsdp', None, 'rep'), may hold values from -0.1875 to 0.1875
- condition_bias: bfloat16 [6912], P('fsdp'), may hold values from -3 to 3
- input_weight: bfloat16 [1152, 3, 1152], P('fsdp', None, 'rep'), may hold values from -0.1875 to 0.1875
- input_bias: bfloat16 [2304], P('fsdp'), may hold values from -3 to 3
- attend_weight: bfloat16 [1152, 1152], P('fsdp', 'rep'), may hold values from -3 to 3
- attend_bias: bfloat16 [1152], P('fsdp'), may hold values from -3 to 3
- expand_weight: bfloat16 [1152, 4608], P('fsdp', 'rep'), may hold values from -0.1875 to 0.1875
- expand_bias: bfloat16 [4608], P('fsdp'), may hold values from -3 to 3
- reduce_weight: bfloat16 [1152, 4608], P('fsdp', 'rep'), may hold values from -0.09375 to 0.09375
- reduce_bias: bfloat16 [1152], P('fsdp'), may hold values from -3 to 3
- cotangent: bfloat16 [8, 1024, 1152], P('fsdp', 'rep'), may hold values from -6 to 6
Outputs:
- output: bfloat16 [8, 1024, 1152], P('fsdp', 'rep')
- token_grad: float32 [8, 1024, 1152], P('fsdp', 'rep')
- condition_grad: float32 [8, 4, 1152], P('fsdp')
- condition_weight_grad: float32 [1152, 6, 1152], P('fsdp', None, 'rep')
- condition_bias_grad: float32 [6912], P('fsdp')
- input_weight_grad: float32 [1152, 3, 1152], P('fsdp', None, 'rep')
- input_bias_grad: float32 [2304], P('fsdp')
- attend_weight_grad: float32 [1152, 1152], P('fsdp', 'rep')
- attend_bias_grad: float32 [1152], P('fsdp')
- expand_weight_grad: float32 [1152, 4608], P('fsdp', 'rep')
- expand_bias_grad: float32 [4608], P('fsdp')
- reduce_weight_grad: float32 [1152, 4608], P('fsdp', 'rep')
- reduce_bias_grad: float32 [1152], P('fsdp')
The draws below stay inside these ranges and needn't reach their ends.
Inputs may be any that keep to these rules, and one draw needn't show every extreme that they name: `lengths`: each row holds either one image of 1024 patches in slot 0 with the other slots 0, or 4 images of 256 patches; 4 rows are of the first kind. `segments`: the slot of each patch agrees with lengths.
All inputs are finite; a program needn't handle non-finite values.
Results may differ from the reference program's by a relative error of at most 0.014.
The reference program's roundings to bfloat16 on the way count: a program that leaves them out, or rounds other values in their place, can miss the bound.
Values may be sent and summed in bfloat16 or wider, within the bound.
A program may use at most 192 MiB of HBM per device.

```python
import math
import jax
import jax.numpy as jnp
from jax import lax

D = 1152
HEADS = 16
FF = 4608
ROW_LEN = 1024
SLOTS = 4
ROWS = 8


def single_rows(key):
    order = jax.random.permutation(jax.random.fold_in(key, 11), ROWS)
    return order < ROWS // 2


def draw_lengths(key, part):
    single = single_rows(key)
    small = jnp.full((ROWS, SLOTS), ROW_LEN // SLOTS, jnp.int32)
    whole = jnp.zeros((ROWS, SLOTS), jnp.int32).at[:, 0].set(ROW_LEN)
    return jnp.where(single[:, None], whole, small)


def draw_segments(key, part):
    single = single_rows(key)
    places = jnp.arange(ROW_LEN, dtype=jnp.int32) // (ROW_LEN // SLOTS)
    return jnp.where(single[:, None], jnp.zeros((ROWS, ROW_LEN), jnp.int32), places[None, :]).astype(jnp.int32)


def with_spikes(drawn, key, source, target, shards_of, factor):
    def block_of(dim):
        return (jnp.arange(drawn.shape[dim]) // (drawn.shape[dim] // shards_of)).reshape((-1,) + (1,) * (drawn.ndim - 1 - dim))

    first = jax.random.permutation(key, shards_of)[block_of(target)]
    far = (block_of(target) + shards_of // 2) % shards_of
    return jnp.where((block_of(source) == first) | (block_of(source) == far), factor * drawn, drawn)


def block_scale(rng, shape, shards, low, top_value):
    def one(dim, blocks):
        steps = jax.random.uniform(jax.random.fold_in(jax.random.fold_in(rng, 6), dim), (blocks,), jnp.float32, low / len(shards), top_value / len(shards))
        return jnp.repeat(jnp.exp(steps), shape[dim] // blocks).reshape((-1,) + (1,) * (len(shape) - dim - 1))

    factor_of = one(*shards[0])
    for cut in shards[1:]:
        factor_of = factor_of * one(*cut)
    return factor_of


def scatter_about(stream_key, extent, scale, bound, shards=(), held_as=jnp.bfloat16):
    level = block_scale(stream_key, extent, shards, -0.22, 0.18) if shards else 1.0
    values = jax.random.normal(stream_key, extent, jnp.float32) * scale * level
    return jnp.minimum(jnp.maximum(values, -bound), bound).astype(held_as)


def bell_draw_with(rng, shape, deviation, reach, cuts, heavy, kind=jnp.bfloat16):
    array = deviation * jax.random.normal(rng, shape, jnp.float32)
    if cuts:
        array = array * block_scale(rng, shape, cuts, -0.22, 0.18)
    return jnp.clip(with_spikes(array, jax.random.fold_in(rng, 3), *heavy), -reach, reach).astype(kind)


def setup_inputs(seed: int = 0) -> dict:
    key_list = jax.random.split(jax.random.key(seed), 16)
    tokens = scatter_about(key_list[0], (ROWS, ROW_LEN, D), 1.0, 6.0, ((0, 8), (1, 4)))
    conditions = scatter_about(key_list[1], (ROWS, SLOTS, D), 1.0, 6.0, ((0, 8),))
    lengths = draw_lengths(jax.random.fold_in(key_list[15], 71), 0)
    segments = draw_segments(jax.random.fold_in(key_list[15], 71), 0)
    condition_weight = scatter_about(key_list[4], (D, 6, D), D ** -0.5, 0.1875, ((0, 8), (2, 4)))
    condition_bias = scatter_about(key_list[5], (6 * D,), 0.5, 3.0, ((0, 8),))
    input_weight = scatter_about(key_list[6], (D, 3, D), D ** -0.5, 0.1875, ((0, 8), (2, 4)))
    input_bias = scatter_about(key_list[7], (2 * D,), 0.5, 3.0, ((0, 8),))
    attend_weight = scatter_about(key_list[8], (D, D), (D * SLOTS // ROW_LEN) ** -0.5, 3.0, ((0, 8), (1, 4)))
    attend_bias = scatter_about(key_list[9], (D,), 0.5, 3.0, ((0, 8),))
    expand_weight = scatter_about(key_list[10], (D, FF), D ** -0.5, 0.1875, ((0, 8), (1, 4)))
    expand_bias = scatter_about(key_list[11], (FF,), 0.5, 3.0, ((0, 8),))
    reduce_weight = scatter_about(key_list[12], (D, FF), FF ** -0.5, 0.09375, ((0, 8), (1, 4)))
    reduce_bias = scatter_about(key_list[13], (D,), 0.5, 3.0, ((0, 8),))
    cotangent = bell_draw_with(key_list[14], (ROWS, ROW_LEN, D), 1.0, 6.0, ((0, 8), (1, 4)), (0, 2, 8, 2.0))
    return {"tokens": tokens, "conditions": conditions, "lengths": lengths, "segments": segments, "condition_weight": condition_weight, "condition_bias": condition_bias, "input_weight": input_weight, "input_bias": input_bias, "attend_weight": attend_weight, "attend_bias": attend_bias, "expand_weight": expand_weight, "expand_bias": expand_bias, "reduce_weight": reduce_weight, "reduce_bias": reduce_bias, "cotangent": cotangent}


epsilon = 1e-06
highest = lax.Precision.HIGHEST

@jax.custom_vjp
def low(v):
    return lax.optimization_barrier(v.astype(jnp.bfloat16)).astype(jnp.float32)

@jax.custom_vjp
def low_back(v):
    return v

def low_keep(v):
    return (low(v), None)

def low_pass(kept, grad):
    return (grad,)

def back_keep(v):
    return (v, None)

def back_low(kept, grad):
    return (low(grad),)
low.defvjp(low_keep, low_pass)
low_back.defvjp(back_keep, back_low)

def layer_normed(values):
    center = lax.optimization_barrier(jnp.mean(values, axis=-1, keepdims=True))
    shifted = values - center
    spread = lax.optimization_barrier(jnp.mean(shifted * shifted, axis=-1, keepdims=True))
    return shifted * lax.rsqrt(spread + epsilon)

def modulated(values, shift_term, scale_term):
    return layer_normed(values) * (1.0 + scale_term) + shift_term

def image_index(row_ends, positions):
    return lax.optimization_barrier(jnp.sum((positions[..., :, None] >= row_ends[..., None, :-1]).astype(jnp.int32), axis=-1))

def row_block(params, row_tokens, row_mods, row_segments, row_lengths):
    input_weight, input_bias, attend_weight, attend_bias, expand_weight, expand_bias, reduce_weight, reduce_bias = params
    row_length, model_width = row_tokens.shape
    head_width = model_width // HEADS
    score_scale = 1.0 / math.sqrt(head_width)
    per_token = row_mods[row_segments]
    shift_one, scale_one, gate_one, shift_two, scale_two, gate_two = jnp.split(per_token, 6, axis=1)
    normed_one = low(modulated(row_tokens, shift_one, scale_one))
    joined = jnp.dot(normed_one, input_weight.reshape(model_width, 3 * model_width), precision=highest)
    queries = low(low_back(joined[:, :model_width] + input_bias[:model_width]))
    keys_row = low(low_back(joined[:, model_width:2 * model_width]))
    values_row = low(low_back(joined[:, 2 * model_width:] + input_bias[model_width:]))
    positions = jnp.arange(row_length, dtype=jnp.int32)
    images = image_index(jnp.cumsum(row_lengths, dtype=jnp.int32), positions)
    allowed = images[:, None] == images[None, :]
    shaped = (row_length, HEADS, head_width)
    scores = jnp.einsum('qhd,khd->hqk', queries.reshape(shaped), keys_row.reshape(shaped), precision=highest)
    scores = low_back(scores * score_scale)
    scores = jnp.where(allowed[None], scores, -1e+30)
    row_max = lax.optimization_barrier(jnp.max(scores, axis=-1, keepdims=True))
    powers = jnp.exp(scores - row_max)
    weights_low = low(powers / lax.optimization_barrier(jnp.sum(powers, axis=-1, keepdims=True)))
    mixed = jnp.einsum('hqk,khd->qhd', weights_low, values_row.reshape(shaped), precision=highest)
    attended = low(low_back(mixed.reshape(row_length, model_width)))
    branch = low_back(jnp.dot(attended, attend_weight.T, precision=highest) + attend_bias)
    middle = row_tokens + gate_one * branch
    normed_two = low(modulated(middle, shift_two, scale_two))
    inner = low_back(jnp.dot(normed_two, expand_weight, precision=highest) + expand_bias)
    active = low(jax.nn.gelu(inner, approximate=True))
    outer = low_back(jnp.dot(active, reduce_weight.T, precision=highest) + reduce_bias)
    return middle + gate_two * outer

def reference(tokens, conditions, lengths, segments, condition_weight, condition_bias, input_weight, input_bias, attend_weight, attend_bias, expand_weight, expand_bias, reduce_weight, reduce_bias, cotangent):
    floats = tuple((item.astype(jnp.float32) for item in (tokens, conditions, condition_weight, condition_bias, input_weight, input_bias, attend_weight, attend_bias, expand_weight, expand_bias, reduce_weight, reduce_bias)))

    def forward(token_values, condition_values, weight_values, bias_values, *params):
        activated = low(jax.nn.silu(condition_values))
        blocks = jnp.einsum('rsd,dkm->rskm', activated, weight_values, precision=highest) + bias_values.reshape(6, -1)
        modulation = low_back(blocks.reshape(blocks.shape[0], blocks.shape[1], -1))
        checked = jax.checkpoint(row_block)

        def through(carry, inputs):
            return (carry, checked(params, *inputs))
        _, result = lax.scan(through, None, (token_values, modulation, segments, lengths))
        return result
    primal, pullback = jax.vjp(forward, *floats)
    grads = pullback(cotangent.astype(jnp.float32))
    return (primal.astype(jnp.bfloat16), grads[0], grads[1], grads[2], grads[3], grads[4], grads[5], grads[6], grads[7], grads[8], grads[9], grads[10], grads[11])
```

```python
import math

import jax
import jax.numpy as jnp
from jax import lax
from jax.sharding import PartitionSpec as P

HEAD_DIM = 72


epsilon = 1e-06
highest = lax.Precision.HIGHEST
float_type = jnp.float32
brain_type = jnp.bfloat16


def layer_normed(values):
    center = jnp.mean(values, axis=-1, keepdims=True)
    shifted = values - center
    spread = jnp.mean(shifted * shifted, axis=-1, keepdims=True)
    return shifted * lax.rsqrt(spread + epsilon)


def modulated(values, shift_term, scale_term):
    return layer_normed(values) * (1.0 + scale_term) + shift_term


def gelu_tanh(values):
    return jax.nn.gelu(values, approximate=True)


def image_index(row_ends, positions):
    return jnp.sum((positions[..., :, None] >= row_ends[..., None, :-1]).astype(jnp.int32), axis=-1)


def across(left, right):
    return lax.dot_general(left, right, (((0,), (0,)), ((), ())), preferred_element_type=float_type)


def against(left, right):
    return lax.dot_general(left, right, (((1,), (1,)), ((), ())), preferred_element_type=float_type)


def column_sums(values):
    return jnp.sum(values.astype(float_type), axis=0)


def spread_columns(own_part, total, start):
    empty = jnp.zeros(own_part.shape[:-1] + (total,), float_type)
    return lax.dynamic_update_slice_in_dim(empty, own_part, start, own_part.ndim - 1)


def gather_block(*weights):
    return tuple(lax.all_gather(item, "fsdp", axis=0, tiled=True) for item in weights)


def local(
    tokens,
    conditions,
    lengths,
    segments,
    condition_weight,
    condition_bias,
    input_weight,
    input_bias,
    attend_weight,
    attend_bias,
    expand_weight,
    expand_bias,
    reduce_weight,
    reduce_bias,
    cotangent,
):
    row_count, quarter, model_width = tokens.shape
    slot_count = conditions.shape[1]
    group_size = lax.axis_size("rep")
    group_place = lax.axis_index("rep")
    row_length = quarter * group_size
    own_width = condition_weight.shape[2]
    column_start = group_place * own_width
    hidden_width = expand_weight.shape[1]
    hidden_start = group_place * hidden_width
    local_heads = own_width // HEAD_DIM
    score_scale = 1.0 / math.sqrt(HEAD_DIM)
    patch_count = row_count * quarter
    image_count = row_count * slot_count
    key_place = jnp.arange(row_length, dtype=jnp.int32)
    row_ends = jnp.cumsum(lengths, axis=1, dtype=jnp.int32)
    row_images = image_index(row_ends, key_place)
    allowed = row_images[:, :, None] == row_images[:, None, :]

    def whole_rows(values):
        joined_rows = lax.all_gather(
            values.reshape(row_count, quarter, -1), "rep", axis=1, tiled=True
        )
        return joined_rows.reshape(row_count * row_length, -1)

    def own_rows(values):
        summed = lax.psum_scatter(
            values.reshape(row_count, row_length, -1), "rep", scatter_dimension=1, tiled=True
        )
        return summed.reshape(patch_count, -1)

    fsdp_size = lax.axis_size("fsdp")
    fsdp_place = lax.axis_index("fsdp")
    own_depth = condition_weight.shape[0]
    condition_values = conditions.astype(float_type)
    activated_own = jax.nn.silu(condition_values).reshape(image_count, model_width).astype(brain_type)
    activated_all = lax.all_gather(activated_own, "fsdp", axis=0, tiled=True)
    activated = lax.dynamic_slice_in_dim(activated_all, fsdp_place * own_depth, own_depth, 1)
    local_biases = (condition_bias, input_bias, attend_bias, expand_bias, reduce_bias)
    bias_sizes = [item.shape[0] for item in local_biases]
    bias_ends = [sum(bias_sizes[:k]) for k in range(len(bias_sizes) + 1)]
    bias_table = lax.all_gather(jnp.concatenate(local_biases), "fsdp", axis=0, tiled=False)
    condition_bias_all, input_bias_all, attend_bias_all, expand_bias_all, reduce_bias_all = [
        bias_table[:, low:high].reshape(-1) for low, high in zip(bias_ends[:-1], bias_ends[1:])
    ]
    condition_bias_own = lax.dynamic_slice_in_dim(
        condition_bias_all.reshape(6, model_width), column_start, own_width, 1
    )
    modulation_parts = jnp.einsum(
        "id,dkm->ikm", activated, condition_weight, preferred_element_type=float_type
    )
    modulation_own = (
        lax.psum_scatter(modulation_parts, "fsdp", scatter_dimension=0, tiled=True)
        + condition_bias_own[None]
    )
    modulation = lax.all_gather(modulation_own, "rep", axis=2, tiled=True).reshape(
        row_count, slot_count, -1
    )
    slot_table = (
        segments[:, :, None] == jnp.arange(slot_count, dtype=jnp.int32)[None, None, :]
    ).astype(float_type)
    per_token = jnp.einsum("rqs,rsm->rqm", slot_table, modulation, precision=highest).reshape(
        patch_count, -1
    )
    shift_one, scale_one, gate_one, shift_two, scale_two, gate_two = jnp.split(per_token, 6, axis=1)
    token_values = tokens.reshape(patch_count, model_width).astype(float_type)

    def split_heads(values):
        return values.reshape(row_count, row_length, local_heads, HEAD_DIM).transpose(2, 0, 1, 3)

    def merge_heads(values):
        return values.transpose(1, 2, 0, 3).reshape(row_count * row_length, own_width)

    def allowed_scores(query_head, key_head):
        scores = (
            jnp.einsum("rqd,rkd->rqk", query_head, key_head, preferred_element_type=float_type)
            * score_scale
        )
        return jnp.where(allowed, scores, -1e30)

    def head_forward(parts):
        query_head, key_head, value_head = parts
        scores = allowed_scores(query_head, key_head)
        row_max = jnp.max(scores, axis=-1, keepdims=True)
        powers = jnp.exp(scores - row_max)
        totals = jnp.sum(powers, axis=-1, keepdims=True)
        weights_low = (powers / totals).astype(brain_type)
        mixed = jnp.einsum(
            "rqk,rkd->rqd", weights_low, value_head, preferred_element_type=float_type
        )
        return (mixed, row_max + jnp.log(totals))

    def head_backward(parts):
        query_head, key_head, value_head, grad_head, log_head = parts
        scores = allowed_scores(query_head, key_head)
        probable = jnp.exp(scores - log_head)
        prob_grad = jnp.einsum(
            "rqd,rkd->rqk", grad_head, value_head, preferred_element_type=float_type
        )
        score_grad = (
            probable * (prob_grad - jnp.sum(probable * prob_grad, axis=-1, keepdims=True))
        ).astype(brain_type)
        query_part = (
            jnp.einsum("rqk,rkd->rqd", score_grad, key_head, preferred_element_type=float_type)
            * score_scale
        )
        key_part = (
            jnp.einsum("rqk,rqd->rkd", score_grad, query_head, preferred_element_type=float_type)
            * score_scale
        )
        value_part = jnp.einsum(
            "rqk,rqd->rkd",
            probable.astype(brain_type),
            grad_head,
            preferred_element_type=float_type,
        )
        return (query_part, key_part, value_part)

    def trunk(gathered):
        (
            input_all,
            input_bias_all,
            attend_all,
            attend_bias_all,
            expand_all,
            expand_bias_all,
            reduce_all,
            reduce_bias_all,
        ) = gathered
        bias_pair = lax.dynamic_slice_in_dim(
            input_bias_all.reshape(2, model_width), column_start, own_width, 1
        )
        expand_bias_own = lax.dynamic_slice_in_dim(expand_bias_all, hidden_start, hidden_width, 0)
        normed_one = modulated(token_values, shift_one, scale_one).astype(brain_type)
        whole_one = whole_rows(normed_one)
        joined = jnp.einsum("nd,dkm->nkm", whole_one, input_all, preferred_element_type=float_type)
        queries = (joined[:, 0] + bias_pair[0]).astype(brain_type)
        keys_row = joined[:, 1].astype(brain_type)
        values_row = (joined[:, 2] + bias_pair[1]).astype(brain_type)
        query_heads = split_heads(queries)
        key_heads = split_heads(keys_row)
        value_heads = split_heads(values_row)
        mixed, log_totals = lax.map(head_forward, (query_heads, key_heads, value_heads))
        attended = merge_heads(mixed).astype(brain_type)
        branch = own_rows(against(attended, attend_all)) + attend_bias_all
        middle = token_values + gate_one * branch
        normed_two = modulated(middle, shift_two, scale_two).astype(brain_type)
        whole_two = whole_rows(normed_two)
        inner = jnp.dot(whole_two, expand_all, preferred_element_type=float_type) + expand_bias_own
        active = gelu_tanh(inner).astype(brain_type)
        outer = own_rows(against(active, reduce_all)) + reduce_bias_all
        result = middle + gate_two * outer
        return (
            result,
            gathered,
            whole_one,
            query_heads,
            key_heads,
            value_heads,
            log_totals,
            attended,
            branch,
            middle,
            whole_two,
            inner,
            active,
            outer,
        )

    input_all, attend_all, expand_all, reduce_all = gather_block(
        input_weight, attend_weight, expand_weight, reduce_weight
    )
    state = trunk(
        (
            input_all,
            input_bias_all,
            attend_all,
            attend_bias_all,
            expand_all,
            expand_bias_all,
            reduce_all,
            reduce_bias_all,
        )
    )
    output = state[0].astype(brain_type).reshape(row_count, quarter, model_width)
    (
        _,
        gathered,
        whole_one,
        query_heads,
        key_heads,
        value_heads,
        log_totals,
        attended,
        branch,
        middle,
        whole_two,
        inner,
        active,
        outer,
    ) = state
    upstream = cotangent.reshape(patch_count, model_width).astype(float_type)
    outer_grad = (gate_two * upstream).astype(brain_type)
    gate_two_grad = upstream * outer
    outer_whole = whole_rows(outer_grad)
    reduce_grad = across(outer_whole, active)
    reduce_bias_grad = column_sums(outer_grad)
    active_grad = jnp.dot(outer_whole, reduce_all, preferred_element_type=float_type)
    _, gelu_back = jax.vjp(gelu_tanh, inner)
    inner_grad = gelu_back(active_grad)[0].astype(brain_type)
    expand_grad = across(whole_two, inner_grad)
    expand_bias_full = spread_columns(
        column_sums(inner_grad), hidden_width * group_size, hidden_start
    )
    two_grad = own_rows(against(inner_grad, expand_all))
    _, second_back = jax.vjp(modulated, middle, shift_two, scale_two)
    middle_norm_grad, shift_two_grad, scale_two_grad = second_back(two_grad)
    middle_grad = upstream + middle_norm_grad
    gate_one_grad = middle_grad * branch
    branch_grad = (gate_one * middle_grad).astype(brain_type)
    branch_whole = whole_rows(branch_grad)
    attend_grad = across(branch_whole, attended)
    attend_bias_grad = column_sums(branch_grad)
    attended_grad = jnp.dot(branch_whole, attend_all, preferred_element_type=float_type).astype(
        brain_type
    )
    grad_heads = split_heads(attended_grad)
    query_parts, key_parts, value_parts = lax.map(
        head_backward, (query_heads, key_heads, value_heads, grad_heads, log_totals)
    )
    query_low = merge_heads(query_parts).astype(brain_type)
    key_low = merge_heads(key_parts).astype(brain_type)
    value_low = merge_heads(value_parts).astype(brain_type)
    joined_grad = jnp.stack([query_low, key_low, value_low], axis=1)
    input_grad = jnp.einsum(
        "nd,nkm->dkm", whole_one, joined_grad, preferred_element_type=float_type
    )
    input_bias_pair = jnp.stack([column_sums(query_low), column_sums(value_low)])
    input_bias_full = spread_columns(input_bias_pair, model_width, column_start).reshape(-1)
    one_grad = own_rows(
        jnp.einsum("nkm,dkm->nd", joined_grad, input_all, preferred_element_type=float_type)
    )
    _, first_back = jax.vjp(modulated, token_values, shift_one, scale_one)
    token_norm_grad, shift_one_grad, scale_one_grad = first_back(one_grad)
    token_grad = (middle_grad + token_norm_grad).reshape(row_count, quarter, model_width)
    six_grads = jnp.stack(
        [
            shift_one_grad,
            scale_one_grad,
            gate_one_grad,
            shift_two_grad,
            scale_two_grad,
            gate_two_grad,
        ],
        axis=1,
    ).reshape(row_count, quarter, 6, model_width)
    modulation_part = jnp.einsum("rqs,rqkm->rskm", slot_table, six_grads, precision=highest)
    modulation_grad = lax.psum_scatter(modulation_part, "rep", scatter_dimension=3, tiled=True)
    modulation_low = lax.all_gather(
        modulation_grad.reshape(image_count, 6, own_width).astype(brain_type),
        "fsdp",
        axis=0,
        tiled=True,
    )
    condition_weight_final = jnp.einsum(
        "id,ikm->dkm", activated, modulation_low, preferred_element_type=float_type
    )
    condition_bias_full = lax.all_gather(
        column_sums(modulation_low), "rep", axis=1, tiled=True
    ).reshape(-1)
    bias_depth = condition_bias.shape[0]
    condition_bias_final = lax.dynamic_slice_in_dim(
        condition_bias_full, fsdp_place * bias_depth, bias_depth, 0
    )
    activated_part = jnp.einsum(
        "ikm,dkm->id", modulation_low, condition_weight, preferred_element_type=float_type
    )
    activated_wide = lax.all_to_all(
        activated_part.reshape(fsdp_size, image_count, own_depth), "fsdp", 0, 0
    )
    activated_row = jnp.transpose(activated_wide, (1, 0, 2)).reshape(image_count, model_width)
    bias_rows = jnp.concatenate(
        [
            item.reshape(fsdp_size, -1)
            for item in (input_bias_full, attend_bias_grad, expand_bias_full, reduce_bias_grad)
        ],
        axis=1,
    )
    bias_own = lax.psum_scatter(bias_rows, "fsdp", scatter_dimension=0, tiled=True).reshape(-1)
    activated_grad, bias_sum = lax.psum((activated_row, bias_own), "rep")
    input_bias_final, attend_bias_final, expand_bias_final, reduce_bias_final = jnp.split(
        bias_sum, [end - bias_sizes[0] for end in bias_ends[2:-1]]
    )
    input_final, attend_final, expand_final, reduce_final = [
        lax.psum_scatter(item.astype(brain_type), "fsdp", scatter_dimension=0, tiled=True).astype(
            float_type
        )
        for item in (input_grad, attend_grad, expand_grad, reduce_grad)
    ]
    _, silu_back = jax.vjp(jax.nn.silu, condition_values)
    condition_grad = silu_back(activated_grad.reshape(row_count, slot_count, model_width))[0]
    return (
        output,
        token_grad,
        condition_grad,
        condition_weight_final,
        condition_bias_final,
        input_final,
        input_bias_final,
        attend_final,
        attend_bias_final,
        expand_final,
        expand_bias_final,
        reduce_final,
        reduce_bias_final,
    )


def solution(mesh):
    in_specs = (
        P("fsdp", "rep", None),
        P("fsdp", None, None),
        P("fsdp", None),
        P("fsdp", "rep"),
        P("fsdp", None, "rep"),
        P("fsdp"),
        P("fsdp", None, "rep"),
        P("fsdp"),
        P("fsdp", "rep"),
        P("fsdp"),
        P("fsdp", "rep"),
        P("fsdp"),
        P("fsdp", "rep"),
        P("fsdp"),
        P("fsdp", "rep", None),
    )
    out_specs = (
        P("fsdp", "rep", None),
        P("fsdp", "rep", None),
        P("fsdp", None, None),
        P("fsdp", None, "rep"),
        P("fsdp"),
        P("fsdp", None, "rep"),
        P("fsdp"),
        P("fsdp", "rep"),
        P("fsdp"),
        P("fsdp", "rep"),
        P("fsdp"),
        P("fsdp", "rep"),
        P("fsdp"),
    )
    return jax.shard_map(local, mesh=mesh, in_specs=in_specs, out_specs=out_specs, check_vma=False)
```

```python
import functools
import math

import jax
import jax.numpy as jnp
from jax import lax
from jax.experimental import pallas as pl
from jax.experimental.pallas import tpu as pltpu
from jax.sharding import PartitionSpec as P

HEAD_DIM = 72


epsilon = 1e-06
highest = lax.Precision.HIGHEST
float_type = jnp.float32
brain_type = jnp.bfloat16


def layer_normed(values):
    center = jnp.mean(values, axis=-1, keepdims=True)
    shifted = values - center
    spread = jnp.mean(shifted * shifted, axis=-1, keepdims=True)
    return shifted * lax.rsqrt(spread + epsilon)


def modulated(values, shift_term, scale_term):
    return layer_normed(values) * (1.0 + scale_term) + shift_term


def gelu_tanh(values):
    return jax.nn.gelu(values, approximate=True)


def image_index(row_ends, positions):
    return jnp.sum((positions[..., :, None] >= row_ends[..., None, :-1]).astype(jnp.int32), axis=-1)


def across(left, right):
    return lax.dot_general(left, right, (((0,), (0,)), ((), ())), preferred_element_type=float_type)


def against(left, right):
    return lax.dot_general(left, right, (((1,), (1,)), ((), ())), preferred_element_type=float_type)


def column_sums(values):
    return jnp.sum(values.astype(float_type), axis=0)


def spread_columns(own_part, total, start):
    empty = jnp.zeros(own_part.shape[:-1] + (total,), float_type)
    return lax.dynamic_update_slice_in_dim(empty, own_part, start, own_part.ndim - 1)


def gather_block(*weights):
    return tuple(lax.all_gather(item, "fsdp", axis=0, tiled=True) for item in weights)


def plain_local(
    tokens,
    conditions,
    lengths,
    segments,
    condition_weight,
    condition_bias,
    input_weight,
    input_bias,
    attend_weight,
    attend_bias,
    expand_weight,
    expand_bias,
    reduce_weight,
    reduce_bias,
    cotangent,
):
    row_count, quarter, model_width = tokens.shape
    slot_count = conditions.shape[1]
    group_size = lax.axis_size("rep")
    group_place = lax.axis_index("rep")
    row_length = quarter * group_size
    own_width = condition_weight.shape[2]
    column_start = group_place * own_width
    hidden_width = expand_weight.shape[1]
    hidden_start = group_place * hidden_width
    local_heads = own_width // HEAD_DIM
    score_scale = 1.0 / math.sqrt(HEAD_DIM)
    patch_count = row_count * quarter
    image_count = row_count * slot_count
    key_place = jnp.arange(row_length, dtype=jnp.int32)
    row_ends = jnp.cumsum(lengths, axis=1, dtype=jnp.int32)
    row_images = image_index(row_ends, key_place)
    allowed = row_images[:, :, None] == row_images[:, None, :]

    def whole_rows(values):
        joined_rows = lax.all_gather(
            values.reshape(row_count, quarter, -1), "rep", axis=1, tiled=True
        )
        return joined_rows.reshape(row_count * row_length, -1)

    def own_rows(values):
        summed = lax.psum_scatter(
            values.reshape(row_count, row_length, -1), "rep", scatter_dimension=1, tiled=True
        )
        return summed.reshape(patch_count, -1)

    fsdp_size = lax.axis_size("fsdp")
    fsdp_place = lax.axis_index("fsdp")
    own_depth = condition_weight.shape[0]
    condition_values = conditions.astype(float_type)
    activated_own = jax.nn.silu(condition_values).reshape(image_count, model_width).astype(brain_type)
    activated_all = lax.all_gather(activated_own, "fsdp", axis=0, tiled=True)
    activated = lax.dynamic_slice_in_dim(activated_all, fsdp_place * own_depth, own_depth, 1)
    local_biases = (condition_bias, input_bias, attend_bias, expand_bias, reduce_bias)
    bias_sizes = [item.shape[0] for item in local_biases]
    bias_ends = [sum(bias_sizes[:k]) for k in range(len(bias_sizes) + 1)]
    bias_table = lax.all_gather(jnp.concatenate(local_biases), "fsdp", axis=0, tiled=False)
    condition_bias_all, input_bias_all, attend_bias_all, expand_bias_all, reduce_bias_all = [
        bias_table[:, low:high].reshape(-1) for low, high in zip(bias_ends[:-1], bias_ends[1:])
    ]
    condition_bias_own = lax.dynamic_slice_in_dim(
        condition_bias_all.reshape(6, model_width), column_start, own_width, 1
    )
    modulation_parts = jnp.einsum(
        "id,dkm->ikm", activated, condition_weight, preferred_element_type=float_type
    )
    modulation_own = (
        lax.psum_scatter(modulation_parts, "fsdp", scatter_dimension=0, tiled=True)
        + condition_bias_own[None]
    )
    modulation = lax.all_gather(modulation_own, "rep", axis=2, tiled=True).reshape(
        row_count, slot_count, -1
    )
    slot_table = (
        segments[:, :, None] == jnp.arange(slot_count, dtype=jnp.int32)[None, None, :]
    ).astype(float_type)
    per_token = jnp.einsum("rqs,rsm->rqm", slot_table, modulation, precision=highest).reshape(
        patch_count, -1
    )
    shift_one, scale_one, gate_one, shift_two, scale_two, gate_two = jnp.split(per_token, 6, axis=1)
    token_values = tokens.reshape(patch_count, model_width).astype(float_type)

    def split_heads(values):
        return values.reshape(row_count, row_length, local_heads, HEAD_DIM).transpose(2, 0, 1, 3)

    def merge_heads(values):
        return values.transpose(1, 2, 0, 3).reshape(row_count * row_length, own_width)

    def allowed_scores(query_head, key_head):
        scores = (
            jnp.einsum("rqd,rkd->rqk", query_head, key_head, preferred_element_type=float_type)
            * score_scale
        )
        return jnp.where(allowed, scores, -1e30)

    def head_forward(parts):
        query_head, key_head, value_head = parts
        scores = allowed_scores(query_head, key_head)
        row_max = jnp.max(scores, axis=-1, keepdims=True)
        powers = jnp.exp(scores - row_max)
        totals = jnp.sum(powers, axis=-1, keepdims=True)
        weights_low = (powers / totals).astype(brain_type)
        mixed = jnp.einsum(
            "rqk,rkd->rqd", weights_low, value_head, preferred_element_type=float_type
        )
        return (mixed, row_max + jnp.log(totals))

    def head_backward(parts):
        query_head, key_head, value_head, grad_head, log_head = parts
        scores = allowed_scores(query_head, key_head)
        probable = jnp.exp(scores - log_head)
        prob_grad = jnp.einsum(
            "rqd,rkd->rqk", grad_head, value_head, preferred_element_type=float_type
        )
        score_grad = (
            probable * (prob_grad - jnp.sum(probable * prob_grad, axis=-1, keepdims=True))
        ).astype(brain_type)
        query_part = (
            jnp.einsum("rqk,rkd->rqd", score_grad, key_head, preferred_element_type=float_type)
            * score_scale
        )
        key_part = (
            jnp.einsum("rqk,rqd->rkd", score_grad, query_head, preferred_element_type=float_type)
            * score_scale
        )
        value_part = jnp.einsum(
            "rqk,rqd->rkd",
            probable.astype(brain_type),
            grad_head,
            preferred_element_type=float_type,
        )
        return (query_part, key_part, value_part)

    def trunk(gathered):
        (
            input_all,
            input_bias_all,
            attend_all,
            attend_bias_all,
            expand_all,
            expand_bias_all,
            reduce_all,
            reduce_bias_all,
        ) = gathered
        bias_pair = lax.dynamic_slice_in_dim(
            input_bias_all.reshape(2, model_width), column_start, own_width, 1
        )
        expand_bias_own = lax.dynamic_slice_in_dim(expand_bias_all, hidden_start, hidden_width, 0)
        normed_one = modulated(token_values, shift_one, scale_one).astype(brain_type)
        whole_one = whole_rows(normed_one)
        joined = jnp.einsum("nd,dkm->nkm", whole_one, input_all, preferred_element_type=float_type)
        queries = (joined[:, 0] + bias_pair[0]).astype(brain_type)
        keys_row = joined[:, 1].astype(brain_type)
        values_row = (joined[:, 2] + bias_pair[1]).astype(brain_type)
        query_heads = split_heads(queries)
        key_heads = split_heads(keys_row)
        value_heads = split_heads(values_row)
        mixed, log_totals = lax.map(head_forward, (query_heads, key_heads, value_heads))
        attended = merge_heads(mixed).astype(brain_type)
        branch = own_rows(against(attended, attend_all)) + attend_bias_all
        middle = token_values + gate_one * branch
        normed_two = modulated(middle, shift_two, scale_two).astype(brain_type)
        whole_two = whole_rows(normed_two)
        inner = jnp.dot(whole_two, expand_all, preferred_element_type=float_type) + expand_bias_own
        active = gelu_tanh(inner).astype(brain_type)
        outer = own_rows(against(active, reduce_all)) + reduce_bias_all
        result = middle + gate_two * outer
        return (
            result,
            gathered,
            whole_one,
            query_heads,
            key_heads,
            value_heads,
            log_totals,
            attended,
            branch,
            middle,
            whole_two,
            inner,
            active,
            outer,
        )

    input_all, attend_all, expand_all, reduce_all = gather_block(
        input_weight, attend_weight, expand_weight, reduce_weight
    )
    state = trunk(
        (
            input_all,
            input_bias_all,
            attend_all,
            attend_bias_all,
            expand_all,
            expand_bias_all,
            reduce_all,
            reduce_bias_all,
        )
    )
    output = state[0].astype(brain_type).reshape(row_count, quarter, model_width)
    (
        _,
        gathered,
        whole_one,
        query_heads,
        key_heads,
        value_heads,
        log_totals,
        attended,
        branch,
        middle,
        whole_two,
        inner,
        active,
        outer,
    ) = state
    upstream = cotangent.reshape(patch_count, model_width).astype(float_type)
    outer_grad = (gate_two * upstream).astype(brain_type)
    gate_two_grad = upstream * outer
    outer_whole = whole_rows(outer_grad)
    reduce_grad = across(outer_whole, active)
    reduce_bias_grad = column_sums(outer_grad)
    active_grad = jnp.dot(outer_whole, reduce_all, preferred_element_type=float_type)
    _, gelu_back = jax.vjp(gelu_tanh, inner)
    inner_grad = gelu_back(active_grad)[0].astype(brain_type)
    expand_grad = across(whole_two, inner_grad)
    expand_bias_full = spread_columns(
        column_sums(inner_grad), hidden_width * group_size, hidden_start
    )
    two_grad = own_rows(against(inner_grad, expand_all))
    _, second_back = jax.vjp(modulated, middle, shift_two, scale_two)
    middle_norm_grad, shift_two_grad, scale_two_grad = second_back(two_grad)
    middle_grad = upstream + middle_norm_grad
    gate_one_grad = middle_grad * branch
    branch_grad = (gate_one * middle_grad).astype(brain_type)
    branch_whole = whole_rows(branch_grad)
    attend_grad = across(branch_whole, attended)
    attend_bias_grad = column_sums(branch_grad)
    attended_grad = jnp.dot(branch_whole, attend_all, preferred_element_type=float_type).astype(
        brain_type
    )
    grad_heads = split_heads(attended_grad)
    query_parts, key_parts, value_parts = lax.map(
        head_backward, (query_heads, key_heads, value_heads, grad_heads, log_totals)
    )
    query_low = merge_heads(query_parts).astype(brain_type)
    key_low = merge_heads(key_parts).astype(brain_type)
    value_low = merge_heads(value_parts).astype(brain_type)
    joined_grad = jnp.stack([query_low, key_low, value_low], axis=1)
    input_grad = jnp.einsum(
        "nd,nkm->dkm", whole_one, joined_grad, preferred_element_type=float_type
    )
    input_bias_pair = jnp.stack([column_sums(query_low), column_sums(value_low)])
    input_bias_full = spread_columns(input_bias_pair, model_width, column_start).reshape(-1)
    one_grad = own_rows(
        jnp.einsum("nkm,dkm->nd", joined_grad, input_all, preferred_element_type=float_type)
    )
    _, first_back = jax.vjp(modulated, token_values, shift_one, scale_one)
    token_norm_grad, shift_one_grad, scale_one_grad = first_back(one_grad)
    token_grad = (middle_grad + token_norm_grad).reshape(row_count, quarter, model_width)
    six_grads = jnp.stack(
        [
            shift_one_grad,
            scale_one_grad,
            gate_one_grad,
            shift_two_grad,
            scale_two_grad,
            gate_two_grad,
        ],
        axis=1,
    ).reshape(row_count, quarter, 6, model_width)
    modulation_part = jnp.einsum("rqs,rqkm->rskm", slot_table, six_grads, precision=highest)
    modulation_grad = lax.psum_scatter(modulation_part, "rep", scatter_dimension=3, tiled=True)
    modulation_low = lax.all_gather(
        modulation_grad.reshape(image_count, 6, own_width).astype(brain_type),
        "fsdp",
        axis=0,
        tiled=True,
    )
    condition_weight_final = jnp.einsum(
        "id,ikm->dkm", activated, modulation_low, preferred_element_type=float_type
    )
    condition_bias_full = lax.all_gather(
        column_sums(modulation_low), "rep", axis=1, tiled=True
    ).reshape(-1)
    bias_depth = condition_bias.shape[0]
    condition_bias_final = lax.dynamic_slice_in_dim(
        condition_bias_full, fsdp_place * bias_depth, bias_depth, 0
    )
    activated_part = jnp.einsum(
        "ikm,dkm->id", modulation_low, condition_weight, preferred_element_type=float_type
    )
    activated_wide = lax.all_to_all(
        activated_part.reshape(fsdp_size, image_count, own_depth), "fsdp", 0, 0
    )
    activated_row = jnp.transpose(activated_wide, (1, 0, 2)).reshape(image_count, model_width)
    bias_rows = jnp.concatenate(
        [
            item.reshape(fsdp_size, -1)
            for item in (input_bias_full, attend_bias_grad, expand_bias_full, reduce_bias_grad)
        ],
        axis=1,
    )
    bias_own = lax.psum_scatter(bias_rows, "fsdp", scatter_dimension=0, tiled=True).reshape(-1)
    activated_grad, bias_sum = lax.psum((activated_row, bias_own), "rep")
    input_bias_final, attend_bias_final, expand_bias_final, reduce_bias_final = jnp.split(
        bias_sum, [end - bias_sizes[0] for end in bias_ends[2:-1]]
    )
    input_final, attend_final, expand_final, reduce_final = [
        lax.psum_scatter(item.astype(brain_type), "fsdp", scatter_dimension=0, tiled=True).astype(
            float_type
        )
        for item in (input_grad, attend_grad, expand_grad, reduce_grad)
    ]
    _, silu_back = jax.vjp(jax.nn.silu, condition_values)
    condition_grad = silu_back(activated_grad.reshape(row_count, slot_count, model_width))[0]
    return (
        output,
        token_grad,
        condition_grad,
        condition_weight_final,
        condition_bias_final,
        input_final,
        input_bias_final,
        attend_final,
        attend_bias_final,
        expand_final,
        expand_bias_final,
        reduce_final,
        reduce_bias_final,
    )


MESH = pl.DeviceIdType.MESH
HEAD_PAD = 128
TOP_VMEM = 60 * 1024 * 1024


def aligned(index, step):
    return pl.ds(pl.multiple_of(index * step, step), step)


class Links:
    def __init__(self, fsdp_size, group_size):
        self.fsdp_size = fsdp_size
        self.group_size = group_size
        self.depth = fsdp_size // 2
        self.place = lax.axis_index("fsdp")
        self.member = lax.axis_index("rep")
        self.level = self.place // 2
        self.side = self.place % 2
        self.core = self.member % 2
        self.half = self.member // 2

    def to_place(self, place):
        return (place, self.member)

    def to_member(self, member):
        return (self.place, member)

    @property
    def core_mate(self):
        return self.half * 2 + 1 - self.core

    @property
    def half_mate(self):
        return (1 - self.half) * 2 + self.core

    @property
    def far_mate(self):
        return (1 - self.half) * 2 + 1 - self.core

    @property
    def side_mate(self):
        return self.level * 2 + 1 - self.side

    def level_at(self, shift):
        return lax.rem(self.level + shift + self.depth, self.depth)

    def meet(self):
        barrier = pltpu.get_barrier_semaphore()
        count = 0
        for shift in range(1, self.fsdp_size):
            target = lax.rem(self.place + shift, self.fsdp_size)
            pl.semaphore_signal(barrier, inc=1, device_id=self.to_place(target), device_id_type=MESH)
            count += 1
        for shift in range(1, self.group_size):
            target = lax.rem(self.member + shift, self.group_size)
            pl.semaphore_signal(barrier, inc=1, device_id=self.to_member(target), device_id_type=MESH)
            count += 1
        pl.semaphore_wait(barrier, count)


class Sends:
    def __init__(self, send_sems, recv_sems):
        self.send_sems = send_sems
        self.recv_sems = recv_sems
        self.used = 0
        self.open = []

    def slot(self):
        self.used += 1
        return self.used - 1

    def copy(self, slot, source, target, device):
        return pltpu.make_async_remote_copy(
            src_ref=source,
            dst_ref=target,
            send_sem=self.send_sems.at[slot],
            recv_sem=self.recv_sems.at[slot],
            device_id=device,
            device_id_type=MESH,
        )

    def start(self, slot, source, target, device):
        made = self.copy(slot, source, target, device)
        made.start()
        self.open.append(made)

    def arrived(self, slot, target, device):
        self.copy(slot, target, target, device).wait_recv()

    def finish(self):
        for made in self.open:
            made.wait_send()


class GroupGather:
    def __init__(self, links, sends, buffer, quarter):
        self.links, self.sends, self.buffer, self.quarter = links, sends, buffer, quarter
        self.slots = [sends.slot() for _ in range(3)]

    def rows(self, member):
        return self.buffer.at[aligned(member, self.quarter), :]

    def start_core(self):
        own = self.rows(self.links.member)
        mate = self.links.to_member(self.links.core_mate)
        self.sends.start(self.slots[0], own, own, mate)

    def start_half(self):
        own = self.rows(self.links.member)
        self.sends.start(self.slots[1], own, own, self.links.to_member(self.links.half_mate))

    def await_core(self):
        mate = self.links.core_mate
        self.sends.arrived(self.slots[0], self.rows(mate), self.links.to_member(mate))

    def pass_on(self):
        mate = self.links.half_mate
        self.sends.arrived(self.slots[1], self.rows(mate), self.links.to_member(mate))
        passed = self.rows(mate)
        self.sends.start(
            self.slots[2], passed, passed, self.links.to_member(self.links.core_mate)
        )

    def await_far(self):
        mate = self.links.core_mate
        self.sends.arrived(self.slots[2], self.rows(self.links.far_mate), self.links.to_member(mate))


class GroupSum:
    def __init__(self, links, sends, lent, got, crossing, crossed, total):
        self.links, self.sends = links, sends
        self.lent, self.got, self.crossing, self.crossed, self.total = (
            lent,
            got,
            crossing,
            crossed,
            total,
        )
        self.slots = [sends.slot() for _ in range(3)]

    def round(self, step, compute):
        links = self.links
        half = lax.rem(links.half + 1 - step + 2, 2)
        mate = links.to_member(links.core_mate)
        self.lent[step] = compute(half * 2 + 1 - links.core).astype(brain_type)
        self.sends.start(self.slots[step], self.lent.at[step], self.got.at[step], mate)
        self.total[...] = compute(half * 2 + links.core)
        self.sends.arrived(self.slots[step], self.got.at[step], mate)
        if step == 0:
            self.crossing[...] = (self.total[...] + self.got[0].astype(float_type)).astype(
                brain_type
            )
            self.sends.start(
                self.slots[2], self.crossing, self.crossed, links.to_member(links.half_mate)
            )

    def await_cross(self):
        self.sends.arrived(
            self.slots[2], self.crossed, self.links.to_member(self.links.half_mate)
        )

    def rows(self, rows):
        return (
            self.total[rows, :]
            + self.got[1, rows, :].astype(float_type)
            + self.crossed[rows, :].astype(float_type)
        )


def normed_rows(values):
    center = jnp.mean(values, axis=-1, keepdims=True)
    shifted = values - center
    spread = jnp.mean(shifted * shifted, axis=-1, keepdims=True)
    root = lax.rsqrt(spread + epsilon)
    return shifted * root, root


def spread_heads(source, target, rows, first, heads, target_first):
    for head in range(heads):
        low, to = HEAD_DIM * (first + head), HEAD_PAD * (target_first + head)
        target[rows, to : to + HEAD_DIM] = source[rows, low : low + HEAD_DIM]


def forward_kernel(
    sizes,
    tokens,
    upstream,
    act_send,
    cond_weight,
    bias_table,
    slot_mask,
    mask_bias,
    weight_zero,
    weight_one,
    weight_two,
    mod_out,
    bias_out,
    one_out,
    heads_out,
    log_out,
    mixed_out,
    branch_out,
    middle_out,
    two_out,
    upper_out,
    input_out,
    attend_out,
    expand_out,
    reduce_out,
    act_got,
    mod_parts,
    mod_got,
    mod_row,
    group_got,
    weights,
    normed,
    lent,
    got,
    crossing,
    crossed,
    total,
    one,
    two,
    upper,
    heads,
    mixed,
    input_pad,
    attend_pad,
    send_sems,
    recv_sems,
    local_sems,
):
    fsdp_size, group_size, quarter, width, own_width, shard = sizes
    links = Links(fsdp_size, group_size)
    sends = Sends(send_sems, recv_sems)
    blocks = (weight_zero, weight_one, weight_two)
    local_heads = own_width // HEAD_DIM
    head_span = local_heads * HEAD_PAD
    chunk = 32
    chunks = quarter // chunk

    act_slots = [sends.slot() for _ in range(fsdp_size)]
    mod_slots = [sends.slot() for _ in range(fsdp_size)]
    group_slots = [sends.slot() for _ in range(group_size)]
    level_slots = [[sends.slot() for _ in range(links.depth)] for _ in blocks]
    side_slots = [[sends.slot() for _ in range(links.depth)] for _ in blocks]
    gather_one = GroupGather(links, sends, one, quarter)
    gather_two = GroupGather(links, sends, two, quarter)
    gather_upper = GroupGather(links, sends, upper, quarter)
    branch_sum = GroupSum(links, sends, lent, got, crossing, crossed, total)
    opened = []

    def shard_rows(block, place):
        return weights.at[block, aligned(place, shard), :]

    def offer(block):
        own = shard_rows(block, links.place)
        for shift in range(1, links.depth):
            target = links.level_at(shift) * 2 + links.side
            sends.start(level_slots[block][shift], blocks[block], own, links.to_place(target))
        sends.start(side_slots[block][0], blocks[block], own, links.to_place(links.side_mate))
        kept = pltpu.make_async_copy(blocks[block], own, local_sems.at[block])
        kept.start()
        return kept

    def relay(block, shift):
        source = links.level_at(-shift) * 2 + links.side
        rows = shard_rows(block, source)
        sends.arrived(level_slots[block][shift], rows, links.to_place(source))
        sends.start(side_slots[block][shift], rows, rows, links.to_place(links.side_mate))
        return source

    def side_arrived(block, shift):
        source = links.level_at(-shift) * 2 + 1 - links.side
        sends.arrived(
            side_slots[block][shift], shard_rows(block, source), links.to_place(links.side_mate)
        )
        return source

    def keep(index, source, target):
        made = pltpu.make_async_copy(source, target, local_sems.at[index])
        made.start()
        opened.append(made)

    links.meet()
    for shift in range(1, fsdp_size):
        target = lax.rem(links.place + shift, fsdp_size)
        sends.start(
            act_slots[shift], act_send.at[target], act_got.at[links.place], links.to_place(target)
        )
    act_got[pl.ds(links.place, 1)] = act_send[pl.ds(links.place, 1)]
    kept_zero = offer(0)

    input_pad[...] = jnp.zeros_like(input_pad)
    attend_pad[...] = jnp.zeros_like(attend_pad)

    def norm_tokens(index, carry):
        rows = aligned(index, chunk)
        normed[rows, :] = normed_rows(tokens[rows, :].astype(float_type))[0]
        return carry

    lax.fori_loop(0, chunks, norm_tokens, 0)

    for shift in range(1, fsdp_size):
        source = lax.rem(links.place + fsdp_size - shift, fsdp_size)
        sends.arrived(act_slots[shift], act_got.at[source], links.to_place(source))
    activated = act_got[...].reshape(fsdp_size * 8, shard).astype(brain_type)
    mod_parts[...] = (
        jnp.dot(activated, cond_weight[...], preferred_element_type=float_type).reshape(
            fsdp_size, 8, 6 * own_width
        )
        + bias_table[...][None]
    )
    for shift in range(1, fsdp_size):
        target = lax.rem(links.place + shift, fsdp_size)
        sends.start(
            mod_slots[shift], mod_parts.at[target], mod_got.at[links.place], links.to_place(target)
        )
    mod_got[pl.ds(links.place, 1)] = mod_parts[pl.ds(links.place, 1)]
    kept_zero.wait()

    def spread_shard(place):
        rows = aligned(place, shard)
        spread_heads(weights.at[0], input_pad, rows, 0, 3 * local_heads, 0)
        spread_heads(weights.at[0], attend_pad, rows, 3 * local_heads, local_heads, 0)

    spread_shard(links.place)
    for shift in range(1, fsdp_size):
        source = lax.rem(links.place + fsdp_size - shift, fsdp_size)
        sends.arrived(mod_slots[shift], mod_got.at[source], links.to_place(source))
    summed = mod_got[0]
    for index in range(1, fsdp_size):
        summed = summed + mod_got[index]
    mod_row[...] = summed
    for shift in range(1, group_size):
        target = lax.rem(links.member + shift, group_size)
        sends.start(group_slots[shift], mod_row, group_got.at[links.member], links.to_member(target))
    group_got[pl.ds(links.member, 1)] = mod_row[...][None]
    bias_out[...] = mod_row[...]
    for shift in range(1, group_size):
        source = lax.rem(links.member + group_size - shift, group_size)
        sends.arrived(group_slots[shift], group_got.at[source], links.to_member(source))
    chosen = slot_mask[:, 0:1]
    for index in range(6):
        full = jnp.concatenate(
            [
                group_got[member, :, index * own_width : (index + 1) * own_width]
                for member in range(group_size)
            ],
            axis=1,
        )
        mod_out[index : index + 1, :] = jnp.sum(full * chosen, axis=0, keepdims=True)
    mod_out[6:8, :] = jnp.zeros((2, width), float_type)

    own_rows = links.member * quarter

    def first_norm(index, carry):
        rows = aligned(index, chunk)
        to = pl.ds(pl.multiple_of(own_rows + index * chunk, chunk), chunk)
        one[to, :] = (normed[rows, :] * (1.0 + mod_out[1:2, :]) + mod_out[0:1, :]).astype(brain_type)
        return carry

    lax.fori_loop(0, chunks, first_norm, 0)
    gather_one.start_half()
    gather_one.start_core()

    def upper_rows(index, carry):
        rows = aligned(index, chunk)
        to = pl.ds(pl.multiple_of(own_rows + index * chunk, chunk), chunk)
        upper[to, :] = (mod_out[5:6, :] * upstream[rows, :].astype(float_type)).astype(brain_type)
        return carry

    lax.fori_loop(0, chunks, upper_rows, 0)

    for shift in range(1, links.depth):
        spread_shard(relay(0, shift))
    kept_one = offer(1)
    gather_one.pass_on()
    gather_upper.start_half()
    gather_upper.start_core()
    gather_one.await_core()
    for shift in range(links.depth):
        spread_shard(side_arrived(0, shift))
    gather_one.await_far()
    keep(3, one, one_out)
    keep(4, input_pad, input_out)
    keep(5, attend_pad, attend_out)

    bias_pad = mod_row[7:8, 0 : 2 * head_span]

    def project(index, carry):
        rows = aligned(index, quarter)
        values = jnp.dot(one[rows, :], input_pad[...], preferred_element_type=float_type)
        heads[rows, 0:head_span] = (values[:, 0:head_span] + bias_pad[:, 0:head_span]).astype(
            brain_type
        )
        heads[rows, head_span : 2 * head_span] = values[:, head_span : 2 * head_span].astype(
            brain_type
        )
        heads[rows, 2 * head_span :] = (
            values[:, 2 * head_span :] + bias_pad[:, head_span:]
        ).astype(brain_type)
        return carry

    lax.fori_loop(0, group_size, project, 0)
    keep(6, heads, heads_out)

    power_scale = math.log2(math.e) / math.sqrt(HEAD_DIM)

    def attend(step, carry):
        head, part = step // group_size, step % group_size
        rows = aligned(part, quarter)

        def columns(base):
            return aligned(base * local_heads + head, HEAD_PAD)

        raw = lax.dot_general(
            heads[rows, columns(0)],
            heads[:, columns(1)],
            (((1,), (1,)), ((), ())),
            preferred_element_type=float_type,
        )
        scores = jnp.concatenate(
            [
                raw[:, other * quarter : (other + 1) * quarter] + mask_bias[part, other]
                for other in range(group_size)
            ],
            axis=1,
        )
        top = jnp.max(scores, axis=1, keepdims=True)
        powers = jnp.exp2(scores * power_scale - top * power_scale)
        totals = jnp.sum(powers, axis=1, keepdims=True)
        value = jnp.dot(
            powers.astype(brain_type), heads[:, columns(2)], preferred_element_type=float_type
        )
        mixed[rows, aligned(head, HEAD_PAD)] = (value / totals).astype(brain_type)
        log_out[head, rows, :] = top * power_scale + jnp.log2(totals)
        for shift in range(1, links.depth):

            @pl.when(step == 2 + 4 * shift)
            def _():
                relay_in_loop(1, shift)

        @pl.when(step == 4)
        def _():
            gather_upper_in_loop()

        return carry

    def relay_in_loop(block, shift):
        source = links.level_at(-shift) * 2 + links.side
        rows = shard_rows(block, source)
        sends.arrived(level_slots[block][shift], rows, links.to_place(source))
        sends.copy(
            side_slots[block][shift], rows, rows, links.to_place(links.side_mate)
        ).start()

    def gather_upper_in_loop():
        mate = links.half_mate
        passed = gather_upper.rows(mate)
        sends.arrived(gather_upper.slots[1], passed, links.to_member(mate))
        sends.copy(
            gather_upper.slots[2], passed, passed, links.to_member(links.core_mate)
        ).start()

    lax.fori_loop(0, local_heads * group_size, attend, 0)
    for shift in range(1, links.depth):
        source = links.level_at(-shift) * 2 + links.side
        rows = shard_rows(1, source)
        sends.open.append(
            sends.copy(side_slots[1][shift], rows, rows, links.to_place(links.side_mate))
        )
    passed = gather_upper.rows(links.half_mate)
    sends.open.append(
        sends.copy(gather_upper.slots[2], passed, passed, links.to_member(links.core_mate))
    )
    kept_two = offer(2)
    keep(7, mixed, mixed_out)

    def branch_part(member):
        return lax.dot_general(
            mixed[aligned(member, quarter), :],
            attend_pad[...],
            (((1,), (1,)), ((), ())),
            preferred_element_type=float_type,
        )

    branch_sum.round(0, branch_part)
    branch_sum.round(1, branch_part)
    gather_upper.await_core()
    gather_upper.await_far()
    keep(8, upper, upper_out)
    branch_sum.await_cross()

    def second_norm(index, carry):
        rows = aligned(index, chunk)
        to = pl.ds(pl.multiple_of(own_rows + index * chunk, chunk), chunk)
        branch = branch_sum.rows(rows) + mod_row[5:6, 0:width]
        branch_out[rows, :] = branch
        middle = tokens[rows, :].astype(float_type) + mod_out[2:3, :] * branch
        middle_out[rows, :] = middle
        two[to, :] = (normed_rows(middle)[0] * (1.0 + mod_out[4:5, :]) + mod_out[3:4, :]).astype(
            brain_type
        )
        return carry

    lax.fori_loop(0, chunks, second_norm, 0)
    gather_two.start_half()
    gather_two.start_core()
    for shift in range(1, links.depth):
        relay(2, shift)
    gather_two.pass_on()
    kept_one.wait()
    for shift in range(links.depth):
        side_arrived(1, shift)
    keep(9, weights.at[1], expand_out)
    gather_two.await_core()
    gather_two.await_far()
    keep(10, two, two_out)
    kept_two.wait()
    for shift in range(links.depth):
        side_arrived(2, shift)
    keep(11, weights.at[2], reduce_out)
    for made in opened:
        made.wait()
    sends.finish()


def run_forward(
    sizes, tokens, upstream, act_send, cond_weight, bias_table, slot_mask, mask_bias, weights
):
    fsdp_size, group_size, quarter, width, own_width, shard = sizes
    row_length = quarter * group_size
    local_heads = own_width // HEAD_DIM
    span = local_heads * HEAD_PAD
    hidden = weights[1].shape[1]
    in_vmem = pl.BlockSpec(memory_space=pltpu.VMEM)
    anywhere = pl.BlockSpec(memory_space=pl.ANY)
    shape = jax.ShapeDtypeStruct
    out_shape = (
        shape((8, width), float_type),
        shape((8, 6 * own_width), float_type),
        shape((row_length, width), brain_type),
        shape((row_length, 3 * span), brain_type),
        shape((local_heads, row_length, 1), float_type),
        shape((row_length, span), brain_type),
        shape((quarter, width), float_type),
        shape((quarter, width), float_type),
        shape((row_length, width), brain_type),
        shape((row_length, width), brain_type),
        shape((width, 3 * span), brain_type),
        shape((width, span), brain_type),
        shape((width, hidden), brain_type),
        shape((width, hidden), brain_type),
    )
    out_specs = (
        in_vmem,
        in_vmem,
        anywhere,
        anywhere,
        in_vmem,
        anywhere,
        in_vmem,
        in_vmem,
        anywhere,
        anywhere,
        anywhere,
        anywhere,
        anywhere,
        anywhere,
    )
    copies = 2 * fsdp_size + group_size + 6 * (fsdp_size // 2) + 3 * 3 + 3
    vmem = pltpu.VMEM
    scratch = [
        vmem((fsdp_size, 8, shard), float_type),
        vmem((fsdp_size, 8, 6 * own_width), float_type),
        vmem((fsdp_size, 8, 6 * own_width), float_type),
        vmem((8, 6 * own_width), float_type),
        vmem((group_size, 8, 6 * own_width), float_type),
        vmem((3, width, hidden), brain_type),
        vmem((quarter, width), float_type),
        vmem((2, quarter, width), brain_type),
        vmem((2, quarter, width), brain_type),
        vmem((quarter, width), brain_type),
        vmem((quarter, width), brain_type),
        vmem((quarter, width), float_type),
        vmem((row_length, width), brain_type),
        vmem((row_length, width), brain_type),
        vmem((row_length, width), brain_type),
        vmem((row_length, 3 * span), brain_type),
        vmem((row_length, span), brain_type),
        vmem((width, 3 * span), brain_type),
        vmem((width, span), brain_type),
        pltpu.SemaphoreType.DMA((copies,)),
        pltpu.SemaphoreType.DMA((copies,)),
        pltpu.SemaphoreType.DMA((12,)),
    ]
    return pl.pallas_call(
        functools.partial(forward_kernel, sizes),
        out_shape=out_shape,
        in_specs=[in_vmem] * 6 + [pl.BlockSpec(memory_space=pltpu.SMEM)] + [in_vmem] * 3,
        out_specs=out_specs,
        scratch_shapes=scratch,
        compiler_params=pltpu.CompilerParams(
            collective_id=0, has_side_effects=True, vmem_limit_bytes=TOP_VMEM
        ),
        name="forward_row",
    )(tokens, upstream, act_send, cond_weight, bias_table, slot_mask, mask_bias, *weights)


def fast_inputs(sizes, conditions, lengths, segments, condition_weight, biases):
    fsdp_size, group_size, quarter, width, own_width, shard = sizes
    place, member = lax.axis_index("fsdp"), lax.axis_index("rep")
    condition_bias, input_bias, attend_bias, expand_bias, reduce_bias = biases
    slot_count = conditions.shape[1]
    span = 6 * own_width
    column_start = member * own_width
    activated = jax.nn.silu(conditions[0].astype(float_type)).astype(brain_type).astype(float_type)
    act_send = jnp.pad(
        activated.reshape(slot_count, fsdp_size, shard).transpose(1, 0, 2),
        ((0, 0), (0, 8 - slot_count), (0, 0)),
    )

    def placed(own):
        empty = jnp.zeros((own.shape[0] * fsdp_size,), float_type)
        return lax.dynamic_update_slice_in_dim(
            empty, own.astype(float_type), place * own.shape[0], 0
        )

    def to_span(values):
        return jnp.pad(values, (0, span - values.shape[0]))

    condition_row = lax.dynamic_slice_in_dim(
        placed(condition_bias).reshape(6, width), column_start, own_width, 1
    ).reshape(-1)
    hidden = expand_bias.shape[0] * fsdp_size // group_size
    expand_row = lax.dynamic_slice_in_dim(placed(expand_bias), member * hidden, hidden, 0)
    pair = lax.dynamic_slice_in_dim(
        placed(input_bias).reshape(2, width), column_start, own_width, 1
    ).reshape(2, -1, HEAD_DIM)
    pair_row = jnp.pad(pair, ((0, 0), (0, 0), (0, HEAD_PAD - HEAD_DIM))).reshape(-1)
    bias_table = jnp.stack(
        [condition_row] * slot_count
        + [
            to_span(expand_row),
            to_span(placed(attend_bias)),
            to_span(placed(reduce_bias)),
            to_span(pair_row),
        ]
    )
    slot_mask = jnp.broadcast_to(
        (jnp.arange(8, dtype=jnp.int32) == segments[0, 0]).astype(float_type)[:, None], (8, 128)
    )
    row_ends = jnp.cumsum(lengths[0], dtype=jnp.int32)
    images = image_index(row_ends, jnp.arange(group_size, dtype=jnp.int32) * quarter)
    mask_bias = jnp.where(images[:, None] == images[None, :], 0.0, -1e30).astype(float_type)
    cond_flat = condition_weight.reshape(shard, span)
    return act_send, cond_flat, bias_table, slot_mask, mask_bias


def fast_local(
    tokens,
    conditions,
    lengths,
    segments,
    condition_weight,
    condition_bias,
    input_weight,
    input_bias,
    attend_weight,
    attend_bias,
    expand_weight,
    expand_bias,
    reduce_weight,
    reduce_bias,
    cotangent,
):
    row_count, quarter, model_width = tokens.shape
    slot_count = conditions.shape[1]
    group_size = lax.axis_size("rep")
    group_place = lax.axis_index("rep")
    fsdp_size = lax.axis_size("fsdp")
    fsdp_place = lax.axis_index("fsdp")
    row_length = quarter * group_size
    own_depth, _, own_width = condition_weight.shape
    column_start = group_place * own_width
    hidden_width = expand_weight.shape[1]
    hidden_start = group_place * hidden_width
    local_heads = own_width // HEAD_DIM
    score_scale = 1.0 / math.sqrt(HEAD_DIM)
    patch_count = quarter
    image_count = slot_count
    sizes = (fsdp_size, group_size, quarter, model_width, own_width, own_depth)
    act_send, cond_flat, bias_table, slot_mask, mask_bias = fast_inputs(
        sizes,
        conditions,
        lengths,
        segments,
        condition_weight,
        (condition_bias, input_bias, attend_bias, expand_bias, reduce_bias),
    )
    weight_zero = jnp.concatenate([input_weight.reshape(own_depth, -1), attend_weight], axis=1)
    upstream_low = cotangent.reshape(quarter, model_width)
    (
        mods,
        bias_rows,
        whole_one,
        heads,
        log_rows,
        attended_pad,
        branch,
        middle,
        whole_two,
        outer_whole,
        input_pad,
        attend_pad,
        expand_all,
        reduce_all,
    ) = run_forward(
        sizes,
        tokens.reshape(quarter, model_width),
        upstream_low,
        act_send,
        cond_flat,
        bias_table,
        slot_mask,
        mask_bias,
        (weight_zero, expand_weight, reduce_weight),
    )
    shift_one, scale_one, gate_one, shift_two, scale_two, gate_two = [
        jnp.broadcast_to(mods[k : k + 1], (quarter, model_width)) for k in range(6)
    ]
    input_all = input_pad.reshape(model_width, 3, local_heads, HEAD_PAD)[..., :HEAD_DIM].reshape(
        model_width, 3, own_width
    )
    attend_all = attend_pad.reshape(model_width, local_heads, HEAD_PAD)[..., :HEAD_DIM].reshape(
        model_width, own_width
    )
    attended = attended_pad.reshape(row_length, local_heads, HEAD_PAD)[..., :HEAD_DIM].reshape(
        row_length, own_width
    )
    expand_bias_own = bias_rows[4, :hidden_width]
    reduce_bias_all = bias_rows[6, :model_width]
    joined_heads = heads.reshape(row_length, 3, local_heads, HEAD_PAD)[..., :HEAD_DIM]
    query_heads, key_heads, value_heads = [
        joined_heads[:, k].transpose(1, 0, 2)[:, None] for k in range(3)
    ]
    log_totals = log_rows[:, None] * math.log(2.0)
    token_values = tokens.reshape(patch_count, model_width).astype(float_type)
    key_place = jnp.arange(row_length, dtype=jnp.int32)
    row_ends = jnp.cumsum(lengths, axis=1, dtype=jnp.int32)
    row_images = image_index(row_ends, key_place)
    allowed = row_images[:, :, None] == row_images[:, None, :]
    slot_table = (
        segments[:, :, None] == jnp.arange(slot_count, dtype=jnp.int32)[None, None, :]
    ).astype(float_type)

    def whole_rows(values):
        return lax.all_gather(values, "rep", axis=0, tiled=True)

    def own_rows(values):
        return lax.psum_scatter(values, "rep", scatter_dimension=0, tiled=True)

    def split_heads(values):
        return values.reshape(row_count, row_length, local_heads, HEAD_DIM).transpose(2, 0, 1, 3)

    def merge_heads(values):
        return values.transpose(1, 2, 0, 3).reshape(row_count * row_length, own_width)

    def head_backward(parts):
        query_head, key_head, value_head, grad_head, log_head = parts
        scores = (
            jnp.einsum("rqd,rkd->rqk", query_head, key_head, preferred_element_type=float_type)
            * score_scale
        )
        scores = jnp.where(allowed, scores, -1e30)
        probable = jnp.exp(scores - log_head)
        prob_grad = jnp.einsum(
            "rqd,rkd->rqk", grad_head, value_head, preferred_element_type=float_type
        )
        score_grad = (
            probable * (prob_grad - jnp.sum(probable * prob_grad, axis=-1, keepdims=True))
        ).astype(brain_type)
        query_part = (
            jnp.einsum("rqk,rkd->rqd", score_grad, key_head, preferred_element_type=float_type)
            * score_scale
        )
        key_part = (
            jnp.einsum("rqk,rqd->rkd", score_grad, query_head, preferred_element_type=float_type)
            * score_scale
        )
        value_part = jnp.einsum(
            "rqk,rqd->rkd",
            probable.astype(brain_type),
            grad_head,
            preferred_element_type=float_type,
        )
        return (query_part, key_part, value_part)

    inner = jnp.dot(whole_two, expand_all, preferred_element_type=float_type) + expand_bias_own
    active = gelu_tanh(inner).astype(brain_type)
    outer = own_rows(against(active, reduce_all)) + reduce_bias_all
    result = middle + gate_two * outer
    output = result.astype(brain_type).reshape(row_count, quarter, model_width)
    upstream = upstream_low.astype(float_type)
    gate_two_grad = upstream * outer
    outer_grad = (gate_two * upstream).astype(brain_type)
    reduce_grad = across(outer_whole, active)
    reduce_bias_grad = column_sums(outer_grad)
    active_grad = jnp.dot(outer_whole, reduce_all, preferred_element_type=float_type)
    _, gelu_back = jax.vjp(gelu_tanh, inner)
    inner_grad = gelu_back(active_grad)[0].astype(brain_type)
    expand_grad = across(whole_two, inner_grad)
    expand_bias_full = spread_columns(
        column_sums(inner_grad), hidden_width * group_size, hidden_start
    )
    two_grad = own_rows(against(inner_grad, expand_all))
    _, second_back = jax.vjp(modulated, middle, shift_two, scale_two)
    middle_norm_grad, shift_two_grad, scale_two_grad = second_back(two_grad)
    middle_grad = upstream + middle_norm_grad
    gate_one_grad = middle_grad * branch
    branch_grad = (gate_one * middle_grad).astype(brain_type)
    branch_whole = whole_rows(branch_grad)
    attend_grad = across(branch_whole, attended)
    attend_bias_grad = column_sums(branch_grad)
    attended_grad = jnp.dot(branch_whole, attend_all, preferred_element_type=float_type).astype(
        brain_type
    )
    grad_heads = split_heads(attended_grad)
    query_parts, key_parts, value_parts = lax.map(
        head_backward, (query_heads, key_heads, value_heads, grad_heads, log_totals)
    )
    query_low = merge_heads(query_parts).astype(brain_type)
    key_low = merge_heads(key_parts).astype(brain_type)
    value_low = merge_heads(value_parts).astype(brain_type)
    joined_grad = jnp.stack([query_low, key_low, value_low], axis=1)
    input_grad = jnp.einsum(
        "nd,nkm->dkm", whole_one, joined_grad, preferred_element_type=float_type
    )
    input_bias_pair = jnp.stack([column_sums(query_low), column_sums(value_low)])
    input_bias_full = spread_columns(input_bias_pair, model_width, column_start).reshape(-1)
    one_grad = own_rows(
        jnp.einsum("nkm,dkm->nd", joined_grad, input_all, preferred_element_type=float_type)
    )
    _, first_back = jax.vjp(modulated, token_values, shift_one, scale_one)
    token_norm_grad, shift_one_grad, scale_one_grad = first_back(one_grad)
    token_grad = (middle_grad + token_norm_grad).reshape(row_count, quarter, model_width)
    six_grads = jnp.stack(
        [
            shift_one_grad,
            scale_one_grad,
            gate_one_grad,
            shift_two_grad,
            scale_two_grad,
            gate_two_grad,
        ],
        axis=1,
    ).reshape(row_count, quarter, 6, model_width)
    condition_values = conditions.astype(float_type)
    activated_own = jax.nn.silu(condition_values).reshape(image_count, model_width)
    activated_all = lax.all_gather(activated_own.astype(brain_type), "fsdp", axis=0, tiled=True)
    activated = lax.dynamic_slice_in_dim(activated_all, fsdp_place * own_depth, own_depth, 1)
    modulation_part = jnp.einsum("rqs,rqkm->rskm", slot_table, six_grads, precision=highest)
    bias_sizes = [
        item.shape[0] for item in (condition_bias, input_bias, attend_bias, expand_bias, reduce_bias)
    ]
    bias_ends = [sum(bias_sizes[:k]) for k in range(len(bias_sizes) + 1)]
    modulation_grad = lax.psum_scatter(modulation_part, "rep", scatter_dimension=3, tiled=True)
    modulation_low = lax.all_gather(
        modulation_grad.reshape(image_count, 6, own_width).astype(brain_type),
        "fsdp",
        axis=0,
        tiled=True,
    )
    condition_weight_final = jnp.einsum(
        "id,ikm->dkm", activated, modulation_low, preferred_element_type=float_type
    )
    condition_bias_full = lax.all_gather(
        column_sums(modulation_low), "rep", axis=1, tiled=True
    ).reshape(-1)
    bias_depth = condition_bias.shape[0]
    condition_bias_final = lax.dynamic_slice_in_dim(
        condition_bias_full, fsdp_place * bias_depth, bias_depth, 0
    )
    activated_part = jnp.einsum(
        "ikm,dkm->id", modulation_low, condition_weight, preferred_element_type=float_type
    )
    activated_wide = lax.all_to_all(
        activated_part.reshape(fsdp_size, image_count, own_depth), "fsdp", 0, 0
    )
    activated_row = jnp.transpose(activated_wide, (1, 0, 2)).reshape(image_count, model_width)
    bias_rows = jnp.concatenate(
        [
            item.reshape(fsdp_size, -1)
            for item in (input_bias_full, attend_bias_grad, expand_bias_full, reduce_bias_grad)
        ],
        axis=1,
    )
    bias_own = lax.psum_scatter(bias_rows, "fsdp", scatter_dimension=0, tiled=True).reshape(-1)
    activated_grad, bias_sum = lax.psum((activated_row, bias_own), "rep")
    input_bias_final, attend_bias_final, expand_bias_final, reduce_bias_final = jnp.split(
        bias_sum, [end - bias_sizes[0] for end in bias_ends[2:-1]]
    )
    input_final, attend_final, expand_final, reduce_final = [
        lax.psum_scatter(item.astype(brain_type), "fsdp", scatter_dimension=0, tiled=True).astype(
            float_type
        )
        for item in (input_grad, attend_grad, expand_grad, reduce_grad)
    ]
    _, silu_back = jax.vjp(jax.nn.silu, condition_values)
    condition_grad = silu_back(activated_grad.reshape(row_count, slot_count, model_width))[0]
    return (
        output,
        token_grad,
        condition_grad,
        condition_weight_final,
        condition_bias_final,
        input_final,
        input_bias_final,
        attend_final,
        attend_bias_final,
        expand_final,
        expand_bias_final,
        reduce_final,
        reduce_bias_final,
    )


def solution(mesh):
    in_specs = (
        P("fsdp", "rep", None),
        P("fsdp", None, None),
        P("fsdp", None),
        P("fsdp", "rep"),
        P("fsdp", None, "rep"),
        P("fsdp"),
        P("fsdp", None, "rep"),
        P("fsdp"),
        P("fsdp", "rep"),
        P("fsdp"),
        P("fsdp", "rep"),
        P("fsdp"),
        P("fsdp", "rep"),
        P("fsdp"),
        P("fsdp", "rep", None),
    )
    out_specs = (
        P("fsdp", "rep", None),
        P("fsdp", "rep", None),
        P("fsdp", None, None),
        P("fsdp", None, "rep"),
        P("fsdp"),
        P("fsdp", None, "rep"),
        P("fsdp"),
        P("fsdp", "rep"),
        P("fsdp"),
        P("fsdp", "rep"),
        P("fsdp"),
        P("fsdp", "rep"),
        P("fsdp"),
    )
    local = fast_local if mesh.shape["fsdp"] == 8 else plain_local
    return jax.shard_map(local, mesh=mesh, in_specs=in_specs, out_specs=out_specs, check_vma=False)
```

```python
import functools
import math

import jax
import jax.numpy as jnp
from jax import lax
from jax.experimental import pallas as pl
from jax.experimental.pallas import tpu as pltpu
from jax.sharding import PartitionSpec as P

HEAD_DIM = 72


epsilon = 1e-06
highest = lax.Precision.HIGHEST
float_type = jnp.float32
brain_type = jnp.bfloat16


def layer_normed(values):
    center = jnp.mean(values, axis=-1, keepdims=True)
    shifted = values - center
    spread = jnp.mean(shifted * shifted, axis=-1, keepdims=True)
    return shifted * lax.rsqrt(spread + epsilon)


def modulated(values, shift_term, scale_term):
    return layer_normed(values) * (1.0 + scale_term) + shift_term


def gelu_tanh(values):
    return jax.nn.gelu(values, approximate=True)


def image_index(row_ends, positions):
    return jnp.sum((positions[..., :, None] >= row_ends[..., None, :-1]).astype(jnp.int32), axis=-1)


def across(left, right):
    return lax.dot_general(left, right, (((0,), (0,)), ((), ())), preferred_element_type=float_type)


def against(left, right):
    return lax.dot_general(left, right, (((1,), (1,)), ((), ())), preferred_element_type=float_type)


def column_sums(values):
    return jnp.sum(values.astype(float_type), axis=0)


def spread_columns(own_part, total, start):
    empty = jnp.zeros(own_part.shape[:-1] + (total,), float_type)
    return lax.dynamic_update_slice_in_dim(empty, own_part, start, own_part.ndim - 1)


def gather_block(*weights):
    return tuple(lax.all_gather(item, "fsdp", axis=0, tiled=True) for item in weights)


def plain_local(
    tokens,
    conditions,
    lengths,
    segments,
    condition_weight,
    condition_bias,
    input_weight,
    input_bias,
    attend_weight,
    attend_bias,
    expand_weight,
    expand_bias,
    reduce_weight,
    reduce_bias,
    cotangent,
):
    row_count, quarter, model_width = tokens.shape
    slot_count = conditions.shape[1]
    group_size = lax.axis_size("rep")
    group_place = lax.axis_index("rep")
    row_length = quarter * group_size
    own_width = condition_weight.shape[2]
    column_start = group_place * own_width
    hidden_width = expand_weight.shape[1]
    hidden_start = group_place * hidden_width
    local_heads = own_width // HEAD_DIM
    score_scale = 1.0 / math.sqrt(HEAD_DIM)
    patch_count = row_count * quarter
    image_count = row_count * slot_count
    key_place = jnp.arange(row_length, dtype=jnp.int32)
    row_ends = jnp.cumsum(lengths, axis=1, dtype=jnp.int32)
    row_images = image_index(row_ends, key_place)
    allowed = row_images[:, :, None] == row_images[:, None, :]

    def whole_rows(values):
        joined_rows = lax.all_gather(
            values.reshape(row_count, quarter, -1), "rep", axis=1, tiled=True
        )
        return joined_rows.reshape(row_count * row_length, -1)

    def own_rows(values):
        summed = lax.psum_scatter(
            values.reshape(row_count, row_length, -1), "rep", scatter_dimension=1, tiled=True
        )
        return summed.reshape(patch_count, -1)

    fsdp_size = lax.axis_size("fsdp")
    fsdp_place = lax.axis_index("fsdp")
    own_depth = condition_weight.shape[0]
    condition_values = conditions.astype(float_type)
    activated_own = jax.nn.silu(condition_values).reshape(image_count, model_width).astype(brain_type)
    activated_all = lax.all_gather(activated_own, "fsdp", axis=0, tiled=True)
    activated = lax.dynamic_slice_in_dim(activated_all, fsdp_place * own_depth, own_depth, 1)
    local_biases = (condition_bias, input_bias, attend_bias, expand_bias, reduce_bias)
    bias_sizes = [item.shape[0] for item in local_biases]
    bias_ends = [sum(bias_sizes[:k]) for k in range(len(bias_sizes) + 1)]
    bias_table = lax.all_gather(jnp.concatenate(local_biases), "fsdp", axis=0, tiled=False)
    condition_bias_all, input_bias_all, attend_bias_all, expand_bias_all, reduce_bias_all = [
        bias_table[:, low:high].reshape(-1) for low, high in zip(bias_ends[:-1], bias_ends[1:])
    ]
    condition_bias_own = lax.dynamic_slice_in_dim(
        condition_bias_all.reshape(6, model_width), column_start, own_width, 1
    )
    modulation_parts = jnp.einsum(
        "id,dkm->ikm", activated, condition_weight, preferred_element_type=float_type
    )
    modulation_own = (
        lax.psum_scatter(modulation_parts, "fsdp", scatter_dimension=0, tiled=True)
        + condition_bias_own[None]
    )
    modulation = lax.all_gather(modulation_own, "rep", axis=2, tiled=True).reshape(
        row_count, slot_count, -1
    )
    slot_table = (
        segments[:, :, None] == jnp.arange(slot_count, dtype=jnp.int32)[None, None, :]
    ).astype(float_type)
    per_token = jnp.einsum("rqs,rsm->rqm", slot_table, modulation, precision=highest).reshape(
        patch_count, -1
    )
    shift_one, scale_one, gate_one, shift_two, scale_two, gate_two = jnp.split(per_token, 6, axis=1)
    token_values = tokens.reshape(patch_count, model_width).astype(float_type)

    def split_heads(values):
        return values.reshape(row_count, row_length, local_heads, HEAD_DIM).transpose(2, 0, 1, 3)

    def merge_heads(values):
        return values.transpose(1, 2, 0, 3).reshape(row_count * row_length, own_width)

    def allowed_scores(query_head, key_head):
        scores = (
            jnp.einsum("rqd,rkd->rqk", query_head, key_head, preferred_element_type=float_type)
            * score_scale
        )
        return jnp.where(allowed, scores, -1e30)

    def head_forward(parts):
        query_head, key_head, value_head = parts
        scores = allowed_scores(query_head, key_head)
        row_max = jnp.max(scores, axis=-1, keepdims=True)
        powers = jnp.exp(scores - row_max)
        totals = jnp.sum(powers, axis=-1, keepdims=True)
        weights_low = (powers / totals).astype(brain_type)
        mixed = jnp.einsum(
            "rqk,rkd->rqd", weights_low, value_head, preferred_element_type=float_type
        )
        return (mixed, row_max + jnp.log(totals))

    def head_backward(parts):
        query_head, key_head, value_head, grad_head, log_head = parts
        scores = allowed_scores(query_head, key_head)
        probable = jnp.exp(scores - log_head)
        prob_grad = jnp.einsum(
            "rqd,rkd->rqk", grad_head, value_head, preferred_element_type=float_type
        )
        score_grad = (
            probable * (prob_grad - jnp.sum(probable * prob_grad, axis=-1, keepdims=True))
        ).astype(brain_type)
        query_part = (
            jnp.einsum("rqk,rkd->rqd", score_grad, key_head, preferred_element_type=float_type)
            * score_scale
        )
        key_part = (
            jnp.einsum("rqk,rqd->rkd", score_grad, query_head, preferred_element_type=float_type)
            * score_scale
        )
        value_part = jnp.einsum(
            "rqk,rqd->rkd",
            probable.astype(brain_type),
            grad_head,
            preferred_element_type=float_type,
        )
        return (query_part, key_part, value_part)

    def trunk(gathered):
        (
            input_all,
            input_bias_all,
            attend_all,
            attend_bias_all,
            expand_all,
            expand_bias_all,
            reduce_all,
            reduce_bias_all,
        ) = gathered
        bias_pair = lax.dynamic_slice_in_dim(
            input_bias_all.reshape(2, model_width), column_start, own_width, 1
        )
        expand_bias_own = lax.dynamic_slice_in_dim(expand_bias_all, hidden_start, hidden_width, 0)
        normed_one = modulated(token_values, shift_one, scale_one).astype(brain_type)
        whole_one = whole_rows(normed_one)
        joined = jnp.einsum("nd,dkm->nkm", whole_one, input_all, preferred_element_type=float_type)
        queries = (joined[:, 0] + bias_pair[0]).astype(brain_type)
        keys_row = joined[:, 1].astype(brain_type)
        values_row = (joined[:, 2] + bias_pair[1]).astype(brain_type)
        query_heads = split_heads(queries)
        key_heads = split_heads(keys_row)
        value_heads = split_heads(values_row)
        mixed, log_totals = lax.map(head_forward, (query_heads, key_heads, value_heads))
        attended = merge_heads(mixed).astype(brain_type)
        branch = own_rows(against(attended, attend_all)) + attend_bias_all
        middle = token_values + gate_one * branch
        normed_two = modulated(middle, shift_two, scale_two).astype(brain_type)
        whole_two = whole_rows(normed_two)
        inner = jnp.dot(whole_two, expand_all, preferred_element_type=float_type) + expand_bias_own
        active = gelu_tanh(inner).astype(brain_type)
        outer = own_rows(against(active, reduce_all)) + reduce_bias_all
        result = middle + gate_two * outer
        return (
            result,
            gathered,
            whole_one,
            query_heads,
            key_heads,
            value_heads,
            log_totals,
            attended,
            branch,
            middle,
            whole_two,
            inner,
            active,
            outer,
        )

    input_all, attend_all, expand_all, reduce_all = gather_block(
        input_weight, attend_weight, expand_weight, reduce_weight
    )
    state = trunk(
        (
            input_all,
            input_bias_all,
            attend_all,
            attend_bias_all,
            expand_all,
            expand_bias_all,
            reduce_all,
            reduce_bias_all,
        )
    )
    output = state[0].astype(brain_type).reshape(row_count, quarter, model_width)
    (
        _,
        gathered,
        whole_one,
        query_heads,
        key_heads,
        value_heads,
        log_totals,
        attended,
        branch,
        middle,
        whole_two,
        inner,
        active,
        outer,
    ) = state
    upstream = cotangent.reshape(patch_count, model_width).astype(float_type)
    outer_grad = (gate_two * upstream).astype(brain_type)
    gate_two_grad = upstream * outer
    outer_whole = whole_rows(outer_grad)
    reduce_grad = across(outer_whole, active)
    reduce_bias_grad = column_sums(outer_grad)
    active_grad = jnp.dot(outer_whole, reduce_all, preferred_element_type=float_type)
    _, gelu_back = jax.vjp(gelu_tanh, inner)
    inner_grad = gelu_back(active_grad)[0].astype(brain_type)
    expand_grad = across(whole_two, inner_grad)
    expand_bias_full = spread_columns(
        column_sums(inner_grad), hidden_width * group_size, hidden_start
    )
    two_grad = own_rows(against(inner_grad, expand_all))
    _, second_back = jax.vjp(modulated, middle, shift_two, scale_two)
    middle_norm_grad, shift_two_grad, scale_two_grad = second_back(two_grad)
    middle_grad = upstream + middle_norm_grad
    gate_one_grad = middle_grad * branch
    branch_grad = (gate_one * middle_grad).astype(brain_type)
    branch_whole = whole_rows(branch_grad)
    attend_grad = across(branch_whole, attended)
    attend_bias_grad = column_sums(branch_grad)
    attended_grad = jnp.dot(branch_whole, attend_all, preferred_element_type=float_type).astype(
        brain_type
    )
    grad_heads = split_heads(attended_grad)
    query_parts, key_parts, value_parts = lax.map(
        head_backward, (query_heads, key_heads, value_heads, grad_heads, log_totals)
    )
    query_low = merge_heads(query_parts).astype(brain_type)
    key_low = merge_heads(key_parts).astype(brain_type)
    value_low = merge_heads(value_parts).astype(brain_type)
    joined_grad = jnp.stack([query_low, key_low, value_low], axis=1)
    input_grad = jnp.einsum(
        "nd,nkm->dkm", whole_one, joined_grad, preferred_element_type=float_type
    )
    input_bias_pair = jnp.stack([column_sums(query_low), column_sums(value_low)])
    input_bias_full = spread_columns(input_bias_pair, model_width, column_start).reshape(-1)
    one_grad = own_rows(
        jnp.einsum("nkm,dkm->nd", joined_grad, input_all, preferred_element_type=float_type)
    )
    _, first_back = jax.vjp(modulated, token_values, shift_one, scale_one)
    token_norm_grad, shift_one_grad, scale_one_grad = first_back(one_grad)
    token_grad = (middle_grad + token_norm_grad).reshape(row_count, quarter, model_width)
    six_grads = jnp.stack(
        [
            shift_one_grad,
            scale_one_grad,
            gate_one_grad,
            shift_two_grad,
            scale_two_grad,
            gate_two_grad,
        ],
        axis=1,
    ).reshape(row_count, quarter, 6, model_width)
    modulation_part = jnp.einsum("rqs,rqkm->rskm", slot_table, six_grads, precision=highest)
    modulation_grad = lax.psum_scatter(modulation_part, "rep", scatter_dimension=3, tiled=True)
    modulation_low = lax.all_gather(
        modulation_grad.reshape(image_count, 6, own_width).astype(brain_type),
        "fsdp",
        axis=0,
        tiled=True,
    )
    condition_weight_final = jnp.einsum(
        "id,ikm->dkm", activated, modulation_low, preferred_element_type=float_type
    )
    condition_bias_full = lax.all_gather(
        column_sums(modulation_low), "rep", axis=1, tiled=True
    ).reshape(-1)
    bias_depth = condition_bias.shape[0]
    condition_bias_final = lax.dynamic_slice_in_dim(
        condition_bias_full, fsdp_place * bias_depth, bias_depth, 0
    )
    activated_part = jnp.einsum(
        "ikm,dkm->id", modulation_low, condition_weight, preferred_element_type=float_type
    )
    activated_wide = lax.all_to_all(
        activated_part.reshape(fsdp_size, image_count, own_depth), "fsdp", 0, 0
    )
    activated_row = jnp.transpose(activated_wide, (1, 0, 2)).reshape(image_count, model_width)
    bias_rows = jnp.concatenate(
        [
            item.reshape(fsdp_size, -1)
            for item in (input_bias_full, attend_bias_grad, expand_bias_full, reduce_bias_grad)
        ],
        axis=1,
    )
    bias_own = lax.psum_scatter(bias_rows, "fsdp", scatter_dimension=0, tiled=True).reshape(-1)
    activated_grad, bias_sum = lax.psum((activated_row, bias_own), "rep")
    input_bias_final, attend_bias_final, expand_bias_final, reduce_bias_final = jnp.split(
        bias_sum, [end - bias_sizes[0] for end in bias_ends[2:-1]]
    )
    input_final, attend_final, expand_final, reduce_final = [
        lax.psum_scatter(item.astype(brain_type), "fsdp", scatter_dimension=0, tiled=True).astype(
            float_type
        )
        for item in (input_grad, attend_grad, expand_grad, reduce_grad)
    ]
    _, silu_back = jax.vjp(jax.nn.silu, condition_values)
    condition_grad = silu_back(activated_grad.reshape(row_count, slot_count, model_width))[0]
    return (
        output,
        token_grad,
        condition_grad,
        condition_weight_final,
        condition_bias_final,
        input_final,
        input_bias_final,
        attend_final,
        attend_bias_final,
        expand_final,
        expand_bias_final,
        reduce_final,
        reduce_bias_final,
    )


MESH = pl.DeviceIdType.MESH
HEAD_PAD = 128
TOP_VMEM = 60 * 1024 * 1024


def aligned(index, step):
    return pl.ds(pl.multiple_of(index * step, step), step)


class Links:
    def __init__(self, fsdp_size, group_size):
        self.fsdp_size = fsdp_size
        self.group_size = group_size
        self.depth = fsdp_size // 2
        self.place = lax.axis_index("fsdp")
        self.member = lax.axis_index("rep")
        self.level = self.place // 2
        self.side = self.place % 2
        self.core = self.member % 2
        self.half = self.member // 2

    def to_place(self, place):
        return (place, self.member)

    def to_member(self, member):
        return (self.place, member)

    @property
    def core_mate(self):
        return self.half * 2 + 1 - self.core

    @property
    def half_mate(self):
        return (1 - self.half) * 2 + self.core

    @property
    def far_mate(self):
        return (1 - self.half) * 2 + 1 - self.core

    @property
    def side_mate(self):
        return self.level * 2 + 1 - self.side

    def level_at(self, shift):
        return lax.rem(self.level + shift + self.depth, self.depth)

    def meet(self):
        barrier = pltpu.get_barrier_semaphore()
        count = 0
        for shift in range(1, self.fsdp_size):
            target = lax.rem(self.place + shift, self.fsdp_size)
            pl.semaphore_signal(barrier, inc=1, device_id=self.to_place(target), device_id_type=MESH)
            count += 1
        for shift in range(1, self.group_size):
            target = lax.rem(self.member + shift, self.group_size)
            pl.semaphore_signal(barrier, inc=1, device_id=self.to_member(target), device_id_type=MESH)
            count += 1
        pl.semaphore_wait(barrier, count)


class Sends:
    def __init__(self, send_sems, recv_sems):
        self.send_sems = send_sems
        self.recv_sems = recv_sems
        self.used = 0
        self.open = []

    def slot(self):
        self.used += 1
        return self.used - 1

    def copy(self, slot, source, target, device):
        return pltpu.make_async_remote_copy(
            src_ref=source,
            dst_ref=target,
            send_sem=self.send_sems.at[slot],
            recv_sem=self.recv_sems.at[slot],
            device_id=device,
            device_id_type=MESH,
        )

    def start(self, slot, source, target, device):
        made = self.copy(slot, source, target, device)
        made.start()
        self.open.append(made)

    def arrived(self, slot, target, device):
        self.copy(slot, target, target, device).wait_recv()

    def finish(self):
        for made in self.open:
            made.wait_send()


class GroupGather:
    def __init__(self, links, sends, buffer, quarter):
        self.links, self.sends, self.buffer, self.quarter = links, sends, buffer, quarter
        self.slots = [sends.slot() for _ in range(3)]

    def rows(self, member):
        return self.buffer.at[aligned(member, self.quarter), :]

    def start_core(self):
        own = self.rows(self.links.member)
        mate = self.links.to_member(self.links.core_mate)
        self.sends.start(self.slots[0], own, own, mate)

    def start_half(self):
        own = self.rows(self.links.member)
        self.sends.start(self.slots[1], own, own, self.links.to_member(self.links.half_mate))

    def await_core(self):
        mate = self.links.core_mate
        self.sends.arrived(self.slots[0], self.rows(mate), self.links.to_member(mate))

    def pass_on(self):
        mate = self.links.half_mate
        self.sends.arrived(self.slots[1], self.rows(mate), self.links.to_member(mate))
        passed = self.rows(mate)
        self.sends.start(
            self.slots[2], passed, passed, self.links.to_member(self.links.core_mate)
        )

    def await_far(self):
        mate = self.links.core_mate
        self.sends.arrived(self.slots[2], self.rows(self.links.far_mate), self.links.to_member(mate))


class GroupSum:
    def __init__(self, links, sends, lent, got, crossing, crossed, total):
        self.links, self.sends = links, sends
        self.lent, self.got, self.crossing, self.crossed, self.total = (
            lent,
            got,
            crossing,
            crossed,
            total,
        )
        self.slots = [sends.slot() for _ in range(3)]

    def member_of(self, step):
        half = lax.rem(self.links.half + 1 - step // 2 + 2, 2)
        core = lax.rem(self.links.core + 1 - step % 2 + 2, 2)
        return half * 2 + core

    def lend(self, index):
        mate = self.links.to_member(self.links.core_mate)
        return self.sends.copy(
            self.slots[0] + index, self.lent.at[index], self.got.at[index], mate
        )

    def cross(self):
        mate = self.links.to_member(self.links.half_mate)
        return self.sends.copy(self.slots[2], self.crossing, self.crossed, mate)

    def step(self, step, value, crosses):
        index = step // 2
        self.total[...] = value

        @pl.when(step % 2 == 0)
        def _():
            self.lent[index] = self.total[...].astype(brain_type)
            self.lend(index).start()

        @pl.when(step % 2 == 1)
        def _():
            self.lend(index).wait_recv()

        @pl.when(step == 1)
        def _():
            self.crossing[...] = (self.total[...] + self.got[0].astype(float_type)).astype(
                brain_type
            )
            if crosses:
                self.cross().start()

    def note(self, crosses):
        self.sends.open += [self.lend(0), self.lend(1)]
        if crosses:
            self.sends.open.append(self.cross())

    def await_cross(self):
        self.sends.arrived(
            self.slots[2], self.crossed, self.links.to_member(self.links.half_mate)
        )

    def rows(self, rows):
        return (
            self.total[rows, :]
            + self.got[1, rows, :].astype(float_type)
            + self.crossed[rows, :].astype(float_type)
        )


def normed_rows(values):
    center = jnp.mean(values, axis=-1, keepdims=True)
    shifted = values - center
    spread = jnp.mean(shifted * shifted, axis=-1, keepdims=True)
    root = lax.rsqrt(spread + epsilon)
    return shifted * root, root


def spread_heads(source, target, rows, first, heads, target_first):
    for head in range(heads):
        low, to = HEAD_DIM * (first + head), HEAD_PAD * (target_first + head)
        target[rows, to : to + HEAD_DIM] = source[rows, low : low + HEAD_DIM]


def forward_kernel(
    sizes,
    tokens,
    upstream,
    act_send,
    cond_weight,
    bias_table,
    slot_mask,
    mask_bias,
    weight_zero,
    weight_one,
    weight_two,
    mod_out,
    bias_out,
    one_out,
    heads_out,
    log_out,
    mixed_out,
    branch_out,
    middle_out,
    two_out,
    upper_out,
    input_out,
    attend_out,
    expand_out,
    reduce_out,
    act_got,
    mod_parts,
    mod_got,
    mod_row,
    group_got,
    weights,
    normed,
    lent,
    got,
    crossing,
    crossed,
    total,
    one,
    two,
    upper,
    heads,
    mixed,
    input_pad,
    attend_pad,
    send_sems,
    recv_sems,
    local_sems,
):
    fsdp_size, group_size, quarter, width, own_width, shard = sizes
    links = Links(fsdp_size, group_size)
    sends = Sends(send_sems, recv_sems)
    blocks = (weight_zero, weight_one, weight_two)
    local_heads = own_width // HEAD_DIM
    head_span = local_heads * HEAD_PAD
    chunk = 32
    chunks = quarter // chunk

    act_slots = [sends.slot() for _ in range(fsdp_size)]
    mod_slots = [sends.slot() for _ in range(fsdp_size)]
    group_slots = [sends.slot() for _ in range(group_size)]
    level_slots = [[sends.slot() for _ in range(links.depth)] for _ in blocks]
    side_slots = [[sends.slot() for _ in range(links.depth)] for _ in blocks]
    gather_one = GroupGather(links, sends, one, quarter)
    gather_two = GroupGather(links, sends, two, quarter)
    gather_upper = GroupGather(links, sends, upper, quarter)
    branch_sum = GroupSum(links, sends, lent, got, crossing, crossed, total)
    opened = []

    def shard_rows(block, place):
        return weights.at[block, aligned(place, shard), :]

    def offer(block):
        own = shard_rows(block, links.place)
        for shift in range(1, links.depth):
            target = links.level_at(shift) * 2 + links.side
            sends.start(level_slots[block][shift], blocks[block], own, links.to_place(target))
        sends.start(side_slots[block][0], blocks[block], own, links.to_place(links.side_mate))
        kept = pltpu.make_async_copy(blocks[block], own, local_sems.at[block])
        kept.start()
        return kept

    def relay(block, shift):
        source = links.level_at(-shift) * 2 + links.side
        rows = shard_rows(block, source)
        sends.arrived(level_slots[block][shift], rows, links.to_place(source))
        sends.start(side_slots[block][shift], rows, rows, links.to_place(links.side_mate))
        return source

    def side_arrived(block, shift):
        source = links.level_at(-shift) * 2 + 1 - links.side
        sends.arrived(
            side_slots[block][shift], shard_rows(block, source), links.to_place(links.side_mate)
        )
        return source

    def keep(index, source, target):
        made = pltpu.make_async_copy(source, target, local_sems.at[index])
        made.start()
        opened.append(made)

    links.meet()
    for shift in range(1, fsdp_size):
        target = lax.rem(links.place + shift, fsdp_size)
        sends.start(
            act_slots[shift], act_send.at[target], act_got.at[links.place], links.to_place(target)
        )
    act_got[pl.ds(links.place, 1)] = act_send[pl.ds(links.place, 1)]
    kept_zero = offer(0)

    input_pad[...] = jnp.zeros_like(input_pad)
    attend_pad[...] = jnp.zeros_like(attend_pad)

    def norm_tokens(index, carry):
        rows = aligned(index, chunk)
        normed[rows, :] = normed_rows(tokens[rows, :].astype(float_type))[0]
        return carry

    lax.fori_loop(0, chunks, norm_tokens, 0)

    for shift in range(1, fsdp_size):
        source = lax.rem(links.place + fsdp_size - shift, fsdp_size)
        sends.arrived(act_slots[shift], act_got.at[source], links.to_place(source))
    activated = act_got[...].reshape(fsdp_size * 8, shard).astype(brain_type)
    mod_parts[...] = (
        jnp.dot(activated, cond_weight[...], preferred_element_type=float_type).reshape(
            fsdp_size, 8, 6 * own_width
        )
        + bias_table[...][None]
    )
    for shift in range(1, fsdp_size):
        target = lax.rem(links.place + shift, fsdp_size)
        sends.start(
            mod_slots[shift], mod_parts.at[target], mod_got.at[links.place], links.to_place(target)
        )
    mod_got[pl.ds(links.place, 1)] = mod_parts[pl.ds(links.place, 1)]
    kept_zero.wait()

    def spread_shard(place):
        rows = aligned(place, shard)
        spread_heads(weights.at[0], input_pad, rows, 0, 3 * local_heads, 0)
        spread_heads(weights.at[0], attend_pad, rows, 3 * local_heads, local_heads, 0)

    spread_shard(links.place)
    for shift in range(1, fsdp_size):
        source = lax.rem(links.place + fsdp_size - shift, fsdp_size)
        sends.arrived(mod_slots[shift], mod_got.at[source], links.to_place(source))
    summed = mod_got[0]
    for index in range(1, fsdp_size):
        summed = summed + mod_got[index]
    mod_row[...] = summed
    for shift in range(1, group_size):
        target = lax.rem(links.member + shift, group_size)
        sends.start(group_slots[shift], mod_row, group_got.at[links.member], links.to_member(target))
    group_got[pl.ds(links.member, 1)] = mod_row[...][None]
    bias_out[...] = mod_row[...]
    for shift in range(1, group_size):
        source = lax.rem(links.member + group_size - shift, group_size)
        sends.arrived(group_slots[shift], group_got.at[source], links.to_member(source))
    chosen = slot_mask[:, 0:1]
    for index in range(6):
        full = jnp.concatenate(
            [
                group_got[member, :, index * own_width : (index + 1) * own_width]
                for member in range(group_size)
            ],
            axis=1,
        )
        mod_out[index : index + 1, :] = jnp.sum(full * chosen, axis=0, keepdims=True)
    mod_out[6:8, :] = jnp.zeros((2, width), float_type)

    own_rows = links.member * quarter

    def first_norm(index, carry):
        rows = aligned(index, chunk)
        to = pl.ds(pl.multiple_of(own_rows + index * chunk, chunk), chunk)
        one[to, :] = (normed[rows, :] * (1.0 + mod_out[1:2, :]) + mod_out[0:1, :]).astype(brain_type)
        return carry

    lax.fori_loop(0, chunks, first_norm, 0)
    gather_one.start_half()
    gather_one.start_core()

    def upper_rows(index, carry):
        rows = aligned(index, chunk)
        to = pl.ds(pl.multiple_of(own_rows + index * chunk, chunk), chunk)
        upper[to, :] = (mod_out[5:6, :] * upstream[rows, :].astype(float_type)).astype(brain_type)
        return carry

    lax.fori_loop(0, chunks, upper_rows, 0)

    for shift in range(1, links.depth):
        spread_shard(relay(0, shift))
    kept_one = offer(1)
    gather_one.pass_on()
    gather_upper.start_half()
    gather_upper.start_core()
    gather_one.await_core()
    for shift in range(links.depth):
        spread_shard(side_arrived(0, shift))
    gather_one.await_far()
    keep(3, one, one_out)
    keep(4, input_pad, input_out)
    keep(5, attend_pad, attend_out)

    bias_pad = mod_row[7:8, 0 : 2 * head_span]

    def project(index, carry):
        rows = aligned(index, quarter)
        values = jnp.dot(one[rows, :], input_pad[...], preferred_element_type=float_type)
        heads[rows, 0:head_span] = (values[:, 0:head_span] + bias_pad[:, 0:head_span]).astype(
            brain_type
        )
        heads[rows, head_span : 2 * head_span] = values[:, head_span : 2 * head_span].astype(
            brain_type
        )
        heads[rows, 2 * head_span :] = (
            values[:, 2 * head_span :] + bias_pad[:, head_span:]
        ).astype(brain_type)
        return carry

    lax.fori_loop(0, group_size, project, 0)
    keep(6, heads, heads_out)

    power_scale = math.log2(math.e) / math.sqrt(HEAD_DIM)

    def attend(step, carry):
        head, part = step // group_size, step % group_size
        rows = aligned(part, quarter)

        def columns(base):
            return aligned(base * local_heads + head, HEAD_PAD)

        raw = lax.dot_general(
            heads[rows, columns(0)],
            heads[:, columns(1)],
            (((1,), (1,)), ((), ())),
            preferred_element_type=float_type,
        )
        scores = jnp.concatenate(
            [
                raw[:, other * quarter : (other + 1) * quarter] + mask_bias[part, other]
                for other in range(group_size)
            ],
            axis=1,
        )
        top = jnp.max(scores, axis=1, keepdims=True)
        powers = jnp.exp2(scores * power_scale - top * power_scale)
        totals = jnp.sum(powers, axis=1, keepdims=True)
        value = jnp.dot(
            powers.astype(brain_type), heads[:, columns(2)], preferred_element_type=float_type
        )
        mixed[rows, aligned(head, HEAD_PAD)] = (value / totals).astype(brain_type)
        turned = jnp.transpose(
            jnp.broadcast_to(top * power_scale + jnp.log2(totals), (quarter, HEAD_PAD))
        )
        log_out[head, :, rows] = turned[0:8, :]
        for shift in range(1, links.depth):

            @pl.when(step == 2 + 4 * shift)
            def _():
                relay_in_loop(1, shift)

        @pl.when(step == 4)
        def _():
            gather_upper_in_loop()

        return carry

    def relay_in_loop(block, shift):
        source = links.level_at(-shift) * 2 + links.side
        rows = shard_rows(block, source)
        sends.arrived(level_slots[block][shift], rows, links.to_place(source))
        sends.copy(
            side_slots[block][shift], rows, rows, links.to_place(links.side_mate)
        ).start()

    def gather_upper_in_loop():
        mate = links.half_mate
        passed = gather_upper.rows(mate)
        sends.arrived(gather_upper.slots[1], passed, links.to_member(mate))
        sends.copy(
            gather_upper.slots[2], passed, passed, links.to_member(links.core_mate)
        ).start()

    lax.fori_loop(0, local_heads * group_size, attend, 0)
    for shift in range(1, links.depth):
        source = links.level_at(-shift) * 2 + links.side
        rows = shard_rows(1, source)
        sends.open.append(
            sends.copy(side_slots[1][shift], rows, rows, links.to_place(links.side_mate))
        )
    passed = gather_upper.rows(links.half_mate)
    sends.open.append(
        sends.copy(gather_upper.slots[2], passed, passed, links.to_member(links.core_mate))
    )
    kept_two = offer(2)
    keep(7, mixed, mixed_out)

    def branch_part(member):
        return lax.dot_general(
            mixed[aligned(member, quarter), :],
            attend_pad[...],
            (((1,), (1,)), ((), ())),
            preferred_element_type=float_type,
        )

    def branch_step(step, carry):
        branch_sum.step(step, branch_part(branch_sum.member_of(step)), True)
        return carry

    lax.fori_loop(0, group_size, branch_step, 0)
    branch_sum.note(True)
    gather_upper.await_core()
    gather_upper.await_far()
    keep(8, upper, upper_out)
    branch_sum.await_cross()

    def second_norm(index, carry):
        rows = aligned(index, chunk)
        to = pl.ds(pl.multiple_of(own_rows + index * chunk, chunk), chunk)
        branch = branch_sum.rows(rows) + mod_row[5:6, 0:width]
        branch_out[rows, :] = branch
        middle = tokens[rows, :].astype(float_type) + mod_out[2:3, :] * branch
        middle_out[rows, :] = middle
        two[to, :] = (normed_rows(middle)[0] * (1.0 + mod_out[4:5, :]) + mod_out[3:4, :]).astype(
            brain_type
        )
        return carry

    lax.fori_loop(0, chunks, second_norm, 0)
    gather_two.start_half()
    gather_two.start_core()
    for shift in range(1, links.depth):
        relay(2, shift)
    gather_two.pass_on()
    kept_one.wait()
    for shift in range(links.depth):
        side_arrived(1, shift)
    keep(9, weights.at[1], expand_out)
    gather_two.await_core()
    gather_two.await_far()
    keep(10, two, two_out)
    kept_two.wait()
    for shift in range(links.depth):
        side_arrived(2, shift)
    keep(11, weights.at[2], reduce_out)
    for made in opened:
        made.wait()
    sends.finish()


def run_forward(
    sizes, tokens, upstream, act_send, cond_weight, bias_table, slot_mask, mask_bias, weights
):
    fsdp_size, group_size, quarter, width, own_width, shard = sizes
    row_length = quarter * group_size
    local_heads = own_width // HEAD_DIM
    span = local_heads * HEAD_PAD
    hidden = weights[1].shape[1]
    in_vmem = pl.BlockSpec(memory_space=pltpu.VMEM)
    anywhere = pl.BlockSpec(memory_space=pl.ANY)
    shape = jax.ShapeDtypeStruct
    out_shape = (
        shape((8, width), float_type),
        shape((8, 6 * own_width), float_type),
        shape((row_length, width), brain_type),
        shape((row_length, 3 * span), brain_type),
        shape((local_heads, 8, row_length), float_type),
        shape((row_length, span), brain_type),
        shape((quarter, width), float_type),
        shape((quarter, width), float_type),
        shape((row_length, width), brain_type),
        shape((row_length, width), brain_type),
        shape((width, 3 * span), brain_type),
        shape((width, span), brain_type),
        shape((width, hidden), brain_type),
        shape((width, hidden), brain_type),
    )
    out_specs = (
        in_vmem,
        in_vmem,
        anywhere,
        anywhere,
        in_vmem,
        anywhere,
        in_vmem,
        in_vmem,
        anywhere,
        anywhere,
        anywhere,
        anywhere,
        anywhere,
        anywhere,
    )
    copies = 2 * fsdp_size + group_size + 6 * (fsdp_size // 2) + 3 * 3 + 3
    vmem = pltpu.VMEM
    scratch = [
        vmem((fsdp_size, 8, shard), float_type),
        vmem((fsdp_size, 8, 6 * own_width), float_type),
        vmem((fsdp_size, 8, 6 * own_width), float_type),
        vmem((8, 6 * own_width), float_type),
        vmem((group_size, 8, 6 * own_width), float_type),
        vmem((3, width, hidden), brain_type),
        vmem((quarter, width), float_type),
        vmem((2, quarter, width), brain_type),
        vmem((2, quarter, width), brain_type),
        vmem((quarter, width), brain_type),
        vmem((quarter, width), brain_type),
        vmem((quarter, width), float_type),
        vmem((row_length, width), brain_type),
        vmem((row_length, width), brain_type),
        vmem((row_length, width), brain_type),
        vmem((row_length, 3 * span), brain_type),
        vmem((row_length, span), brain_type),
        vmem((width, 3 * span), brain_type),
        vmem((width, span), brain_type),
        pltpu.SemaphoreType.DMA((copies,)),
        pltpu.SemaphoreType.DMA((copies,)),
        pltpu.SemaphoreType.DMA((12,)),
    ]
    return pl.pallas_call(
        functools.partial(forward_kernel, sizes),
        out_shape=out_shape,
        in_specs=[in_vmem] * 6 + [pl.BlockSpec(memory_space=pltpu.SMEM)] + [in_vmem] * 3,
        out_specs=out_specs,
        scratch_shapes=scratch,
        compiler_params=pltpu.CompilerParams(
            collective_id=0, has_side_effects=True, vmem_limit_bytes=TOP_VMEM
        ),
        name="forward_row",
    )(tokens, upstream, act_send, cond_weight, bias_table, slot_mask, mask_bias, *weights)


class ShardSum:
    def __init__(self, links, sends, block, side_got, level_got, shard):
        self.links, self.sends, self.block = links, sends, block
        self.side_got, self.level_got, self.shard = side_got, level_got, shard
        self.side_slots = [sends.slot() for _ in range(links.depth)]
        self.level_slots = [sends.slot() for _ in range(links.depth)]

    def order(self):
        return list(range(1, self.links.depth)) + [0]

    def rows(self, place):
        return aligned(place, self.shard)

    def start(self):
        links = self.links
        for shift in self.order():
            level = links.level_at(shift)
            self.sends.start(
                self.side_slots[shift],
                self.block.at[self.rows(level * 2 + 1 - links.side), :],
                self.side_got.at[shift],
                links.to_place(links.side_mate),
            )

    def fold(self, shift, note=True):
        links = self.links
        self.sends.arrived(
            self.side_slots[shift], self.side_got.at[shift], links.to_place(links.side_mate)
        )
        if shift:
            target = links.level_at(shift) * 2 + links.side
            rows = self.rows(target)
            self.block[rows, :] = (
                self.block[rows, :].astype(float_type) + self.side_got[shift].astype(float_type)
            ).astype(brain_type)
            self.push(shift).start()
            if note:
                self.sends.open.append(self.push(shift))

    def push(self, shift):
        links = self.links
        target = links.level_at(shift) * 2 + links.side
        return self.sends.copy(
            self.level_slots[shift],
            self.block.at[self.rows(target), :],
            self.level_got.at[shift],
            links.to_place(target),
        )

    def total(self):
        links = self.links
        summed = self.block[self.rows(links.place), :].astype(float_type) + self.side_got[0].astype(
            float_type
        )
        for shift in range(1, links.depth):
            source = links.level_at(-shift) * 2 + links.side
            self.sends.arrived(
                self.level_slots[shift], self.level_got.at[shift], links.to_place(source)
            )
            summed = summed + self.level_got[shift].astype(float_type)
        return summed


def fold_rows(values):
    count, width = values.shape
    return jnp.sum(values.reshape(count // 8, 8, width), axis=0)


def gelu_pair(values):
    root = math.sqrt(2.0 / math.pi)
    square = values * values
    bend = jnp.tanh(values * (root + root * 0.044715 * square))
    half = 0.5 * (1.0 + bend)
    slope = half + (0.5 * values) * (1.0 - bend * bend) * (root + root * 3 * 0.044715 * square)
    return values * half, slope


def across_rows(left, right):
    return lax.dot_general(left, right, (((0,), (0,)), ((), ())), preferred_element_type=float_type)


def middle_kernel(
    sizes,
    two,
    upper,
    expand,
    reduce,
    mods,
    biases,
    middle,
    branch,
    upstream,
    attend_pad,
    mixed,
    far_out,
    near_out,
    grads_out,
    attend_out,
    expand_out,
    reduce_out,
    slope_out,
    sums_out,
    active,
    inner_grad,
    lent_t,
    got_t,
    crossing_t,
    crossed_t,
    total_t,
    lent_o,
    got_o,
    branch_whole,
    reduce_grad,
    side_got,
    level_got,
    expand_grad,
    sums,
    send_sems,
    recv_sems,
    local_sems,
):
    fsdp_size, group_size, quarter, width, own_width, shard = sizes
    links = Links(fsdp_size, group_size)
    sends = Sends(send_sems, recv_sems)
    local_heads = own_width // HEAD_DIM
    chunk = 32
    chunks = quarter // chunk
    two_sum = GroupSum(links, sends, lent_t, got_t, crossing_t, crossed_t, total_t)
    outer_sum = GroupSum(links, sends, lent_o, got_o, far_out, None, near_out)
    gather = GroupGather(links, sends, branch_whole, quarter)
    reduce_sum = ShardSum(links, sends, reduce_grad, side_got, level_got, shard)
    links.meet()
    sums[...] = jnp.zeros_like(sums)
    hidden = expand.shape[1]

    def feed(step, carry):
        rows = aligned(two_sum.member_of(step), quarter)
        inner = (
            jnp.dot(two[rows, :], expand[...], preferred_element_type=float_type)
            + biases[4:5, 0:hidden]
        )
        active_grad = jnp.dot(upper[rows, :], reduce[...], preferred_element_type=float_type)
        value, slope = gelu_pair(inner)
        active[rows, :] = value.astype(brain_type)
        low = (active_grad * slope).astype(brain_type)
        inner_grad[rows, :] = low
        sums[4] = sums[4] + fold_rows(low.astype(float_type))
        two_sum.step(step, against(inner_grad[rows, :], expand[...]), True)
        outer_sum.step(step, against(active[rows, :], reduce[...]), False)
        return carry

    lax.fori_loop(0, group_size, feed, 0)
    two_sum.note(True)
    outer_sum.note(False)

    def near_rows(index, carry):
        rows = aligned(index, chunk)
        near_out[rows, :] = near_out[rows, :] + got_o[1, rows, :].astype(float_type)
        return carry

    lax.fori_loop(0, chunks, near_rows, 0)

    part = 384

    def reduce_part(index, carry):
        columns = aligned(index, part)
        reduce_grad[columns, :] = across_rows(upper[:, columns], active[...]).astype(brain_type)
        return carry

    lax.fori_loop(0, width // part, reduce_part, 0)
    reduce_sum.start()
    two_sum.await_cross()
    own_rows = links.member * quarter

    def second_back(index, carry):
        rows = aligned(index, chunk)
        to = pl.ds(pl.multiple_of(own_rows + index * chunk, chunk), chunk)
        two_grad = two_sum.rows(rows)
        normed, root = normed_rows(middle[rows, :])
        scaled = two_grad * (1.0 + mods[4:5, :])
        centered = (
            scaled
            - jnp.mean(scaled, axis=-1, keepdims=True)
            - normed * jnp.mean(scaled * normed, axis=-1, keepdims=True)
        )
        slope = upstream[rows, :].astype(float_type) + root * centered
        slope_out[rows, :] = slope
        low = (mods[2:3, :] * slope).astype(brain_type)
        branch_whole[to, :] = low
        sums[0] = sums[0] + fold_rows(slope * branch[rows, :])
        sums[1] = sums[1] + fold_rows(two_grad)
        sums[2] = sums[2] + fold_rows(two_grad * normed)
        sums[3] = sums[3] + fold_rows(low.astype(float_type))
        sums[5] = sums[5] + fold_rows(upper[to, :].astype(float_type))
        return carry

    lax.fori_loop(0, chunks, second_back, 0)
    gather.start_half()
    gather.start_core()

    def expand_part(index, carry):
        columns = aligned(index, part)
        expand_grad[columns, :] = across_rows(two[:, columns], inner_grad[...]).astype(brain_type)
        return carry

    lax.fori_loop(0, width // part, expand_part, 0)
    kept_expand = pltpu.make_async_copy(expand_grad, expand_out, local_sems.at[0])
    kept_expand.start()
    reduce_sum.fold(1)
    for index in range(6):
        sums_out[index : index + 1, :] = jnp.sum(sums[index], axis=0, keepdims=True)
    sums_out[6:8, :] = jnp.zeros((2, width), float_type)
    gather.pass_on()
    reduce_sum.fold(2)
    gather.await_core()
    gather.await_far()

    def head_grads(index, carry):
        rows = aligned(index, quarter)
        grads_out[rows, :] = jnp.dot(
            branch_whole[rows, :], attend_pad[...], preferred_element_type=float_type
        ).astype(brain_type)
        return carry

    lax.fori_loop(0, group_size, head_grads, 0)

    def attend_part(index, carry):
        columns = aligned(index, part)
        value = across_rows(branch_whole[:, columns], mixed[...])
        for head in range(local_heads):
            attend_out[columns, head * HEAD_DIM : (head + 1) * HEAD_DIM] = value[
                :, head * HEAD_PAD : head * HEAD_PAD + HEAD_DIM
            ].astype(brain_type)
        return carry

    lax.fori_loop(0, width // part, attend_part, 0)
    reduce_sum.fold(3)
    reduce_sum.fold(0)
    reduce_out[...] = reduce_sum.total()
    kept_expand.wait()
    sends.finish()


def run_middle(sizes, *arrays):
    fsdp_size, group_size, quarter, width, own_width, shard = sizes
    row_length = quarter * group_size
    span = own_width // HEAD_DIM * HEAD_PAD
    hidden = arrays[2].shape[1]
    depth = fsdp_size // 2
    in_vmem = pl.BlockSpec(memory_space=pltpu.VMEM)
    anywhere = pl.BlockSpec(memory_space=pl.ANY)
    shape = jax.ShapeDtypeStruct
    vmem = pltpu.VMEM
    copies = 3 + 3 + 3 + 2 * depth
    return pl.pallas_call(
        functools.partial(middle_kernel, sizes),
        out_shape=(
            shape((quarter, width), brain_type),
            shape((quarter, width), float_type),
            shape((row_length, span), brain_type),
            shape((width, own_width), brain_type),
            shape((width, hidden), brain_type),
            shape((shard, hidden), float_type),
            shape((quarter, width), float_type),
            shape((8, width), float_type),
        ),
        in_specs=[in_vmem] * len(arrays),
        out_specs=(in_vmem, in_vmem, in_vmem, in_vmem, anywhere, in_vmem, in_vmem, in_vmem),
        scratch_shapes=[
            vmem((row_length, hidden), brain_type),
            vmem((row_length, hidden), brain_type),
            vmem((2, quarter, width), brain_type),
            vmem((2, quarter, width), brain_type),
            vmem((quarter, width), brain_type),
            vmem((quarter, width), brain_type),
            vmem((quarter, width), float_type),
            vmem((2, quarter, width), brain_type),
            vmem((2, quarter, width), brain_type),
            vmem((row_length, width), brain_type),
            vmem((width, hidden), brain_type),
            vmem((depth, shard, hidden), brain_type),
            vmem((depth, shard, hidden), brain_type),
            vmem((width, hidden), brain_type),
            vmem((6, 8, width), float_type),
            pltpu.SemaphoreType.DMA((copies,)),
            pltpu.SemaphoreType.DMA((copies,)),
            pltpu.SemaphoreType.DMA((1,)),
        ],
        compiler_params=pltpu.CompilerParams(
            collective_id=1, has_side_effects=True, vmem_limit_bytes=TOP_VMEM
        ),
        name="middle_row",
    )(*arrays)


def backward_kernel(
    sizes,
    heads,
    logs,
    head_grads,
    mixed,
    one,
    input_pad,
    tokens,
    mods,
    biases,
    slope,
    upstream,
    middle,
    far_sum,
    near_sum,
    expand_grad,
    attend_grad,
    sums_in,
    cond_weight,
    act_send,
    slot_mask,
    mask_bias,
    output_out,
    token_out,
    act_out,
    cond_out,
    bias_out,
    expand_out,
    input_out,
    crossed_o,
    joined,
    query_sum,
    delta_rows,
    lent,
    got,
    crossing,
    crossed,
    total,
    expand_block,
    input_block,
    side_one,
    level_one,
    side_zero,
    level_zero,
    sums,
    slabs,
    slab_got,
    place_slab,
    place_got,
    act_part,
    act_got,
    act_group,
    bias_row,
    act_all,
    send_sems,
    recv_sems,
    local_sems,
):
    fsdp_size, group_size, quarter, width, own_width, shard = sizes
    links = Links(fsdp_size, group_size)
    sends = Sends(send_sems, recv_sems)
    local_heads = own_width // HEAD_DIM
    span = local_heads * HEAD_PAD
    row_length = quarter * group_size
    chunk = 32
    chunks = quarter // chunk
    one_sum = GroupSum(links, sends, lent, got, crossing, crossed, total)
    expand_sum = ShardSum(links, sends, expand_block, side_one, level_one, shard)
    input_sum = ShardSum(links, sends, input_block, side_zero, level_zero, shard)
    outer_slot = sends.slot()
    act_slots = [sends.slot() for _ in range(fsdp_size)]
    slab_slots = [sends.slot() for _ in range(group_size)]
    place_slots = [sends.slot() for _ in range(fsdp_size)]
    part_slots = [sends.slot() for _ in range(fsdp_size)]
    row_slots = [sends.slot() for _ in range(group_size)]
    bias_slots = [sends.slot() for _ in range(group_size)]

    def to_places(slots, source_of, target):
        for shift in range(1, fsdp_size):
            place = lax.rem(links.place + shift, fsdp_size)
            sends.start(
                slots[shift], source_of(place), target.at[links.place], links.to_place(place)
            )

    def from_places(slots, target):
        for shift in range(1, fsdp_size):
            place = lax.rem(links.place + fsdp_size - shift, fsdp_size)
            sends.arrived(slots[shift], target.at[place], links.to_place(place))

    def to_members(slots, source_of, target):
        for shift in range(1, group_size):
            member = lax.rem(links.member + shift, group_size)
            sends.start(
                slots[shift], source_of(member), target.at[links.member], links.to_member(member)
            )

    def from_members(slots, target):
        for shift in range(1, group_size):
            member = lax.rem(links.member + group_size - shift, group_size)
            sends.arrived(slots[shift], target.at[member], links.to_member(member))

    links.meet()
    sends.start(outer_slot, far_sum, crossed_o, links.to_member(links.half_mate))
    kept = pltpu.make_async_copy(expand_grad, expand_block, local_sems.at[0])
    kept.start()
    to_places(act_slots, lambda place: act_send.at[place], act_all)
    act_all[pl.ds(links.place, 1)] = act_send[pl.ds(links.place, 1)]
    sums[...] = jnp.zeros_like(sums)
    kept.wait()
    expand_sum.start()
    attend_first = 3 * own_width
    input_block[:, attend_first : attend_first + own_width] = attend_grad[...]

    power_scale = math.log2(math.e) / math.sqrt(HEAD_DIM)
    score_scale = 1.0 / math.sqrt(HEAD_DIM)

    def columns(base, head):
        return aligned(base * local_heads + head, HEAD_PAD)

    def head_deltas(head, carry):
        product = head_grads[:, columns(0, head)].astype(float_type) * mixed[
            :, columns(0, head)
        ].astype(float_type)
        delta = jnp.sum(product, axis=1, keepdims=True)
        turned = jnp.transpose(jnp.broadcast_to(delta, (row_length, HEAD_PAD)))
        delta_rows[head] = turned[0:8, :]
        return carry

    lax.fori_loop(0, local_heads, head_deltas, 0)

    def attend_back(step, carry):
        head, part = step // group_size, step % group_size
        rows = aligned(part, quarter)
        query = heads[:, columns(0, head)]
        key = heads[rows, columns(1, head)]
        value = heads[rows, columns(2, head)]
        grad = head_grads[:, columns(0, head)]
        shift = jnp.concatenate(
            [
                mask_bias[part, other]
                - logs[head, 0:1, other * quarter : (other + 1) * quarter]
                for other in range(group_size)
            ],
            axis=1,
        )
        probable = jnp.exp2(against(key, query) * power_scale + shift)
        value_grad = jnp.dot(probable.astype(brain_type), grad, preferred_element_type=float_type)
        score_grad = (probable * (against(value, grad) - delta_rows[head, 0:1, :])).astype(
            brain_type
        )
        key_grad = jnp.dot(score_grad, query, preferred_element_type=float_type)
        joined[rows, columns(1, head)] = (key_grad * score_scale).astype(brain_type)
        joined[rows, columns(2, head)] = value_grad.astype(brain_type)
        query_grad = across_rows(score_grad, key)

        @pl.when(part == 0)
        def _():
            query_sum[...] = query_grad

        @pl.when(part > 0)
        def _():
            query_sum[...] = query_sum[...] + query_grad

        @pl.when(part == group_size - 1)
        def _():
            joined[:, columns(0, head)] = (query_sum[...] * score_scale).astype(brain_type)

        for index, late in ((1, 5), (2, 9), (3, 13)):

            @pl.when(step == late)
            def _():
                expand_sum.fold(index, False)

        return carry

    lax.fori_loop(0, group_size * local_heads, attend_back, 0)
    for index in range(1, links.depth):
        sends.open.append(expand_sum.push(index))

    part = 384

    def input_part(index, carry):
        picked = aligned(index, part)
        value = across_rows(one[:, picked], joined[...])
        for head in range(3 * local_heads):
            input_block[picked, head * HEAD_DIM : (head + 1) * HEAD_DIM] = value[
                :, head * HEAD_PAD : head * HEAD_PAD + HEAD_DIM
            ].astype(brain_type)
        return carry

    lax.fori_loop(0, width // part, input_part, 0)
    input_sum.start()

    def one_step(step, carry):
        rows = aligned(one_sum.member_of(step), quarter)
        one_sum.step(step, against(joined[rows, :], input_pad[...]), True)
        return carry

    lax.fori_loop(0, group_size, one_step, 0)
    one_sum.note(True)
    expand_sum.fold(0)

    sends.arrived(outer_slot, crossed_o, links.to_member(links.half_mate))

    def finish_rows(index, carry):
        rows = aligned(index, chunk)
        outer = (
            near_sum[rows, :] + crossed_o[rows, :].astype(float_type) + biases[6:7, 0:width]
        )
        output_out[rows, :] = (middle[rows, :] + mods[5:6, :] * outer).astype(brain_type)
        sums[2] = sums[2] + fold_rows(upstream[rows, :].astype(float_type) * outer)
        return carry

    lax.fori_loop(0, chunks, finish_rows, 0)

    def pair_sums(index, carry):
        rows = aligned(index, 128)
        sums[3, :, 0:span] = sums[3, :, 0:span] + fold_rows(
            joined[rows, 0:span].astype(float_type)
        )
        sums[4, :, 0:span] = sums[4, :, 0:span] + fold_rows(
            joined[rows, 2 * span : 3 * span].astype(float_type)
        )
        return carry

    lax.fori_loop(0, row_length // 128, pair_sums, 0)
    input_sum.fold(1)
    expand_out[...] = expand_sum.total()
    one_sum.await_cross()

    def first_back(index, carry):
        rows = aligned(index, chunk)
        one_grad = one_sum.rows(rows)
        normed, root = normed_rows(tokens[rows, :].astype(float_type))
        scaled = one_grad * (1.0 + mods[1:2, :])
        centered = (
            scaled
            - jnp.mean(scaled, axis=-1, keepdims=True)
            - normed * jnp.mean(scaled * normed, axis=-1, keepdims=True)
        )
        token_out[rows, :] = slope[rows, :] + root * centered
        sums[0] = sums[0] + fold_rows(one_grad)
        sums[1] = sums[1] + fold_rows(one_grad * normed)
        return carry

    lax.fori_loop(0, chunks, first_back, 0)

    def summed(index):
        return jnp.sum(sums[index], axis=0, keepdims=True)

    six = (
        summed(0),
        summed(1),
        sums_in[0:1, :],
        sums_in[1:2, :],
        sums_in[2:3, :],
        summed(2),
    )
    slabs[...] = jnp.zeros_like(slabs)
    slots = slot_mask[0:4, 0:1]
    for member in range(group_size):
        low, high = member * own_width, (member + 1) * own_width
        for index in range(6):
            to = slice(index * own_width, (index + 1) * own_width)
            slabs[member, 0:4, to] = slots * six[index][:, low:high]
        slabs[member, 4:5, 0:own_width] = sums_in[3:4, low:high]
        slabs[member, 5:6, 0:own_width] = sums_in[5:6, low:high]
    to_members(slab_slots, lambda member: slabs.at[member], slab_got)
    slab_got[pl.ds(links.member, 1)] = slabs[pl.ds(links.member, 1)]
    input_sum.fold(2)
    from_members(slab_slots, slab_got)
    row = slab_got[0]
    for member in range(1, group_size):
        row = row + slab_got[member]
    place_slab[...] = row
    place_slab[0:4, :] = row[0:4, :].astype(brain_type).astype(float_type)
    place_slab[6:7, 0:width] = sums_in[4:5, :]
    place_slab[7:8, 0:span] = summed(3)[:, 0:span]
    place_slab[7:8, span : 2 * span] = summed(4)[:, 0:span]
    to_places(place_slots, lambda place: place_slab, place_got)
    place_got[pl.ds(links.place, 1)] = place_slab[...][None]
    input_sum.fold(3)
    from_places(act_slots, act_all)
    from_places(place_slots, place_got)
    low_rows = place_got[...].reshape(fsdp_size * 8, 6 * own_width).astype(brain_type)
    act_part[...] = against(low_rows, cond_weight[...]).reshape(fsdp_size, 8, shard)
    to_places(part_slots, lambda place: act_part.at[place], act_got)
    act_got[pl.ds(links.place, 1)] = act_part[pl.ds(links.place, 1)]
    bias_sum = place_got[0]
    for place in range(1, fsdp_size):
        bias_sum = bias_sum + place_got[place]
    bias_row[...] = bias_sum
    bias_row[0:1, :] = jnp.sum(bias_sum[0:4, :], axis=0, keepdims=True)
    to_members(bias_slots, lambda member: bias_row, bias_out)
    bias_out[pl.ds(links.member, 1)] = bias_row[...][None]
    cond_out[...] = across_rows(
        act_all[...].reshape(fsdp_size * 8, shard).astype(brain_type), low_rows
    )
    from_places(part_slots, act_got)
    to_members(row_slots, lambda member: act_got, act_group)
    act_group[pl.ds(links.member, 1)] = act_got[...][None]
    input_sum.fold(0)
    from_members(row_slots, act_group)
    from_members(bias_slots, bias_out)
    act_sum = act_group[0]
    for member in range(1, group_size):
        act_sum = act_sum + act_group[member]
    act_out[...] = act_sum
    input_out[...] = input_sum.total()
    sends.finish()


def run_backward(sizes, *arrays):
    fsdp_size, group_size, quarter, width, own_width, shard = sizes
    row_length = quarter * group_size
    local_heads = own_width // HEAD_DIM
    span = local_heads * HEAD_PAD
    hidden = arrays[14].shape[1]
    depth = fsdp_size // 2
    six = 6 * own_width
    in_vmem = pl.BlockSpec(memory_space=pltpu.VMEM)
    anywhere = pl.BlockSpec(memory_space=pl.ANY)
    shape = jax.ShapeDtypeStruct
    vmem = pltpu.VMEM
    copies = 3 + 4 * depth + 1 + 3 * fsdp_size + 3 * group_size
    in_specs = [in_vmem] * len(arrays)
    in_specs[14] = anywhere
    in_specs[-1] = pl.BlockSpec(memory_space=pltpu.SMEM)
    return pl.pallas_call(
        functools.partial(backward_kernel, sizes),
        out_shape=(
            shape((quarter, width), brain_type),
            shape((quarter, width), float_type),
            shape((fsdp_size, 8, shard), float_type),
            shape((shard, six), float_type),
            shape((group_size, 8, six), float_type),
            shape((shard, hidden), float_type),
            shape((shard, 4 * own_width), float_type),
        ),
        in_specs=in_specs,
        out_specs=(in_vmem,) * 7,
        scratch_shapes=[
            vmem((quarter, width), brain_type),
            vmem((row_length, 3 * span), brain_type),
            vmem((row_length, HEAD_PAD), float_type),
            vmem((local_heads, 8, row_length), float_type),
            vmem((2, quarter, width), brain_type),
            vmem((2, quarter, width), brain_type),
            vmem((quarter, width), brain_type),
            vmem((quarter, width), brain_type),
            vmem((quarter, width), float_type),
            vmem((width, hidden), brain_type),
            vmem((width, 4 * own_width), brain_type),
            vmem((depth, shard, hidden), brain_type),
            vmem((depth, shard, hidden), brain_type),
            vmem((depth, shard, 4 * own_width), brain_type),
            vmem((depth, shard, 4 * own_width), brain_type),
            vmem((5, 8, width), float_type),
            vmem((group_size, 8, six), float_type),
            vmem((group_size, 8, six), float_type),
            vmem((8, six), float_type),
            vmem((fsdp_size, 8, six), float_type),
            vmem((fsdp_size, 8, shard), float_type),
            vmem((fsdp_size, 8, shard), float_type),
            vmem((group_size, fsdp_size, 8, shard), float_type),
            vmem((8, six), float_type),
            vmem((fsdp_size, 8, shard), float_type),
            pltpu.SemaphoreType.DMA((copies,)),
            pltpu.SemaphoreType.DMA((copies,)),
            pltpu.SemaphoreType.DMA((1,)),
        ],
        compiler_params=pltpu.CompilerParams(
            collective_id=2, has_side_effects=True, vmem_limit_bytes=TOP_VMEM
        ),
        name="backward_row",
    )(*arrays)


def fast_inputs(sizes, conditions, lengths, segments, condition_weight, biases):
    fsdp_size, group_size, quarter, width, own_width, shard = sizes
    place, member = lax.axis_index("fsdp"), lax.axis_index("rep")
    condition_bias, input_bias, attend_bias, expand_bias, reduce_bias = biases
    slot_count = conditions.shape[1]
    span = 6 * own_width
    column_start = member * own_width
    activated = jax.nn.silu(conditions[0].astype(float_type)).astype(brain_type).astype(float_type)
    act_send = jnp.pad(
        activated.reshape(slot_count, fsdp_size, shard).transpose(1, 0, 2),
        ((0, 0), (0, 8 - slot_count), (0, 0)),
    )

    def placed(own):
        empty = jnp.zeros((own.shape[0] * fsdp_size,), float_type)
        return lax.dynamic_update_slice_in_dim(
            empty, own.astype(float_type), place * own.shape[0], 0
        )

    def to_span(values):
        return jnp.pad(values, (0, span - values.shape[0]))

    condition_row = lax.dynamic_slice_in_dim(
        placed(condition_bias).reshape(6, width), column_start, own_width, 1
    ).reshape(-1)
    hidden = expand_bias.shape[0] * fsdp_size // group_size
    expand_row = lax.dynamic_slice_in_dim(placed(expand_bias), member * hidden, hidden, 0)
    pair = lax.dynamic_slice_in_dim(
        placed(input_bias).reshape(2, width), column_start, own_width, 1
    ).reshape(2, -1, HEAD_DIM)
    pair_row = jnp.pad(pair, ((0, 0), (0, 0), (0, HEAD_PAD - HEAD_DIM))).reshape(-1)
    bias_table = jnp.stack(
        [condition_row] * slot_count
        + [
            to_span(expand_row),
            to_span(placed(attend_bias)),
            to_span(placed(reduce_bias)),
            to_span(pair_row),
        ]
    )
    slot_mask = jnp.broadcast_to(
        (jnp.arange(8, dtype=jnp.int32) == segments[0, 0]).astype(float_type)[:, None], (8, 128)
    )
    row_ends = jnp.cumsum(lengths[0], dtype=jnp.int32)
    images = image_index(row_ends, jnp.arange(group_size, dtype=jnp.int32) * quarter)
    mask_bias = jnp.where(images[:, None] == images[None, :], 0.0, -1e30).astype(float_type)
    cond_flat = condition_weight.reshape(shard, span)
    return act_send, cond_flat, bias_table, slot_mask, mask_bias


def fast_local(
    tokens,
    conditions,
    lengths,
    segments,
    condition_weight,
    condition_bias,
    input_weight,
    input_bias,
    attend_weight,
    attend_bias,
    expand_weight,
    expand_bias,
    reduce_weight,
    reduce_bias,
    cotangent,
):
    _, quarter, width = tokens.shape
    slot_count = conditions.shape[1]
    group_size, member = lax.axis_size("rep"), lax.axis_index("rep")
    fsdp_size, place = lax.axis_size("fsdp"), lax.axis_index("fsdp")
    shard, _, own_width = condition_weight.shape
    span = own_width // HEAD_DIM * HEAD_PAD
    hidden = expand_weight.shape[1]
    sizes = (fsdp_size, group_size, quarter, width, own_width, shard)
    act_send, cond_flat, bias_table, slot_mask, mask_bias = fast_inputs(
        sizes,
        conditions,
        lengths,
        segments,
        condition_weight,
        (condition_bias, input_bias, attend_bias, expand_bias, reduce_bias),
    )
    weight_zero = jnp.concatenate([input_weight.reshape(shard, -1), attend_weight], axis=1)
    token_rows = tokens.reshape(quarter, width)
    upstream = cotangent.reshape(quarter, width)
    (
        mods,
        biases,
        one,
        heads,
        logs,
        mixed,
        branch,
        middle,
        two,
        upper,
        input_pad,
        attend_pad,
        expand_all,
        reduce_all,
    ) = run_forward(
        sizes,
        token_rows,
        upstream,
        act_send,
        cond_flat,
        bias_table,
        slot_mask,
        mask_bias,
        (weight_zero, expand_weight, reduce_weight),
    )
    (far_sum, near_sum, head_grads, attend_grad, expand_grad, reduce_final, slope, sums) = (
        run_middle(
            sizes,
            two,
            upper,
            expand_all,
            reduce_all,
            mods,
            biases,
            middle,
            branch,
            upstream,
            attend_pad,
            mixed,
        )
    )
    (output, token_grad, act_grad, cond_grad, bias_rows, expand_final, joint_final) = run_backward(
        sizes,
        heads,
        logs,
        head_grads,
        mixed,
        one,
        input_pad,
        token_rows,
        mods,
        biases,
        slope,
        upstream,
        middle,
        far_sum,
        near_sum,
        expand_grad,
        attend_grad,
        sums,
        cond_flat,
        act_send,
        slot_mask,
        mask_bias,
    )

    def owned(values):
        depth = values.shape[0] // fsdp_size
        return lax.dynamic_slice_in_dim(values, place * depth, depth, 0)

    condition_bias_final = owned(
        bias_rows[:, 0, :].reshape(group_size, 6, own_width).transpose(1, 0, 2).reshape(-1)
    )
    attend_bias_final = owned(bias_rows[:, 4, :own_width].reshape(-1))
    reduce_bias_final = owned(bias_rows[:, 5, :own_width].reshape(-1))
    expand_bias_final = owned(bias_rows[:, 6, :hidden].reshape(-1))
    input_bias_final = owned(
        bias_rows[:, 7, : 2 * span]
        .reshape(group_size, 2, span // HEAD_PAD, HEAD_PAD)[..., :HEAD_DIM]
        .transpose(1, 0, 2, 3)
        .reshape(-1)
    )
    condition_values = conditions.astype(float_type)
    _, silu_back = jax.vjp(jax.nn.silu, condition_values)
    act_rows = act_grad[:, :slot_count].transpose(1, 0, 2).reshape(1, slot_count, width)
    condition_grad = silu_back(act_rows)[0]
    return (
        output[None],
        token_grad[None],
        condition_grad,
        cond_grad.reshape(shard, 6, own_width),
        condition_bias_final,
        joint_final[:, : 3 * own_width].reshape(shard, 3, own_width),
        input_bias_final,
        joint_final[:, 3 * own_width :],
        attend_bias_final,
        expand_final,
        expand_bias_final,
        reduce_final,
        reduce_bias_final,
    )


def solution(mesh):
    in_specs = (
        P("fsdp", "rep", None),
        P("fsdp", None, None),
        P("fsdp", None),
        P("fsdp", "rep"),
        P("fsdp", None, "rep"),
        P("fsdp"),
        P("fsdp", None, "rep"),
        P("fsdp"),
        P("fsdp", "rep"),
        P("fsdp"),
        P("fsdp", "rep"),
        P("fsdp"),
        P("fsdp", "rep"),
        P("fsdp"),
        P("fsdp", "rep", None),
    )
    out_specs = (
        P("fsdp", "rep", None),
        P("fsdp", "rep", None),
        P("fsdp", None, None),
        P("fsdp", None, "rep"),
        P("fsdp"),
        P("fsdp", None, "rep"),
        P("fsdp"),
        P("fsdp", "rep"),
        P("fsdp"),
        P("fsdp", "rep"),
        P("fsdp"),
        P("fsdp", "rep"),
        P("fsdp"),
    )
    local = fast_local if mesh.shape["fsdp"] == 8 else plain_local
    return jax.shard_map(local, mesh=mesh, in_specs=in_specs, out_specs=out_specs, check_vma=False)
```

```python
import functools
import math

import jax
import jax.numpy as jnp
from jax import lax
from jax.experimental import pallas as pl
from jax.experimental.pallas import tpu as pltpu
from jax.sharding import PartitionSpec as P

HEAD_DIM = 72


epsilon = 1e-06
highest = lax.Precision.HIGHEST
float_type = jnp.float32
brain_type = jnp.bfloat16


def layer_normed(values):
    center = jnp.mean(values, axis=-1, keepdims=True)
    shifted = values - center
    spread = jnp.mean(shifted * shifted, axis=-1, keepdims=True)
    return shifted * lax.rsqrt(spread + epsilon)


def modulated(values, shift_term, scale_term):
    return layer_normed(values) * (1.0 + scale_term) + shift_term


def gelu_tanh(values):
    return jax.nn.gelu(values, approximate=True)


def image_index(row_ends, positions):
    return jnp.sum((positions[..., :, None] >= row_ends[..., None, :-1]).astype(jnp.int32), axis=-1)


def across(left, right):
    return lax.dot_general(left, right, (((0,), (0,)), ((), ())), preferred_element_type=float_type)


def against(left, right):
    return lax.dot_general(left, right, (((1,), (1,)), ((), ())), preferred_element_type=float_type)


def column_sums(values):
    return jnp.sum(values.astype(float_type), axis=0)


def spread_columns(own_part, total, start):
    empty = jnp.zeros(own_part.shape[:-1] + (total,), float_type)
    return lax.dynamic_update_slice_in_dim(empty, own_part, start, own_part.ndim - 1)


def gather_block(*weights):
    return tuple(lax.all_gather(item, "fsdp", axis=0, tiled=True) for item in weights)


def plain_local(
    tokens,
    conditions,
    lengths,
    segments,
    condition_weight,
    condition_bias,
    input_weight,
    input_bias,
    attend_weight,
    attend_bias,
    expand_weight,
    expand_bias,
    reduce_weight,
    reduce_bias,
    cotangent,
):
    row_count, quarter, model_width = tokens.shape
    slot_count = conditions.shape[1]
    group_size = lax.axis_size("rep")
    group_place = lax.axis_index("rep")
    row_length = quarter * group_size
    own_width = condition_weight.shape[2]
    column_start = group_place * own_width
    hidden_width = expand_weight.shape[1]
    hidden_start = group_place * hidden_width
    local_heads = own_width // HEAD_DIM
    score_scale = 1.0 / math.sqrt(HEAD_DIM)
    patch_count = row_count * quarter
    image_count = row_count * slot_count
    key_place = jnp.arange(row_length, dtype=jnp.int32)
    row_ends = jnp.cumsum(lengths, axis=1, dtype=jnp.int32)
    row_images = image_index(row_ends, key_place)
    allowed = row_images[:, :, None] == row_images[:, None, :]

    def whole_rows(values):
        joined_rows = lax.all_gather(
            values.reshape(row_count, quarter, -1), "rep", axis=1, tiled=True
        )
        return joined_rows.reshape(row_count * row_length, -1)

    def own_rows(values):
        summed = lax.psum_scatter(
            values.reshape(row_count, row_length, -1), "rep", scatter_dimension=1, tiled=True
        )
        return summed.reshape(patch_count, -1)

    fsdp_size = lax.axis_size("fsdp")
    fsdp_place = lax.axis_index("fsdp")
    own_depth = condition_weight.shape[0]
    condition_values = conditions.astype(float_type)
    activated_own = jax.nn.silu(condition_values).reshape(image_count, model_width).astype(brain_type)
    activated_all = lax.all_gather(activated_own, "fsdp", axis=0, tiled=True)
    activated = lax.dynamic_slice_in_dim(activated_all, fsdp_place * own_depth, own_depth, 1)
    local_biases = (condition_bias, input_bias, attend_bias, expand_bias, reduce_bias)
    bias_sizes = [item.shape[0] for item in local_biases]
    bias_ends = [sum(bias_sizes[:k]) for k in range(len(bias_sizes) + 1)]
    bias_table = lax.all_gather(jnp.concatenate(local_biases), "fsdp", axis=0, tiled=False)
    condition_bias_all, input_bias_all, attend_bias_all, expand_bias_all, reduce_bias_all = [
        bias_table[:, low:high].reshape(-1) for low, high in zip(bias_ends[:-1], bias_ends[1:])
    ]
    condition_bias_own = lax.dynamic_slice_in_dim(
        condition_bias_all.reshape(6, model_width), column_start, own_width, 1
    )
    modulation_parts = jnp.einsum(
        "id,dkm->ikm", activated, condition_weight, preferred_element_type=float_type
    )
    modulation_own = (
        lax.psum_scatter(modulation_parts, "fsdp", scatter_dimension=0, tiled=True)
        + condition_bias_own[None]
    )
    modulation = lax.all_gather(modulation_own, "rep", axis=2, tiled=True).reshape(
        row_count, slot_count, -1
    )
    slot_table = (
        segments[:, :, None] == jnp.arange(slot_count, dtype=jnp.int32)[None, None, :]
    ).astype(float_type)
    per_token = jnp.einsum("rqs,rsm->rqm", slot_table, modulation, precision=highest).reshape(
        patch_count, -1
    )
    shift_one, scale_one, gate_one, shift_two, scale_two, gate_two = jnp.split(per_token, 6, axis=1)
    token_values = tokens.reshape(patch_count, model_width).astype(float_type)

    def split_heads(values):
        return values.reshape(row_count, row_length, local_heads, HEAD_DIM).transpose(2, 0, 1, 3)

    def merge_heads(values):
        return values.transpose(1, 2, 0, 3).reshape(row_count * row_length, own_width)

    def allowed_scores(query_head, key_head):
        scores = (
            jnp.einsum("rqd,rkd->rqk", query_head, key_head, preferred_element_type=float_type)
            * score_scale
        )
        return jnp.where(allowed, scores, -1e30)

    def head_forward(parts):
        query_head, key_head, value_head = parts
        scores = allowed_scores(query_head, key_head)
        row_max = jnp.max(scores, axis=-1, keepdims=True)
        powers = jnp.exp(scores - row_max)
        totals = jnp.sum(powers, axis=-1, keepdims=True)
        weights_low = (powers / totals).astype(brain_type)
        mixed = jnp.einsum(
            "rqk,rkd->rqd", weights_low, value_head, preferred_element_type=float_type
        )
        return (mixed, row_max + jnp.log(totals))

    def head_backward(parts):
        query_head, key_head, value_head, grad_head, log_head = parts
        scores = allowed_scores(query_head, key_head)
        probable = jnp.exp(scores - log_head)
        prob_grad = jnp.einsum(
            "rqd,rkd->rqk", grad_head, value_head, preferred_element_type=float_type
        )
        score_grad = (
            probable * (prob_grad - jnp.sum(probable * prob_grad, axis=-1, keepdims=True))
        ).astype(brain_type)
        query_part = (
            jnp.einsum("rqk,rkd->rqd", score_grad, key_head, preferred_element_type=float_type)
            * score_scale
        )
        key_part = (
            jnp.einsum("rqk,rqd->rkd", score_grad, query_head, preferred_element_type=float_type)
            * score_scale
        )
        value_part = jnp.einsum(
            "rqk,rqd->rkd",
            probable.astype(brain_type),
            grad_head,
            preferred_element_type=float_type,
        )
        return (query_part, key_part, value_part)

    def trunk(gathered):
        (
            input_all,
            input_bias_all,
            attend_all,
            attend_bias_all,
            expand_all,
            expand_bias_all,
            reduce_all,
            reduce_bias_all,
        ) = gathered
        bias_pair = lax.dynamic_slice_in_dim(
            input_bias_all.reshape(2, model_width), column_start, own_width, 1
        )
        expand_bias_own = lax.dynamic_slice_in_dim(expand_bias_all, hidden_start, hidden_width, 0)
        normed_one = modulated(token_values, shift_one, scale_one).astype(brain_type)
        whole_one = whole_rows(normed_one)
        joined = jnp.einsum("nd,dkm->nkm", whole_one, input_all, preferred_element_type=float_type)
        queries = (joined[:, 0] + bias_pair[0]).astype(brain_type)
        keys_row = joined[:, 1].astype(brain_type)
        values_row = (joined[:, 2] + bias_pair[1]).astype(brain_type)
        query_heads = split_heads(queries)
        key_heads = split_heads(keys_row)
        value_heads = split_heads(values_row)
        mixed, log_totals = lax.map(head_forward, (query_heads, key_heads, value_heads))
        attended = merge_heads(mixed).astype(brain_type)
        branch = own_rows(against(attended, attend_all)) + attend_bias_all
        middle = token_values + gate_one * branch
        normed_two = modulated(middle, shift_two, scale_two).astype(brain_type)
        whole_two = whole_rows(normed_two)
        inner = jnp.dot(whole_two, expand_all, preferred_element_type=float_type) + expand_bias_own
        active = gelu_tanh(inner).astype(brain_type)
        outer = own_rows(against(active, reduce_all)) + reduce_bias_all
        result = middle + gate_two * outer
        return (
            result,
            gathered,
            whole_one,
            query_heads,
            key_heads,
            value_heads,
            log_totals,
            attended,
            branch,
            middle,
            whole_two,
            inner,
            active,
            outer,
        )

    input_all, attend_all, expand_all, reduce_all = gather_block(
        input_weight, attend_weight, expand_weight, reduce_weight
    )
    state = trunk(
        (
            input_all,
            input_bias_all,
            attend_all,
            attend_bias_all,
            expand_all,
            expand_bias_all,
            reduce_all,
            reduce_bias_all,
        )
    )
    output = state[0].astype(brain_type).reshape(row_count, quarter, model_width)
    (
        _,
        gathered,
        whole_one,
        query_heads,
        key_heads,
        value_heads,
        log_totals,
        attended,
        branch,
        middle,
        whole_two,
        inner,
        active,
        outer,
    ) = state
    upstream = cotangent.reshape(patch_count, model_width).astype(float_type)
    outer_grad = (gate_two * upstream).astype(brain_type)
    gate_two_grad = upstream * outer
    outer_whole = whole_rows(outer_grad)
    reduce_grad = across(outer_whole, active)
    reduce_bias_grad = column_sums(outer_grad)
    active_grad = jnp.dot(outer_whole, reduce_all, preferred_element_type=float_type)
    _, gelu_back = jax.vjp(gelu_tanh, inner)
    inner_grad = gelu_back(active_grad)[0].astype(brain_type)
    expand_grad = across(whole_two, inner_grad)
    expand_bias_full = spread_columns(
        column_sums(inner_grad), hidden_width * group_size, hidden_start
    )
    two_grad = own_rows(against(inner_grad, expand_all))
    _, second_back = jax.vjp(modulated, middle, shift_two, scale_two)
    middle_norm_grad, shift_two_grad, scale_two_grad = second_back(two_grad)
    middle_grad = upstream + middle_norm_grad
    gate_one_grad = middle_grad * branch
    branch_grad = (gate_one * middle_grad).astype(brain_type)
    branch_whole = whole_rows(branch_grad)
    attend_grad = across(branch_whole, attended)
    attend_bias_grad = column_sums(branch_grad)
    attended_grad = jnp.dot(branch_whole, attend_all, preferred_element_type=float_type).astype(
        brain_type
    )
    grad_heads = split_heads(attended_grad)
    query_parts, key_parts, value_parts = lax.map(
        head_backward, (query_heads, key_heads, value_heads, grad_heads, log_totals)
    )
    query_low = merge_heads(query_parts).astype(brain_type)
    key_low = merge_heads(key_parts).astype(brain_type)
    value_low = merge_heads(value_parts).astype(brain_type)
    joined_grad = jnp.stack([query_low, key_low, value_low], axis=1)
    input_grad = jnp.einsum(
        "nd,nkm->dkm", whole_one, joined_grad, preferred_element_type=float_type
    )
    input_bias_pair = jnp.stack([column_sums(query_low), column_sums(value_low)])
    input_bias_full = spread_columns(input_bias_pair, model_width, column_start).reshape(-1)
    one_grad = own_rows(
        jnp.einsum("nkm,dkm->nd", joined_grad, input_all, preferred_element_type=float_type)
    )
    _, first_back = jax.vjp(modulated, token_values, shift_one, scale_one)
    token_norm_grad, shift_one_grad, scale_one_grad = first_back(one_grad)
    token_grad = (middle_grad + token_norm_grad).reshape(row_count, quarter, model_width)
    six_grads = jnp.stack(
        [
            shift_one_grad,
            scale_one_grad,
            gate_one_grad,
            shift_two_grad,
            scale_two_grad,
            gate_two_grad,
        ],
        axis=1,
    ).reshape(row_count, quarter, 6, model_width)
    modulation_part = jnp.einsum("rqs,rqkm->rskm", slot_table, six_grads, precision=highest)
    modulation_grad = lax.psum_scatter(modulation_part, "rep", scatter_dimension=3, tiled=True)
    modulation_low = lax.all_gather(
        modulation_grad.reshape(image_count, 6, own_width).astype(brain_type),
        "fsdp",
        axis=0,
        tiled=True,
    )
    condition_weight_final = jnp.einsum(
        "id,ikm->dkm", activated, modulation_low, preferred_element_type=float_type
    )
    condition_bias_full = lax.all_gather(
        column_sums(modulation_low), "rep", axis=1, tiled=True
    ).reshape(-1)
    bias_depth = condition_bias.shape[0]
    condition_bias_final = lax.dynamic_slice_in_dim(
        condition_bias_full, fsdp_place * bias_depth, bias_depth, 0
    )
    activated_part = jnp.einsum(
        "ikm,dkm->id", modulation_low, condition_weight, preferred_element_type=float_type
    )
    activated_wide = lax.all_to_all(
        activated_part.reshape(fsdp_size, image_count, own_depth), "fsdp", 0, 0
    )
    activated_row = jnp.transpose(activated_wide, (1, 0, 2)).reshape(image_count, model_width)
    bias_rows = jnp.concatenate(
        [
            item.reshape(fsdp_size, -1)
            for item in (input_bias_full, attend_bias_grad, expand_bias_full, reduce_bias_grad)
        ],
        axis=1,
    )
    bias_own = lax.psum_scatter(bias_rows, "fsdp", scatter_dimension=0, tiled=True).reshape(-1)
    activated_grad, bias_sum = lax.psum((activated_row, bias_own), "rep")
    input_bias_final, attend_bias_final, expand_bias_final, reduce_bias_final = jnp.split(
        bias_sum, [end - bias_sizes[0] for end in bias_ends[2:-1]]
    )
    input_final, attend_final, expand_final, reduce_final = [
        lax.psum_scatter(item.astype(brain_type), "fsdp", scatter_dimension=0, tiled=True).astype(
            float_type
        )
        for item in (input_grad, attend_grad, expand_grad, reduce_grad)
    ]
    _, silu_back = jax.vjp(jax.nn.silu, condition_values)
    condition_grad = silu_back(activated_grad.reshape(row_count, slot_count, model_width))[0]
    return (
        output,
        token_grad,
        condition_grad,
        condition_weight_final,
        condition_bias_final,
        input_final,
        input_bias_final,
        attend_final,
        attend_bias_final,
        expand_final,
        expand_bias_final,
        reduce_final,
        reduce_bias_final,
    )


MESH = pl.DeviceIdType.MESH
HEAD_PAD = 128
TOP_VMEM = 60 * 1024 * 1024


def aligned(index, step):
    return pl.ds(pl.multiple_of(index * step, step), step)


class Links:
    def __init__(self, fsdp_size, group_size):
        self.fsdp_size = fsdp_size
        self.group_size = group_size
        self.depth = fsdp_size // 2
        self.place = lax.axis_index("fsdp")
        self.member = lax.axis_index("rep")
        self.level = self.place // 2
        self.side = self.place % 2
        self.core = self.member % 2
        self.half = self.member // 2

    def to_place(self, place):
        return (place, self.member)

    def to_member(self, member):
        return (self.place, member)

    @property
    def core_mate(self):
        return self.half * 2 + 1 - self.core

    @property
    def half_mate(self):
        return (1 - self.half) * 2 + self.core

    @property
    def far_mate(self):
        return (1 - self.half) * 2 + 1 - self.core

    @property
    def side_mate(self):
        return self.level * 2 + 1 - self.side

    def level_at(self, shift):
        return lax.rem(self.level + shift + self.depth, self.depth)

    def meet(self):
        barrier = pltpu.get_barrier_semaphore()
        count = 0
        for shift in range(1, self.fsdp_size):
            target = lax.rem(self.place + shift, self.fsdp_size)
            pl.semaphore_signal(barrier, inc=1, device_id=self.to_place(target), device_id_type=MESH)
            count += 1
        for shift in range(1, self.group_size):
            target = lax.rem(self.member + shift, self.group_size)
            pl.semaphore_signal(barrier, inc=1, device_id=self.to_member(target), device_id_type=MESH)
            count += 1
        pl.semaphore_wait(barrier, count)


class Sends:
    def __init__(self, send_sems, recv_sems):
        self.send_sems = send_sems
        self.recv_sems = recv_sems
        self.used = 0
        self.open = []

    def slot(self):
        self.used += 1
        return self.used - 1

    def copy(self, slot, source, target, device):
        return pltpu.make_async_remote_copy(
            src_ref=source,
            dst_ref=target,
            send_sem=self.send_sems.at[slot],
            recv_sem=self.recv_sems.at[slot],
            device_id=device,
            device_id_type=MESH,
        )

    def start(self, slot, source, target, device):
        made = self.copy(slot, source, target, device)
        made.start()
        self.open.append(made)

    def arrived(self, slot, target, device):
        self.copy(slot, target, target, device).wait_recv()

    def finish(self):
        for made in self.open:
            made.wait_send()


class GroupGather:
    def __init__(self, links, sends, buffer, quarter):
        self.links, self.sends, self.buffer, self.quarter = links, sends, buffer, quarter
        self.slots = [sends.slot() for _ in range(3)]

    def rows(self, member):
        return self.buffer.at[aligned(member, self.quarter), :]

    def start_core(self):
        own = self.rows(self.links.member)
        mate = self.links.to_member(self.links.core_mate)
        self.sends.start(self.slots[0], own, own, mate)

    def start_half(self):
        own = self.rows(self.links.member)
        self.sends.start(self.slots[1], own, own, self.links.to_member(self.links.half_mate))

    def await_core(self):
        mate = self.links.core_mate
        self.sends.arrived(self.slots[0], self.rows(mate), self.links.to_member(mate))

    def pass_on(self):
        mate = self.links.half_mate
        self.sends.arrived(self.slots[1], self.rows(mate), self.links.to_member(mate))
        passed = self.rows(mate)
        self.sends.start(
            self.slots[2], passed, passed, self.links.to_member(self.links.core_mate)
        )

    def await_far(self):
        mate = self.links.core_mate
        self.sends.arrived(self.slots[2], self.rows(self.links.far_mate), self.links.to_member(mate))


class GroupSum:
    def __init__(self, links, sends, lent, got, crossing, crossed, total):
        self.links, self.sends = links, sends
        self.lent, self.got, self.crossing, self.crossed, self.total = (
            lent,
            got,
            crossing,
            crossed,
            total,
        )
        self.slots = [sends.slot() for _ in range(3)]

    def member_of(self, step):
        half = lax.rem(self.links.half + 1 - step // 2 + 2, 2)
        core = lax.rem(self.links.core + 1 - step % 2 + 2, 2)
        return half * 2 + core

    def lend(self, index):
        mate = self.links.to_member(self.links.core_mate)
        return self.sends.copy(
            self.slots[0] + index, self.lent.at[index], self.got.at[index], mate
        )

    def cross(self):
        mate = self.links.to_member(self.links.half_mate)
        return self.sends.copy(self.slots[2], self.crossing, self.crossed, mate)

    def step(self, step, value, crosses):
        index = step // 2
        self.total[...] = value

        @pl.when(step % 2 == 0)
        def _():
            self.lent[index] = self.total[...].astype(brain_type)
            self.lend(index).start()

        @pl.when(step % 2 == 1)
        def _():
            self.lend(index).wait_recv()

        @pl.when(step == 1)
        def _():
            self.crossing[...] = (self.total[...] + self.got[0].astype(float_type)).astype(
                brain_type
            )
            if crosses:
                self.cross().start()

    def note(self, crosses):
        self.sends.open += [self.lend(0), self.lend(1)]
        if crosses:
            self.sends.open.append(self.cross())

    def await_cross(self):
        self.sends.arrived(
            self.slots[2], self.crossed, self.links.to_member(self.links.half_mate)
        )

    def rows(self, rows):
        return (
            self.total[rows, :]
            + self.got[1, rows, :].astype(float_type)
            + self.crossed[rows, :].astype(float_type)
        )


def normed_rows(values):
    center = jnp.mean(values, axis=-1, keepdims=True)
    shifted = values - center
    spread = jnp.mean(shifted * shifted, axis=-1, keepdims=True)
    root = lax.rsqrt(spread + epsilon)
    return shifted * root, root


def spread_heads(source, target, rows, first, heads, target_first):
    for head in range(heads):
        low, to = HEAD_DIM * (first + head), HEAD_PAD * (target_first + head)
        target[rows, to : to + HEAD_DIM] = source[rows, low : low + HEAD_DIM]


def forward_kernel(
    sizes,
    tokens,
    upstream,
    act_send,
    cond_weight,
    bias_table,
    slot_mask,
    mask_bias,
    weight_zero,
    weight_one,
    weight_two,
    mod_out,
    bias_out,
    one_out,
    heads_out,
    log_out,
    mixed_out,
    branch_out,
    middle_out,
    two_out,
    upper_out,
    input_out,
    attend_out,
    expand_out,
    reduce_out,
    act_got,
    mod_parts,
    mod_got,
    mod_row,
    group_got,
    weights,
    normed,
    lent,
    got,
    crossing,
    crossed,
    total,
    one,
    two,
    upper,
    heads,
    mixed,
    input_pad,
    attend_pad,
    send_sems,
    recv_sems,
    local_sems,
):
    fsdp_size, group_size, quarter, width, own_width, shard = sizes
    links = Links(fsdp_size, group_size)
    sends = Sends(send_sems, recv_sems)
    blocks = (weight_zero, weight_one, weight_two)
    local_heads = own_width // HEAD_DIM
    head_span = local_heads * HEAD_PAD
    chunk = 32
    chunks = quarter // chunk

    act_slots = [sends.slot() for _ in range(fsdp_size)]
    mod_slots = [sends.slot() for _ in range(fsdp_size)]
    group_slots = [sends.slot() for _ in range(group_size)]
    level_slots = [[sends.slot() for _ in range(links.depth)] for _ in blocks]
    side_slots = [[sends.slot() for _ in range(links.depth)] for _ in blocks]
    onward_slots = [sends.slot() for _ in blocks]
    gather_one = GroupGather(links, sends, one, quarter)
    gather_two = GroupGather(links, sends, two, quarter)
    gather_upper = GroupGather(links, sends, upper, quarter)
    branch_sum = GroupSum(links, sends, lent, got, crossing, crossed, total)
    opened = []

    def shard_rows(block, place):
        return weights.at[block, aligned(place, shard), :]

    inner = links.level * (links.depth - 1 - links.level) > 0
    near = jnp.where(links.level < 2, 3, 1)
    order = (2, near, 4 - near)

    def level_copy(block, shift):
        own = shard_rows(block, links.place)
        target = links.level_at(shift) * 2 + links.side
        return sends.copy(
            level_slots[block][0] + shift, blocks[block], own, links.to_place(target)
        )

    def offer_levels(block):
        level_copy(block, 2).start()
        level_copy(block, 4 - near).start()

        @pl.when(inner)
        def _():
            level_copy(block, near).start()

    def offer_side(block):
        own = shard_rows(block, links.place)
        sends.start(side_slots[block][0], blocks[block], own, links.to_place(links.side_mate))

    def keep_own(block):
        kept = pltpu.make_async_copy(
            blocks[block], shard_rows(block, links.place), local_sems.at[block]
        )
        kept.start()
        return kept

    def forward_copy(block):
        rows = shard_rows(block, links.level_at(2) * 2 + links.side)
        return pltpu.make_async_remote_copy(
            src_ref=rows,
            dst_ref=rows,
            send_sem=send_sems.at[onward_slots[block]],
            recv_sem=recv_sems.at[level_slots[block][0] + 2 * links.level - 1],
            device_id=links.to_place((3 * links.level - 3) * 2 + links.side),
            device_id_type=MESH,
        )

    def side_copy(block, shift):
        rows = shard_rows(block, links.level_at(-shift) * 2 + links.side)
        return sends.copy(
            side_slots[block][0] + shift, rows, rows, links.to_place(links.side_mate)
        )

    def relay(block, index):
        shift = order[index]
        source = links.level_at(-shift) * 2 + links.side
        rows = shard_rows(block, source)
        sends.arrived(level_slots[block][0] + shift, rows, links.to_place(source))
        if index == 0:

            @pl.when(inner)
            def _():
                forward_copy(block).start()

        side_copy(block, shift).start()
        return source

    def side_arrived(block, index):
        shift = order[index - 1] if index else 0
        source = links.level_at(-shift) * 2 + 1 - links.side
        sends.arrived(
            side_slots[block][0] + shift, shard_rows(block, source), links.to_place(links.side_mate)
        )
        return source

    def finish_weights(block):
        level_copy(block, 2).wait_send()
        level_copy(block, 4 - near).wait_send()

        @pl.when(inner)
        def _():
            level_copy(block, near).wait_send()
            forward_copy(block).wait_send()

        for shift in order:
            side_copy(block, shift).wait_send()

    def keep(index, source, target):
        made = pltpu.make_async_copy(source, target, local_sems.at[index])
        made.start()
        opened.append(made)

    links.meet()
    for shift in range(1, fsdp_size):
        target = lax.rem(links.place + shift, fsdp_size)
        sends.start(
            act_slots[shift], act_send.at[target], act_got.at[links.place], links.to_place(target)
        )
    act_got[pl.ds(links.place, 1)] = act_send[pl.ds(links.place, 1)]
    kept_zero, kept_one, kept_two = [keep_own(block) for block in range(3)]

    def norm_tokens(index, carry):
        rows = aligned(index, chunk)
        normed[rows, :] = normed_rows(tokens[rows, :].astype(float_type))[0]
        return carry

    for shift in range(1, fsdp_size):
        source = lax.rem(links.place + fsdp_size - shift, fsdp_size)
        sends.arrived(act_slots[shift], act_got.at[source], links.to_place(source))
    activated = act_got[...].reshape(fsdp_size * 8, shard).astype(brain_type)
    mod_parts[...] = (
        jnp.dot(activated, cond_weight[...], preferred_element_type=float_type).reshape(
            fsdp_size, 8, 6 * own_width
        )
        + bias_table[...][None]
    )
    for shift in range(1, fsdp_size):
        target = lax.rem(links.place + shift, fsdp_size)
        sends.start(
            mod_slots[shift], mod_parts.at[target], mod_got.at[links.place], links.to_place(target)
        )
    for block in range(3):
        offer_levels(block)
    offer_side(0)
    offer_side(1)
    mod_got[pl.ds(links.place, 1)] = mod_parts[pl.ds(links.place, 1)]
    lax.fori_loop(0, chunks, norm_tokens, 0)
    input_pad[...] = jnp.zeros_like(input_pad)
    attend_pad[...] = jnp.zeros_like(attend_pad)
    kept_zero.wait()

    def spread_shard(place):
        rows = aligned(place, shard)
        spread_heads(weights.at[0], input_pad, rows, 0, 3 * local_heads, 0)
        spread_heads(weights.at[0], attend_pad, rows, 3 * local_heads, local_heads, 0)

    spread_shard(links.place)
    for shift in range(1, fsdp_size):
        source = lax.rem(links.place + fsdp_size - shift, fsdp_size)
        sends.arrived(mod_slots[shift], mod_got.at[source], links.to_place(source))
    summed = mod_got[0]
    for index in range(1, fsdp_size):
        summed = summed + mod_got[index]
    mod_row[...] = summed
    for shift in range(1, group_size):
        target = lax.rem(links.member + shift, group_size)
        sends.start(group_slots[shift], mod_row, group_got.at[links.member], links.to_member(target))
    group_got[pl.ds(links.member, 1)] = mod_row[...][None]
    bias_out[...] = mod_row[...]
    for shift in range(1, group_size):
        source = lax.rem(links.member + group_size - shift, group_size)
        sends.arrived(group_slots[shift], group_got.at[source], links.to_member(source))
    chosen = slot_mask[:, 0:1]
    for index in range(6):
        full = jnp.concatenate(
            [
                group_got[member, :, index * own_width : (index + 1) * own_width]
                for member in range(group_size)
            ],
            axis=1,
        )
        mod_out[index : index + 1, :] = jnp.sum(full * chosen, axis=0, keepdims=True)
    mod_out[6:8, :] = jnp.zeros((2, width), float_type)

    own_rows = links.member * quarter

    def first_norm(index, carry):
        rows = aligned(index, chunk)
        to = pl.ds(pl.multiple_of(own_rows + index * chunk, chunk), chunk)
        one[to, :] = (normed[rows, :] * (1.0 + mod_out[1:2, :]) + mod_out[0:1, :]).astype(brain_type)
        return carry

    lax.fori_loop(0, chunks, first_norm, 0)
    gather_one.start_half()
    gather_one.start_core()
    first_sources = [relay(0, index) for index in range(links.depth - 1)]
    offer_side(2)

    def upper_rows(index, carry):
        rows = aligned(index, chunk)
        to = pl.ds(pl.multiple_of(own_rows + index * chunk, chunk), chunk)
        upper[to, :] = (mod_out[5:6, :] * upstream[rows, :].astype(float_type)).astype(brain_type)
        return carry

    lax.fori_loop(0, chunks, upper_rows, 0)

    for source in first_sources:
        spread_shard(source)
    gather_one.pass_on()
    gather_upper.start_half()
    gather_upper.start_core()
    gather_one.await_core()
    for shift in range(links.depth):
        spread_shard(side_arrived(0, shift))
    gather_one.await_far()
    keep(3, one, one_out)
    keep(4, input_pad, input_out)
    keep(5, attend_pad, attend_out)

    bias_pad = mod_row[7:8, 0 : 2 * head_span]

    def project(index, carry):
        rows = aligned(index, quarter)
        values = jnp.dot(one[rows, :], input_pad[...], preferred_element_type=float_type)
        heads[rows, 0:head_span] = (values[:, 0:head_span] + bias_pad[:, 0:head_span]).astype(
            brain_type
        )
        heads[rows, head_span : 2 * head_span] = values[:, head_span : 2 * head_span].astype(
            brain_type
        )
        heads[rows, 2 * head_span :] = (
            values[:, 2 * head_span :] + bias_pad[:, head_span:]
        ).astype(brain_type)
        return carry

    lax.fori_loop(0, group_size, project, 0)
    keep(6, heads, heads_out)

    power_scale = math.log2(math.e) / math.sqrt(HEAD_DIM)

    def attend(head, turn):
        part = branch_sum.member_of(turn)
        step = turn * local_heads + head
        rows = aligned(part, quarter)

        def columns(base):
            return aligned(base * local_heads + head, HEAD_PAD)

        raw = lax.dot_general(
            heads[rows, columns(0)],
            heads[:, columns(1)],
            (((1,), (1,)), ((), ())),
            preferred_element_type=float_type,
        )
        scores = jnp.concatenate(
            [
                raw[:, other * quarter : (other + 1) * quarter] + mask_bias[part, other]
                for other in range(group_size)
            ],
            axis=1,
        )
        top = jnp.max(scores, axis=1, keepdims=True)
        powers = jnp.exp2(scores * power_scale - top * power_scale)
        totals = jnp.sum(powers, axis=1, keepdims=True)
        value = jnp.dot(
            powers.astype(brain_type), heads[:, columns(2)], preferred_element_type=float_type
        )
        mixed[rows, aligned(head, HEAD_PAD)] = (value / totals).astype(brain_type)
        turned = jnp.transpose(
            jnp.broadcast_to(top * power_scale + jnp.log2(totals), (quarter, HEAD_PAD))
        )
        log_out[head, :, rows] = turned[0:8, :]
        for index, late in enumerate((1, 3, 5)):

            @pl.when(step == late)
            def _():
                relay(1, index)

        @pl.when(step == 4)
        def _():
            gather_upper_in_loop()

        return turn

    def gather_upper_in_loop():
        mate = links.half_mate
        passed = gather_upper.rows(mate)
        sends.arrived(gather_upper.slots[1], passed, links.to_member(mate))
        sends.copy(
            gather_upper.slots[2], passed, passed, links.to_member(links.core_mate)
        ).start()

    def branch_part(member):
        return lax.dot_general(
            mixed[aligned(member, quarter), :],
            attend_pad[...],
            (((1,), (1,)), ((), ())),
            preferred_element_type=float_type,
        )

    def attend_turn(turn, carry):
        lax.fori_loop(0, local_heads, attend, turn)
        branch_sum.step(turn, branch_part(branch_sum.member_of(turn)), True)
        return carry

    lax.fori_loop(0, group_size, attend_turn, 0)
    passed = gather_upper.rows(links.half_mate)
    sends.open.append(
        sends.copy(gather_upper.slots[2], passed, passed, links.to_member(links.core_mate))
    )
    keep(7, mixed, mixed_out)
    branch_sum.note(True)
    gather_upper.await_core()
    gather_upper.await_far()
    keep(8, upper, upper_out)
    for index in range(links.depth - 1):
        relay(2, index)
    branch_sum.await_cross()

    def second_norm(index, carry):
        rows = aligned(index, chunk)
        to = pl.ds(pl.multiple_of(own_rows + index * chunk, chunk), chunk)
        branch = branch_sum.rows(rows) + mod_row[5:6, 0:width]
        branch_out[rows, :] = branch
        middle = tokens[rows, :].astype(float_type) + mod_out[2:3, :] * branch
        middle_out[rows, :] = middle
        two[to, :] = (normed_rows(middle)[0] * (1.0 + mod_out[4:5, :]) + mod_out[3:4, :]).astype(
            brain_type
        )
        return carry

    lax.fori_loop(0, chunks, second_norm, 0)
    gather_two.start_half()
    gather_two.start_core()
    gather_two.pass_on()
    kept_one.wait()
    for shift in range(links.depth):
        side_arrived(1, shift)
    keep(9, weights.at[1], expand_out)
    gather_two.await_core()
    gather_two.await_far()
    keep(10, two, two_out)
    kept_two.wait()
    for shift in range(links.depth):
        side_arrived(2, shift)
    keep(11, weights.at[2], reduce_out)
    for made in opened:
        made.wait()
    for block in range(3):
        finish_weights(block)
    sends.finish()


def run_forward(
    sizes, tokens, upstream, act_send, cond_weight, bias_table, slot_mask, mask_bias, weights
):
    fsdp_size, group_size, quarter, width, own_width, shard = sizes
    row_length = quarter * group_size
    local_heads = own_width // HEAD_DIM
    span = local_heads * HEAD_PAD
    hidden = weights[1].shape[1]
    in_vmem = pl.BlockSpec(memory_space=pltpu.VMEM)
    anywhere = pl.BlockSpec(memory_space=pl.ANY)
    shape = jax.ShapeDtypeStruct
    out_shape = (
        shape((8, width), float_type),
        shape((8, 6 * own_width), float_type),
        shape((row_length, width), brain_type),
        shape((row_length, 3 * span), brain_type),
        shape((local_heads, 8, row_length), float_type),
        shape((row_length, span), brain_type),
        shape((quarter, width), float_type),
        shape((quarter, width), float_type),
        shape((row_length, width), brain_type),
        shape((row_length, width), brain_type),
        shape((width, 3 * span), brain_type),
        shape((width, span), brain_type),
        shape((width, hidden), brain_type),
        shape((width, hidden), brain_type),
    )
    out_specs = (
        in_vmem,
        in_vmem,
        anywhere,
        anywhere,
        in_vmem,
        anywhere,
        in_vmem,
        in_vmem,
        anywhere,
        anywhere,
        anywhere,
        anywhere,
        anywhere,
        anywhere,
    )
    copies = 2 * fsdp_size + group_size + 6 * (fsdp_size // 2) + 3 * 3 + 6
    vmem = pltpu.VMEM
    scratch = [
        vmem((fsdp_size, 8, shard), float_type),
        vmem((fsdp_size, 8, 6 * own_width), float_type),
        vmem((fsdp_size, 8, 6 * own_width), float_type),
        vmem((8, 6 * own_width), float_type),
        vmem((group_size, 8, 6 * own_width), float_type),
        vmem((3, width, hidden), brain_type),
        vmem((quarter, width), float_type),
        vmem((2, quarter, width), brain_type),
        vmem((2, quarter, width), brain_type),
        vmem((quarter, width), brain_type),
        vmem((quarter, width), brain_type),
        vmem((quarter, width), float_type),
        vmem((row_length, width), brain_type),
        vmem((row_length, width), brain_type),
        vmem((row_length, width), brain_type),
        vmem((row_length, 3 * span), brain_type),
        vmem((row_length, span), brain_type),
        vmem((width, 3 * span), brain_type),
        vmem((width, span), brain_type),
        pltpu.SemaphoreType.DMA((copies,)),
        pltpu.SemaphoreType.DMA((copies,)),
        pltpu.SemaphoreType.DMA((12,)),
    ]
    return pl.pallas_call(
        functools.partial(forward_kernel, sizes),
        out_shape=out_shape,
        in_specs=[in_vmem] * 6 + [pl.BlockSpec(memory_space=pltpu.SMEM)] + [in_vmem] * 3,
        out_specs=out_specs,
        scratch_shapes=scratch,
        compiler_params=pltpu.CompilerParams(
            collective_id=0, has_side_effects=True, vmem_limit_bytes=TOP_VMEM
        ),
        name="forward_row",
    )(tokens, upstream, act_send, cond_weight, bias_table, slot_mask, mask_bias, *weights)


class ShardSum:
    def __init__(self, links, sends, block, side_got, level_got, shard):
        self.links, self.sends, self.block = links, sends, block
        self.side_got, self.level_got, self.shard = side_got, level_got, shard
        self.side_slots = [sends.slot() for _ in range(links.depth)]
        self.level_slots = [sends.slot() for _ in range(links.depth)]

    def order(self):
        return list(range(1, self.links.depth)) + [0]

    def rows(self, place):
        return aligned(place, self.shard)

    def start(self):
        links = self.links
        for shift in self.order():
            level = links.level_at(shift)
            self.sends.start(
                self.side_slots[shift],
                self.block.at[self.rows(level * 2 + 1 - links.side), :],
                self.side_got.at[shift],
                links.to_place(links.side_mate),
            )

    def fold(self, shift, note=True):
        links = self.links
        self.sends.arrived(
            self.side_slots[shift], self.side_got.at[shift], links.to_place(links.side_mate)
        )
        if shift:
            target = links.level_at(shift) * 2 + links.side
            rows = self.rows(target)
            self.block[rows, :] = (
                self.block[rows, :].astype(float_type) + self.side_got[shift].astype(float_type)
            ).astype(brain_type)
            self.push(shift).start()
            if note:
                self.sends.open.append(self.push(shift))

    def push(self, shift):
        links = self.links
        target = links.level_at(shift) * 2 + links.side
        return self.sends.copy(
            self.level_slots[shift],
            self.block.at[self.rows(target), :],
            self.level_got.at[shift],
            links.to_place(target),
        )

    def total(self):
        links = self.links
        summed = self.block[self.rows(links.place), :].astype(float_type) + self.side_got[0].astype(
            float_type
        )
        for shift in range(1, links.depth):
            source = links.level_at(-shift) * 2 + links.side
            self.sends.arrived(
                self.level_slots[shift], self.level_got.at[shift], links.to_place(source)
            )
            summed = summed + self.level_got[shift].astype(float_type)
        return summed


def fold_rows(values):
    count, width = values.shape
    return jnp.sum(values.reshape(count // 8, 8, width), axis=0)


def gelu_pair(values):
    root = math.sqrt(2.0 / math.pi)
    square = values * values
    bend = jnp.tanh(values * (root + root * 0.044715 * square))
    half = 0.5 * (1.0 + bend)
    slope = half + (0.5 * values) * (1.0 - bend * bend) * (root + root * 3 * 0.044715 * square)
    return values * half, slope


def across_rows(left, right):
    return lax.dot_general(left, right, (((0,), (0,)), ((), ())), preferred_element_type=float_type)


def middle_kernel(
    sizes,
    two,
    upper,
    expand,
    reduce,
    mods,
    biases,
    middle,
    branch,
    upstream,
    attend_pad,
    mixed,
    far_out,
    near_out,
    grads_out,
    attend_out,
    expand_out,
    reduce_out,
    slope_out,
    sums_out,
    active,
    inner_grad,
    lent_t,
    got_t,
    crossing_t,
    crossed_t,
    total_t,
    lent_o,
    got_o,
    branch_whole,
    reduce_grad,
    side_got,
    level_got,
    expand_grad,
    sums,
    send_sems,
    recv_sems,
    local_sems,
):
    fsdp_size, group_size, quarter, width, own_width, shard = sizes
    links = Links(fsdp_size, group_size)
    sends = Sends(send_sems, recv_sems)
    local_heads = own_width // HEAD_DIM
    chunk = 32
    chunks = quarter // chunk
    two_sum = GroupSum(links, sends, lent_t, got_t, crossing_t, crossed_t, total_t)
    outer_sum = GroupSum(links, sends, lent_o, got_o, far_out, None, near_out)
    gather = GroupGather(links, sends, branch_whole, quarter)
    reduce_sum = ShardSum(links, sends, reduce_grad, side_got, level_got, shard)
    links.meet()
    sums[...] = jnp.zeros_like(sums)
    hidden = expand.shape[1]

    def feed(step, carry):
        rows = aligned(two_sum.member_of(step), quarter)
        inner = (
            jnp.dot(two[rows, :], expand[...], preferred_element_type=float_type)
            + biases[4:5, 0:hidden]
        )
        active_grad = jnp.dot(upper[rows, :], reduce[...], preferred_element_type=float_type)
        value, slope = gelu_pair(inner)
        active[rows, :] = value.astype(brain_type)
        low = (active_grad * slope).astype(brain_type)
        inner_grad[rows, :] = low
        sums[4] = sums[4] + fold_rows(low.astype(float_type))
        two_sum.step(step, against(inner_grad[rows, :], expand[...]), True)
        outer_sum.step(step, against(active[rows, :], reduce[...]), False)
        return carry

    lax.fori_loop(0, group_size, feed, 0)
    two_sum.note(True)
    outer_sum.note(False)

    def near_rows(index, carry):
        rows = aligned(index, chunk)
        near_out[rows, :] = near_out[rows, :] + got_o[1, rows, :].astype(float_type)
        return carry

    lax.fori_loop(0, chunks, near_rows, 0)

    part = 384

    def reduce_part(index, carry):
        columns = aligned(index, part)
        reduce_grad[columns, :] = across_rows(upper[:, columns], active[...]).astype(brain_type)
        return carry

    lax.fori_loop(0, width // part, reduce_part, 0)
    reduce_sum.start()
    two_sum.await_cross()
    own_rows = links.member * quarter

    def second_back(index, carry):
        rows = aligned(index, chunk)
        to = pl.ds(pl.multiple_of(own_rows + index * chunk, chunk), chunk)
        two_grad = two_sum.rows(rows)
        normed, root = normed_rows(middle[rows, :])
        scaled = two_grad * (1.0 + mods[4:5, :])
        centered = (
            scaled
            - jnp.mean(scaled, axis=-1, keepdims=True)
            - normed * jnp.mean(scaled * normed, axis=-1, keepdims=True)
        )
        slope = upstream[rows, :].astype(float_type) + root * centered
        slope_out[rows, :] = slope
        low = (mods[2:3, :] * slope).astype(brain_type)
        branch_whole[to, :] = low
        sums[0] = sums[0] + fold_rows(slope * branch[rows, :])
        sums[1] = sums[1] + fold_rows(two_grad)
        sums[2] = sums[2] + fold_rows(two_grad * normed)
        sums[3] = sums[3] + fold_rows(low.astype(float_type))
        sums[5] = sums[5] + fold_rows(upper[to, :].astype(float_type))
        return carry

    lax.fori_loop(0, chunks, second_back, 0)
    gather.start_half()
    gather.start_core()

    def expand_part(index, carry):
        columns = aligned(index, part)
        expand_grad[columns, :] = across_rows(two[:, columns], inner_grad[...]).astype(brain_type)
        return carry

    lax.fori_loop(0, width // part, expand_part, 0)
    kept_expand = pltpu.make_async_copy(expand_grad, expand_out, local_sems.at[0])
    kept_expand.start()
    reduce_sum.fold(1)
    for index in range(6):
        sums_out[index : index + 1, :] = jnp.sum(sums[index], axis=0, keepdims=True)
    sums_out[6:8, :] = jnp.zeros((2, width), float_type)
    gather.pass_on()
    reduce_sum.fold(2)
    gather.await_core()
    gather.await_far()

    def head_grads(index, carry):
        rows = aligned(index, quarter)
        grads_out[rows, :] = jnp.dot(
            branch_whole[rows, :], attend_pad[...], preferred_element_type=float_type
        ).astype(brain_type)
        return carry

    lax.fori_loop(0, group_size, head_grads, 0)

    def attend_part(index, carry):
        columns = aligned(index, part)
        value = across_rows(branch_whole[:, columns], mixed[...])
        for head in range(local_heads):
            attend_out[columns, head * HEAD_DIM : (head + 1) * HEAD_DIM] = value[
                :, head * HEAD_PAD : head * HEAD_PAD + HEAD_DIM
            ].astype(brain_type)
        return carry

    lax.fori_loop(0, width // part, attend_part, 0)
    reduce_sum.fold(3)
    reduce_sum.fold(0)
    reduce_out[...] = reduce_sum.total()
    kept_expand.wait()
    sends.finish()


def run_middle(sizes, *arrays):
    fsdp_size, group_size, quarter, width, own_width, shard = sizes
    row_length = quarter * group_size
    span = own_width // HEAD_DIM * HEAD_PAD
    hidden = arrays[2].shape[1]
    depth = fsdp_size // 2
    in_vmem = pl.BlockSpec(memory_space=pltpu.VMEM)
    anywhere = pl.BlockSpec(memory_space=pl.ANY)
    shape = jax.ShapeDtypeStruct
    vmem = pltpu.VMEM
    copies = 3 + 3 + 3 + 2 * depth
    return pl.pallas_call(
        functools.partial(middle_kernel, sizes),
        out_shape=(
            shape((quarter, width), brain_type),
            shape((quarter, width), float_type),
            shape((row_length, span), brain_type),
            shape((width, own_width), brain_type),
            shape((width, hidden), brain_type),
            shape((shard, hidden), float_type),
            shape((quarter, width), float_type),
            shape((8, width), float_type),
        ),
        in_specs=[in_vmem] * len(arrays),
        out_specs=(in_vmem, in_vmem, in_vmem, in_vmem, anywhere, in_vmem, in_vmem, in_vmem),
        scratch_shapes=[
            vmem((row_length, hidden), brain_type),
            vmem((row_length, hidden), brain_type),
            vmem((2, quarter, width), brain_type),
            vmem((2, quarter, width), brain_type),
            vmem((quarter, width), brain_type),
            vmem((quarter, width), brain_type),
            vmem((quarter, width), float_type),
            vmem((2, quarter, width), brain_type),
            vmem((2, quarter, width), brain_type),
            vmem((row_length, width), brain_type),
            vmem((width, hidden), brain_type),
            vmem((depth, shard, hidden), brain_type),
            vmem((depth, shard, hidden), brain_type),
            vmem((width, hidden), brain_type),
            vmem((6, 8, width), float_type),
            pltpu.SemaphoreType.DMA((copies,)),
            pltpu.SemaphoreType.DMA((copies,)),
            pltpu.SemaphoreType.DMA((1,)),
        ],
        compiler_params=pltpu.CompilerParams(
            collective_id=1, has_side_effects=True, vmem_limit_bytes=TOP_VMEM
        ),
        name="middle_row",
    )(*arrays)


def backward_kernel(
    sizes,
    heads,
    logs,
    head_grads,
    mixed,
    one,
    input_pad,
    tokens,
    mods,
    biases,
    slope,
    upstream,
    middle,
    far_sum,
    near_sum,
    expand_grad,
    attend_grad,
    sums_in,
    cond_weight,
    act_send,
    slot_mask,
    mask_bias,
    output_out,
    token_out,
    act_out,
    cond_out,
    bias_out,
    expand_out,
    input_out,
    crossed_o,
    joined,
    query_sum,
    delta_rows,
    lent,
    got,
    crossing,
    crossed,
    total,
    expand_block,
    input_block,
    side_one,
    level_one,
    side_zero,
    level_zero,
    sums,
    slabs,
    slab_got,
    place_slab,
    place_got,
    act_part,
    act_got,
    act_group,
    bias_row,
    act_all,
    send_sems,
    recv_sems,
    local_sems,
):
    fsdp_size, group_size, quarter, width, own_width, shard = sizes
    links = Links(fsdp_size, group_size)
    sends = Sends(send_sems, recv_sems)
    local_heads = own_width // HEAD_DIM
    span = local_heads * HEAD_PAD
    row_length = quarter * group_size
    chunk = 32
    chunks = quarter // chunk
    one_sum = GroupSum(links, sends, lent, got, crossing, crossed, total)
    expand_sum = ShardSum(links, sends, expand_block, side_one, level_one, shard)
    input_sum = ShardSum(links, sends, input_block, side_zero, level_zero, shard)
    outer_slot = sends.slot()
    act_slots = [sends.slot() for _ in range(fsdp_size)]
    slab_slots = [sends.slot() for _ in range(group_size)]
    place_slots = [sends.slot() for _ in range(fsdp_size)]
    part_slots = [sends.slot() for _ in range(fsdp_size)]
    row_slots = [sends.slot() for _ in range(group_size)]
    bias_slots = [sends.slot() for _ in range(group_size)]

    def to_places(slots, source_of, target):
        for shift in range(1, fsdp_size):
            place = lax.rem(links.place + shift, fsdp_size)
            sends.start(
                slots[shift], source_of(place), target.at[links.place], links.to_place(place)
            )

    def from_places(slots, target):
        for shift in range(1, fsdp_size):
            place = lax.rem(links.place + fsdp_size - shift, fsdp_size)
            sends.arrived(slots[shift], target.at[place], links.to_place(place))

    def to_members(slots, source_of, target):
        for shift in range(1, group_size):
            member = lax.rem(links.member + shift, group_size)
            sends.start(
                slots[shift], source_of(member), target.at[links.member], links.to_member(member)
            )

    def from_members(slots, target):
        for shift in range(1, group_size):
            member = lax.rem(links.member + group_size - shift, group_size)
            sends.arrived(slots[shift], target.at[member], links.to_member(member))

    links.meet()
    sends.start(outer_slot, far_sum, crossed_o, links.to_member(links.half_mate))
    kept = pltpu.make_async_copy(expand_grad, expand_block, local_sems.at[0])
    kept.start()
    to_places(act_slots, lambda place: act_send.at[place], act_all)
    act_all[pl.ds(links.place, 1)] = act_send[pl.ds(links.place, 1)]
    sums[...] = jnp.zeros_like(sums)
    kept.wait()
    expand_sum.start()
    attend_first = 3 * own_width
    input_block[:, attend_first : attend_first + own_width] = attend_grad[...]

    power_scale = math.log2(math.e) / math.sqrt(HEAD_DIM)
    score_scale = 1.0 / math.sqrt(HEAD_DIM)

    def columns(base, head):
        return aligned(base * local_heads + head, HEAD_PAD)

    def head_deltas(head, carry):
        product = head_grads[:, columns(0, head)].astype(float_type) * mixed[
            :, columns(0, head)
        ].astype(float_type)
        delta = jnp.sum(product, axis=1, keepdims=True)
        turned = jnp.transpose(jnp.broadcast_to(delta, (row_length, HEAD_PAD)))
        delta_rows[head] = turned[0:8, :]
        return carry

    lax.fori_loop(0, local_heads, head_deltas, 0)

    def attend_back(step, carry):
        head, part = step // group_size, step % group_size
        rows = aligned(part, quarter)
        query = heads[:, columns(0, head)]
        key = heads[rows, columns(1, head)]
        value = heads[rows, columns(2, head)]
        grad = head_grads[:, columns(0, head)]
        shift = jnp.concatenate(
            [
                mask_bias[part, other]
                - logs[head, 0:1, other * quarter : (other + 1) * quarter]
                for other in range(group_size)
            ],
            axis=1,
        )
        probable = jnp.exp2(against(key, query) * power_scale + shift)
        value_grad = jnp.dot(probable.astype(brain_type), grad, preferred_element_type=float_type)
        score_grad = (probable * (against(value, grad) - delta_rows[head, 0:1, :])).astype(
            brain_type
        )
        key_grad = jnp.dot(score_grad, query, preferred_element_type=float_type)
        joined[rows, columns(1, head)] = (key_grad * score_scale).astype(brain_type)
        joined[rows, columns(2, head)] = value_grad.astype(brain_type)
        query_grad = across_rows(score_grad, key)

        @pl.when(part == 0)
        def _():
            query_sum[...] = query_grad

        @pl.when(part > 0)
        def _():
            query_sum[...] = query_sum[...] + query_grad

        @pl.when(part == group_size - 1)
        def _():
            joined[:, columns(0, head)] = (query_sum[...] * score_scale).astype(brain_type)

        for index, late in ((1, 5), (2, 9), (3, 13)):

            @pl.when(step == late)
            def _():
                expand_sum.fold(index, False)

        return carry

    lax.fori_loop(0, group_size * local_heads, attend_back, 0)
    for index in range(1, links.depth):
        sends.open.append(expand_sum.push(index))

    part = 384

    def input_part(index, carry):
        picked = aligned(index, part)
        value = across_rows(one[:, picked], joined[...])
        for head in range(3 * local_heads):
            input_block[picked, head * HEAD_DIM : (head + 1) * HEAD_DIM] = value[
                :, head * HEAD_PAD : head * HEAD_PAD + HEAD_DIM
            ].astype(brain_type)
        return carry

    lax.fori_loop(0, width // part, input_part, 0)
    input_sum.start()

    def one_step(step, carry):
        rows = aligned(one_sum.member_of(step), quarter)
        one_sum.step(step, against(joined[rows, :], input_pad[...]), True)
        return carry

    lax.fori_loop(0, group_size, one_step, 0)
    one_sum.note(True)
    expand_sum.fold(0)

    sends.arrived(outer_slot, crossed_o, links.to_member(links.half_mate))

    def finish_rows(index, carry):
        rows = aligned(index, chunk)
        outer = (
            near_sum[rows, :] + crossed_o[rows, :].astype(float_type) + biases[6:7, 0:width]
        )
        output_out[rows, :] = (middle[rows, :] + mods[5:6, :] * outer).astype(brain_type)
        sums[2] = sums[2] + fold_rows(upstream[rows, :].astype(float_type) * outer)
        return carry

    lax.fori_loop(0, chunks, finish_rows, 0)

    def pair_sums(index, carry):
        rows = aligned(index, 128)
        sums[3, :, 0:span] = sums[3, :, 0:span] + fold_rows(
            joined[rows, 0:span].astype(float_type)
        )
        sums[4, :, 0:span] = sums[4, :, 0:span] + fold_rows(
            joined[rows, 2 * span : 3 * span].astype(float_type)
        )
        return carry

    lax.fori_loop(0, row_length // 128, pair_sums, 0)
    input_sum.fold(1)
    expand_out[...] = expand_sum.total()
    one_sum.await_cross()

    def first_back(index, carry):
        rows = aligned(index, chunk)
        one_grad = one_sum.rows(rows)
        normed, root = normed_rows(tokens[rows, :].astype(float_type))
        scaled = one_grad * (1.0 + mods[1:2, :])
        centered = (
            scaled
            - jnp.mean(scaled, axis=-1, keepdims=True)
            - normed * jnp.mean(scaled * normed, axis=-1, keepdims=True)
        )
        token_out[rows, :] = slope[rows, :] + root * centered
        sums[0] = sums[0] + fold_rows(one_grad)
        sums[1] = sums[1] + fold_rows(one_grad * normed)
        return carry

    lax.fori_loop(0, chunks, first_back, 0)

    def summed(index):
        return jnp.sum(sums[index], axis=0, keepdims=True)

    six = (
        summed(0),
        summed(1),
        sums_in[0:1, :],
        sums_in[1:2, :],
        sums_in[2:3, :],
        summed(2),
    )
    slabs[...] = jnp.zeros_like(slabs)
    slots = slot_mask[0:4, 0:1]
    for member in range(group_size):
        low, high = member * own_width, (member + 1) * own_width
        for index in range(6):
            to = slice(index * own_width, (index + 1) * own_width)
            slabs[member, 0:4, to] = slots * six[index][:, low:high]
        slabs[member, 4:5, 0:own_width] = sums_in[3:4, low:high]
        slabs[member, 5:6, 0:own_width] = sums_in[5:6, low:high]
    to_members(slab_slots, lambda member: slabs.at[member], slab_got)
    slab_got[pl.ds(links.member, 1)] = slabs[pl.ds(links.member, 1)]
    input_sum.fold(2)
    from_members(slab_slots, slab_got)
    row = slab_got[0]
    for member in range(1, group_size):
        row = row + slab_got[member]
    place_slab[...] = row
    place_slab[0:4, :] = row[0:4, :].astype(brain_type).astype(float_type)
    place_slab[6:7, 0:width] = sums_in[4:5, :]
    place_slab[7:8, 0:span] = summed(3)[:, 0:span]
    place_slab[7:8, span : 2 * span] = summed(4)[:, 0:span]
    to_places(place_slots, lambda place: place_slab, place_got)
    place_got[pl.ds(links.place, 1)] = place_slab[...][None]
    input_sum.fold(3)
    from_places(act_slots, act_all)
    from_places(place_slots, place_got)
    low_rows = place_got[...].reshape(fsdp_size * 8, 6 * own_width).astype(brain_type)
    act_part[...] = against(low_rows, cond_weight[...]).reshape(fsdp_size, 8, shard)
    to_places(part_slots, lambda place: act_part.at[place], act_got)
    act_got[pl.ds(links.place, 1)] = act_part[pl.ds(links.place, 1)]
    bias_sum = place_got[0]
    for place in range(1, fsdp_size):
        bias_sum = bias_sum + place_got[place]
    bias_row[...] = bias_sum
    bias_row[0:1, :] = jnp.sum(bias_sum[0:4, :], axis=0, keepdims=True)
    to_members(bias_slots, lambda member: bias_row, bias_out)
    bias_out[pl.ds(links.member, 1)] = bias_row[...][None]
    cond_out[...] = across_rows(
        act_all[...].reshape(fsdp_size * 8, shard).astype(brain_type), low_rows
    )
    from_places(part_slots, act_got)
    to_members(row_slots, lambda member: act_got, act_group)
    act_group[pl.ds(links.member, 1)] = act_got[...][None]
    input_sum.fold(0)
    from_members(row_slots, act_group)
    from_members(bias_slots, bias_out)
    act_sum = act_group[0]
    for member in range(1, group_size):
        act_sum = act_sum + act_group[member]
    act_out[...] = act_sum
    input_out[...] = input_sum.total()
    sends.finish()


def run_backward(sizes, *arrays):
    fsdp_size, group_size, quarter, width, own_width, shard = sizes
    row_length = quarter * group_size
    local_heads = own_width // HEAD_DIM
    span = local_heads * HEAD_PAD
    hidden = arrays[14].shape[1]
    depth = fsdp_size // 2
    six = 6 * own_width
    in_vmem = pl.BlockSpec(memory_space=pltpu.VMEM)
    anywhere = pl.BlockSpec(memory_space=pl.ANY)
    shape = jax.ShapeDtypeStruct
    vmem = pltpu.VMEM
    copies = 3 + 4 * depth + 1 + 3 * fsdp_size + 3 * group_size
    in_specs = [in_vmem] * len(arrays)
    in_specs[14] = anywhere
    in_specs[-1] = pl.BlockSpec(memory_space=pltpu.SMEM)
    return pl.pallas_call(
        functools.partial(backward_kernel, sizes),
        out_shape=(
            shape((quarter, width), brain_type),
            shape((quarter, width), float_type),
            shape((fsdp_size, 8, shard), float_type),
            shape((shard, six), float_type),
            shape((group_size, 8, six), float_type),
            shape((shard, hidden), float_type),
            shape((shard, 4 * own_width), float_type),
        ),
        in_specs=in_specs,
        out_specs=(in_vmem,) * 7,
        scratch_shapes=[
            vmem((quarter, width), brain_type),
            vmem((row_length, 3 * span), brain_type),
            vmem((row_length, HEAD_PAD), float_type),
            vmem((local_heads, 8, row_length), float_type),
            vmem((2, quarter, width), brain_type),
            vmem((2, quarter, width), brain_type),
            vmem((quarter, width), brain_type),
            vmem((quarter, width), brain_type),
            vmem((quarter, width), float_type),
            vmem((width, hidden), brain_type),
            vmem((width, 4 * own_width), brain_type),
            vmem((depth, shard, hidden), brain_type),
            vmem((depth, shard, hidden), brain_type),
            vmem((depth, shard, 4 * own_width), brain_type),
            vmem((depth, shard, 4 * own_width), brain_type),
            vmem((5, 8, width), float_type),
            vmem((group_size, 8, six), float_type),
            vmem((group_size, 8, six), float_type),
            vmem((8, six), float_type),
            vmem((fsdp_size, 8, six), float_type),
            vmem((fsdp_size, 8, shard), float_type),
            vmem((fsdp_size, 8, shard), float_type),
            vmem((group_size, fsdp_size, 8, shard), float_type),
            vmem((8, six), float_type),
            vmem((fsdp_size, 8, shard), float_type),
            pltpu.SemaphoreType.DMA((copies,)),
            pltpu.SemaphoreType.DMA((copies,)),
            pltpu.SemaphoreType.DMA((1,)),
        ],
        compiler_params=pltpu.CompilerParams(
            collective_id=2, has_side_effects=True, vmem_limit_bytes=TOP_VMEM
        ),
        name="backward_row",
    )(*arrays)


def fast_inputs(sizes, conditions, lengths, segments, condition_weight, biases):
    fsdp_size, group_size, quarter, width, own_width, shard = sizes
    place, member = lax.axis_index("fsdp"), lax.axis_index("rep")
    condition_bias, input_bias, attend_bias, expand_bias, reduce_bias = biases
    slot_count = conditions.shape[1]
    span = 6 * own_width
    column_start = member * own_width
    activated = jax.nn.silu(conditions[0].astype(float_type)).astype(brain_type).astype(float_type)
    act_send = jnp.pad(
        activated.reshape(slot_count, fsdp_size, shard).transpose(1, 0, 2),
        ((0, 0), (0, 8 - slot_count), (0, 0)),
    )

    def placed(own):
        empty = jnp.zeros((own.shape[0] * fsdp_size,), float_type)
        return lax.dynamic_update_slice_in_dim(
            empty, own.astype(float_type), place * own.shape[0], 0
        )

    def to_span(values):
        return jnp.pad(values, (0, span - values.shape[0]))

    condition_row = lax.dynamic_slice_in_dim(
        placed(condition_bias).reshape(6, width), column_start, own_width, 1
    ).reshape(-1)
    hidden = expand_bias.shape[0] * fsdp_size // group_size
    expand_row = lax.dynamic_slice_in_dim(placed(expand_bias), member * hidden, hidden, 0)
    pair = lax.dynamic_slice_in_dim(
        placed(input_bias).reshape(2, width), column_start, own_width, 1
    ).reshape(2, -1, HEAD_DIM)
    pair_row = jnp.pad(pair, ((0, 0), (0, 0), (0, HEAD_PAD - HEAD_DIM))).reshape(-1)
    bias_table = jnp.stack(
        [condition_row] * slot_count
        + [
            to_span(expand_row),
            to_span(placed(attend_bias)),
            to_span(placed(reduce_bias)),
            to_span(pair_row),
        ]
    )
    slot_mask = jnp.broadcast_to(
        (jnp.arange(8, dtype=jnp.int32) == segments[0, 0]).astype(float_type)[:, None], (8, 128)
    )
    row_ends = jnp.cumsum(lengths[0], dtype=jnp.int32)
    images = image_index(row_ends, jnp.arange(group_size, dtype=jnp.int32) * quarter)
    mask_bias = jnp.where(images[:, None] == images[None, :], 0.0, -1e30).astype(float_type)
    cond_flat = condition_weight.reshape(shard, span)
    return act_send, cond_flat, bias_table, slot_mask, mask_bias


def fast_local(
    tokens,
    conditions,
    lengths,
    segments,
    condition_weight,
    condition_bias,
    input_weight,
    input_bias,
    attend_weight,
    attend_bias,
    expand_weight,
    expand_bias,
    reduce_weight,
    reduce_bias,
    cotangent,
):
    _, quarter, width = tokens.shape
    slot_count = conditions.shape[1]
    group_size, member = lax.axis_size("rep"), lax.axis_index("rep")
    fsdp_size, place = lax.axis_size("fsdp"), lax.axis_index("fsdp")
    shard, _, own_width = condition_weight.shape
    span = own_width // HEAD_DIM * HEAD_PAD
    hidden = expand_weight.shape[1]
    sizes = (fsdp_size, group_size, quarter, width, own_width, shard)
    act_send, cond_flat, bias_table, slot_mask, mask_bias = fast_inputs(
        sizes,
        conditions,
        lengths,
        segments,
        condition_weight,
        (condition_bias, input_bias, attend_bias, expand_bias, reduce_bias),
    )
    weight_zero = jnp.concatenate([input_weight.reshape(shard, -1), attend_weight], axis=1)
    token_rows = tokens.reshape(quarter, width)
    upstream = cotangent.reshape(quarter, width)
    (
        mods,
        biases,
        one,
        heads,
        logs,
        mixed,
        branch,
        middle,
        two,
        upper,
        input_pad,
        attend_pad,
        expand_all,
        reduce_all,
    ) = run_forward(
        sizes,
        token_rows,
        upstream,
        act_send,
        cond_flat,
        bias_table,
        slot_mask,
        mask_bias,
        (weight_zero, expand_weight, reduce_weight),
    )
    (far_sum, near_sum, head_grads, attend_grad, expand_grad, reduce_final, slope, sums) = (
        run_middle(
            sizes,
            two,
            upper,
            expand_all,
            reduce_all,
            mods,
            biases,
            middle,
            branch,
            upstream,
            attend_pad,
            mixed,
        )
    )
    (output, token_grad, act_grad, cond_grad, bias_rows, expand_final, joint_final) = run_backward(
        sizes,
        heads,
        logs,
        head_grads,
        mixed,
        one,
        input_pad,
        token_rows,
        mods,
        biases,
        slope,
        upstream,
        middle,
        far_sum,
        near_sum,
        expand_grad,
        attend_grad,
        sums,
        cond_flat,
        act_send,
        slot_mask,
        mask_bias,
    )

    def owned(values):
        depth = values.shape[0] // fsdp_size
        return lax.dynamic_slice_in_dim(values, place * depth, depth, 0)

    condition_bias_final = owned(
        bias_rows[:, 0, :].reshape(group_size, 6, own_width).transpose(1, 0, 2).reshape(-1)
    )
    attend_bias_final = owned(bias_rows[:, 4, :own_width].reshape(-1))
    reduce_bias_final = owned(bias_rows[:, 5, :own_width].reshape(-1))
    expand_bias_final = owned(bias_rows[:, 6, :hidden].reshape(-1))
    input_bias_final = owned(
        bias_rows[:, 7, : 2 * span]
        .reshape(group_size, 2, span // HEAD_PAD, HEAD_PAD)[..., :HEAD_DIM]
        .transpose(1, 0, 2, 3)
        .reshape(-1)
    )
    condition_values = conditions.astype(float_type)
    _, silu_back = jax.vjp(jax.nn.silu, condition_values)
    act_rows = act_grad[:, :slot_count].transpose(1, 0, 2).reshape(1, slot_count, width)
    condition_grad = silu_back(act_rows)[0]
    return (
        output[None],
        token_grad[None],
        condition_grad,
        cond_grad.reshape(shard, 6, own_width),
        condition_bias_final,
        joint_final[:, : 3 * own_width].reshape(shard, 3, own_width),
        input_bias_final,
        joint_final[:, 3 * own_width :],
        attend_bias_final,
        expand_final,
        expand_bias_final,
        reduce_final,
        reduce_bias_final,
    )


def solution(mesh):
    in_specs = (
        P("fsdp", "rep", None),
        P("fsdp", None, None),
        P("fsdp", None),
        P("fsdp", "rep"),
        P("fsdp", None, "rep"),
        P("fsdp"),
        P("fsdp", None, "rep"),
        P("fsdp"),
        P("fsdp", "rep"),
        P("fsdp"),
        P("fsdp", "rep"),
        P("fsdp"),
        P("fsdp", "rep"),
        P("fsdp"),
        P("fsdp", "rep", None),
    )
    out_specs = (
        P("fsdp", "rep", None),
        P("fsdp", "rep", None),
        P("fsdp", None, None),
        P("fsdp", None, "rep"),
        P("fsdp"),
        P("fsdp", None, "rep"),
        P("fsdp"),
        P("fsdp", "rep"),
        P("fsdp"),
        P("fsdp", "rep"),
        P("fsdp"),
        P("fsdp", "rep"),
        P("fsdp"),
    )
    local = fast_local if mesh.shape["fsdp"] == 8 else plain_local
    return jax.shard_map(local, mesh=mesh, in_specs=in_specs, out_specs=out_specs, check_vma=False)
```

```python
import functools
import math

import jax
import jax.numpy as jnp
from jax import lax
from jax.experimental import pallas as pl
from jax.experimental.pallas import tpu as pltpu
from jax.sharding import PartitionSpec as P

HEAD_DIM = 72


epsilon = 1e-06
highest = lax.Precision.HIGHEST
float_type = jnp.float32
brain_type = jnp.bfloat16


def layer_normed(values):
    center = jnp.mean(values, axis=-1, keepdims=True)
    shifted = values - center
    spread = jnp.mean(shifted * shifted, axis=-1, keepdims=True)
    return shifted * lax.rsqrt(spread + epsilon)


def modulated(values, shift_term, scale_term):
    return layer_normed(values) * (1.0 + scale_term) + shift_term


def gelu_tanh(values):
    return jax.nn.gelu(values, approximate=True)


def image_index(row_ends, positions):
    return jnp.sum((positions[..., :, None] >= row_ends[..., None, :-1]).astype(jnp.int32), axis=-1)


def across(left, right):
    return lax.dot_general(left, right, (((0,), (0,)), ((), ())), preferred_element_type=float_type)


def against(left, right):
    return lax.dot_general(left, right, (((1,), (1,)), ((), ())), preferred_element_type=float_type)


def column_sums(values):
    return jnp.sum(values.astype(float_type), axis=0)


def spread_columns(own_part, total, start):
    empty = jnp.zeros(own_part.shape[:-1] + (total,), float_type)
    return lax.dynamic_update_slice_in_dim(empty, own_part, start, own_part.ndim - 1)


def gather_block(*weights):
    return tuple(lax.all_gather(item, "fsdp", axis=0, tiled=True) for item in weights)


def plain_local(
    tokens,
    conditions,
    lengths,
    segments,
    condition_weight,
    condition_bias,
    input_weight,
    input_bias,
    attend_weight,
    attend_bias,
    expand_weight,
    expand_bias,
    reduce_weight,
    reduce_bias,
    cotangent,
):
    row_count, quarter, model_width = tokens.shape
    slot_count = conditions.shape[1]
    group_size = lax.axis_size("rep")
    group_place = lax.axis_index("rep")
    row_length = quarter * group_size
    own_width = condition_weight.shape[2]
    column_start = group_place * own_width
    hidden_width = expand_weight.shape[1]
    hidden_start = group_place * hidden_width
    local_heads = own_width // HEAD_DIM
    score_scale = 1.0 / math.sqrt(HEAD_DIM)
    patch_count = row_count * quarter
    image_count = row_count * slot_count
    key_place = jnp.arange(row_length, dtype=jnp.int32)
    row_ends = jnp.cumsum(lengths, axis=1, dtype=jnp.int32)
    row_images = image_index(row_ends, key_place)
    allowed = row_images[:, :, None] == row_images[:, None, :]

    def whole_rows(values):
        joined_rows = lax.all_gather(
            values.reshape(row_count, quarter, -1), "rep", axis=1, tiled=True
        )
        return joined_rows.reshape(row_count * row_length, -1)

    def own_rows(values):
        summed = lax.psum_scatter(
            values.reshape(row_count, row_length, -1), "rep", scatter_dimension=1, tiled=True
        )
        return summed.reshape(patch_count, -1)

    fsdp_size = lax.axis_size("fsdp")
    fsdp_place = lax.axis_index("fsdp")
    own_depth = condition_weight.shape[0]
    condition_values = conditions.astype(float_type)
    activated_own = jax.nn.silu(condition_values).reshape(image_count, model_width).astype(brain_type)
    activated_all = lax.all_gather(activated_own, "fsdp", axis=0, tiled=True)
    activated = lax.dynamic_slice_in_dim(activated_all, fsdp_place * own_depth, own_depth, 1)
    local_biases = (condition_bias, input_bias, attend_bias, expand_bias, reduce_bias)
    share_sizes = [item.shape[0] for item in local_biases]
    bias_ends = [sum(share_sizes[:k]) for k in range(len(share_sizes) + 1)]
    bias_table = lax.all_gather(jnp.concatenate(local_biases), "fsdp", axis=0, tiled=False)
    condition_bias_all, input_bias_all, attend_bias_all, expand_bias_all, reduce_bias_all = [
        bias_table[:, low:high].reshape(-1) for low, high in zip(bias_ends[:-1], bias_ends[1:])
    ]
    condition_bias_own = lax.dynamic_slice_in_dim(
        condition_bias_all.reshape(6, model_width), column_start, own_width, 1
    )
    modulation_parts = jnp.einsum(
        "id,dkm->ikm", activated, condition_weight, preferred_element_type=float_type
    )
    modulation_own = (
        lax.psum_scatter(modulation_parts, "fsdp", scatter_dimension=0, tiled=True)
        + condition_bias_own[None]
    )
    modulation = lax.all_gather(modulation_own, "rep", axis=2, tiled=True).reshape(
        row_count, slot_count, -1
    )
    slot_table = (
        segments[:, :, None] == jnp.arange(slot_count, dtype=jnp.int32)[None, None, :]
    ).astype(float_type)
    per_token = jnp.einsum("rqs,rsm->rqm", slot_table, modulation, precision=highest).reshape(
        patch_count, -1
    )
    shift_one, scale_one, gate_one, shift_two, scale_two, gate_two = jnp.split(per_token, 6, axis=1)
    token_values = tokens.reshape(patch_count, model_width).astype(float_type)

    def split_heads(values):
        return values.reshape(row_count, row_length, local_heads, HEAD_DIM).transpose(2, 0, 1, 3)

    def merge_heads(values):
        return values.transpose(1, 2, 0, 3).reshape(row_count * row_length, own_width)

    def allowed_scores(query_head, key_head):
        scores = (
            jnp.einsum("rqd,rkd->rqk", query_head, key_head, preferred_element_type=float_type)
            * score_scale
        )
        return jnp.where(allowed, scores, -1e30)

    def head_forward(parts):
        query_head, key_head, value_head = parts
        scores = allowed_scores(query_head, key_head)
        row_max = jnp.max(scores, axis=-1, keepdims=True)
        powers = jnp.exp(scores - row_max)
        totals = jnp.sum(powers, axis=-1, keepdims=True)
        weights_low = (powers / totals).astype(brain_type)
        mixed = jnp.einsum(
            "rqk,rkd->rqd", weights_low, value_head, preferred_element_type=float_type
        )
        return (mixed, row_max + jnp.log(totals))

    def head_backward(parts):
        query_head, key_head, value_head, grad_head, log_head = parts
        scores = allowed_scores(query_head, key_head)
        probable = jnp.exp(scores - log_head)
        prob_grad = jnp.einsum(
            "rqd,rkd->rqk", grad_head, value_head, preferred_element_type=float_type
        )
        score_grad = (
            probable * (prob_grad - jnp.sum(probable * prob_grad, axis=-1, keepdims=True))
        ).astype(brain_type)
        query_part = (
            jnp.einsum("rqk,rkd->rqd", score_grad, key_head, preferred_element_type=float_type)
            * score_scale
        )
        key_part = (
            jnp.einsum("rqk,rqd->rkd", score_grad, query_head, preferred_element_type=float_type)
            * score_scale
        )
        value_part = jnp.einsum(
            "rqk,rqd->rkd",
            probable.astype(brain_type),
            grad_head,
            preferred_element_type=float_type,
        )
        return (query_part, key_part, value_part)

    def trunk(gathered):
        (
            input_all,
            input_bias_all,
            attend_all,
            attend_bias_all,
            expand_all,
            expand_bias_all,
            reduce_all,
            reduce_bias_all,
        ) = gathered
        bias_pair = lax.dynamic_slice_in_dim(
            input_bias_all.reshape(2, model_width), column_start, own_width, 1
        )
        expand_bias_own = lax.dynamic_slice_in_dim(expand_bias_all, hidden_start, hidden_width, 0)
        normed_one = modulated(token_values, shift_one, scale_one).astype(brain_type)
        whole_one = whole_rows(normed_one)
        joined = jnp.einsum("nd,dkm->nkm", whole_one, input_all, preferred_element_type=float_type)
        queries = (joined[:, 0] + bias_pair[0]).astype(brain_type)
        keys_row = joined[:, 1].astype(brain_type)
        values_row = (joined[:, 2] + bias_pair[1]).astype(brain_type)
        query_heads = split_heads(queries)
        key_heads = split_heads(keys_row)
        value_heads = split_heads(values_row)
        mixed, log_totals = lax.map(head_forward, (query_heads, key_heads, value_heads))
        attended = merge_heads(mixed).astype(brain_type)
        branch = own_rows(against(attended, attend_all)) + attend_bias_all
        middle = token_values + gate_one * branch
        normed_two = modulated(middle, shift_two, scale_two).astype(brain_type)
        whole_two = whole_rows(normed_two)
        inner = jnp.dot(whole_two, expand_all, preferred_element_type=float_type) + expand_bias_own
        active = gelu_tanh(inner).astype(brain_type)
        outer = own_rows(against(active, reduce_all)) + reduce_bias_all
        result = middle + gate_two * outer
        return (
            result,
            gathered,
            whole_one,
            query_heads,
            key_heads,
            value_heads,
            log_totals,
            attended,
            branch,
            middle,
            whole_two,
            inner,
            active,
            outer,
        )

    input_all, attend_all, expand_all, reduce_all = gather_block(
        input_weight, attend_weight, expand_weight, reduce_weight
    )
    state = trunk(
        (
            input_all,
            input_bias_all,
            attend_all,
            attend_bias_all,
            expand_all,
            expand_bias_all,
            reduce_all,
            reduce_bias_all,
        )
    )
    output = state[0].astype(brain_type).reshape(row_count, quarter, model_width)
    (
        _,
        gathered,
        whole_one,
        query_heads,
        key_heads,
        value_heads,
        log_totals,
        attended,
        branch,
        middle,
        whole_two,
        inner,
        active,
        outer,
    ) = state
    upstream = cotangent.reshape(patch_count, model_width).astype(float_type)
    outer_grad = (gate_two * upstream).astype(brain_type)
    gate_two_grad = upstream * outer
    outer_whole = whole_rows(outer_grad)
    reduce_grad = across(outer_whole, active)
    reduce_bias_grad = column_sums(outer_grad)
    active_grad = jnp.dot(outer_whole, reduce_all, preferred_element_type=float_type)
    _, gelu_back = jax.vjp(gelu_tanh, inner)
    inner_grad = gelu_back(active_grad)[0].astype(brain_type)
    expand_grad = across(whole_two, inner_grad)
    expand_bias_full = spread_columns(
        column_sums(inner_grad), hidden_width * group_size, hidden_start
    )
    two_grad = own_rows(against(inner_grad, expand_all))
    _, second_back = jax.vjp(modulated, middle, shift_two, scale_two)
    middle_norm_grad, shift_two_grad, scale_two_grad = second_back(two_grad)
    middle_grad = upstream + middle_norm_grad
    gate_one_grad = middle_grad * branch
    branch_grad = (gate_one * middle_grad).astype(brain_type)
    branch_whole = whole_rows(branch_grad)
    attend_grad = across(branch_whole, attended)
    attend_bias_grad = column_sums(branch_grad)
    attended_grad = jnp.dot(branch_whole, attend_all, preferred_element_type=float_type).astype(
        brain_type
    )
    grad_heads = split_heads(attended_grad)
    query_parts, key_parts, value_parts = lax.map(
        head_backward, (query_heads, key_heads, value_heads, grad_heads, log_totals)
    )
    query_low = merge_heads(query_parts).astype(brain_type)
    key_low = merge_heads(key_parts).astype(brain_type)
    value_low = merge_heads(value_parts).astype(brain_type)
    joined_grad = jnp.stack([query_low, key_low, value_low], axis=1)
    input_grad = jnp.einsum(
        "nd,nkm->dkm", whole_one, joined_grad, preferred_element_type=float_type
    )
    input_bias_pair = jnp.stack([column_sums(query_low), column_sums(value_low)])
    input_bias_full = spread_columns(input_bias_pair, model_width, column_start).reshape(-1)
    one_grad = own_rows(
        jnp.einsum("nkm,dkm->nd", joined_grad, input_all, preferred_element_type=float_type)
    )
    _, first_back = jax.vjp(modulated, token_values, shift_one, scale_one)
    token_norm_grad, shift_one_grad, scale_one_grad = first_back(one_grad)
    token_grad = (middle_grad + token_norm_grad).reshape(row_count, quarter, model_width)
    six_grads = jnp.stack(
        [
            shift_one_grad,
            scale_one_grad,
            gate_one_grad,
            shift_two_grad,
            scale_two_grad,
            gate_two_grad,
        ],
        axis=1,
    ).reshape(row_count, quarter, 6, model_width)
    modulation_part = jnp.einsum("rqs,rqkm->rskm", slot_table, six_grads, precision=highest)
    modulation_grad = lax.psum_scatter(modulation_part, "rep", scatter_dimension=3, tiled=True)
    modulation_low = lax.all_gather(
        modulation_grad.reshape(image_count, 6, own_width).astype(brain_type),
        "fsdp",
        axis=0,
        tiled=True,
    )
    condition_weight_final = jnp.einsum(
        "id,ikm->dkm", activated, modulation_low, preferred_element_type=float_type
    )
    condition_bias_full = lax.all_gather(
        column_sums(modulation_low), "rep", axis=1, tiled=True
    ).reshape(-1)
    bias_depth = condition_bias.shape[0]
    condition_bias_final = lax.dynamic_slice_in_dim(
        condition_bias_full, fsdp_place * bias_depth, bias_depth, 0
    )
    activated_part = jnp.einsum(
        "ikm,dkm->id", modulation_low, condition_weight, preferred_element_type=float_type
    )
    activated_wide = lax.all_to_all(
        activated_part.reshape(fsdp_size, image_count, own_depth), "fsdp", 0, 0
    )
    activated_row = jnp.transpose(activated_wide, (1, 0, 2)).reshape(image_count, model_width)
    bias_rows = jnp.concatenate(
        [
            item.reshape(fsdp_size, -1)
            for item in (input_bias_full, attend_bias_grad, expand_bias_full, reduce_bias_grad)
        ],
        axis=1,
    )
    bias_own = lax.psum_scatter(bias_rows, "fsdp", scatter_dimension=0, tiled=True).reshape(-1)
    activated_grad, bias_sum = lax.psum((activated_row, bias_own), "rep")
    input_bias_final, attend_bias_final, expand_bias_final, reduce_bias_final = jnp.split(
        bias_sum, [end - share_sizes[0] for end in bias_ends[2:-1]]
    )
    input_final, attend_final, expand_final, reduce_final = [
        lax.psum_scatter(item.astype(brain_type), "fsdp", scatter_dimension=0, tiled=True).astype(
            float_type
        )
        for item in (input_grad, attend_grad, expand_grad, reduce_grad)
    ]
    _, silu_back = jax.vjp(jax.nn.silu, condition_values)
    condition_grad = silu_back(activated_grad.reshape(row_count, slot_count, model_width))[0]
    return (
        output,
        token_grad,
        condition_grad,
        condition_weight_final,
        condition_bias_final,
        input_final,
        input_bias_final,
        attend_final,
        attend_bias_final,
        expand_final,
        expand_bias_final,
        reduce_final,
        reduce_bias_final,
    )


MESH = pl.DeviceIdType.MESH
HEAD_PAD = 128
TOP_VMEM = 60 * 1024 * 1024


def aligned(index, step):
    return pl.ds(pl.multiple_of(index * step, step), step)


class Links:
    def __init__(self, fsdp_size, group_size):
        self.fsdp_size = fsdp_size
        self.group_size = group_size
        self.depth = fsdp_size // 2
        self.place = lax.axis_index("fsdp")
        self.member = lax.axis_index("rep")
        self.level = self.place // 2
        self.side = self.place % 2
        self.core = self.member % 2
        self.half = self.member // 2

    def to_place(self, place):
        return (place, self.member)

    def to_member(self, member):
        return (self.place, member)

    @property
    def core_mate(self):
        return self.half * 2 + 1 - self.core

    @property
    def half_mate(self):
        return (1 - self.half) * 2 + self.core

    @property
    def far_mate(self):
        return (1 - self.half) * 2 + 1 - self.core

    @property
    def side_mate(self):
        return self.level * 2 + 1 - self.side

    def level_at(self, shift):
        return lax.rem(self.level + shift + self.depth, self.depth)

    def meet(self):
        self.await_all(self.greet())

    def await_all(self, count):
        pl.semaphore_wait(pltpu.get_barrier_semaphore(), count)

    def greet(self):
        barrier = pltpu.get_barrier_semaphore()
        count = 0
        for shift in range(1, self.fsdp_size):
            target = lax.rem(self.place + shift, self.fsdp_size)
            pl.semaphore_signal(barrier, inc=1, device_id=self.to_place(target), device_id_type=MESH)
            count += 1
        for shift in range(1, self.group_size):
            target = lax.rem(self.member + shift, self.group_size)
            pl.semaphore_signal(barrier, inc=1, device_id=self.to_member(target), device_id_type=MESH)
            count += 1
        return count


class Sends:
    def __init__(self, send_sems, recv_sems):
        self.send_sems = send_sems
        self.recv_sems = recv_sems
        self.used = 0
        self.open = []

    def slot(self):
        self.used += 1
        return self.used - 1

    def copy(self, slot, source, target, device):
        return pltpu.make_async_remote_copy(
            src_ref=source,
            dst_ref=target,
            send_sem=self.send_sems.at[slot],
            recv_sem=self.recv_sems.at[slot],
            device_id=device,
            device_id_type=MESH,
        )

    def start(self, slot, source, target, device):
        made = self.copy(slot, source, target, device)
        made.start()
        self.open.append(made)

    def arrived(self, slot, target, device):
        self.copy(slot, target, target, device).wait_recv()

    def finish(self):
        for made in self.open:
            made.wait_send()


class GroupGather:
    def __init__(self, links, sends, buffer, quarter):
        self.links, self.sends, self.buffer, self.quarter = links, sends, buffer, quarter
        self.slots = [sends.slot() for _ in range(3)]

    def rows(self, member):
        return self.buffer.at[aligned(member, self.quarter), :]

    def start_core(self):
        own = self.rows(self.links.member)
        mate = self.links.to_member(self.links.core_mate)
        self.sends.start(self.slots[0], own, own, mate)

    def start_half(self):
        own = self.rows(self.links.member)
        self.sends.start(self.slots[1], own, own, self.links.to_member(self.links.half_mate))

    def await_core(self):
        mate = self.links.core_mate
        self.sends.arrived(self.slots[0], self.rows(mate), self.links.to_member(mate))

    def pass_on(self):
        mate = self.links.half_mate
        self.sends.arrived(self.slots[1], self.rows(mate), self.links.to_member(mate))
        passed = self.rows(mate)
        self.sends.start(
            self.slots[2], passed, passed, self.links.to_member(self.links.core_mate)
        )

    def await_far(self):
        mate = self.links.core_mate
        self.sends.arrived(self.slots[2], self.rows(self.links.far_mate), self.links.to_member(mate))


class GroupSum:
    def __init__(self, links, sends, lent, got, crossing, crossed, total):
        self.links, self.sends = links, sends
        self.lent, self.got, self.crossing, self.crossed, self.total = (
            lent,
            got,
            crossing,
            crossed,
            total,
        )
        self.slots = [sends.slot() for _ in range(3)]

    def member_of(self, step):
        half = lax.rem(self.links.half + 1 - step // 2 + 2, 2)
        core = lax.rem(self.links.core + 1 - step % 2 + 2, 2)
        return half * 2 + core

    def lend(self, index):
        mate = self.links.to_member(self.links.core_mate)
        return self.sends.copy(
            self.slots[0] + index, self.lent.at[index], self.got.at[index], mate
        )

    def cross(self):
        mate = self.links.to_member(self.links.half_mate)
        return self.sends.copy(self.slots[2], self.crossing, self.crossed, mate)

    def step(self, step, value, crosses):
        index = step // 2
        self.total[...] = value

        @pl.when(step % 2 == 0)
        def _():
            self.lent[index] = self.total[...].astype(brain_type)
            self.lend(index).start()

        @pl.when(step % 2 == 1)
        def _():
            self.lend(index).wait_recv()

        @pl.when(step == 1)
        def _():
            self.crossing[...] = (self.total[...] + self.got[0].astype(float_type)).astype(
                brain_type
            )
            if crosses:
                self.cross().start()

    def note(self, crosses):
        self.sends.open += [self.lend(0), self.lend(1)]
        if crosses:
            self.sends.open.append(self.cross())

    def await_cross(self):
        self.sends.arrived(
            self.slots[2], self.crossed, self.links.to_member(self.links.half_mate)
        )

    def rows(self, rows):
        return (
            self.total[rows, :]
            + self.got[1, rows, :].astype(float_type)
            + self.crossed[rows, :].astype(float_type)
        )


def normed_rows(values):
    center = jnp.mean(values, axis=-1, keepdims=True)
    shifted = values - center
    spread = jnp.mean(shifted * shifted, axis=-1, keepdims=True)
    root = lax.rsqrt(spread + epsilon)
    return shifted * root, root


def spread_heads(source, target, rows, first, heads, target_first):
    for head in range(heads):
        low, to = HEAD_DIM * (first + head), HEAD_PAD * (target_first + head)
        target[rows, to : to + HEAD_DIM] = source[rows, low : low + HEAD_DIM]


def slot_column(segments):
    slots = lax.broadcasted_iota(jnp.int32, (8, HEAD_PAD), 0)
    return jnp.where(slots == segments[0:1, 0:HEAD_PAD], 1.0, 0.0)


def image_at(lengths, start):
    end, image = 0, 0
    for slot in range(lengths.shape[1] - 1):
        end = end + lengths[0, slot]
        image = image + jnp.where(start >= end, 1, 0)
    return image


def pair_mask(lengths, first, second):
    return jnp.where(image_at(lengths, first) == image_at(lengths, second), 0.0, -1e30)


def chosen(flag, values):
    return values * jnp.where(flag, 1.0, 0.0)


def bias_sizes(fsdp_size, width, hidden_total):
    return [size // fsdp_size for size in (6 * width, 2 * width, width, hidden_total, width)]


def own_biases(links, bias_vector, bias_table, own_width, sizes):
    place, member = links.place, links.member
    group_size = links.group_size
    starts = [sum(sizes[:index]) for index in range(6)]

    def piece(index, low, size):
        return bias_vector[0:1, starts[index] + low : starts[index] + low + size]

    bias_table[...] = jnp.zeros_like(bias_table)
    blocks = sizes[0] // own_width
    for kind in range(6):
        row = sum(
            chosen(
                place * blocks + index == kind * group_size + member,
                piece(0, index * own_width, own_width),
            )
            for index in range(blocks)
        )
        bias_table[0:4, kind * own_width : (kind + 1) * own_width] = jnp.broadcast_to(
            row, (4, own_width)
        )
    per_member = links.fsdp_size // group_size
    for part in range(per_member):
        bias_table[4:5, part * sizes[3] : (part + 1) * sizes[3]] = chosen(
            place == member * per_member + part, piece(3, 0, sizes[3])
        )
    for row, index in ((5, 2), (6, 4)):
        for other in range(links.fsdp_size):
            bias_table[row : row + 1, other * sizes[index] : (other + 1) * sizes[index]] = chosen(
                place == other, piece(index, 0, sizes[index])
            )
    local_heads = own_width // HEAD_DIM
    for pair in range(2):
        for head in range(local_heads):
            to = (pair * local_heads + head) * HEAD_PAD
            bias_table[7:8, to : to + HEAD_DIM] = chosen(
                place == pair * group_size + member, piece(1, head * HEAD_DIM, HEAD_DIM)
            )


def owned_biases(links, bias_rows, final, own_width, sizes, starts):
    place = links.place
    group_size, fsdp_size = links.group_size, links.fsdp_size
    blocks = sizes[0] // own_width
    final[...] = jnp.zeros_like(final)
    for index in range(blocks):
        total = 0.0
        for owner in range(fsdp_size):
            kind, member = divmod(owner * blocks + index, group_size)
            total = total + chosen(
                place == owner,
                bias_rows[member, 0:1, kind * own_width : (kind + 1) * own_width],
            )
        to = starts[0] + index * own_width
        final[:, to : to + own_width] = total
    local_heads = own_width // HEAD_DIM
    for head in range(local_heads):
        total = 0.0
        for owner in range(fsdp_size):
            pair, member = divmod(owner, group_size)
            low = (pair * local_heads + head) * HEAD_PAD
            total = total + chosen(place == owner, bias_rows[member, 7:8, low : low + HEAD_DIM])
        to = starts[1] + head * HEAD_DIM
        final[:, to : to + HEAD_DIM] = total
    per_member = fsdp_size // group_size
    for index, row in ((2, 4), (4, 5), (3, 6)):
        size = sizes[index]
        total = 0.0
        for owner in range(fsdp_size):
            member, part = divmod(owner, per_member)
            total = total + chosen(
                place == owner, bias_rows[member, row : row + 1, part * size : (part + 1) * size]
            )
        final[:, starts[index] : starts[index] + size] = total


def forward_kernel(
    sizes,
    tokens,
    upstream,
    conditions,
    segments,
    cond_weight,
    bias_vector,
    lengths,
    input_weight,
    attend_weight,
    weight_one,
    weight_two,
    mod_out,
    bias_out,
    one_out,
    heads_out,
    log_out,
    mixed_out,
    branch_out,
    middle_out,
    two_out,
    upper_out,
    input_out,
    attend_out,
    expand_out,
    reduce_out,
    act_out,
    act_send,
    bias_table,
    weight_zero,
    act_got,
    mod_parts,
    mod_got,
    mod_row,
    group_got,
    weights,
    normed,
    lent,
    got,
    crossing,
    crossed,
    total,
    one,
    two,
    upper,
    heads,
    mixed,
    input_pad,
    attend_pad,
    send_sems,
    recv_sems,
    local_sems,
):
    fsdp_size, group_size, quarter, width, own_width, shard = sizes
    links = Links(fsdp_size, group_size)
    sends = Sends(send_sems, recv_sems)
    blocks = (weight_zero, weight_one, weight_two)
    local_heads = own_width // HEAD_DIM
    head_span = local_heads * HEAD_PAD
    chunk = 32
    chunks = quarter // chunk

    act_slots = [sends.slot() for _ in range(fsdp_size)]
    mod_slots = [sends.slot() for _ in range(fsdp_size)]
    group_slots = [sends.slot() for _ in range(group_size)]
    level_slots = [[sends.slot() for _ in range(links.depth)] for _ in blocks]
    side_slots = [[sends.slot() for _ in range(links.depth)] for _ in blocks]
    onward_slots = [sends.slot() for _ in blocks]
    gather_one = GroupGather(links, sends, one, quarter)
    gather_two = GroupGather(links, sends, two, quarter)
    gather_upper = GroupGather(links, sends, upper, quarter)
    branch_sum = GroupSum(links, sends, lent, got, crossing, crossed, total)
    opened = []

    def shard_rows(block, place):
        return weights.at[block, aligned(place, shard), :]

    inner = links.level * (links.depth - 1 - links.level) > 0
    near = jnp.where(links.level < 2, 3, 1)
    order = (2, near, 4 - near)

    def level_copy(block, shift):
        own = shard_rows(block, links.place)
        target = links.level_at(shift) * 2 + links.side
        return sends.copy(
            level_slots[block][0] + shift, blocks[block], own, links.to_place(target)
        )

    def offer_levels(block):
        level_copy(block, 2).start()
        level_copy(block, 4 - near).start()

        @pl.when(inner)
        def _():
            level_copy(block, near).start()

    def offer_side(block):
        own = shard_rows(block, links.place)
        sends.start(side_slots[block][0], blocks[block], own, links.to_place(links.side_mate))

    def keep_own(block):
        kept = pltpu.make_async_copy(
            blocks[block], shard_rows(block, links.place), local_sems.at[block]
        )
        kept.start()
        return kept

    def forward_copy(block):
        rows = shard_rows(block, links.level_at(2) * 2 + links.side)
        return pltpu.make_async_remote_copy(
            src_ref=rows,
            dst_ref=rows,
            send_sem=send_sems.at[onward_slots[block]],
            recv_sem=recv_sems.at[level_slots[block][0] + 2 * links.level - 1],
            device_id=links.to_place((3 * links.level - 3) * 2 + links.side),
            device_id_type=MESH,
        )

    def side_copy(block, shift):
        rows = shard_rows(block, links.level_at(-shift) * 2 + links.side)
        return sends.copy(
            side_slots[block][0] + shift, rows, rows, links.to_place(links.side_mate)
        )

    def relay(block, index):
        shift = order[index]
        source = links.level_at(-shift) * 2 + links.side
        rows = shard_rows(block, source)
        sends.arrived(level_slots[block][0] + shift, rows, links.to_place(source))
        if index == 0:

            @pl.when(inner)
            def _():
                forward_copy(block).start()

        side_copy(block, shift).start()
        return source

    def side_arrived(block, index):
        shift = order[index - 1] if index else 0
        source = links.level_at(-shift) * 2 + 1 - links.side
        sends.arrived(
            side_slots[block][0] + shift, shard_rows(block, source), links.to_place(links.side_mate)
        )
        return source

    def finish_weights(block):
        level_copy(block, 2).wait_send()
        level_copy(block, 4 - near).wait_send()

        @pl.when(inner)
        def _():
            level_copy(block, near).wait_send()
            forward_copy(block).wait_send()

        for shift in order:
            side_copy(block, shift).wait_send()

    def keep(index, source, target):
        made = pltpu.make_async_copy(source, target, local_sems.at[index])
        made.start()
        opened.append(made)

    greeted = links.greet()
    raw = conditions[...].astype(float_type)
    activated = (raw / (1.0 + jnp.exp(-raw))).astype(brain_type).astype(float_type)
    act_send[...] = jnp.zeros_like(act_send)
    for place in range(fsdp_size):
        act_send[place, 0:4, :] = activated[:, place * shard : (place + 1) * shard]
    for index in range(3):
        weight_zero[:, index * own_width : (index + 1) * own_width] = input_weight[index]
    weight_zero[:, 3 * own_width : 4 * own_width] = attend_weight[...]
    links.await_all(greeted)
    for shift in range(1, fsdp_size):
        target = lax.rem(links.place + shift, fsdp_size)
        sends.start(
            act_slots[shift], act_send.at[target], act_got.at[links.place], links.to_place(target)
        )
    act_got[pl.ds(links.place, 1)] = act_send[pl.ds(links.place, 1)]
    kept_zero, kept_one, kept_two = [keep_own(block) for block in range(3)]
    hidden_total = weight_one.shape[1] * group_size
    own_biases(links, bias_vector, bias_table, own_width, bias_sizes(fsdp_size, width, hidden_total))

    def norm_tokens(index, carry):
        rows = aligned(index, chunk)
        normed[rows, :] = normed_rows(tokens[rows, :].astype(float_type))[0]
        return carry

    for shift in range(1, fsdp_size):
        source = lax.rem(links.place + fsdp_size - shift, fsdp_size)
        sends.arrived(act_slots[shift], act_got.at[source], links.to_place(source))
    activated = act_got[...].reshape(fsdp_size * 8, shard).astype(brain_type)
    for index in range(6):
        to = slice(index * own_width, (index + 1) * own_width)
        mod_parts[:, :, to] = (
            jnp.dot(activated, cond_weight[index], preferred_element_type=float_type).reshape(
                fsdp_size, 8, own_width
            )
            + bias_table[:, to][None]
        )
    act_out[...] = act_got[...]
    for shift in range(1, fsdp_size):
        target = lax.rem(links.place + shift, fsdp_size)
        sends.start(
            mod_slots[shift], mod_parts.at[target], mod_got.at[links.place], links.to_place(target)
        )
    for block in range(3):
        offer_levels(block)
    offer_side(0)
    offer_side(1)
    mod_got[pl.ds(links.place, 1)] = mod_parts[pl.ds(links.place, 1)]
    lax.fori_loop(0, chunks, norm_tokens, 0)
    input_pad[...] = jnp.zeros_like(input_pad)
    attend_pad[...] = jnp.zeros_like(attend_pad)
    kept_zero.wait()

    def spread_shard(place):
        rows = aligned(place, shard)
        spread_heads(weights.at[0], input_pad, rows, 0, 3 * local_heads, 0)
        spread_heads(weights.at[0], attend_pad, rows, 3 * local_heads, local_heads, 0)

    spread_shard(links.place)
    for shift in range(1, fsdp_size):
        source = lax.rem(links.place + fsdp_size - shift, fsdp_size)
        sends.arrived(mod_slots[shift], mod_got.at[source], links.to_place(source))
    summed = mod_got[0]
    for index in range(1, fsdp_size):
        summed = summed + mod_got[index]
    mod_row[...] = summed
    for shift in range(1, group_size):
        target = lax.rem(links.member + shift, group_size)
        sends.start(group_slots[shift], mod_row, group_got.at[links.member], links.to_member(target))
    group_got[pl.ds(links.member, 1)] = mod_row[...][None]
    bias_out[...] = mod_row[...]
    for shift in range(1, group_size):
        source = lax.rem(links.member + group_size - shift, group_size)
        sends.arrived(group_slots[shift], group_got.at[source], links.to_member(source))
    slot = slot_column(segments)[:, 0:1]
    for index in range(6):
        full = jnp.concatenate(
            [
                group_got[member, :, index * own_width : (index + 1) * own_width]
                for member in range(group_size)
            ],
            axis=1,
        )
        mod_out[index : index + 1, :] = jnp.sum(full * slot, axis=0, keepdims=True)
    mod_out[6:8, :] = jnp.zeros((2, width), float_type)

    own_rows = links.member * quarter

    def first_norm(index, carry):
        rows = aligned(index, chunk)
        to = pl.ds(pl.multiple_of(own_rows + index * chunk, chunk), chunk)
        one[to, :] = (normed[rows, :] * (1.0 + mod_out[1:2, :]) + mod_out[0:1, :]).astype(brain_type)
        return carry

    lax.fori_loop(0, chunks, first_norm, 0)
    gather_one.start_half()
    gather_one.start_core()
    first_sources = [relay(0, index) for index in range(links.depth - 1)]
    offer_side(2)

    def upper_rows(index, carry):
        rows = aligned(index, chunk)
        to = pl.ds(pl.multiple_of(own_rows + index * chunk, chunk), chunk)
        upper[to, :] = (mod_out[5:6, :] * upstream[rows, :].astype(float_type)).astype(brain_type)
        return carry

    lax.fori_loop(0, chunks, upper_rows, 0)

    for source in first_sources:
        spread_shard(source)
    gather_one.pass_on()
    gather_upper.start_half()
    gather_upper.start_core()
    gather_one.await_core()
    for shift in range(links.depth):
        spread_shard(side_arrived(0, shift))
    gather_one.await_far()
    keep(3, one, one_out)
    keep(4, input_pad, input_out)
    keep(5, attend_pad, attend_out)

    bias_pad = mod_row[7:8, 0 : 2 * head_span]

    def project(index, carry):
        rows = aligned(index, quarter)
        values = jnp.dot(one[rows, :], input_pad[...], preferred_element_type=float_type)
        heads[rows, 0:head_span] = (values[:, 0:head_span] + bias_pad[:, 0:head_span]).astype(
            brain_type
        )
        heads[rows, head_span : 2 * head_span] = values[:, head_span : 2 * head_span].astype(
            brain_type
        )
        heads[rows, 2 * head_span :] = (
            values[:, 2 * head_span :] + bias_pad[:, head_span:]
        ).astype(brain_type)
        return carry

    lax.fori_loop(0, group_size, project, 0)
    keep(6, heads, heads_out)

    power_scale = math.log2(math.e) / math.sqrt(HEAD_DIM)

    def attend(head, turn):
        part = branch_sum.member_of(turn)
        step = turn * local_heads + head
        rows = aligned(part, quarter)

        def columns(base):
            return aligned(base * local_heads + head, HEAD_PAD)

        raw = lax.dot_general(
            heads[rows, columns(0)],
            heads[:, columns(1)],
            (((1,), (1,)), ((), ())),
            preferred_element_type=float_type,
        )
        scores = jnp.concatenate(
            [
                raw[:, other * quarter : (other + 1) * quarter]
                + pair_mask(lengths, part * quarter, other * quarter)
                for other in range(group_size)
            ],
            axis=1,
        )
        top = jnp.max(scores, axis=1, keepdims=True)
        powers = jnp.exp2(scores * power_scale - top * power_scale)
        totals = jnp.sum(powers, axis=1, keepdims=True)
        value = jnp.dot(
            powers.astype(brain_type), heads[:, columns(2)], preferred_element_type=float_type
        )
        mixed[rows, aligned(head, HEAD_PAD)] = (value / totals).astype(brain_type)
        turned = jnp.transpose(
            jnp.broadcast_to(top * power_scale + jnp.log2(totals), (quarter, HEAD_PAD))
        )
        log_out[head, :, rows] = turned[0:8, :]
        for index, late in enumerate((1, 3, 5)):

            @pl.when(step == late)
            def _():
                relay(1, index)

        @pl.when(step == 4)
        def _():
            gather_upper_in_loop()

        return turn

    def gather_upper_in_loop():
        mate = links.half_mate
        passed = gather_upper.rows(mate)
        sends.arrived(gather_upper.slots[1], passed, links.to_member(mate))
        sends.copy(
            gather_upper.slots[2], passed, passed, links.to_member(links.core_mate)
        ).start()

    def branch_part(member):
        return lax.dot_general(
            mixed[aligned(member, quarter), :],
            attend_pad[...],
            (((1,), (1,)), ((), ())),
            preferred_element_type=float_type,
        )

    def attend_turn(turn, carry):
        lax.fori_loop(0, local_heads, attend, turn)
        branch_sum.step(turn, branch_part(branch_sum.member_of(turn)), True)
        return carry

    lax.fori_loop(0, group_size, attend_turn, 0)
    passed = gather_upper.rows(links.half_mate)
    sends.open.append(
        sends.copy(gather_upper.slots[2], passed, passed, links.to_member(links.core_mate))
    )
    keep(7, mixed, mixed_out)
    branch_sum.note(True)
    gather_upper.await_core()
    gather_upper.await_far()
    keep(8, upper, upper_out)
    for index in range(links.depth - 1):
        relay(2, index)
    branch_sum.await_cross()

    def second_norm(index, carry):
        rows = aligned(index, chunk)
        to = pl.ds(pl.multiple_of(own_rows + index * chunk, chunk), chunk)
        branch = branch_sum.rows(rows) + mod_row[5:6, 0:width]
        branch_out[rows, :] = branch
        middle = tokens[rows, :].astype(float_type) + mod_out[2:3, :] * branch
        middle_out[rows, :] = middle
        two[to, :] = (normed_rows(middle)[0] * (1.0 + mod_out[4:5, :]) + mod_out[3:4, :]).astype(
            brain_type
        )
        return carry

    lax.fori_loop(0, chunks, second_norm, 0)
    gather_two.start_half()
    gather_two.start_core()
    gather_two.pass_on()
    kept_one.wait()
    for shift in range(links.depth):
        side_arrived(1, shift)
    keep(9, weights.at[1], expand_out)
    gather_two.await_core()
    gather_two.await_far()
    keep(10, two, two_out)
    kept_two.wait()
    for shift in range(links.depth):
        side_arrived(2, shift)
    keep(11, weights.at[2], reduce_out)
    for made in opened:
        made.wait()
    for block in range(3):
        finish_weights(block)
    sends.finish()


def run_forward(
    sizes, tokens, upstream, conditions, segments, cond_weight, bias_vector, lengths, weights
):
    fsdp_size, group_size, quarter, width, own_width, shard = sizes
    row_length = quarter * group_size
    local_heads = own_width // HEAD_DIM
    span = local_heads * HEAD_PAD
    hidden = weights[2].shape[1]
    in_vmem = pl.BlockSpec(memory_space=pltpu.VMEM)
    anywhere = pl.BlockSpec(memory_space=pl.ANY)
    shape = jax.ShapeDtypeStruct
    out_shape = (
        shape((8, width), float_type),
        shape((8, 6 * own_width), float_type),
        shape((row_length, width), brain_type),
        shape((row_length, 3 * span), brain_type),
        shape((local_heads, 8, row_length), float_type),
        shape((row_length, span), brain_type),
        shape((quarter, width), float_type),
        shape((quarter, width), float_type),
        shape((row_length, width), brain_type),
        shape((row_length, width), brain_type),
        shape((width, 3 * span), brain_type),
        shape((width, span), brain_type),
        shape((width, hidden), brain_type),
        shape((width, hidden), brain_type),
        shape((fsdp_size, 8, shard), float_type),
    )
    out_specs = (
        in_vmem,
        in_vmem,
        anywhere,
        anywhere,
        in_vmem,
        anywhere,
        in_vmem,
        in_vmem,
        anywhere,
        anywhere,
        anywhere,
        anywhere,
        anywhere,
        anywhere,
        in_vmem,
    )
    copies = 2 * fsdp_size + group_size + 6 * (fsdp_size // 2) + 3 * 3 + 6
    vmem = pltpu.VMEM
    scratch = [
        vmem((fsdp_size, 8, shard), float_type),
        vmem((8, 6 * own_width), float_type),
        vmem((shard, 4 * own_width), brain_type),
        vmem((fsdp_size, 8, shard), float_type),
        vmem((fsdp_size, 8, 6 * own_width), float_type),
        vmem((fsdp_size, 8, 6 * own_width), float_type),
        vmem((8, 6 * own_width), float_type),
        vmem((group_size, 8, 6 * own_width), float_type),
        vmem((3, width, hidden), brain_type),
        vmem((quarter, width), float_type),
        vmem((2, quarter, width), brain_type),
        vmem((2, quarter, width), brain_type),
        vmem((quarter, width), brain_type),
        vmem((quarter, width), brain_type),
        vmem((quarter, width), float_type),
        vmem((row_length, width), brain_type),
        vmem((row_length, width), brain_type),
        vmem((row_length, width), brain_type),
        vmem((row_length, 3 * span), brain_type),
        vmem((row_length, span), brain_type),
        vmem((width, 3 * span), brain_type),
        vmem((width, span), brain_type),
        pltpu.SemaphoreType.DMA((copies,)),
        pltpu.SemaphoreType.DMA((copies,)),
        pltpu.SemaphoreType.DMA((12,)),
    ]
    return pl.pallas_call(
        functools.partial(forward_kernel, sizes),
        out_shape=out_shape,
        in_specs=[in_vmem] * 6 + [pl.BlockSpec(memory_space=pltpu.SMEM)] + [in_vmem] * 4,
        out_specs=out_specs,
        scratch_shapes=scratch,
        compiler_params=pltpu.CompilerParams(
            collective_id=0, has_side_effects=True, vmem_limit_bytes=TOP_VMEM
        ),
        name="forward_row",
    )(tokens, upstream, conditions, segments, cond_weight, bias_vector, lengths, *weights)


class ShardSum:
    def __init__(self, links, sends, block, side_got, level_got, shard):
        self.links, self.sends, self.block = links, sends, block
        self.side_got, self.level_got, self.shard = side_got, level_got, shard
        self.side_slots = [sends.slot() for _ in range(links.depth)]
        self.level_slots = [sends.slot() for _ in range(links.depth)]

    def order(self):
        return list(range(1, self.links.depth)) + [0]

    def rows(self, place):
        return aligned(place, self.shard)

    def start(self):
        links = self.links
        for shift in self.order():
            level = links.level_at(shift)
            self.sends.start(
                self.side_slots[shift],
                self.block.at[self.rows(level * 2 + 1 - links.side), :],
                self.side_got.at[shift],
                links.to_place(links.side_mate),
            )

    def fold(self, shift, note=True):
        links = self.links
        self.sends.arrived(
            self.side_slots[shift], self.side_got.at[shift], links.to_place(links.side_mate)
        )
        if shift:
            target = links.level_at(shift) * 2 + links.side
            rows = self.rows(target)
            self.block[rows, :] = (
                self.block[rows, :].astype(float_type) + self.side_got[shift].astype(float_type)
            ).astype(brain_type)
            self.push(shift).start()
            if note:
                self.sends.open.append(self.push(shift))

    def push(self, shift):
        links = self.links
        target = links.level_at(shift) * 2 + links.side
        return self.sends.copy(
            self.level_slots[shift],
            self.block.at[self.rows(target), :],
            self.level_got.at[shift],
            links.to_place(target),
        )

    def total(self):
        links = self.links
        summed = self.block[self.rows(links.place), :].astype(float_type) + self.side_got[0].astype(
            float_type
        )
        for shift in range(1, links.depth):
            source = links.level_at(-shift) * 2 + links.side
            self.sends.arrived(
                self.level_slots[shift], self.level_got.at[shift], links.to_place(source)
            )
            summed = summed + self.level_got[shift].astype(float_type)
        return summed


def fold_rows(values):
    count, width = values.shape
    return jnp.sum(values.reshape(count // 8, 8, width), axis=0)


def gelu_pair(values):
    root = math.sqrt(2.0 / math.pi)
    square = values * values
    bend = jnp.tanh(values * (root + root * 0.044715 * square))
    half = 0.5 * (1.0 + bend)
    slope = half + (0.5 * values) * (1.0 - bend * bend) * (root + root * 3 * 0.044715 * square)
    return values * half, slope


def across_rows(left, right):
    return lax.dot_general(left, right, (((0,), (0,)), ((), ())), preferred_element_type=float_type)


def middle_kernel(
    sizes,
    two,
    upper,
    expand,
    reduce,
    mods,
    biases,
    middle,
    branch,
    upstream,
    attend_pad,
    mixed,
    far_out,
    near_out,
    grads_out,
    attend_out,
    expand_out,
    reduce_out,
    slope_out,
    sums_out,
    active,
    inner_grad,
    lent_t,
    got_t,
    crossing_t,
    crossed_t,
    total_t,
    lent_o,
    got_o,
    branch_whole,
    reduce_grad,
    side_got,
    level_got,
    expand_grad,
    sums,
    send_sems,
    recv_sems,
    local_sems,
):
    fsdp_size, group_size, quarter, width, own_width, shard = sizes
    links = Links(fsdp_size, group_size)
    sends = Sends(send_sems, recv_sems)
    local_heads = own_width // HEAD_DIM
    chunk = 32
    chunks = quarter // chunk
    two_sum = GroupSum(links, sends, lent_t, got_t, crossing_t, crossed_t, total_t)
    outer_sum = GroupSum(links, sends, lent_o, got_o, far_out, None, near_out)
    gather = GroupGather(links, sends, branch_whole, quarter)
    reduce_sum = ShardSum(links, sends, reduce_grad, side_got, level_got, shard)
    links.meet()
    sums[...] = jnp.zeros_like(sums)
    hidden = expand.shape[1]

    def feed(step, carry):
        rows = aligned(two_sum.member_of(step), quarter)
        inner = (
            jnp.dot(two[rows, :], expand[...], preferred_element_type=float_type)
            + biases[4:5, 0:hidden]
        )
        active_grad = jnp.dot(upper[rows, :], reduce[...], preferred_element_type=float_type)
        value, slope = gelu_pair(inner)
        active[rows, :] = value.astype(brain_type)
        low = (active_grad * slope).astype(brain_type)
        inner_grad[rows, :] = low
        sums[4] = sums[4] + fold_rows(low.astype(float_type))
        two_sum.step(step, against(inner_grad[rows, :], expand[...]), True)
        outer_sum.step(step, against(active[rows, :], reduce[...]), False)
        return carry

    lax.fori_loop(0, group_size, feed, 0)
    two_sum.note(True)
    outer_sum.note(False)

    def near_rows(index, carry):
        rows = aligned(index, chunk)
        near_out[rows, :] = near_out[rows, :] + got_o[1, rows, :].astype(float_type)
        return carry

    lax.fori_loop(0, chunks, near_rows, 0)

    part = 384

    def reduce_part(index, carry):
        columns = aligned(index, part)
        reduce_grad[columns, :] = across_rows(upper[:, columns], active[...]).astype(brain_type)
        return carry

    lax.fori_loop(0, width // part, reduce_part, 0)
    reduce_sum.start()
    two_sum.await_cross()
    own_rows = links.member * quarter

    def second_back(index, carry):
        rows = aligned(index, chunk)
        to = pl.ds(pl.multiple_of(own_rows + index * chunk, chunk), chunk)
        two_grad = two_sum.rows(rows)
        normed, root = normed_rows(middle[rows, :])
        scaled = two_grad * (1.0 + mods[4:5, :])
        centered = (
            scaled
            - jnp.mean(scaled, axis=-1, keepdims=True)
            - normed * jnp.mean(scaled * normed, axis=-1, keepdims=True)
        )
        slope = upstream[rows, :].astype(float_type) + root * centered
        slope_out[rows, :] = slope
        low = (mods[2:3, :] * slope).astype(brain_type)
        branch_whole[to, :] = low
        sums[0] = sums[0] + fold_rows(slope * branch[rows, :])
        sums[1] = sums[1] + fold_rows(two_grad)
        sums[2] = sums[2] + fold_rows(two_grad * normed)
        sums[3] = sums[3] + fold_rows(low.astype(float_type))
        sums[5] = sums[5] + fold_rows(upper[to, :].astype(float_type))
        return carry

    lax.fori_loop(0, chunks, second_back, 0)
    gather.start_half()
    gather.start_core()

    def expand_part(index, carry):
        columns = aligned(index, part)
        expand_grad[columns, :] = across_rows(two[:, columns], inner_grad[...]).astype(brain_type)
        return carry

    lax.fori_loop(0, width // part, expand_part, 0)
    kept_expand = pltpu.make_async_copy(expand_grad, expand_out, local_sems.at[0])
    kept_expand.start()
    reduce_sum.fold(1)
    for index in range(6):
        sums_out[index : index + 1, :] = jnp.sum(sums[index], axis=0, keepdims=True)
    sums_out[6:8, :] = jnp.zeros((2, width), float_type)
    gather.pass_on()
    reduce_sum.fold(2)
    gather.await_core()
    gather.await_far()

    def head_grads(index, carry):
        rows = aligned(index, quarter)
        grads_out[rows, :] = jnp.dot(
            branch_whole[rows, :], attend_pad[...], preferred_element_type=float_type
        ).astype(brain_type)
        return carry

    lax.fori_loop(0, group_size, head_grads, 0)

    def attend_part(index, carry):
        columns = aligned(index, part)
        value = across_rows(branch_whole[:, columns], mixed[...])
        for head in range(local_heads):
            attend_out[columns, head * HEAD_DIM : (head + 1) * HEAD_DIM] = value[
                :, head * HEAD_PAD : head * HEAD_PAD + HEAD_DIM
            ].astype(brain_type)
        return carry

    lax.fori_loop(0, width // part, attend_part, 0)
    reduce_sum.fold(3)
    reduce_sum.fold(0)
    reduce_out[...] = reduce_sum.total()
    kept_expand.wait()
    sends.finish()


def run_middle(sizes, *arrays):
    fsdp_size, group_size, quarter, width, own_width, shard = sizes
    row_length = quarter * group_size
    span = own_width // HEAD_DIM * HEAD_PAD
    hidden = arrays[2].shape[1]
    depth = fsdp_size // 2
    in_vmem = pl.BlockSpec(memory_space=pltpu.VMEM)
    anywhere = pl.BlockSpec(memory_space=pl.ANY)
    shape = jax.ShapeDtypeStruct
    vmem = pltpu.VMEM
    copies = 3 + 3 + 3 + 2 * depth
    return pl.pallas_call(
        functools.partial(middle_kernel, sizes),
        out_shape=(
            shape((quarter, width), brain_type),
            shape((quarter, width), float_type),
            shape((row_length, span), brain_type),
            shape((width, own_width), brain_type),
            shape((width, hidden), brain_type),
            shape((shard, hidden), float_type),
            shape((quarter, width), float_type),
            shape((8, width), float_type),
        ),
        in_specs=[in_vmem] * len(arrays),
        out_specs=(in_vmem, in_vmem, in_vmem, in_vmem, anywhere, in_vmem, in_vmem, in_vmem),
        scratch_shapes=[
            vmem((row_length, hidden), brain_type),
            vmem((row_length, hidden), brain_type),
            vmem((2, quarter, width), brain_type),
            vmem((2, quarter, width), brain_type),
            vmem((quarter, width), brain_type),
            vmem((quarter, width), brain_type),
            vmem((quarter, width), float_type),
            vmem((2, quarter, width), brain_type),
            vmem((2, quarter, width), brain_type),
            vmem((row_length, width), brain_type),
            vmem((width, hidden), brain_type),
            vmem((depth, shard, hidden), brain_type),
            vmem((depth, shard, hidden), brain_type),
            vmem((width, hidden), brain_type),
            vmem((6, 8, width), float_type),
            pltpu.SemaphoreType.DMA((copies,)),
            pltpu.SemaphoreType.DMA((copies,)),
            pltpu.SemaphoreType.DMA((1,)),
        ],
        compiler_params=pltpu.CompilerParams(
            collective_id=1, has_side_effects=True, vmem_limit_bytes=TOP_VMEM
        ),
        name="middle_row",
    )(*arrays)


def backward_kernel(
    sizes,
    heads,
    logs,
    head_grads,
    mixed,
    one,
    input_pad,
    tokens,
    mods,
    biases,
    slope,
    upstream,
    middle,
    far_sum,
    near_sum,
    expand_grad,
    attend_grad,
    sums_in,
    cond_weight,
    act_all,
    conditions,
    segments,
    lengths,
    output_out,
    token_out,
    act_out,
    cond_out,
    bias_final,
    expand_out,
    input_out,
    attend_out,
    crossed_o,
    joined,
    query_sum,
    delta_rows,
    lent,
    got,
    crossing,
    crossed,
    total,
    expand_block,
    input_block,
    side_one,
    level_one,
    side_zero,
    level_zero,
    sums,
    slabs,
    slab_got,
    place_slab,
    place_got,
    act_part,
    act_got,
    act_group,
    bias_row,
    bias_out,
    send_sems,
    recv_sems,
    local_sems,
):
    fsdp_size, group_size, quarter, width, own_width, shard = sizes
    links = Links(fsdp_size, group_size)
    sends = Sends(send_sems, recv_sems)
    local_heads = own_width // HEAD_DIM
    span = local_heads * HEAD_PAD
    row_length = quarter * group_size
    chunk = 32
    chunks = quarter // chunk
    one_sum = GroupSum(links, sends, lent, got, crossing, crossed, total)
    expand_sum = ShardSum(links, sends, expand_block, side_one, level_one, shard)
    input_sum = ShardSum(links, sends, input_block, side_zero, level_zero, shard)
    outer_slot = sends.slot()
    slab_slots = [sends.slot() for _ in range(group_size)]
    place_slots = [sends.slot() for _ in range(fsdp_size)]
    part_slots = [sends.slot() for _ in range(fsdp_size)]
    row_slots = [sends.slot() for _ in range(group_size)]
    bias_slots = [sends.slot() for _ in range(group_size)]

    def to_places(slots, source_of, target):
        for shift in range(1, fsdp_size):
            place = lax.rem(links.place + shift, fsdp_size)
            sends.start(
                slots[shift], source_of(place), target.at[links.place], links.to_place(place)
            )

    def from_places(slots, target):
        for shift in range(1, fsdp_size):
            place = lax.rem(links.place + fsdp_size - shift, fsdp_size)
            sends.arrived(slots[shift], target.at[place], links.to_place(place))

    def to_members(slots, source_of, target):
        for shift in range(1, group_size):
            member = lax.rem(links.member + shift, group_size)
            sends.start(
                slots[shift], source_of(member), target.at[links.member], links.to_member(member)
            )

    def from_members(slots, target):
        for shift in range(1, group_size):
            member = lax.rem(links.member + group_size - shift, group_size)
            sends.arrived(slots[shift], target.at[member], links.to_member(member))

    links.meet()
    sends.start(outer_slot, far_sum, crossed_o, links.to_member(links.half_mate))
    kept = pltpu.make_async_copy(expand_grad, expand_block, local_sems.at[0])
    kept.start()
    sums[...] = jnp.zeros_like(sums)
    kept.wait()
    expand_sum.start()
    attend_first = 3 * own_width
    input_block[:, attend_first : attend_first + own_width] = attend_grad[...]

    power_scale = math.log2(math.e) / math.sqrt(HEAD_DIM)
    score_scale = 1.0 / math.sqrt(HEAD_DIM)

    def columns(base, head):
        return aligned(base * local_heads + head, HEAD_PAD)

    def head_deltas(head, carry):
        product = head_grads[:, columns(0, head)].astype(float_type) * mixed[
            :, columns(0, head)
        ].astype(float_type)
        delta = jnp.sum(product, axis=1, keepdims=True)
        turned = jnp.transpose(jnp.broadcast_to(delta, (row_length, HEAD_PAD)))
        delta_rows[head] = turned[0:8, :]
        return carry

    lax.fori_loop(0, local_heads, head_deltas, 0)

    def attend_back(step, carry):
        head, part = step // group_size, step % group_size
        rows = aligned(part, quarter)
        query = heads[:, columns(0, head)]
        key = heads[rows, columns(1, head)]
        value = heads[rows, columns(2, head)]
        grad = head_grads[:, columns(0, head)]
        shift = jnp.concatenate(
            [
                pair_mask(lengths, part * quarter, other * quarter)
                - logs[head, 0:1, other * quarter : (other + 1) * quarter]
                for other in range(group_size)
            ],
            axis=1,
        )
        probable = jnp.exp2(against(key, query) * power_scale + shift)
        value_grad = jnp.dot(probable.astype(brain_type), grad, preferred_element_type=float_type)
        score_grad = (probable * (against(value, grad) - delta_rows[head, 0:1, :])).astype(
            brain_type
        )
        key_grad = jnp.dot(score_grad, query, preferred_element_type=float_type)
        joined[rows, columns(1, head)] = (key_grad * score_scale).astype(brain_type)
        joined[rows, columns(2, head)] = value_grad.astype(brain_type)
        query_grad = across_rows(score_grad, key)

        @pl.when(part == 0)
        def _():
            query_sum[...] = query_grad

        @pl.when(part > 0)
        def _():
            query_sum[...] = query_sum[...] + query_grad

        @pl.when(part == group_size - 1)
        def _():
            joined[:, columns(0, head)] = (query_sum[...] * score_scale).astype(brain_type)

        for index, late in ((1, 5), (2, 9), (3, 13)):

            @pl.when(step == late)
            def _():
                expand_sum.fold(index, False)

        return carry

    lax.fori_loop(0, group_size * local_heads, attend_back, 0)
    for index in range(1, links.depth):
        sends.open.append(expand_sum.push(index))

    part = 384

    def input_part(index, carry):
        picked = aligned(index, part)
        value = across_rows(one[:, picked], joined[...])
        for head in range(3 * local_heads):
            input_block[picked, head * HEAD_DIM : (head + 1) * HEAD_DIM] = value[
                :, head * HEAD_PAD : head * HEAD_PAD + HEAD_DIM
            ].astype(brain_type)
        return carry

    lax.fori_loop(0, width // part, input_part, 0)
    input_sum.start()

    def one_step(step, carry):
        rows = aligned(one_sum.member_of(step), quarter)
        one_sum.step(step, against(joined[rows, :], input_pad[...]), True)
        return carry

    lax.fori_loop(0, group_size, one_step, 0)
    one_sum.note(True)
    expand_sum.fold(0)

    sends.arrived(outer_slot, crossed_o, links.to_member(links.half_mate))

    def finish_rows(index, carry):
        rows = aligned(index, chunk)
        outer = (
            near_sum[rows, :] + crossed_o[rows, :].astype(float_type) + biases[6:7, 0:width]
        )
        output_out[rows, :] = (middle[rows, :] + mods[5:6, :] * outer).astype(brain_type)
        sums[2] = sums[2] + fold_rows(upstream[rows, :].astype(float_type) * outer)
        return carry

    lax.fori_loop(0, chunks, finish_rows, 0)

    def pair_sums(index, carry):
        rows = aligned(index, 128)
        sums[3, :, 0:span] = sums[3, :, 0:span] + fold_rows(
            joined[rows, 0:span].astype(float_type)
        )
        sums[4, :, 0:span] = sums[4, :, 0:span] + fold_rows(
            joined[rows, 2 * span : 3 * span].astype(float_type)
        )
        return carry

    lax.fori_loop(0, row_length // 128, pair_sums, 0)
    input_sum.fold(1)
    expand_out[...] = expand_sum.total()
    one_sum.await_cross()

    def first_back(index, carry):
        rows = aligned(index, chunk)
        one_grad = one_sum.rows(rows)
        normed, root = normed_rows(tokens[rows, :].astype(float_type))
        scaled = one_grad * (1.0 + mods[1:2, :])
        centered = (
            scaled
            - jnp.mean(scaled, axis=-1, keepdims=True)
            - normed * jnp.mean(scaled * normed, axis=-1, keepdims=True)
        )
        token_out[rows, :] = slope[rows, :] + root * centered
        sums[0] = sums[0] + fold_rows(one_grad)
        sums[1] = sums[1] + fold_rows(one_grad * normed)
        return carry

    lax.fori_loop(0, chunks, first_back, 0)

    def summed(index):
        return jnp.sum(sums[index], axis=0, keepdims=True)

    six = (
        summed(0),
        summed(1),
        sums_in[0:1, :],
        sums_in[1:2, :],
        sums_in[2:3, :],
        summed(2),
    )
    slabs[...] = jnp.zeros_like(slabs)
    slots = slot_column(segments)[0:4, 0:1]
    for member in range(group_size):
        low, high = member * own_width, (member + 1) * own_width
        for index in range(6):
            to = slice(index * own_width, (index + 1) * own_width)
            slabs[member, 0:4, to] = slots * six[index][:, low:high]
        slabs[member, 4:5, 0:own_width] = sums_in[3:4, low:high]
        slabs[member, 5:6, 0:own_width] = sums_in[5:6, low:high]
    to_members(slab_slots, lambda member: slabs.at[member], slab_got)
    slab_got[pl.ds(links.member, 1)] = slabs[pl.ds(links.member, 1)]
    input_sum.fold(2)
    from_members(slab_slots, slab_got)
    row = slab_got[0]
    for member in range(1, group_size):
        row = row + slab_got[member]
    place_slab[...] = row
    place_slab[0:4, :] = row[0:4, :].astype(brain_type).astype(float_type)
    place_slab[6:7, 0:width] = sums_in[4:5, :]
    place_slab[7:8, 0:span] = summed(3)[:, 0:span]
    place_slab[7:8, span : 2 * span] = summed(4)[:, 0:span]
    to_places(place_slots, lambda place: place_slab, place_got)
    place_got[pl.ds(links.place, 1)] = place_slab[...][None]
    input_sum.fold(3)
    from_places(place_slots, place_got)
    low_rows = place_got[...].reshape(fsdp_size * 8, 6 * own_width).astype(brain_type)
    parts = [low_rows[:, index * own_width : (index + 1) * own_width] for index in range(6)]
    act_part[...] = sum(
        against(values, cond_weight[index]) for index, values in enumerate(parts)
    ).reshape(fsdp_size, 8, shard)
    to_places(part_slots, lambda place: act_part.at[place], act_got)
    act_got[pl.ds(links.place, 1)] = act_part[pl.ds(links.place, 1)]
    bias_sum = place_got[0]
    for place in range(1, fsdp_size):
        bias_sum = bias_sum + place_got[place]
    bias_row[...] = bias_sum
    bias_row[0:1, :] = jnp.sum(bias_sum[0:4, :], axis=0, keepdims=True)
    to_members(bias_slots, lambda member: bias_row, bias_out)
    bias_out[pl.ds(links.member, 1)] = bias_row[...][None]
    activated = act_all[...].reshape(fsdp_size * 8, shard).astype(brain_type)
    for index, values in enumerate(parts):
        cond_out[index] = across_rows(activated, values)
    from_places(part_slots, act_got)
    to_members(row_slots, lambda member: act_got, act_group)
    act_group[pl.ds(links.member, 1)] = act_got[...][None]
    input_sum.fold(0)
    from_members(row_slots, act_group)
    from_members(bias_slots, bias_out)
    act_sum = act_group[0]
    for member in range(1, group_size):
        act_sum = act_sum + act_group[member]
    raw = conditions[...].astype(float_type)
    gate = 1.0 / (1.0 + jnp.exp(-raw))
    slope_silu = gate * (1.0 + raw * (1.0 - gate))
    for place in range(fsdp_size):
        to = slice(place * shard, (place + 1) * shard)
        act_out[:, to] = act_sum[place, 0:4, :] * slope_silu[:, to]
    sizes_all = bias_sizes(fsdp_size, width, expand_block.shape[1] * group_size)
    owned_biases(links, bias_out, bias_final, own_width, sizes_all, bias_starts(sizes_all))
    joint = input_sum.total()
    for index in range(3):
        input_out[index] = joint[:, index * own_width : (index + 1) * own_width]
    attend_out[...] = joint[:, attend_first:]
    sends.finish()


def bias_starts(sizes):
    starts = [0]
    for size in sizes:
        starts.append(starts[-1] + (size + HEAD_PAD - 1) // HEAD_PAD * HEAD_PAD)
    return starts


def run_backward(sizes, *arrays):
    fsdp_size, group_size, quarter, width, own_width, shard = sizes
    row_length = quarter * group_size
    local_heads = own_width // HEAD_DIM
    span = local_heads * HEAD_PAD
    hidden = arrays[14].shape[1]
    depth = fsdp_size // 2
    six = 6 * own_width
    in_vmem = pl.BlockSpec(memory_space=pltpu.VMEM)
    anywhere = pl.BlockSpec(memory_space=pl.ANY)
    shape = jax.ShapeDtypeStruct
    vmem = pltpu.VMEM
    copies = 3 + 4 * depth + 1 + 2 * fsdp_size + 3 * group_size
    bias_span = bias_starts(bias_sizes(fsdp_size, width, hidden * group_size))[-1]
    in_specs = [in_vmem] * len(arrays)
    in_specs[14] = anywhere
    in_specs[-1] = pl.BlockSpec(memory_space=pltpu.SMEM)
    return pl.pallas_call(
        functools.partial(backward_kernel, sizes),
        out_shape=(
            shape((quarter, width), brain_type),
            shape((quarter, width), float_type),
            shape((4, width), float_type),
            shape((6, shard, own_width), float_type),
            shape((1, bias_span), float_type),
            shape((shard, hidden), float_type),
            shape((3, shard, own_width), float_type),
            shape((shard, own_width), float_type),
        ),
        in_specs=in_specs,
        out_specs=(in_vmem,) * 8,
        scratch_shapes=[
            vmem((quarter, width), brain_type),
            vmem((row_length, 3 * span), brain_type),
            vmem((row_length, HEAD_PAD), float_type),
            vmem((local_heads, 8, row_length), float_type),
            vmem((2, quarter, width), brain_type),
            vmem((2, quarter, width), brain_type),
            vmem((quarter, width), brain_type),
            vmem((quarter, width), brain_type),
            vmem((quarter, width), float_type),
            vmem((width, hidden), brain_type),
            vmem((width, 4 * own_width), brain_type),
            vmem((depth, shard, hidden), brain_type),
            vmem((depth, shard, hidden), brain_type),
            vmem((depth, shard, 4 * own_width), brain_type),
            vmem((depth, shard, 4 * own_width), brain_type),
            vmem((5, 8, width), float_type),
            vmem((group_size, 8, six), float_type),
            vmem((group_size, 8, six), float_type),
            vmem((8, six), float_type),
            vmem((fsdp_size, 8, six), float_type),
            vmem((fsdp_size, 8, shard), float_type),
            vmem((fsdp_size, 8, shard), float_type),
            vmem((group_size, fsdp_size, 8, shard), float_type),
            vmem((8, six), float_type),
            vmem((group_size, 8, six), float_type),
            pltpu.SemaphoreType.DMA((copies,)),
            pltpu.SemaphoreType.DMA((copies,)),
            pltpu.SemaphoreType.DMA((1,)),
        ],
        compiler_params=pltpu.CompilerParams(
            collective_id=2, has_side_effects=True, vmem_limit_bytes=TOP_VMEM
        ),
        name="backward_row",
    )(*arrays)


def deliver_kernel(sizes, count, bias_row, *refs):
    sources, targets = refs[:count], refs[count : 2 * count]
    shares = refs[2 * count : 2 * count + len(sizes)]
    buffers = refs[2 * count + len(sizes) : 3 * count + len(sizes)]
    sems = refs[-1]

    def taken(index):
        return pltpu.make_async_copy(sources[index], buffers[index], sems.at[index])

    def given(index):
        return pltpu.make_async_copy(buffers[index], targets[index], sems.at[count + index])

    for index in range(count):
        taken(index).start()
    for start, size, share in zip(bias_starts(sizes), sizes, shares):
        share[...] = bias_row[0, start : start + size]
    for index in range(count):
        taken(index).wait()
        given(index).start()
    for index in range(count):
        given(index).wait()


def deliver(bias_row, sizes, *arrays):
    count = len(arrays)
    in_vmem = pl.BlockSpec(memory_space=pltpu.VMEM)
    anywhere = pl.BlockSpec(memory_space=pl.ANY)
    shape = jax.ShapeDtypeStruct
    return pl.pallas_call(
        functools.partial(deliver_kernel, sizes, count),
        out_shape=[shape(item.shape, item.dtype) for item in arrays]
        + [shape((size,), float_type) for size in sizes],
        in_specs=[in_vmem] + [anywhere] * count,
        out_specs=[anywhere] * count + [in_vmem] * len(sizes),
        scratch_shapes=[pltpu.VMEM(item.shape, item.dtype) for item in arrays]
        + [pltpu.SemaphoreType.DMA((2 * count,))],
        compiler_params=pltpu.CompilerParams(vmem_limit_bytes=TOP_VMEM),
        name="deliver_row",
    )(bias_row, *arrays)


def fast_local(
    tokens,
    conditions,
    lengths,
    segments,
    condition_weight,
    condition_bias,
    input_weight,
    input_bias,
    attend_weight,
    attend_bias,
    expand_weight,
    expand_bias,
    reduce_weight,
    reduce_bias,
    cotangent,
):
    _, quarter, width = tokens.shape
    group_size, fsdp_size = lax.axis_size("rep"), lax.axis_size("fsdp")
    shard, _, own_width = condition_weight.shape
    hidden = expand_weight.shape[1]
    sizes = (fsdp_size, group_size, quarter, width, own_width, shard)
    biases = (condition_bias, input_bias, attend_bias, expand_bias, reduce_bias)
    bias_total = sum(item.shape[0] for item in biases)
    bias_end = (bias_total + 1023) // 1024 * 1024
    bias_vector, start = 0.0, 0
    for item in biases:
        end = start + item.shape[0]
        bias_vector = bias_vector + jnp.pad(item.astype(float_type), (start, bias_end - end))
        start = end
    bias_vector = bias_vector[None]
    cond_blocks = condition_weight.transpose(1, 0, 2)
    condition_rows = conditions[0]
    token_rows = tokens.reshape(quarter, width)
    upstream = cotangent.reshape(quarter, width)
    (
        mods,
        biases,
        one,
        heads,
        logs,
        mixed,
        branch,
        middle,
        two,
        upper,
        input_pad,
        attend_pad,
        expand_all,
        reduce_all,
        act_all,
    ) = run_forward(
        sizes,
        token_rows,
        upstream,
        condition_rows,
        segments,
        cond_blocks,
        bias_vector,
        lengths,
        (input_weight.transpose(1, 0, 2), attend_weight, expand_weight, reduce_weight),
    )
    (far_sum, near_sum, head_grads, attend_grad, expand_grad, reduce_final, slope, sums) = (
        run_middle(
            sizes,
            two,
            upper,
            expand_all,
            reduce_all,
            mods,
            biases,
            middle,
            branch,
            upstream,
            attend_pad,
            mixed,
        )
    )
    (
        output,
        token_grad,
        condition_grad,
        cond_grad,
        bias_final,
        expand_final,
        input_final,
        attend_final,
    ) = run_backward(
        sizes,
        heads,
        logs,
        head_grads,
        mixed,
        one,
        input_pad,
        token_rows,
        mods,
        biases,
        slope,
        upstream,
        middle,
        far_sum,
        near_sum,
        expand_grad,
        attend_grad,
        sums,
        cond_blocks,
        act_all,
        condition_rows,
        segments,
        lengths,
    )

    (
        output,
        token_grad,
        condition_grad,
        cond_grad,
        input_final,
        attend_final,
        expand_final,
        reduce_final,
        condition_bias_final,
        input_bias_final,
        attend_bias_final,
        expand_bias_final,
        reduce_bias_final,
    ) = deliver(
        bias_final,
        bias_sizes(fsdp_size, width, hidden * group_size),
        output,
        token_grad,
        condition_grad,
        cond_grad,
        input_final,
        attend_final,
        expand_final,
        reduce_final,
    )
    return (
        output[None],
        token_grad[None],
        condition_grad[None],
        cond_grad.transpose(1, 0, 2),
        condition_bias_final,
        input_final.transpose(1, 0, 2),
        input_bias_final,
        attend_final,
        attend_bias_final,
        expand_final,
        expand_bias_final,
        reduce_final,
        reduce_bias_final,
    )


def solution(mesh):
    in_specs = (
        P("fsdp", "rep", None),
        P("fsdp", None, None),
        P("fsdp", None),
        P("fsdp", "rep"),
        P("fsdp", None, "rep"),
        P("fsdp"),
        P("fsdp", None, "rep"),
        P("fsdp"),
        P("fsdp", "rep"),
        P("fsdp"),
        P("fsdp", "rep"),
        P("fsdp"),
        P("fsdp", "rep"),
        P("fsdp"),
        P("fsdp", "rep", None),
    )
    out_specs = (
        P("fsdp", "rep", None),
        P("fsdp", "rep", None),
        P("fsdp", None, None),
        P("fsdp", None, "rep"),
        P("fsdp"),
        P("fsdp", None, "rep"),
        P("fsdp"),
        P("fsdp", "rep"),
        P("fsdp"),
        P("fsdp", "rep"),
        P("fsdp"),
        P("fsdp", "rep"),
        P("fsdp"),
    )
    local = fast_local if mesh.shape["fsdp"] == 8 else plain_local
    return jax.shard_map(local, mesh=mesh, in_specs=in_specs, out_specs=out_specs, check_vma=False)
```

```python
import functools
import math

import jax
import jax.numpy as jnp
from jax import lax
from jax.experimental import pallas as pl
from jax.experimental.pallas import tpu as pltpu
from jax.sharding import PartitionSpec as P

HEAD_DIM = 72


epsilon = 1e-06
highest = lax.Precision.HIGHEST
float_type = jnp.float32
brain_type = jnp.bfloat16


def layer_normed(values):
    center = jnp.mean(values, axis=-1, keepdims=True)
    shifted = values - center
    spread = jnp.mean(shifted * shifted, axis=-1, keepdims=True)
    return shifted * lax.rsqrt(spread + epsilon)


def modulated(values, shift_term, scale_term):
    return layer_normed(values) * (1.0 + scale_term) + shift_term


def gelu_tanh(values):
    return jax.nn.gelu(values, approximate=True)


def image_index(row_ends, positions):
    return jnp.sum((positions[..., :, None] >= row_ends[..., None, :-1]).astype(jnp.int32), axis=-1)


def across(left, right):
    return lax.dot_general(left, right, (((0,), (0,)), ((), ())), preferred_element_type=float_type)


def against(left, right):
    return lax.dot_general(left, right, (((1,), (1,)), ((), ())), preferred_element_type=float_type)


def column_sums(values):
    return jnp.sum(values.astype(float_type), axis=0)


def spread_columns(own_part, total, start):
    empty = jnp.zeros(own_part.shape[:-1] + (total,), float_type)
    return lax.dynamic_update_slice_in_dim(empty, own_part, start, own_part.ndim - 1)


def gather_block(*weights):
    return tuple(lax.all_gather(item, "fsdp", axis=0, tiled=True) for item in weights)


def plain_local(
    tokens,
    conditions,
    lengths,
    segments,
    condition_weight,
    condition_bias,
    input_weight,
    input_bias,
    attend_weight,
    attend_bias,
    expand_weight,
    expand_bias,
    reduce_weight,
    reduce_bias,
    cotangent,
):
    row_count, quarter, model_width = tokens.shape
    slot_count = conditions.shape[1]
    group_size = lax.axis_size("rep")
    group_place = lax.axis_index("rep")
    row_length = quarter * group_size
    own_width = condition_weight.shape[2]
    column_start = group_place * own_width
    hidden_width = expand_weight.shape[1]
    hidden_start = group_place * hidden_width
    local_heads = own_width // HEAD_DIM
    score_scale = 1.0 / math.sqrt(HEAD_DIM)
    patch_count = row_count * quarter
    image_count = row_count * slot_count
    key_place = jnp.arange(row_length, dtype=jnp.int32)
    row_ends = jnp.cumsum(lengths, axis=1, dtype=jnp.int32)
    row_images = image_index(row_ends, key_place)
    allowed = row_images[:, :, None] == row_images[:, None, :]

    def whole_rows(values):
        joined_rows = lax.all_gather(
            values.reshape(row_count, quarter, -1), "rep", axis=1, tiled=True
        )
        return joined_rows.reshape(row_count * row_length, -1)

    def own_rows(values):
        summed = lax.psum_scatter(
            values.reshape(row_count, row_length, -1), "rep", scatter_dimension=1, tiled=True
        )
        return summed.reshape(patch_count, -1)

    fsdp_size = lax.axis_size("fsdp")
    fsdp_place = lax.axis_index("fsdp")
    own_depth = condition_weight.shape[0]
    condition_values = conditions.astype(float_type)
    activated_own = jax.nn.silu(condition_values).reshape(image_count, model_width).astype(brain_type)
    activated_all = lax.all_gather(activated_own, "fsdp", axis=0, tiled=True)
    activated = lax.dynamic_slice_in_dim(activated_all, fsdp_place * own_depth, own_depth, 1)
    local_biases = (condition_bias, input_bias, attend_bias, expand_bias, reduce_bias)
    share_sizes = [item.shape[0] for item in local_biases]
    bias_ends = [sum(share_sizes[:k]) for k in range(len(share_sizes) + 1)]
    bias_table = lax.all_gather(jnp.concatenate(local_biases), "fsdp", axis=0, tiled=False)
    condition_bias_all, input_bias_all, attend_bias_all, expand_bias_all, reduce_bias_all = [
        bias_table[:, low:high].reshape(-1) for low, high in zip(bias_ends[:-1], bias_ends[1:])
    ]
    condition_bias_own = lax.dynamic_slice_in_dim(
        condition_bias_all.reshape(6, model_width), column_start, own_width, 1
    )
    modulation_parts = jnp.einsum(
        "id,dkm->ikm", activated, condition_weight, preferred_element_type=float_type
    )
    modulation_own = (
        lax.psum_scatter(modulation_parts, "fsdp", scatter_dimension=0, tiled=True)
        + condition_bias_own[None]
    )
    modulation = lax.all_gather(modulation_own, "rep", axis=2, tiled=True).reshape(
        row_count, slot_count, -1
    )
    slot_table = (
        segments[:, :, None] == jnp.arange(slot_count, dtype=jnp.int32)[None, None, :]
    ).astype(float_type)
    per_token = jnp.einsum("rqs,rsm->rqm", slot_table, modulation, precision=highest).reshape(
        patch_count, -1
    )
    shift_one, scale_one, gate_one, shift_two, scale_two, gate_two = jnp.split(per_token, 6, axis=1)
    token_values = tokens.reshape(patch_count, model_width).astype(float_type)

    def split_heads(values):
        return values.reshape(row_count, row_length, local_heads, HEAD_DIM).transpose(2, 0, 1, 3)

    def merge_heads(values):
        return values.transpose(1, 2, 0, 3).reshape(row_count * row_length, own_width)

    def allowed_scores(query_head, key_head):
        scores = (
            jnp.einsum("rqd,rkd->rqk", query_head, key_head, preferred_element_type=float_type)
            * score_scale
        )
        return jnp.where(allowed, scores, -1e30)

    def head_forward(parts):
        query_head, key_head, value_head = parts
        scores = allowed_scores(query_head, key_head)
        row_max = jnp.max(scores, axis=-1, keepdims=True)
        powers = jnp.exp(scores - row_max)
        totals = jnp.sum(powers, axis=-1, keepdims=True)
        weights_low = (powers / totals).astype(brain_type)
        mixed = jnp.einsum(
            "rqk,rkd->rqd", weights_low, value_head, preferred_element_type=float_type
        )
        return (mixed, row_max + jnp.log(totals))

    def head_backward(parts):
        query_head, key_head, value_head, grad_head, log_head = parts
        scores = allowed_scores(query_head, key_head)
        probable = jnp.exp(scores - log_head)
        prob_grad = jnp.einsum(
            "rqd,rkd->rqk", grad_head, value_head, preferred_element_type=float_type
        )
        score_grad = (
            probable * (prob_grad - jnp.sum(probable * prob_grad, axis=-1, keepdims=True))
        ).astype(brain_type)
        query_part = (
            jnp.einsum("rqk,rkd->rqd", score_grad, key_head, preferred_element_type=float_type)
            * score_scale
        )
        key_part = (
            jnp.einsum("rqk,rqd->rkd", score_grad, query_head, preferred_element_type=float_type)
            * score_scale
        )
        value_part = jnp.einsum(
            "rqk,rqd->rkd",
            probable.astype(brain_type),
            grad_head,
            preferred_element_type=float_type,
        )
        return (query_part, key_part, value_part)

    def trunk(gathered):
        (
            input_all,
            input_bias_all,
            attend_all,
            attend_bias_all,
            expand_all,
            expand_bias_all,
            reduce_all,
            reduce_bias_all,
        ) = gathered
        bias_pair = lax.dynamic_slice_in_dim(
            input_bias_all.reshape(2, model_width), column_start, own_width, 1
        )
        expand_bias_own = lax.dynamic_slice_in_dim(expand_bias_all, hidden_start, hidden_width, 0)
        normed_one = modulated(token_values, shift_one, scale_one).astype(brain_type)
        whole_one = whole_rows(normed_one)
        joined = jnp.einsum("nd,dkm->nkm", whole_one, input_all, preferred_element_type=float_type)
        queries = (joined[:, 0] + bias_pair[0]).astype(brain_type)
        keys_row = joined[:, 1].astype(brain_type)
        values_row = (joined[:, 2] + bias_pair[1]).astype(brain_type)
        query_heads = split_heads(queries)
        key_heads = split_heads(keys_row)
        value_heads = split_heads(values_row)
        mixed, log_totals = lax.map(head_forward, (query_heads, key_heads, value_heads))
        attended = merge_heads(mixed).astype(brain_type)
        branch = own_rows(against(attended, attend_all)) + attend_bias_all
        middle = token_values + gate_one * branch
        normed_two = modulated(middle, shift_two, scale_two).astype(brain_type)
        whole_two = whole_rows(normed_two)
        inner = jnp.dot(whole_two, expand_all, preferred_element_type=float_type) + expand_bias_own
        active = gelu_tanh(inner).astype(brain_type)
        outer = own_rows(against(active, reduce_all)) + reduce_bias_all
        result = middle + gate_two * outer
        return (
            result,
            gathered,
            whole_one,
            query_heads,
            key_heads,
            value_heads,
            log_totals,
            attended,
            branch,
            middle,
            whole_two,
            inner,
            active,
            outer,
        )

    input_all, attend_all, expand_all, reduce_all = gather_block(
        input_weight, attend_weight, expand_weight, reduce_weight
    )
    state = trunk(
        (
            input_all,
            input_bias_all,
            attend_all,
            attend_bias_all,
            expand_all,
            expand_bias_all,
            reduce_all,
            reduce_bias_all,
        )
    )
    output = state[0].astype(brain_type).reshape(row_count, quarter, model_width)
    (
        _,
        gathered,
        whole_one,
        query_heads,
        key_heads,
        value_heads,
        log_totals,
        attended,
        branch,
        middle,
        whole_two,
        inner,
        active,
        outer,
    ) = state
    upstream = cotangent.reshape(patch_count, model_width).astype(float_type)
    outer_grad = (gate_two * upstream).astype(brain_type)
    gate_two_grad = upstream * outer
    outer_whole = whole_rows(outer_grad)
    reduce_grad = across(outer_whole, active)
    reduce_bias_grad = column_sums(outer_grad)
    active_grad = jnp.dot(outer_whole, reduce_all, preferred_element_type=float_type)
    _, gelu_back = jax.vjp(gelu_tanh, inner)
    inner_grad = gelu_back(active_grad)[0].astype(brain_type)
    expand_grad = across(whole_two, inner_grad)
    expand_bias_full = spread_columns(
        column_sums(inner_grad), hidden_width * group_size, hidden_start
    )
    two_grad = own_rows(against(inner_grad, expand_all))
    _, second_back = jax.vjp(modulated, middle, shift_two, scale_two)
    middle_norm_grad, shift_two_grad, scale_two_grad = second_back(two_grad)
    middle_grad = upstream + middle_norm_grad
    gate_one_grad = middle_grad * branch
    branch_grad = (gate_one * middle_grad).astype(brain_type)
    branch_whole = whole_rows(branch_grad)
    attend_grad = across(branch_whole, attended)
    attend_bias_grad = column_sums(branch_grad)
    attended_grad = jnp.dot(branch_whole, attend_all, preferred_element_type=float_type).astype(
        brain_type
    )
    grad_heads = split_heads(attended_grad)
    query_parts, key_parts, value_parts = lax.map(
        head_backward, (query_heads, key_heads, value_heads, grad_heads, log_totals)
    )
    query_low = merge_heads(query_parts).astype(brain_type)
    key_low = merge_heads(key_parts).astype(brain_type)
    value_low = merge_heads(value_parts).astype(brain_type)
    joined_grad = jnp.stack([query_low, key_low, value_low], axis=1)
    input_grad = jnp.einsum(
        "nd,nkm->dkm", whole_one, joined_grad, preferred_element_type=float_type
    )
    input_bias_pair = jnp.stack([column_sums(query_low), column_sums(value_low)])
    input_bias_full = spread_columns(input_bias_pair, model_width, column_start).reshape(-1)
    one_grad = own_rows(
        jnp.einsum("nkm,dkm->nd", joined_grad, input_all, preferred_element_type=float_type)
    )
    _, first_back = jax.vjp(modulated, token_values, shift_one, scale_one)
    token_norm_grad, shift_one_grad, scale_one_grad = first_back(one_grad)
    token_grad = (middle_grad + token_norm_grad).reshape(row_count, quarter, model_width)
    six_grads = jnp.stack(
        [
            shift_one_grad,
            scale_one_grad,
            gate_one_grad,
            shift_two_grad,
            scale_two_grad,
            gate_two_grad,
        ],
        axis=1,
    ).reshape(row_count, quarter, 6, model_width)
    modulation_part = jnp.einsum("rqs,rqkm->rskm", slot_table, six_grads, precision=highest)
    modulation_grad = lax.psum_scatter(modulation_part, "rep", scatter_dimension=3, tiled=True)
    modulation_low = lax.all_gather(
        modulation_grad.reshape(image_count, 6, own_width).astype(brain_type),
        "fsdp",
        axis=0,
        tiled=True,
    )
    condition_weight_final = jnp.einsum(
        "id,ikm->dkm", activated, modulation_low, preferred_element_type=float_type
    )
    condition_bias_full = lax.all_gather(
        column_sums(modulation_low), "rep", axis=1, tiled=True
    ).reshape(-1)
    bias_depth = condition_bias.shape[0]
    condition_bias_final = lax.dynamic_slice_in_dim(
        condition_bias_full, fsdp_place * bias_depth, bias_depth, 0
    )
    activated_part = jnp.einsum(
        "ikm,dkm->id", modulation_low, condition_weight, preferred_element_type=float_type
    )
    activated_wide = lax.all_to_all(
        activated_part.reshape(fsdp_size, image_count, own_depth), "fsdp", 0, 0
    )
    activated_row = jnp.transpose(activated_wide, (1, 0, 2)).reshape(image_count, model_width)
    bias_rows = jnp.concatenate(
        [
            item.reshape(fsdp_size, -1)
            for item in (input_bias_full, attend_bias_grad, expand_bias_full, reduce_bias_grad)
        ],
        axis=1,
    )
    bias_own = lax.psum_scatter(bias_rows, "fsdp", scatter_dimension=0, tiled=True).reshape(-1)
    activated_grad, bias_sum = lax.psum((activated_row, bias_own), "rep")
    input_bias_final, attend_bias_final, expand_bias_final, reduce_bias_final = jnp.split(
        bias_sum, [end - share_sizes[0] for end in bias_ends[2:-1]]
    )
    input_final, attend_final, expand_final, reduce_final = [
        lax.psum_scatter(item.astype(brain_type), "fsdp", scatter_dimension=0, tiled=True).astype(
            float_type
        )
        for item in (input_grad, attend_grad, expand_grad, reduce_grad)
    ]
    _, silu_back = jax.vjp(jax.nn.silu, condition_values)
    condition_grad = silu_back(activated_grad.reshape(row_count, slot_count, model_width))[0]
    return (
        output,
        token_grad,
        condition_grad,
        condition_weight_final,
        condition_bias_final,
        input_final,
        input_bias_final,
        attend_final,
        attend_bias_final,
        expand_final,
        expand_bias_final,
        reduce_final,
        reduce_bias_final,
    )


MESH = pl.DeviceIdType.MESH
HEAD_PAD = 128
TOP_VMEM = 60 * 1024 * 1024


def aligned(index, step):
    return pl.ds(pl.multiple_of(index * step, step), step)


class Links:
    def __init__(self, fsdp_size, group_size):
        self.fsdp_size = fsdp_size
        self.group_size = group_size
        self.depth = fsdp_size // 2
        self.place = lax.axis_index("fsdp")
        self.member = lax.axis_index("rep")
        self.level = self.place // 2
        self.side = self.place % 2
        self.core = self.member % 2
        self.half = self.member // 2

    def to_place(self, place):
        return (place, self.member)

    def to_member(self, member):
        return (self.place, member)

    @property
    def core_mate(self):
        return self.half * 2 + 1 - self.core

    @property
    def half_mate(self):
        return (1 - self.half) * 2 + self.core

    @property
    def far_mate(self):
        return (1 - self.half) * 2 + 1 - self.core

    @property
    def side_mate(self):
        return self.level * 2 + 1 - self.side

    def level_at(self, shift):
        return lax.rem(self.level + shift + self.depth, self.depth)

    def meet(self):
        self.await_all(self.greet())

    def await_all(self, count):
        pl.semaphore_wait(pltpu.get_barrier_semaphore(), count)

    def greet(self):
        barrier = pltpu.get_barrier_semaphore()
        count = 0
        for shift in range(1, self.fsdp_size):
            target = lax.rem(self.place + shift, self.fsdp_size)
            pl.semaphore_signal(barrier, inc=1, device_id=self.to_place(target), device_id_type=MESH)
            count += 1
        for shift in range(1, self.group_size):
            target = lax.rem(self.member + shift, self.group_size)
            pl.semaphore_signal(barrier, inc=1, device_id=self.to_member(target), device_id_type=MESH)
            count += 1
        return count


class Sends:
    def __init__(self, send_sems, recv_sems):
        self.send_sems = send_sems
        self.recv_sems = recv_sems
        self.used = 0
        self.open = []

    def slot(self):
        self.used += 1
        return self.used - 1

    def copy(self, slot, source, target, device):
        return pltpu.make_async_remote_copy(
            src_ref=source,
            dst_ref=target,
            send_sem=self.send_sems.at[slot],
            recv_sem=self.recv_sems.at[slot],
            device_id=device,
            device_id_type=MESH,
        )

    def start(self, slot, source, target, device):
        made = self.copy(slot, source, target, device)
        made.start()
        self.open.append(made)

    def arrived(self, slot, target, device):
        self.copy(slot, target, target, device).wait_recv()

    def finish(self):
        for made in self.open:
            made.wait_send()


class GroupGather:
    def __init__(self, links, sends, buffer, quarter):
        self.links, self.sends, self.buffer, self.quarter = links, sends, buffer, quarter
        self.slots = [sends.slot() for _ in range(3)]

    def rows(self, member):
        return self.buffer.at[aligned(member, self.quarter), :]

    def start_core(self):
        own = self.rows(self.links.member)
        mate = self.links.to_member(self.links.core_mate)
        self.sends.start(self.slots[0], own, own, mate)

    def start_half(self):
        own = self.rows(self.links.member)
        self.sends.start(self.slots[1], own, own, self.links.to_member(self.links.half_mate))

    def await_core(self):
        mate = self.links.core_mate
        self.sends.arrived(self.slots[0], self.rows(mate), self.links.to_member(mate))

    def pass_on(self):
        mate = self.links.half_mate
        self.sends.arrived(self.slots[1], self.rows(mate), self.links.to_member(mate))
        passed = self.rows(mate)
        self.sends.start(
            self.slots[2], passed, passed, self.links.to_member(self.links.core_mate)
        )

    def await_far(self):
        mate = self.links.core_mate
        self.sends.arrived(self.slots[2], self.rows(self.links.far_mate), self.links.to_member(mate))


class GroupSum:
    def __init__(self, links, sends, lent, got, crossing, crossed, total):
        self.links, self.sends = links, sends
        self.lent, self.got, self.crossing, self.crossed, self.total = (
            lent,
            got,
            crossing,
            crossed,
            total,
        )
        self.slots = [sends.slot() for _ in range(3)]

    def member_of(self, step):
        half = lax.rem(self.links.half + 1 - step // 2 + 2, 2)
        core = lax.rem(self.links.core + 1 - step % 2 + 2, 2)
        return half * 2 + core

    def lend(self, index):
        mate = self.links.to_member(self.links.core_mate)
        return self.sends.copy(
            self.slots[0] + index, self.lent.at[index], self.got.at[index], mate
        )

    def cross(self):
        mate = self.links.to_member(self.links.half_mate)
        return self.sends.copy(self.slots[2], self.crossing, self.crossed, mate)

    def step(self, step, value, crosses):
        index = step // 2
        self.total[...] = value

        @pl.when(step % 2 == 0)
        def _():
            self.lent[index] = self.total[...].astype(brain_type)
            self.lend(index).start()

        @pl.when(step % 2 == 1)
        def _():
            self.lend(index).wait_recv()

        @pl.when(step == 1)
        def _():
            self.crossing[...] = (self.total[...] + self.got[0].astype(float_type)).astype(
                brain_type
            )
            if crosses:
                self.cross().start()

    def note(self, crosses):
        self.sends.open += [self.lend(0), self.lend(1)]
        if crosses:
            self.sends.open.append(self.cross())

    def await_cross(self):
        self.sends.arrived(
            self.slots[2], self.crossed, self.links.to_member(self.links.half_mate)
        )

    def rows(self, rows):
        return (
            self.total[rows, :]
            + self.got[1, rows, :].astype(float_type)
            + self.crossed[rows, :].astype(float_type)
        )


def normed_rows(values):
    center = jnp.mean(values, axis=-1, keepdims=True)
    shifted = values - center
    spread = jnp.mean(shifted * shifted, axis=-1, keepdims=True)
    root = lax.rsqrt(spread + epsilon)
    return shifted * root, root


def spread_heads(source, target, rows, first, heads, target_first):
    for head in range(heads):
        low, to = HEAD_DIM * (first + head), HEAD_PAD * (target_first + head)
        target[rows, to : to + HEAD_DIM] = source[rows, low : low + HEAD_DIM]


def slot_column(segments):
    slots = lax.broadcasted_iota(jnp.int32, (8, HEAD_PAD), 0)
    return jnp.where(slots == segments[0:1, 0:HEAD_PAD], 1.0, 0.0)


def image_at(lengths, start):
    end, image = 0, 0
    for slot in range(lengths.shape[1] - 1):
        end = end + lengths[0, slot]
        image = image + jnp.where(start >= end, 1, 0)
    return image


def pair_mask(lengths, first, second):
    return jnp.where(image_at(lengths, first) == image_at(lengths, second), 0.0, -1e30)


def chosen(flag, values):
    return values * jnp.where(flag, 1.0, 0.0)


def bias_sizes(fsdp_size, width, hidden_total):
    return [size // fsdp_size for size in (6 * width, 2 * width, width, hidden_total, width)]


def own_biases(links, bias_vector, bias_table, own_width, sizes):
    place, member = links.place, links.member
    group_size = links.group_size
    starts = [sum(sizes[:index]) for index in range(6)]

    def piece(index, low, size):
        return bias_vector[0:1, starts[index] + low : starts[index] + low + size]

    bias_table[...] = jnp.zeros_like(bias_table)
    blocks = sizes[0] // own_width
    for kind in range(6):
        row = sum(
            chosen(
                place * blocks + index == kind * group_size + member,
                piece(0, index * own_width, own_width),
            )
            for index in range(blocks)
        )
        bias_table[0:4, kind * own_width : (kind + 1) * own_width] = jnp.broadcast_to(
            row, (4, own_width)
        )
    per_member = links.fsdp_size // group_size
    for part in range(per_member):
        bias_table[4:5, part * sizes[3] : (part + 1) * sizes[3]] = chosen(
            place == member * per_member + part, piece(3, 0, sizes[3])
        )
    for row, index in ((5, 2), (6, 4)):
        for other in range(links.fsdp_size):
            bias_table[row : row + 1, other * sizes[index] : (other + 1) * sizes[index]] = chosen(
                place == other, piece(index, 0, sizes[index])
            )
    local_heads = own_width // HEAD_DIM
    for pair in range(2):
        for head in range(local_heads):
            to = (pair * local_heads + head) * HEAD_PAD
            bias_table[7:8, to : to + HEAD_DIM] = chosen(
                place == pair * group_size + member, piece(1, head * HEAD_DIM, HEAD_DIM)
            )


def owned_biases(links, bias_rows, final, own_width, sizes, starts):
    place = links.place
    group_size, fsdp_size = links.group_size, links.fsdp_size
    blocks = sizes[0] // own_width
    final[...] = jnp.zeros_like(final)
    for index in range(blocks):
        total = 0.0
        for owner in range(fsdp_size):
            kind, member = divmod(owner * blocks + index, group_size)
            total = total + chosen(
                place == owner,
                bias_rows[member, 0:1, kind * own_width : (kind + 1) * own_width],
            )
        to = starts[0] + index * own_width
        final[:, to : to + own_width] = total
    local_heads = own_width // HEAD_DIM
    for head in range(local_heads):
        total = 0.0
        for owner in range(fsdp_size):
            pair, member = divmod(owner, group_size)
            low = (pair * local_heads + head) * HEAD_PAD
            total = total + chosen(place == owner, bias_rows[member, 7:8, low : low + HEAD_DIM])
        to = starts[1] + head * HEAD_DIM
        final[:, to : to + HEAD_DIM] = total
    per_member = fsdp_size // group_size
    for index, row in ((2, 4), (4, 5), (3, 6)):
        size = sizes[index]
        total = 0.0
        for owner in range(fsdp_size):
            member, part = divmod(owner, per_member)
            total = total + chosen(
                place == owner, bias_rows[member, row : row + 1, part * size : (part + 1) * size]
            )
        final[:, starts[index] : starts[index] + size] = total


def forward_kernel(
    sizes,
    tokens,
    upstream,
    conditions,
    segments,
    cond_weight,
    bias_vector,
    lengths,
    input_weight,
    attend_weight,
    weight_one,
    weight_two,
    mod_out,
    bias_out,
    one_out,
    heads_out,
    log_out,
    mixed_out,
    branch_out,
    middle_out,
    two_out,
    upper_out,
    input_out,
    attend_out,
    expand_out,
    reduce_out,
    act_out,
    act_send,
    bias_table,
    weight_zero,
    act_got,
    mod_parts,
    mod_got,
    mod_row,
    group_got,
    weights,
    normed,
    lent,
    got,
    crossing,
    crossed,
    total,
    one,
    two,
    upper,
    heads,
    mixed,
    input_pad,
    attend_pad,
    send_sems,
    recv_sems,
    local_sems,
):
    fsdp_size, group_size, quarter, width, own_width, shard = sizes
    links = Links(fsdp_size, group_size)
    sends = Sends(send_sems, recv_sems)
    blocks = (weight_zero, weight_one, weight_two)
    local_heads = own_width // HEAD_DIM
    head_span = local_heads * HEAD_PAD
    chunk = 32
    chunks = quarter // chunk

    act_slots = [sends.slot() for _ in range(fsdp_size)]
    mod_slots = [sends.slot() for _ in range(fsdp_size)]
    group_slots = [sends.slot() for _ in range(group_size)]
    level_slots = [[sends.slot() for _ in range(links.depth)] for _ in blocks]
    side_slots = [[sends.slot() for _ in range(links.depth)] for _ in blocks]
    onward_slots = [sends.slot() for _ in blocks]
    gather_one = GroupGather(links, sends, one, quarter)
    gather_two = GroupGather(links, sends, two, quarter)
    gather_upper = GroupGather(links, sends, upper, quarter)
    branch_sum = GroupSum(links, sends, lent, got, crossing, crossed, total)
    opened = []

    def shard_rows(block, place):
        return weights.at[block, aligned(place, shard), :]

    inner = links.level * (links.depth - 1 - links.level) > 0
    near = jnp.where(links.level < 2, 3, 1)
    order = (2, near, 4 - near)

    def level_copy(block, shift):
        own = shard_rows(block, links.place)
        target = links.level_at(shift) * 2 + links.side
        return sends.copy(
            level_slots[block][0] + shift, blocks[block], own, links.to_place(target)
        )

    def offer_levels(block):
        level_copy(block, 2).start()
        level_copy(block, 4 - near).start()

        @pl.when(inner)
        def _():
            level_copy(block, near).start()

    def offer_side(block):
        own = shard_rows(block, links.place)
        sends.start(side_slots[block][0], blocks[block], own, links.to_place(links.side_mate))

    def keep_own(block):
        kept = pltpu.make_async_copy(
            blocks[block], shard_rows(block, links.place), local_sems.at[block]
        )
        kept.start()
        return kept

    def forward_copy(block):
        rows = shard_rows(block, links.level_at(2) * 2 + links.side)
        return pltpu.make_async_remote_copy(
            src_ref=rows,
            dst_ref=rows,
            send_sem=send_sems.at[onward_slots[block]],
            recv_sem=recv_sems.at[level_slots[block][0] + 2 * links.level - 1],
            device_id=links.to_place((3 * links.level - 3) * 2 + links.side),
            device_id_type=MESH,
        )

    def side_copy(block, shift):
        rows = shard_rows(block, links.level_at(-shift) * 2 + links.side)
        return sends.copy(
            side_slots[block][0] + shift, rows, rows, links.to_place(links.side_mate)
        )

    def relay(block, index):
        shift = order[index]
        source = links.level_at(-shift) * 2 + links.side
        rows = shard_rows(block, source)
        sends.arrived(level_slots[block][0] + shift, rows, links.to_place(source))
        if index == 0:

            @pl.when(inner)
            def _():
                forward_copy(block).start()

        side_copy(block, shift).start()
        return source

    def side_arrived(block, index):
        shift = order[index - 1] if index else 0
        source = links.level_at(-shift) * 2 + 1 - links.side
        sends.arrived(
            side_slots[block][0] + shift, shard_rows(block, source), links.to_place(links.side_mate)
        )
        return source

    def finish_weights(block):
        level_copy(block, 2).wait_send()
        level_copy(block, 4 - near).wait_send()

        @pl.when(inner)
        def _():
            level_copy(block, near).wait_send()
            forward_copy(block).wait_send()

        for shift in order:
            side_copy(block, shift).wait_send()

    def keep(index, source, target):
        made = pltpu.make_async_copy(source, target, local_sems.at[index])
        made.start()
        opened.append(made)

    greeted = links.greet()
    raw = conditions[...].astype(float_type)
    activated = (raw / (1.0 + jnp.exp(-raw))).astype(brain_type).astype(float_type)
    act_send[...] = jnp.zeros_like(act_send)
    for place in range(fsdp_size):
        act_send[place, 0:4, :] = activated[:, place * shard : (place + 1) * shard]
    for index in range(3):
        weight_zero[:, index * own_width : (index + 1) * own_width] = input_weight[index]
    weight_zero[:, 3 * own_width : 4 * own_width] = attend_weight[...]
    links.await_all(greeted)
    for shift in range(1, fsdp_size):
        target = lax.rem(links.place + shift, fsdp_size)
        sends.start(
            act_slots[shift], act_send.at[target], act_got.at[links.place], links.to_place(target)
        )
    act_got[pl.ds(links.place, 1)] = act_send[pl.ds(links.place, 1)]
    kept_zero, kept_one, kept_two = [keep_own(block) for block in range(3)]
    hidden_total = weight_one.shape[1] * group_size
    own_biases(links, bias_vector, bias_table, own_width, bias_sizes(fsdp_size, width, hidden_total))

    def norm_tokens(index, carry):
        rows = aligned(index, chunk)
        normed[rows, :] = normed_rows(tokens[rows, :].astype(float_type))[0]
        return carry

    for shift in range(1, fsdp_size):
        source = lax.rem(links.place + fsdp_size - shift, fsdp_size)
        sends.arrived(act_slots[shift], act_got.at[source], links.to_place(source))
    activated = act_got[...].reshape(fsdp_size * 8, shard).astype(brain_type)
    for index in range(6):
        to = slice(index * own_width, (index + 1) * own_width)
        mod_parts[:, :, to] = (
            jnp.dot(activated, cond_weight[index], preferred_element_type=float_type).reshape(
                fsdp_size, 8, own_width
            )
            + bias_table[:, to][None]
        )
    act_out[...] = act_got[...]
    for shift in range(1, fsdp_size):
        target = lax.rem(links.place + shift, fsdp_size)
        sends.start(
            mod_slots[shift], mod_parts.at[target], mod_got.at[links.place], links.to_place(target)
        )
    for block in range(3):
        offer_levels(block)
    offer_side(0)
    offer_side(1)
    mod_got[pl.ds(links.place, 1)] = mod_parts[pl.ds(links.place, 1)]
    lax.fori_loop(0, chunks, norm_tokens, 0)
    input_pad[...] = jnp.zeros_like(input_pad)
    attend_pad[...] = jnp.zeros_like(attend_pad)
    kept_zero.wait()

    def spread_shard(place):
        rows = aligned(place, shard)
        spread_heads(weights.at[0], input_pad, rows, 0, 3 * local_heads, 0)
        spread_heads(weights.at[0], attend_pad, rows, 3 * local_heads, local_heads, 0)

    spread_shard(links.place)
    for shift in range(1, fsdp_size):
        source = lax.rem(links.place + fsdp_size - shift, fsdp_size)
        sends.arrived(mod_slots[shift], mod_got.at[source], links.to_place(source))
    summed = mod_got[0]
    for index in range(1, fsdp_size):
        summed = summed + mod_got[index]
    mod_row[...] = summed
    for shift in range(1, group_size):
        target = lax.rem(links.member + shift, group_size)
        sends.start(group_slots[shift], mod_row, group_got.at[links.member], links.to_member(target))
    group_got[pl.ds(links.member, 1)] = mod_row[...][None]
    bias_out[...] = mod_row[...]
    for shift in range(1, group_size):
        source = lax.rem(links.member + group_size - shift, group_size)
        sends.arrived(group_slots[shift], group_got.at[source], links.to_member(source))
    slot = slot_column(segments)[:, 0:1]
    for index in range(6):
        full = jnp.concatenate(
            [
                group_got[member, :, index * own_width : (index + 1) * own_width]
                for member in range(group_size)
            ],
            axis=1,
        )
        mod_out[index : index + 1, :] = jnp.sum(full * slot, axis=0, keepdims=True)
    mod_out[6:8, :] = jnp.zeros((2, width), float_type)

    own_rows = links.member * quarter

    def first_norm(index, carry):
        rows = aligned(index, chunk)
        to = pl.ds(pl.multiple_of(own_rows + index * chunk, chunk), chunk)
        one[to, :] = (normed[rows, :] * (1.0 + mod_out[1:2, :]) + mod_out[0:1, :]).astype(brain_type)
        return carry

    lax.fori_loop(0, chunks, first_norm, 0)
    gather_one.start_half()
    gather_one.start_core()
    first_sources = [relay(0, index) for index in range(links.depth - 1)]
    offer_side(2)

    def upper_rows(index, carry):
        rows = aligned(index, chunk)
        to = pl.ds(pl.multiple_of(own_rows + index * chunk, chunk), chunk)
        upper[to, :] = (mod_out[5:6, :] * upstream[rows, :].astype(float_type)).astype(brain_type)
        return carry

    lax.fori_loop(0, chunks, upper_rows, 0)

    for source in first_sources:
        spread_shard(source)
    gather_one.pass_on()
    gather_upper.start_half()
    gather_upper.start_core()
    gather_one.await_core()
    for shift in range(links.depth):
        spread_shard(side_arrived(0, shift))
    gather_one.await_far()
    keep(3, one, one_out)
    keep(4, input_pad, input_out)
    keep(5, attend_pad, attend_out)

    bias_pad = mod_row[7:8, 0 : 2 * head_span]

    def project(index, carry):
        rows = aligned(index, quarter)
        values = jnp.dot(one[rows, :], input_pad[...], preferred_element_type=float_type)
        heads[rows, 0:head_span] = (values[:, 0:head_span] + bias_pad[:, 0:head_span]).astype(
            brain_type
        )
        heads[rows, head_span : 2 * head_span] = values[:, head_span : 2 * head_span].astype(
            brain_type
        )
        heads[rows, 2 * head_span :] = (
            values[:, 2 * head_span :] + bias_pad[:, head_span:]
        ).astype(brain_type)
        return carry

    lax.fori_loop(0, group_size, project, 0)
    keep(6, heads, heads_out)

    power_scale = math.log2(math.e) / math.sqrt(HEAD_DIM)

    def attend(head, turn):
        part = branch_sum.member_of(turn)
        step = turn * local_heads + head
        rows = aligned(part, quarter)

        def columns(base):
            return aligned(base * local_heads + head, HEAD_PAD)

        raw = lax.dot_general(
            heads[rows, columns(0)],
            heads[:, columns(1)],
            (((1,), (1,)), ((), ())),
            preferred_element_type=float_type,
        )
        scores = jnp.concatenate(
            [
                raw[:, other * quarter : (other + 1) * quarter]
                + pair_mask(lengths, part * quarter, other * quarter)
                for other in range(group_size)
            ],
            axis=1,
        )
        top = jnp.max(scores, axis=1, keepdims=True)
        powers = jnp.exp2(scores * power_scale - top * power_scale)
        totals = jnp.sum(powers, axis=1, keepdims=True)
        value = jnp.dot(
            powers.astype(brain_type), heads[:, columns(2)], preferred_element_type=float_type
        )
        mixed[rows, aligned(head, HEAD_PAD)] = (value / totals).astype(brain_type)
        turned = jnp.transpose(
            jnp.broadcast_to(top * power_scale + jnp.log2(totals), (quarter, HEAD_PAD))
        )
        log_out[head, :, rows] = turned[0:8, :]
        for index, late in enumerate((1, 3, 5)):

            @pl.when(step == late)
            def _():
                relay(1, index)

        @pl.when(step == 4)
        def _():
            gather_upper_in_loop()

        return turn

    def gather_upper_in_loop():
        mate = links.half_mate
        passed = gather_upper.rows(mate)
        sends.arrived(gather_upper.slots[1], passed, links.to_member(mate))
        sends.copy(
            gather_upper.slots[2], passed, passed, links.to_member(links.core_mate)
        ).start()

    def branch_part(member):
        return lax.dot_general(
            mixed[aligned(member, quarter), :],
            attend_pad[...],
            (((1,), (1,)), ((), ())),
            preferred_element_type=float_type,
        )

    def attend_turn(turn, carry):
        lax.fori_loop(0, local_heads, attend, turn)
        branch_sum.step(turn, branch_part(branch_sum.member_of(turn)), True)
        return carry

    lax.fori_loop(0, group_size, attend_turn, 0)
    passed = gather_upper.rows(links.half_mate)
    sends.open.append(
        sends.copy(gather_upper.slots[2], passed, passed, links.to_member(links.core_mate))
    )
    keep(7, mixed, mixed_out)
    branch_sum.note(True)
    gather_upper.await_core()
    gather_upper.await_far()
    keep(8, upper, upper_out)
    for index in range(links.depth - 1):
        relay(2, index)
    branch_sum.await_cross()

    def second_norm(index, carry):
        rows = aligned(index, chunk)
        to = pl.ds(pl.multiple_of(own_rows + index * chunk, chunk), chunk)
        branch = branch_sum.rows(rows) + mod_row[5:6, 0:width]
        branch_out[rows, :] = branch
        middle = tokens[rows, :].astype(float_type) + mod_out[2:3, :] * branch
        middle_out[rows, :] = middle
        two[to, :] = (normed_rows(middle)[0] * (1.0 + mod_out[4:5, :]) + mod_out[3:4, :]).astype(
            brain_type
        )
        return carry

    lax.fori_loop(0, chunks, second_norm, 0)
    gather_two.start_half()
    gather_two.start_core()
    gather_two.pass_on()
    kept_one.wait()
    for shift in range(links.depth):
        side_arrived(1, shift)
    keep(9, weights.at[1], expand_out)
    gather_two.await_core()
    gather_two.await_far()
    keep(10, two, two_out)
    kept_two.wait()
    for shift in range(links.depth):
        side_arrived(2, shift)
    keep(11, weights.at[2], reduce_out)
    for made in opened:
        made.wait()
    for block in range(3):
        finish_weights(block)
    sends.finish()


def run_forward(
    sizes, tokens, upstream, conditions, segments, cond_weight, bias_vector, lengths, weights
):
    fsdp_size, group_size, quarter, width, own_width, shard = sizes
    row_length = quarter * group_size
    local_heads = own_width // HEAD_DIM
    span = local_heads * HEAD_PAD
    hidden = weights[2].shape[1]
    in_vmem = pl.BlockSpec(memory_space=pltpu.VMEM)
    anywhere = pl.BlockSpec(memory_space=pl.ANY)
    shape = jax.ShapeDtypeStruct
    out_shape = (
        shape((8, width), float_type),
        shape((8, 6 * own_width), float_type),
        shape((row_length, width), brain_type),
        shape((row_length, 3 * span), brain_type),
        shape((local_heads, 8, row_length), float_type),
        shape((row_length, span), brain_type),
        shape((quarter, width), float_type),
        shape((quarter, width), float_type),
        shape((row_length, width), brain_type),
        shape((row_length, width), brain_type),
        shape((width, 3 * span), brain_type),
        shape((width, span), brain_type),
        shape((width, hidden), brain_type),
        shape((width, hidden), brain_type),
        shape((fsdp_size, 8, shard), float_type),
    )
    out_specs = (
        in_vmem,
        in_vmem,
        anywhere,
        anywhere,
        in_vmem,
        anywhere,
        in_vmem,
        in_vmem,
        anywhere,
        anywhere,
        anywhere,
        anywhere,
        anywhere,
        anywhere,
        in_vmem,
    )
    copies = 2 * fsdp_size + group_size + 6 * (fsdp_size // 2) + 3 * 3 + 6
    vmem = pltpu.VMEM
    scratch = [
        vmem((fsdp_size, 8, shard), float_type),
        vmem((8, 6 * own_width), float_type),
        vmem((shard, 4 * own_width), brain_type),
        vmem((fsdp_size, 8, shard), float_type),
        vmem((fsdp_size, 8, 6 * own_width), float_type),
        vmem((fsdp_size, 8, 6 * own_width), float_type),
        vmem((8, 6 * own_width), float_type),
        vmem((group_size, 8, 6 * own_width), float_type),
        vmem((3, width, hidden), brain_type),
        vmem((quarter, width), float_type),
        vmem((2, quarter, width), brain_type),
        vmem((2, quarter, width), brain_type),
        vmem((quarter, width), brain_type),
        vmem((quarter, width), brain_type),
        vmem((quarter, width), float_type),
        vmem((row_length, width), brain_type),
        vmem((row_length, width), brain_type),
        vmem((row_length, width), brain_type),
        vmem((row_length, 3 * span), brain_type),
        vmem((row_length, span), brain_type),
        vmem((width, 3 * span), brain_type),
        vmem((width, span), brain_type),
        pltpu.SemaphoreType.DMA((copies,)),
        pltpu.SemaphoreType.DMA((copies,)),
        pltpu.SemaphoreType.DMA((12,)),
    ]
    return pl.pallas_call(
        functools.partial(forward_kernel, sizes),
        out_shape=out_shape,
        in_specs=[in_vmem] * 6 + [pl.BlockSpec(memory_space=pltpu.SMEM)] + [in_vmem] * 4,
        out_specs=out_specs,
        scratch_shapes=scratch,
        compiler_params=pltpu.CompilerParams(
            collective_id=0, has_side_effects=True, vmem_limit_bytes=TOP_VMEM
        ),
        name="forward_row",
    )(tokens, upstream, conditions, segments, cond_weight, bias_vector, lengths, *weights)


class ShardSum:
    def __init__(self, links, sends, block, side_got, level_got, shard, first=None):
        self.links, self.sends, self.block = links, sends, block
        self.side_got, self.level_got, self.shard = side_got, level_got, shard
        if first is None:
            first = sends.used
            sends.used += 2 * links.depth
        self.first = first

    def order(self):
        return list(range(1, self.links.depth)) + [0]

    def rows(self, place):
        return aligned(place, self.shard)

    def side(self, shift):
        links = self.links
        level = links.level_at(shift)
        return self.sends.copy(
            self.first + shift,
            self.block.at[self.rows(level * 2 + 1 - links.side), :],
            self.side_got.at[shift],
            links.to_place(links.side_mate),
        )

    def start(self, note=True):
        for shift in self.order():
            self.side(shift).start()
        if note:
            self.note_sides()

    def note_sides(self):
        self.sends.open += [self.side(shift) for shift in self.order()]

    def fold(self, shift, note=True):
        links = self.links
        self.sends.arrived(
            self.first + shift, self.side_got.at[shift], links.to_place(links.side_mate)
        )
        if shift:
            target = links.level_at(shift) * 2 + links.side
            rows = self.rows(target)
            self.block[rows, :] = (
                self.block[rows, :].astype(float_type) + self.side_got[shift].astype(float_type)
            ).astype(brain_type)
            self.push(shift).start()
            if note:
                self.sends.open.append(self.push(shift))

    def push(self, shift):
        links = self.links
        target = links.level_at(shift) * 2 + links.side
        return self.sends.copy(
            self.first + links.depth + shift,
            self.block.at[self.rows(target), :],
            self.level_got.at[shift],
            links.to_place(target),
        )

    def total(self):
        links = self.links
        summed = self.block[self.rows(links.place), :].astype(float_type) + self.side_got[0].astype(
            float_type
        )
        for shift in range(1, links.depth):
            source = links.level_at(-shift) * 2 + links.side
            self.sends.arrived(
                self.first + links.depth + shift, self.level_got.at[shift], links.to_place(source)
            )
            summed = summed + self.level_got[shift].astype(float_type)
        return summed


def fold_rows(values):
    count, width = values.shape
    return jnp.sum(values.reshape(count // 8, 8, width), axis=0)


def gelu_pair(values):
    root = math.sqrt(2.0 / math.pi)
    square = values * values
    bend = jnp.tanh(values * (root + root * 0.044715 * square))
    half = 0.5 * (1.0 + bend)
    slope = half + (0.5 * values) * (1.0 - bend * bend) * (root + root * 3 * 0.044715 * square)
    return values * half, slope


def across_rows(left, right):
    return lax.dot_general(left, right, (((0,), (0,)), ((), ())), preferred_element_type=float_type)


def middle_kernel(
    sizes,
    two,
    upper,
    expand,
    reduce,
    mods,
    biases,
    middle,
    branch,
    upstream,
    attend_pad,
    mixed,
    far_out,
    near_out,
    grads_out,
    attend_out,
    late_out,
    expand_out,
    reduce_out,
    slope_out,
    sums_out,
    active,
    inner_grad,
    lent_t,
    got_t,
    crossing_t,
    crossed_t,
    total_t,
    lent_o,
    got_o,
    branch_whole,
    pair_blocks,
    side_got,
    level_got,
    last_block,
    side_last,
    level_last,
    sums,
    send_sems,
    recv_sems,
):
    fsdp_size, group_size, quarter, width, own_width, shard = sizes
    links = Links(fsdp_size, group_size)
    sends = Sends(send_sems, recv_sems)
    local_heads = own_width // HEAD_DIM
    chunk = 32
    chunks = quarter // chunk
    two_sum = GroupSum(links, sends, lent_t, got_t, crossing_t, crossed_t, total_t)
    outer_sum = GroupSum(links, sends, lent_o, got_o, far_out, None, near_out)
    gather = GroupGather(links, sends, branch_whole, quarter)
    hidden = expand.shape[1]
    part = 384
    first_slot = sends.used
    pairs = hidden // part - 1
    sends.used += 2 * links.depth * pairs

    def pair_sum(index):
        return ShardSum(
            links,
            sends,
            pair_blocks.at[index],
            side_got.at[index],
            level_got.at[index],
            shard,
            first_slot + 2 * links.depth * index,
        )

    pair_totals = [pair_sum(index) for index in range(pairs)]
    pair_totals.append(ShardSum(links, sends, last_block, side_last, level_last, shard))
    links.meet()
    sums[...] = jnp.zeros_like(sums)

    def feed_part(picked, reduce_target, expand_target):
        def feed_rows(step, carry):
            rows = aligned(step, quarter)
            inner = (
                jnp.dot(two[rows, :], expand[:, picked], preferred_element_type=float_type)
                + biases[4:5, picked]
            )
            active_grad = jnp.dot(
                upper[rows, :], reduce[:, picked], preferred_element_type=float_type
            )
            value, slope = gelu_pair(inner)
            active[rows, picked] = value.astype(brain_type)
            low = (active_grad * slope).astype(brain_type)
            inner_grad[rows, picked] = low
            sums[4, :, picked] = sums[4, :, picked] + fold_rows(low.astype(float_type))
            return carry

        lax.fori_loop(0, group_size, feed_rows, 0)

        def grad_rows(step, carry):
            rows = aligned(step, part)
            reduce_target[rows, :] = across_rows(upper[:, rows], active[:, picked]).astype(
                brain_type
            )
            expand_target[rows, :] = across_rows(two[:, rows], inner_grad[:, picked]).astype(
                brain_type
            )
            return carry

        lax.fori_loop(0, width // part, grad_rows, 0)

    def feed(index, carry):
        feed_part(
            aligned(index, part),
            pair_blocks.at[index, :, 0:part],
            pair_blocks.at[index, :, part : 2 * part],
        )
        pair_sum(index).start(False)
        return carry

    lax.fori_loop(0, pairs, feed, 0)
    for item in pair_totals[:-1]:
        item.note_sides()
    pair_totals[0].fold(1)
    pair_totals[0].fold(2)
    feed_part(pl.ds(pairs * part, part), last_block, late_out)
    pair_totals[2].start()
    pair_totals[0].fold(3)

    def give(step, carry):
        rows = aligned(two_sum.member_of(step), quarter)
        two_sum.step(step, against(inner_grad[rows, :], expand[...]), True)
        outer_sum.step(step, against(active[rows, :], reduce[...]), False)

        @pl.when(step == 1)
        def _():
            pair_totals[0].fold(0)

        @pl.when(step == group_size - 1)
        def _():
            pair_totals[1].fold(1, False)

        return carry

    lax.fori_loop(0, group_size, give, 0)
    sends.open.append(pair_totals[1].push(1))
    two_sum.note(True)
    outer_sum.note(False)

    def near_rows(index, carry):
        rows = aligned(index, chunk)
        near_out[rows, :] = near_out[rows, :] + got_o[1, rows, :].astype(float_type)
        return carry

    lax.fori_loop(0, chunks, near_rows, 0)

    for shift in (2, 3):
        pair_totals[1].fold(shift)
    two_sum.await_cross()
    own_rows = links.member * quarter

    def second_back(index, carry):
        rows = aligned(index, chunk)
        to = pl.ds(pl.multiple_of(own_rows + index * chunk, chunk), chunk)
        two_grad = two_sum.rows(rows)
        normed, root = normed_rows(middle[rows, :])
        scaled = two_grad * (1.0 + mods[4:5, :])
        centered = (
            scaled
            - jnp.mean(scaled, axis=-1, keepdims=True)
            - normed * jnp.mean(scaled * normed, axis=-1, keepdims=True)
        )
        slope = upstream[rows, :].astype(float_type) + root * centered
        slope_out[rows, :] = slope
        low = (mods[2:3, :] * slope).astype(brain_type)
        branch_whole[to, :] = low
        sums[0] = sums[0] + fold_rows(slope * branch[rows, :])
        sums[1] = sums[1] + fold_rows(two_grad)
        sums[2] = sums[2] + fold_rows(two_grad * normed)
        sums[3] = sums[3] + fold_rows(low.astype(float_type))
        sums[5] = sums[5] + fold_rows(upper[to, :].astype(float_type))
        return carry

    lax.fori_loop(0, chunks, second_back, 0)
    gather.start_half()
    gather.start_core()

    for index in range(6):
        sums_out[index : index + 1, :] = jnp.sum(sums[index], axis=0, keepdims=True)
    sums_out[6:8, :] = jnp.zeros((2, width), float_type)
    pair_totals[1].fold(0)
    pair_totals[2].fold(1)
    pair_totals[2].fold(2)
    gather.pass_on()
    pair_totals[2].fold(3)
    gather.await_core()
    gather.await_far()

    def head_grads(index, carry):
        rows = aligned(index, quarter)
        grads_out[rows, :] = jnp.dot(
            branch_whole[rows, :], attend_pad[...], preferred_element_type=float_type
        ).astype(brain_type)
        return carry

    lax.fori_loop(0, group_size, head_grads, 0)

    def attend_part(index, carry):
        columns = aligned(index, part)
        value = across_rows(branch_whole[:, columns], mixed[...])
        for head in range(local_heads):
            attend_out[columns, head * HEAD_DIM : (head + 1) * HEAD_DIM] = value[
                :, head * HEAD_PAD : head * HEAD_PAD + HEAD_DIM
            ].astype(brain_type)
        return carry

    lax.fori_loop(0, width // part, attend_part, 0)
    pair_totals[2].fold(0)
    for index, item in enumerate(pair_totals[:-1]):
        pair = item.total()
        reduce_out[:, index * part : (index + 1) * part] = pair[:, 0:part]
        expand_out[:, index * part : (index + 1) * part] = pair[:, part:]
    reduce_out[:, pairs * part :] = pair_totals[-1].total()
    sends.finish()


def run_middle(sizes, *arrays):
    fsdp_size, group_size, quarter, width, own_width, shard = sizes
    row_length = quarter * group_size
    span = own_width // HEAD_DIM * HEAD_PAD
    hidden = arrays[2].shape[1]
    depth = fsdp_size // 2
    in_vmem = pl.BlockSpec(memory_space=pltpu.VMEM)
    shape = jax.ShapeDtypeStruct
    vmem = pltpu.VMEM
    copies = 3 + 3 + 3 + 2 * depth * (hidden // 384)
    return pl.pallas_call(
        functools.partial(middle_kernel, sizes),
        out_shape=(
            shape((quarter, width), brain_type),
            shape((quarter, width), float_type),
            shape((row_length, span), brain_type),
            shape((width, own_width), brain_type),
            shape((width, 384), brain_type),
            shape((shard, hidden - 384), float_type),
            shape((shard, hidden), float_type),
            shape((quarter, width), float_type),
            shape((8, width), float_type),
        ),
        in_specs=[in_vmem] * len(arrays),
        out_specs=(in_vmem,) * 9,
        scratch_shapes=[
            vmem((row_length, hidden), brain_type),
            vmem((row_length, hidden), brain_type),
            vmem((2, quarter, width), brain_type),
            vmem((2, quarter, width), brain_type),
            vmem((quarter, width), brain_type),
            vmem((quarter, width), brain_type),
            vmem((quarter, width), float_type),
            vmem((2, quarter, width), brain_type),
            vmem((2, quarter, width), brain_type),
            vmem((row_length, width), brain_type),
            vmem((hidden // 384 - 1, width, 768), brain_type),
            vmem((hidden // 384 - 1, depth, shard, 768), brain_type),
            vmem((hidden // 384 - 1, depth, shard, 768), brain_type),
            vmem((width, 384), brain_type),
            vmem((depth, shard, 384), brain_type),
            vmem((depth, shard, 384), brain_type),
            vmem((6, 8, width), float_type),
            pltpu.SemaphoreType.DMA((copies,)),
            pltpu.SemaphoreType.DMA((copies,)),
        ],
        compiler_params=pltpu.CompilerParams(
            collective_id=1, has_side_effects=True, vmem_limit_bytes=TOP_VMEM
        ),
        name="middle_row",
    )(*arrays)


def backward_kernel(
    sizes,
    hidden,
    heads,
    logs,
    head_grads,
    mixed,
    one,
    input_pad,
    tokens,
    mods,
    biases,
    slope,
    upstream,
    middle,
    far_sum,
    near_sum,
    late_grad,
    expand_part,
    attend_grad,
    sums_in,
    cond_weight,
    act_all,
    conditions,
    segments,
    lengths,
    output_out,
    token_out,
    act_out,
    cond_out,
    bias_final,
    expand_out,
    input_out,
    attend_out,
    crossed_o,
    joined,
    query_sum,
    delta_rows,
    lent,
    got,
    crossing,
    crossed,
    total,
    attend_block,
    head_blocks,
    compact,
    side_zero,
    level_zero,
    side_heads,
    level_heads,
    sums,
    slabs,
    slab_got,
    place_slab,
    place_got,
    act_part,
    act_got,
    act_group,
    bias_row,
    bias_out,
    send_sems,
    recv_sems,
):
    fsdp_size, group_size, quarter, width, own_width, shard = sizes
    links = Links(fsdp_size, group_size)
    sends = Sends(send_sems, recv_sems)
    local_heads = own_width // HEAD_DIM
    span = local_heads * HEAD_PAD
    row_length = quarter * group_size
    chunk = 32
    chunks = quarter // chunk
    one_sum = GroupSum(links, sends, lent, got, crossing, crossed, total)
    attend_sum = ShardSum(links, sends, attend_block, side_zero, level_zero, shard)
    head_slot = sends.used
    sends.used += 2 * links.depth * local_heads

    def head_sum(head):
        return ShardSum(
            links,
            sends,
            head_blocks.at[head],
            side_heads.at[head],
            level_heads.at[head],
            shard,
            head_slot + 2 * links.depth * head,
        )

    head_sums = [head_sum(head) for head in range(local_heads)]
    outer_slot = sends.slot()
    slab_slots = [sends.slot() for _ in range(group_size)]
    place_slots = [sends.slot() for _ in range(fsdp_size)]
    part_slots = [sends.slot() for _ in range(fsdp_size)]
    row_slots = [sends.slot() for _ in range(group_size)]
    bias_slots = [sends.slot() for _ in range(group_size)]

    def to_places(slots, source_of, target):
        for shift in range(1, fsdp_size):
            place = lax.rem(links.place + shift, fsdp_size)
            sends.start(
                slots[shift], source_of(place), target.at[links.place], links.to_place(place)
            )

    def from_places(slots, target):
        for shift in range(1, fsdp_size):
            place = lax.rem(links.place + fsdp_size - shift, fsdp_size)
            sends.arrived(slots[shift], target.at[place], links.to_place(place))

    def to_members(slots, source_of, target):
        for shift in range(1, group_size):
            member = lax.rem(links.member + shift, group_size)
            sends.start(
                slots[shift], source_of(member), target.at[links.member], links.to_member(member)
            )

    def from_members(slots, target):
        for shift in range(1, group_size):
            member = lax.rem(links.member + group_size - shift, group_size)
            sends.arrived(slots[shift], target.at[member], links.to_member(member))

    links.meet()
    sends.start(outer_slot, far_sum, crossed_o, links.to_member(links.half_mate))
    sums[...] = jnp.zeros_like(sums)
    late = late_grad.shape[1]
    attend_block[:, 0:late] = late_grad[...]
    attend_block[:, late + own_width :] = jnp.zeros_like(attend_block[:, late + own_width :])
    attend_block[:, late : late + own_width] = attend_grad[...]
    attend_sum.start()
    compact[...] = jnp.zeros_like(compact)

    power_scale = math.log2(math.e) / math.sqrt(HEAD_DIM)
    score_scale = 1.0 / math.sqrt(HEAD_DIM)

    def columns(base, head):
        return aligned(base * local_heads + head, HEAD_PAD)

    def head_deltas(head, carry):
        product = head_grads[:, columns(0, head)].astype(float_type) * mixed[
            :, columns(0, head)
        ].astype(float_type)
        delta = jnp.sum(product, axis=1, keepdims=True)
        turned = jnp.transpose(jnp.broadcast_to(delta, (row_length, HEAD_PAD)))
        delta_rows[head] = turned[0:8, :]
        return carry

    lax.fori_loop(0, local_heads, head_deltas, 0)

    def attend_back(part, head):
        rows = aligned(part, quarter)
        query = heads[:, columns(0, head)]
        key = heads[rows, columns(1, head)]
        value = heads[rows, columns(2, head)]
        grad = head_grads[:, columns(0, head)]
        shift = jnp.concatenate(
            [
                pair_mask(lengths, part * quarter, other * quarter)
                - logs[head, 0:1, other * quarter : (other + 1) * quarter]
                for other in range(group_size)
            ],
            axis=1,
        )
        probable = jnp.exp2(against(key, query) * power_scale + shift)
        value_grad = jnp.dot(probable.astype(brain_type), grad, preferred_element_type=float_type)
        score_grad = (probable * (against(value, grad) - delta_rows[head, 0:1, :])).astype(
            brain_type
        )
        key_grad = jnp.dot(score_grad, query, preferred_element_type=float_type)
        joined[rows, columns(1, head)] = (key_grad * score_scale).astype(brain_type)
        joined[rows, columns(2, head)] = value_grad.astype(brain_type)
        query_grad = across_rows(score_grad, key)

        @pl.when(part == 0)
        def _():
            query_sum[...] = query_grad

        @pl.when(part > 0)
        def _():
            query_sum[...] = query_sum[...] + query_grad

        @pl.when(part == group_size - 1)
        def _():
            joined[:, columns(0, head)] = (query_sum[...] * score_scale).astype(brain_type)

        step = head * group_size + part
        for shift, at in ((1, 3), (2, 5), (3, 8)):

            @pl.when(step == at)
            def _():
                attend_sum.fold(shift, False)

        for shift in range(1, links.depth):

            @pl.when((part == shift) & (head > 2))
            def _():
                head_sum(head - 3).fold(shift, False)

        return head

    block_rows = 384

    def head_back(head, carry):
        lax.fori_loop(0, group_size, attend_back, head)
        for base in range(3):
            compact[:, base * HEAD_DIM : (base + 1) * HEAD_DIM] = joined[:, columns(base, head)][
                :, 0:HEAD_DIM
            ]

        def input_part(index, inner):
            picked = aligned(index, block_rows)
            head_blocks[head, picked, :] = across_rows(one[:, picked], compact[...]).astype(
                brain_type
            )
            return inner

        lax.fori_loop(0, width // block_rows, input_part, 0)
        head_sum(head).start(False)
        return carry

    lax.fori_loop(0, local_heads, head_back, 0)
    for item in head_sums:
        item.note_sides()
    for item in [attend_sum] + head_sums:
        for shift in range(1, links.depth):
            sends.open.append(item.push(shift))

    def one_step(step, carry):
        rows = aligned(one_sum.member_of(step), quarter)
        one_sum.step(step, against(joined[rows, :], input_pad[...]), True)
        for shift in range(1, links.depth):

            @pl.when(step == shift)
            def _():
                head_sums[1].fold(shift, False)

        return carry

    lax.fori_loop(0, group_size, one_step, 0)
    one_sum.note(True)
    for shift in range(1, links.depth):
        head_sums[2].fold(shift, False)

    sends.arrived(outer_slot, crossed_o, links.to_member(links.half_mate))

    def finish_rows(index, carry):
        rows = aligned(index, chunk)
        outer = (
            near_sum[rows, :] + crossed_o[rows, :].astype(float_type) + biases[6:7, 0:width]
        )
        output_out[rows, :] = (middle[rows, :] + mods[5:6, :] * outer).astype(brain_type)
        sums[2] = sums[2] + fold_rows(upstream[rows, :].astype(float_type) * outer)
        return carry

    lax.fori_loop(0, chunks, finish_rows, 0)

    def pair_sums(index, carry):
        rows = aligned(index, 128)
        sums[3, :, 0:span] = sums[3, :, 0:span] + fold_rows(
            joined[rows, 0:span].astype(float_type)
        )
        sums[4, :, 0:span] = sums[4, :, 0:span] + fold_rows(
            joined[rows, 2 * span : 3 * span].astype(float_type)
        )
        return carry

    lax.fori_loop(0, row_length // 128, pair_sums, 0)
    for shift in range(1, links.depth):
        head_sums[3].fold(shift, False)
    one_sum.await_cross()

    def first_back(index, carry):
        rows = aligned(index, chunk)
        one_grad = one_sum.rows(rows)
        normed, root = normed_rows(tokens[rows, :].astype(float_type))
        scaled = one_grad * (1.0 + mods[1:2, :])
        centered = (
            scaled
            - jnp.mean(scaled, axis=-1, keepdims=True)
            - normed * jnp.mean(scaled * normed, axis=-1, keepdims=True)
        )
        token_out[rows, :] = slope[rows, :] + root * centered
        sums[0] = sums[0] + fold_rows(one_grad)
        sums[1] = sums[1] + fold_rows(one_grad * normed)
        return carry

    lax.fori_loop(0, chunks, first_back, 0)

    def summed(index):
        return jnp.sum(sums[index], axis=0, keepdims=True)

    six = (
        summed(0),
        summed(1),
        sums_in[0:1, :],
        sums_in[1:2, :],
        sums_in[2:3, :],
        summed(2),
    )
    slabs[...] = jnp.zeros_like(slabs)
    slots = slot_column(segments)[0:4, 0:1]
    for member in range(group_size):
        low, high = member * own_width, (member + 1) * own_width
        for index in range(6):
            to = slice(index * own_width, (index + 1) * own_width)
            slabs[member, 0:4, to] = slots * six[index][:, low:high]
        slabs[member, 4:5, 0:own_width] = sums_in[3:4, low:high]
        slabs[member, 5:6, 0:own_width] = sums_in[5:6, low:high]
    to_members(slab_slots, lambda member: slabs.at[member], slab_got)
    slab_got[pl.ds(links.member, 1)] = slabs[pl.ds(links.member, 1)]
    from_members(slab_slots, slab_got)
    row = slab_got[0]
    for member in range(1, group_size):
        row = row + slab_got[member]
    place_slab[...] = row
    place_slab[0:4, :] = row[0:4, :].astype(brain_type).astype(float_type)
    place_slab[6:7, 0:width] = sums_in[4:5, :]
    place_slab[7:8, 0:span] = summed(3)[:, 0:span]
    place_slab[7:8, span : 2 * span] = summed(4)[:, 0:span]
    to_places(place_slots, lambda place: place_slab, place_got)
    place_got[pl.ds(links.place, 1)] = place_slab[...][None]
    from_places(place_slots, place_got)
    low_rows = place_got[...].reshape(fsdp_size * 8, 6 * own_width).astype(brain_type)
    parts = [low_rows[:, index * own_width : (index + 1) * own_width] for index in range(6)]
    act_part[...] = sum(
        against(values, cond_weight[index]) for index, values in enumerate(parts)
    ).reshape(fsdp_size, 8, shard)
    to_places(part_slots, lambda place: act_part.at[place], act_got)
    act_got[pl.ds(links.place, 1)] = act_part[pl.ds(links.place, 1)]
    bias_sum = place_got[0]
    for place in range(1, fsdp_size):
        bias_sum = bias_sum + place_got[place]
    bias_row[...] = bias_sum
    bias_row[0:1, :] = jnp.sum(bias_sum[0:4, :], axis=0, keepdims=True)
    to_members(bias_slots, lambda member: bias_row, bias_out)
    bias_out[pl.ds(links.member, 1)] = bias_row[...][None]
    activated = act_all[...].reshape(fsdp_size * 8, shard).astype(brain_type)
    for index, values in enumerate(parts):
        cond_out[index] = across_rows(activated, values)
    from_places(part_slots, act_got)
    to_members(row_slots, lambda member: act_got, act_group)
    act_group[pl.ds(links.member, 1)] = act_got[...][None]
    from_members(row_slots, act_group)
    from_members(bias_slots, bias_out)
    act_sum = act_group[0]
    for member in range(1, group_size):
        act_sum = act_sum + act_group[member]
    raw = conditions[...].astype(float_type)
    gate = 1.0 / (1.0 + jnp.exp(-raw))
    slope_silu = gate * (1.0 + raw * (1.0 - gate))
    for place in range(fsdp_size):
        to = slice(place * shard, (place + 1) * shard)
        act_out[:, to] = act_sum[place, 0:4, :] * slope_silu[:, to]
    sizes_all = bias_sizes(fsdp_size, width, hidden * group_size)
    owned_biases(links, bias_out, bias_final, own_width, sizes_all, bias_starts(sizes_all))
    for item in [attend_sum] + head_sums:
        item.fold(0)
    joint = attend_sum.total()
    expand_out[:, 0 : hidden - late] = expand_part[...]
    expand_out[:, hidden - late :] = joint[:, 0:late]
    attend_out[...] = joint[:, late : late + own_width]
    for head, item in enumerate(head_sums):
        joint = item.total()
        for index in range(3):
            input_out[index, :, head * HEAD_DIM : (head + 1) * HEAD_DIM] = joint[
                :, index * HEAD_DIM : (index + 1) * HEAD_DIM
            ]
    sends.finish()


def bias_starts(sizes):
    starts = [0]
    for size in sizes:
        starts.append(starts[-1] + (size + HEAD_PAD - 1) // HEAD_PAD * HEAD_PAD)
    return starts


def run_backward(sizes, hidden, *arrays):
    fsdp_size, group_size, quarter, width, own_width, shard = sizes
    row_length = quarter * group_size
    local_heads = own_width // HEAD_DIM
    span = local_heads * HEAD_PAD
    depth = fsdp_size // 2
    six = 6 * own_width
    in_vmem = pl.BlockSpec(memory_space=pltpu.VMEM)
    shape = jax.ShapeDtypeStruct
    vmem = pltpu.VMEM
    copies = 3 + 4 * depth + 1 + 2 * fsdp_size + 3 * group_size + 2 * depth * local_heads
    head_span = (3 * HEAD_DIM + HEAD_PAD - 1) // HEAD_PAD * HEAD_PAD
    attend_span = (own_width + 384 + HEAD_PAD - 1) // HEAD_PAD * HEAD_PAD
    bias_span = bias_starts(bias_sizes(fsdp_size, width, hidden * group_size))[-1]
    in_specs = [in_vmem] * len(arrays)
    in_specs[-1] = pl.BlockSpec(memory_space=pltpu.SMEM)
    return pl.pallas_call(
        functools.partial(backward_kernel, sizes, hidden),
        out_shape=(
            shape((quarter, width), brain_type),
            shape((quarter, width), float_type),
            shape((4, width), float_type),
            shape((6, shard, own_width), float_type),
            shape((1, bias_span), float_type),
            shape((shard, hidden), float_type),
            shape((3, shard, own_width), float_type),
            shape((shard, own_width), float_type),
        ),
        in_specs=in_specs,
        out_specs=(in_vmem,) * 8,
        scratch_shapes=[
            vmem((quarter, width), brain_type),
            vmem((row_length, 3 * span), brain_type),
            vmem((row_length, HEAD_PAD), float_type),
            vmem((local_heads, 8, row_length), float_type),
            vmem((2, quarter, width), brain_type),
            vmem((2, quarter, width), brain_type),
            vmem((quarter, width), brain_type),
            vmem((quarter, width), brain_type),
            vmem((quarter, width), float_type),
            vmem((width, attend_span), brain_type),
            vmem((local_heads, width, head_span), brain_type),
            vmem((row_length, head_span), brain_type),
            vmem((depth, shard, attend_span), brain_type),
            vmem((depth, shard, attend_span), brain_type),
            vmem((local_heads, depth, shard, head_span), brain_type),
            vmem((local_heads, depth, shard, head_span), brain_type),
            vmem((5, 8, width), float_type),
            vmem((group_size, 8, six), float_type),
            vmem((group_size, 8, six), float_type),
            vmem((8, six), float_type),
            vmem((fsdp_size, 8, six), float_type),
            vmem((fsdp_size, 8, shard), float_type),
            vmem((fsdp_size, 8, shard), float_type),
            vmem((group_size, fsdp_size, 8, shard), float_type),
            vmem((8, six), float_type),
            vmem((group_size, 8, six), float_type),
            pltpu.SemaphoreType.DMA((copies,)),
            pltpu.SemaphoreType.DMA((copies,)),
        ],
        compiler_params=pltpu.CompilerParams(
            collective_id=2, has_side_effects=True, vmem_limit_bytes=TOP_VMEM
        ),
        name="backward_row",
    )(*arrays)


def deliver_kernel(sizes, count, bias_row, *refs):
    sources, targets = refs[:count], refs[count : 2 * count]
    shares = refs[2 * count : 2 * count + len(sizes)]
    buffers = refs[2 * count + len(sizes) : 3 * count + len(sizes)]
    sems = refs[-1]

    def taken(index):
        return pltpu.make_async_copy(sources[index], buffers[index], sems.at[index])

    def given(index):
        return pltpu.make_async_copy(buffers[index], targets[index], sems.at[count + index])

    for index in range(count):
        taken(index).start()
    for start, size, share in zip(bias_starts(sizes), sizes, shares):
        share[...] = bias_row[0, start : start + size]
    for index in range(count):
        taken(index).wait()
        given(index).start()
    for index in range(count):
        given(index).wait()


def deliver(bias_row, sizes, *arrays):
    count = len(arrays)
    in_vmem = pl.BlockSpec(memory_space=pltpu.VMEM)
    anywhere = pl.BlockSpec(memory_space=pl.ANY)
    shape = jax.ShapeDtypeStruct
    return pl.pallas_call(
        functools.partial(deliver_kernel, sizes, count),
        out_shape=[shape(item.shape, item.dtype) for item in arrays]
        + [shape((size,), float_type) for size in sizes],
        in_specs=[in_vmem] + [anywhere] * count,
        out_specs=[anywhere] * count + [in_vmem] * len(sizes),
        scratch_shapes=[pltpu.VMEM(item.shape, item.dtype) for item in arrays]
        + [pltpu.SemaphoreType.DMA((2 * count,))],
        compiler_params=pltpu.CompilerParams(vmem_limit_bytes=TOP_VMEM),
        name="deliver_row",
    )(bias_row, *arrays)


def fast_local(
    tokens,
    conditions,
    lengths,
    segments,
    condition_weight,
    condition_bias,
    input_weight,
    input_bias,
    attend_weight,
    attend_bias,
    expand_weight,
    expand_bias,
    reduce_weight,
    reduce_bias,
    cotangent,
):
    _, quarter, width = tokens.shape
    group_size, fsdp_size = lax.axis_size("rep"), lax.axis_size("fsdp")
    shard, _, own_width = condition_weight.shape
    hidden = expand_weight.shape[1]
    sizes = (fsdp_size, group_size, quarter, width, own_width, shard)
    biases = (condition_bias, input_bias, attend_bias, expand_bias, reduce_bias)
    bias_total = sum(item.shape[0] for item in biases)
    bias_end = (bias_total + 1023) // 1024 * 1024
    bias_vector, start = 0.0, 0
    for item in biases:
        end = start + item.shape[0]
        bias_vector = bias_vector + jnp.pad(item.astype(float_type), (start, bias_end - end))
        start = end
    bias_vector = bias_vector[None]
    cond_blocks = condition_weight.transpose(1, 0, 2)
    condition_rows = conditions[0]
    token_rows = tokens.reshape(quarter, width)
    upstream = cotangent.reshape(quarter, width)
    (
        mods,
        biases,
        one,
        heads,
        logs,
        mixed,
        branch,
        middle,
        two,
        upper,
        input_pad,
        attend_pad,
        expand_all,
        reduce_all,
        act_all,
    ) = run_forward(
        sizes,
        token_rows,
        upstream,
        condition_rows,
        segments,
        cond_blocks,
        bias_vector,
        lengths,
        (input_weight.transpose(1, 0, 2), attend_weight, expand_weight, reduce_weight),
    )
    (
        far_sum,
        near_sum,
        head_grads,
        attend_grad,
        late_grad,
        expand_part,
        reduce_final,
        slope,
        sums,
    ) = (
        run_middle(
            sizes,
            two,
            upper,
            expand_all,
            reduce_all,
            mods,
            biases,
            middle,
            branch,
            upstream,
            attend_pad,
            mixed,
        )
    )
    (
        output,
        token_grad,
        condition_grad,
        cond_grad,
        bias_final,
        expand_final,
        input_final,
        attend_final,
    ) = run_backward(
        sizes,
        hidden,
        heads,
        logs,
        head_grads,
        mixed,
        one,
        input_pad,
        token_rows,
        mods,
        biases,
        slope,
        upstream,
        middle,
        far_sum,
        near_sum,
        late_grad,
        expand_part,
        attend_grad,
        sums,
        cond_blocks,
        act_all,
        condition_rows,
        segments,
        lengths,
    )

    (
        output,
        token_grad,
        condition_grad,
        cond_grad,
        input_final,
        attend_final,
        expand_final,
        reduce_final,
        condition_bias_final,
        input_bias_final,
        attend_bias_final,
        expand_bias_final,
        reduce_bias_final,
    ) = deliver(
        bias_final,
        bias_sizes(fsdp_size, width, hidden * group_size),
        output,
        token_grad,
        condition_grad,
        cond_grad,
        input_final,
        attend_final,
        expand_final,
        reduce_final,
    )
    return (
        output[None],
        token_grad[None],
        condition_grad[None],
        cond_grad.transpose(1, 0, 2),
        condition_bias_final,
        input_final.transpose(1, 0, 2),
        input_bias_final,
        attend_final,
        attend_bias_final,
        expand_final,
        expand_bias_final,
        reduce_final,
        reduce_bias_final,
    )


def solution(mesh):
    in_specs = (
        P("fsdp", "rep", None),
        P("fsdp", None, None),
        P("fsdp", None),
        P("fsdp", "rep"),
        P("fsdp", None, "rep"),
        P("fsdp"),
        P("fsdp", None, "rep"),
        P("fsdp"),
        P("fsdp", "rep"),
        P("fsdp"),
        P("fsdp", "rep"),
        P("fsdp"),
        P("fsdp", "rep"),
        P("fsdp"),
        P("fsdp", "rep", None),
    )
    out_specs = (
        P("fsdp", "rep", None),
        P("fsdp", "rep", None),
        P("fsdp", None, None),
        P("fsdp", None, "rep"),
        P("fsdp"),
        P("fsdp", None, "rep"),
        P("fsdp"),
        P("fsdp", "rep"),
        P("fsdp"),
        P("fsdp", "rep"),
        P("fsdp"),
        P("fsdp", "rep"),
        P("fsdp"),
    )
    local = fast_local if mesh.shape["fsdp"] == 8 else plain_local
    return jax.shard_map(local, mesh=mesh, in_specs=in_specs, out_specs=out_specs, check_vma=False)
```

```python
import functools
import math

import jax
import jax.numpy as jnp
from jax import lax
from jax.experimental import pallas as pl
from jax.experimental.pallas import tpu as pltpu
from jax.sharding import PartitionSpec as P

HEAD_DIM = 72


epsilon = 1e-06
highest = lax.Precision.HIGHEST
float_type = jnp.float32
brain_type = jnp.bfloat16


def layer_normed(values):
    center = jnp.mean(values, axis=-1, keepdims=True)
    shifted = values - center
    spread = jnp.mean(shifted * shifted, axis=-1, keepdims=True)
    return shifted * lax.rsqrt(spread + epsilon)


def modulated(values, shift_term, scale_term):
    return layer_normed(values) * (1.0 + scale_term) + shift_term


def gelu_tanh(values):
    return jax.nn.gelu(values, approximate=True)


def image_index(row_ends, positions):
    return jnp.sum((positions[..., :, None] >= row_ends[..., None, :-1]).astype(jnp.int32), axis=-1)


def across(left, right):
    return lax.dot_general(left, right, (((0,), (0,)), ((), ())), preferred_element_type=float_type)


def against(left, right):
    return lax.dot_general(left, right, (((1,), (1,)), ((), ())), preferred_element_type=float_type)


def column_sums(values):
    return jnp.sum(values.astype(float_type), axis=0)


def spread_columns(own_part, total, start):
    empty = jnp.zeros(own_part.shape[:-1] + (total,), float_type)
    return lax.dynamic_update_slice_in_dim(empty, own_part, start, own_part.ndim - 1)


def gather_block(*weights):
    return tuple(lax.all_gather(item, "fsdp", axis=0, tiled=True) for item in weights)


def plain_local(
    tokens,
    conditions,
    lengths,
    segments,
    condition_weight,
    condition_bias,
    input_weight,
    input_bias,
    attend_weight,
    attend_bias,
    expand_weight,
    expand_bias,
    reduce_weight,
    reduce_bias,
    cotangent,
):
    row_count, quarter, model_width = tokens.shape
    slot_count = conditions.shape[1]
    group_size = lax.axis_size("rep")
    group_place = lax.axis_index("rep")
    row_length = quarter * group_size
    own_width = condition_weight.shape[2]
    column_start = group_place * own_width
    hidden_width = expand_weight.shape[1]
    hidden_start = group_place * hidden_width
    local_heads = own_width // HEAD_DIM
    score_scale = 1.0 / math.sqrt(HEAD_DIM)
    patch_count = row_count * quarter
    image_count = row_count * slot_count
    key_place = jnp.arange(row_length, dtype=jnp.int32)
    row_ends = jnp.cumsum(lengths, axis=1, dtype=jnp.int32)
    row_images = image_index(row_ends, key_place)
    allowed = row_images[:, :, None] == row_images[:, None, :]

    def whole_rows(values):
        joined_rows = lax.all_gather(
            values.reshape(row_count, quarter, -1), "rep", axis=1, tiled=True
        )
        return joined_rows.reshape(row_count * row_length, -1)

    def own_rows(values):
        summed = lax.psum_scatter(
            values.reshape(row_count, row_length, -1), "rep", scatter_dimension=1, tiled=True
        )
        return summed.reshape(patch_count, -1)

    fsdp_size = lax.axis_size("fsdp")
    fsdp_place = lax.axis_index("fsdp")
    own_depth = condition_weight.shape[0]
    condition_values = conditions.astype(float_type)
    activated_own = jax.nn.silu(condition_values).reshape(image_count, model_width).astype(brain_type)
    activated_all = lax.all_gather(activated_own, "fsdp", axis=0, tiled=True)
    activated = lax.dynamic_slice_in_dim(activated_all, fsdp_place * own_depth, own_depth, 1)
    local_biases = (condition_bias, input_bias, attend_bias, expand_bias, reduce_bias)
    share_sizes = [item.shape[0] for item in local_biases]
    bias_ends = [sum(share_sizes[:k]) for k in range(len(share_sizes) + 1)]
    bias_table = lax.all_gather(jnp.concatenate(local_biases), "fsdp", axis=0, tiled=False)
    condition_bias_all, input_bias_all, attend_bias_all, expand_bias_all, reduce_bias_all = [
        bias_table[:, low:high].reshape(-1) for low, high in zip(bias_ends[:-1], bias_ends[1:])
    ]
    condition_bias_own = lax.dynamic_slice_in_dim(
        condition_bias_all.reshape(6, model_width), column_start, own_width, 1
    )
    modulation_parts = jnp.einsum(
        "id,dkm->ikm", activated, condition_weight, preferred_element_type=float_type
    )
    modulation_own = (
        lax.psum_scatter(modulation_parts, "fsdp", scatter_dimension=0, tiled=True)
        + condition_bias_own[None]
    )
    modulation = lax.all_gather(modulation_own, "rep", axis=2, tiled=True).reshape(
        row_count, slot_count, -1
    )
    slot_table = (
        segments[:, :, None] == jnp.arange(slot_count, dtype=jnp.int32)[None, None, :]
    ).astype(float_type)
    per_token = jnp.einsum("rqs,rsm->rqm", slot_table, modulation, precision=highest).reshape(
        patch_count, -1
    )
    shift_one, scale_one, gate_one, shift_two, scale_two, gate_two = jnp.split(per_token, 6, axis=1)
    token_values = tokens.reshape(patch_count, model_width).astype(float_type)

    def split_heads(values):
        return values.reshape(row_count, row_length, local_heads, HEAD_DIM).transpose(2, 0, 1, 3)

    def merge_heads(values):
        return values.transpose(1, 2, 0, 3).reshape(row_count * row_length, own_width)

    def allowed_scores(query_head, key_head):
        scores = (
            jnp.einsum("rqd,rkd->rqk", query_head, key_head, preferred_element_type=float_type)
            * score_scale
        )
        return jnp.where(allowed, scores, -1e30)

    def head_forward(parts):
        query_head, key_head, value_head = parts
        scores = allowed_scores(query_head, key_head)
        row_max = jnp.max(scores, axis=-1, keepdims=True)
        powers = jnp.exp(scores - row_max)
        totals = jnp.sum(powers, axis=-1, keepdims=True)
        weights_low = (powers / totals).astype(brain_type)
        mixed = jnp.einsum(
            "rqk,rkd->rqd", weights_low, value_head, preferred_element_type=float_type
        )
        return (mixed, row_max + jnp.log(totals))

    def head_backward(parts):
        query_head, key_head, value_head, grad_head, log_head = parts
        scores = allowed_scores(query_head, key_head)
        probable = jnp.exp(scores - log_head)
        prob_grad = jnp.einsum(
            "rqd,rkd->rqk", grad_head, value_head, preferred_element_type=float_type
        )
        score_grad = (
            probable * (prob_grad - jnp.sum(probable * prob_grad, axis=-1, keepdims=True))
        ).astype(brain_type)
        query_part = (
            jnp.einsum("rqk,rkd->rqd", score_grad, key_head, preferred_element_type=float_type)
            * score_scale
        )
        key_part = (
            jnp.einsum("rqk,rqd->rkd", score_grad, query_head, preferred_element_type=float_type)
            * score_scale
        )
        value_part = jnp.einsum(
            "rqk,rqd->rkd",
            probable.astype(brain_type),
            grad_head,
            preferred_element_type=float_type,
        )
        return (query_part, key_part, value_part)

    def trunk(gathered):
        (
            input_all,
            input_bias_all,
            attend_all,
            attend_bias_all,
            expand_all,
            expand_bias_all,
            reduce_all,
            reduce_bias_all,
        ) = gathered
        bias_pair = lax.dynamic_slice_in_dim(
            input_bias_all.reshape(2, model_width), column_start, own_width, 1
        )
        expand_bias_own = lax.dynamic_slice_in_dim(expand_bias_all, hidden_start, hidden_width, 0)
        normed_one = modulated(token_values, shift_one, scale_one).astype(brain_type)
        whole_one = whole_rows(normed_one)
        joined = jnp.einsum("nd,dkm->nkm", whole_one, input_all, preferred_element_type=float_type)
        queries = (joined[:, 0] + bias_pair[0]).astype(brain_type)
        keys_row = joined[:, 1].astype(brain_type)
        values_row = (joined[:, 2] + bias_pair[1]).astype(brain_type)
        query_heads = split_heads(queries)
        key_heads = split_heads(keys_row)
        value_heads = split_heads(values_row)
        mixed, log_totals = lax.map(head_forward, (query_heads, key_heads, value_heads))
        attended = merge_heads(mixed).astype(brain_type)
        branch = own_rows(against(attended, attend_all)) + attend_bias_all
        middle = token_values + gate_one * branch
        normed_two = modulated(middle, shift_two, scale_two).astype(brain_type)
        whole_two = whole_rows(normed_two)
        inner = jnp.dot(whole_two, expand_all, preferred_element_type=float_type) + expand_bias_own
        active = gelu_tanh(inner).astype(brain_type)
        outer = own_rows(against(active, reduce_all)) + reduce_bias_all
        result = middle + gate_two * outer
        return (
            result,
            gathered,
            whole_one,
            query_heads,
            key_heads,
            value_heads,
            log_totals,
            attended,
            branch,
            middle,
            whole_two,
            inner,
            active,
            outer,
        )

    input_all, attend_all, expand_all, reduce_all = gather_block(
        input_weight, attend_weight, expand_weight, reduce_weight
    )
    state = trunk(
        (
            input_all,
            input_bias_all,
            attend_all,
            attend_bias_all,
            expand_all,
            expand_bias_all,
            reduce_all,
            reduce_bias_all,
        )
    )
    output = state[0].astype(brain_type).reshape(row_count, quarter, model_width)
    (
        _,
        gathered,
        whole_one,
        query_heads,
        key_heads,
        value_heads,
        log_totals,
        attended,
        branch,
        middle,
        whole_two,
        inner,
        active,
        outer,
    ) = state
    upstream = cotangent.reshape(patch_count, model_width).astype(float_type)
    outer_grad = (gate_two * upstream).astype(brain_type)
    gate_two_grad = upstream * outer
    outer_whole = whole_rows(outer_grad)
    reduce_grad = across(outer_whole, active)
    reduce_bias_grad = column_sums(outer_grad)
    active_grad = jnp.dot(outer_whole, reduce_all, preferred_element_type=float_type)
    _, gelu_back = jax.vjp(gelu_tanh, inner)
    inner_grad = gelu_back(active_grad)[0].astype(brain_type)
    expand_grad = across(whole_two, inner_grad)
    expand_bias_full = spread_columns(
        column_sums(inner_grad), hidden_width * group_size, hidden_start
    )
    two_grad = own_rows(against(inner_grad, expand_all))
    _, second_back = jax.vjp(modulated, middle, shift_two, scale_two)
    middle_norm_grad, shift_two_grad, scale_two_grad = second_back(two_grad)
    middle_grad = upstream + middle_norm_grad
    gate_one_grad = middle_grad * branch
    branch_grad = (gate_one * middle_grad).astype(brain_type)
    branch_whole = whole_rows(branch_grad)
    attend_grad = across(branch_whole, attended)
    attend_bias_grad = column_sums(branch_grad)
    attended_grad = jnp.dot(branch_whole, attend_all, preferred_element_type=float_type).astype(
        brain_type
    )
    grad_heads = split_heads(attended_grad)
    query_parts, key_parts, value_parts = lax.map(
        head_backward, (query_heads, key_heads, value_heads, grad_heads, log_totals)
    )
    query_low = merge_heads(query_parts).astype(brain_type)
    key_low = merge_heads(key_parts).astype(brain_type)
    value_low = merge_heads(value_parts).astype(brain_type)
    joined_grad = jnp.stack([query_low, key_low, value_low], axis=1)
    input_grad = jnp.einsum(
        "nd,nkm->dkm", whole_one, joined_grad, preferred_element_type=float_type
    )
    input_bias_pair = jnp.stack([column_sums(query_low), column_sums(value_low)])
    input_bias_full = spread_columns(input_bias_pair, model_width, column_start).reshape(-1)
    one_grad = own_rows(
        jnp.einsum("nkm,dkm->nd", joined_grad, input_all, preferred_element_type=float_type)
    )
    _, first_back = jax.vjp(modulated, token_values, shift_one, scale_one)
    token_norm_grad, shift_one_grad, scale_one_grad = first_back(one_grad)
    token_grad = (middle_grad + token_norm_grad).reshape(row_count, quarter, model_width)
    six_grads = jnp.stack(
        [
            shift_one_grad,
            scale_one_grad,
            gate_one_grad,
            shift_two_grad,
            scale_two_grad,
            gate_two_grad,
        ],
        axis=1,
    ).reshape(row_count, quarter, 6, model_width)
    modulation_part = jnp.einsum("rqs,rqkm->rskm", slot_table, six_grads, precision=highest)
    modulation_grad = lax.psum_scatter(modulation_part, "rep", scatter_dimension=3, tiled=True)
    modulation_low = lax.all_gather(
        modulation_grad.reshape(image_count, 6, own_width).astype(brain_type),
        "fsdp",
        axis=0,
        tiled=True,
    )
    condition_weight_final = jnp.einsum(
        "id,ikm->dkm", activated, modulation_low, preferred_element_type=float_type
    )
    condition_bias_full = lax.all_gather(
        column_sums(modulation_low), "rep", axis=1, tiled=True
    ).reshape(-1)
    bias_depth = condition_bias.shape[0]
    condition_bias_final = lax.dynamic_slice_in_dim(
        condition_bias_full, fsdp_place * bias_depth, bias_depth, 0
    )
    activated_part = jnp.einsum(
        "ikm,dkm->id", modulation_low, condition_weight, preferred_element_type=float_type
    )
    activated_wide = lax.all_to_all(
        activated_part.reshape(fsdp_size, image_count, own_depth), "fsdp", 0, 0
    )
    activated_row = jnp.transpose(activated_wide, (1, 0, 2)).reshape(image_count, model_width)
    bias_rows = jnp.concatenate(
        [
            item.reshape(fsdp_size, -1)
            for item in (input_bias_full, attend_bias_grad, expand_bias_full, reduce_bias_grad)
        ],
        axis=1,
    )
    bias_own = lax.psum_scatter(bias_rows, "fsdp", scatter_dimension=0, tiled=True).reshape(-1)
    activated_grad, bias_sum = lax.psum((activated_row, bias_own), "rep")
    input_bias_final, attend_bias_final, expand_bias_final, reduce_bias_final = jnp.split(
        bias_sum, [end - share_sizes[0] for end in bias_ends[2:-1]]
    )
    input_final, attend_final, expand_final, reduce_final = [
        lax.psum_scatter(item.astype(brain_type), "fsdp", scatter_dimension=0, tiled=True).astype(
            float_type
        )
        for item in (input_grad, attend_grad, expand_grad, reduce_grad)
    ]
    _, silu_back = jax.vjp(jax.nn.silu, condition_values)
    condition_grad = silu_back(activated_grad.reshape(row_count, slot_count, model_width))[0]
    return (
        output,
        token_grad,
        condition_grad,
        condition_weight_final,
        condition_bias_final,
        input_final,
        input_bias_final,
        attend_final,
        attend_bias_final,
        expand_final,
        expand_bias_final,
        reduce_final,
        reduce_bias_final,
    )


MESH = pl.DeviceIdType.MESH
HEAD_PAD = 128
TOP_VMEM = 60 * 1024 * 1024


def aligned(index, step):
    return pl.ds(pl.multiple_of(index * step, step), step)


class Links:
    def __init__(self, fsdp_size, group_size):
        self.fsdp_size = fsdp_size
        self.group_size = group_size
        self.depth = fsdp_size // 2
        self.place = lax.axis_index("fsdp")
        self.member = lax.axis_index("rep")
        self.level = self.place // 2
        self.side = self.place % 2
        self.core = self.member % 2
        self.half = self.member // 2

    def to_place(self, place):
        return (place, self.member)

    def to_member(self, member):
        return (self.place, member)

    @property
    def core_mate(self):
        return self.half * 2 + 1 - self.core

    @property
    def half_mate(self):
        return (1 - self.half) * 2 + self.core

    @property
    def far_mate(self):
        return (1 - self.half) * 2 + 1 - self.core

    @property
    def side_mate(self):
        return self.level * 2 + 1 - self.side

    def level_at(self, shift):
        return lax.rem(self.level + shift + self.depth, self.depth)

    def meet(self):
        self.await_all(self.greet())

    def await_all(self, count):
        pl.semaphore_wait(pltpu.get_barrier_semaphore(), count)

    def greet(self):
        barrier = pltpu.get_barrier_semaphore()
        count = 0
        for shift in range(1, self.fsdp_size):
            target = lax.rem(self.place + shift, self.fsdp_size)
            pl.semaphore_signal(barrier, inc=1, device_id=self.to_place(target), device_id_type=MESH)
            count += 1
        for shift in range(1, self.group_size):
            target = lax.rem(self.member + shift, self.group_size)
            pl.semaphore_signal(barrier, inc=1, device_id=self.to_member(target), device_id_type=MESH)
            count += 1
        return count


class Sends:
    def __init__(self, send_sems, recv_sems):
        self.send_sems = send_sems
        self.recv_sems = recv_sems
        self.used = 0
        self.open = []

    def slot(self):
        self.used += 1
        return self.used - 1

    def copy(self, slot, source, target, device):
        return pltpu.make_async_remote_copy(
            src_ref=source,
            dst_ref=target,
            send_sem=self.send_sems.at[slot],
            recv_sem=self.recv_sems.at[slot],
            device_id=device,
            device_id_type=MESH,
        )

    def start(self, slot, source, target, device):
        made = self.copy(slot, source, target, device)
        made.start()
        self.open.append(made)

    def arrived(self, slot, target, device):
        self.copy(slot, target, target, device).wait_recv()

    def finish(self):
        for made in self.open:
            made.wait_send()


class GroupGather:
    def __init__(self, links, sends, buffer, quarter):
        self.links, self.sends, self.buffer, self.quarter = links, sends, buffer, quarter
        self.slots = [sends.slot() for _ in range(3)]

    def rows(self, member):
        return self.buffer.at[aligned(member, self.quarter), :]

    def start_core(self):
        own = self.rows(self.links.member)
        mate = self.links.to_member(self.links.core_mate)
        self.sends.start(self.slots[0], own, own, mate)

    def start_half(self):
        own = self.rows(self.links.member)
        self.sends.start(self.slots[1], own, own, self.links.to_member(self.links.half_mate))

    def await_core(self):
        mate = self.links.core_mate
        self.sends.arrived(self.slots[0], self.rows(mate), self.links.to_member(mate))

    def pass_on(self):
        mate = self.links.half_mate
        self.sends.arrived(self.slots[1], self.rows(mate), self.links.to_member(mate))
        passed = self.rows(mate)
        self.sends.start(
            self.slots[2], passed, passed, self.links.to_member(self.links.core_mate)
        )

    def await_far(self):
        mate = self.links.core_mate
        self.sends.arrived(self.slots[2], self.rows(self.links.far_mate), self.links.to_member(mate))


class GroupSum:
    def __init__(self, links, sends, lent, got, crossing, crossed, total):
        self.links, self.sends = links, sends
        self.lent, self.got, self.crossing, self.crossed, self.total = (
            lent,
            got,
            crossing,
            crossed,
            total,
        )
        self.slots = [sends.slot() for _ in range(3)]

    def member_of(self, step):
        half = lax.rem(self.links.half + 1 - step // 2 + 2, 2)
        core = lax.rem(self.links.core + 1 - step % 2 + 2, 2)
        return half * 2 + core

    def lend(self, index):
        mate = self.links.to_member(self.links.core_mate)
        return self.sends.copy(
            self.slots[0] + index, self.lent.at[index], self.got.at[index], mate
        )

    def cross(self):
        mate = self.links.to_member(self.links.half_mate)
        return self.sends.copy(self.slots[2], self.crossing, self.crossed, mate)

    def step(self, step, value, crosses):
        index = step // 2
        self.total[...] = value

        @pl.when(step % 2 == 0)
        def _():
            self.lent[index] = self.total[...].astype(brain_type)
            self.lend(index).start()

        @pl.when(step % 2 == 1)
        def _():
            self.lend(index).wait_recv()

        @pl.when(step == 1)
        def _():
            self.crossing[...] = (self.total[...] + self.got[0].astype(float_type)).astype(
                brain_type
            )
            if crosses:
                self.cross().start()

    def note(self, crosses):
        self.sends.open += [self.lend(0), self.lend(1)]
        if crosses:
            self.sends.open.append(self.cross())

    def await_cross(self):
        self.sends.arrived(
            self.slots[2], self.crossed, self.links.to_member(self.links.half_mate)
        )

    def rows(self, rows):
        return (
            self.total[rows, :]
            + self.got[1, rows, :].astype(float_type)
            + self.crossed[rows, :].astype(float_type)
        )


def normed_rows(values):
    center = jnp.mean(values, axis=-1, keepdims=True)
    shifted = values - center
    spread = jnp.mean(shifted * shifted, axis=-1, keepdims=True)
    root = lax.rsqrt(spread + epsilon)
    return shifted * root, root


def spread_heads(source, target, rows, first, heads, target_first):
    for head in range(heads):
        low, to = HEAD_DIM * (first + head), HEAD_PAD * (target_first + head)
        target[rows, to : to + HEAD_DIM] = source[rows, low : low + HEAD_DIM]


def slot_column(segments):
    slots = lax.broadcasted_iota(jnp.int32, (8, HEAD_PAD), 0)
    return jnp.where(slots == segments[0:1, 0:HEAD_PAD], 1.0, 0.0)


def image_at(lengths, start):
    end, image = 0, 0
    for slot in range(lengths.shape[1] - 1):
        end = end + lengths[0, slot]
        image = image + jnp.where(start >= end, 1, 0)
    return image


def pair_mask(lengths, first, second):
    return jnp.where(image_at(lengths, first) == image_at(lengths, second), 0.0, -1e30)


def chosen(flag, values):
    return values * jnp.where(flag, 1.0, 0.0)


def bias_sizes(fsdp_size, width, hidden_total):
    return [size // fsdp_size for size in (6 * width, 2 * width, width, hidden_total, width)]


def own_biases(links, bias_vector, bias_table, own_width, sizes):
    place, member = links.place, links.member
    group_size = links.group_size
    starts = [sum(sizes[:index]) for index in range(6)]

    def piece(index, low, size):
        return bias_vector[0:1, starts[index] + low : starts[index] + low + size]

    bias_table[...] = jnp.zeros_like(bias_table)
    blocks = sizes[0] // own_width
    for kind in range(6):
        row = sum(
            chosen(
                place * blocks + index == kind * group_size + member,
                piece(0, index * own_width, own_width),
            )
            for index in range(blocks)
        )
        bias_table[0:4, kind * own_width : (kind + 1) * own_width] = jnp.broadcast_to(
            row, (4, own_width)
        )
    per_member = links.fsdp_size // group_size
    for part in range(per_member):
        bias_table[4:5, part * sizes[3] : (part + 1) * sizes[3]] = chosen(
            place == member * per_member + part, piece(3, 0, sizes[3])
        )
    for row, index in ((5, 2), (6, 4)):
        for other in range(links.fsdp_size):
            bias_table[row : row + 1, other * sizes[index] : (other + 1) * sizes[index]] = chosen(
                place == other, piece(index, 0, sizes[index])
            )
    local_heads = own_width // HEAD_DIM
    for pair in range(2):
        for head in range(local_heads):
            to = (pair * local_heads + head) * HEAD_PAD
            bias_table[7:8, to : to + HEAD_DIM] = chosen(
                place == pair * group_size + member, piece(1, head * HEAD_DIM, HEAD_DIM)
            )


def owned_biases(links, bias_rows, final, own_width, sizes, starts):
    place = links.place
    group_size, fsdp_size = links.group_size, links.fsdp_size
    blocks = sizes[0] // own_width
    final[...] = jnp.zeros_like(final)
    for index in range(blocks):
        total = 0.0
        for owner in range(fsdp_size):
            kind, member = divmod(owner * blocks + index, group_size)
            total = total + chosen(
                place == owner,
                bias_rows[member, 0:1, kind * own_width : (kind + 1) * own_width],
            )
        to = starts[0] + index * own_width
        final[:, to : to + own_width] = total
    local_heads = own_width // HEAD_DIM
    for head in range(local_heads):
        total = 0.0
        for owner in range(fsdp_size):
            pair, member = divmod(owner, group_size)
            low = (pair * local_heads + head) * HEAD_PAD
            total = total + chosen(place == owner, bias_rows[member, 7:8, low : low + HEAD_DIM])
        to = starts[1] + head * HEAD_DIM
        final[:, to : to + HEAD_DIM] = total
    per_member = fsdp_size // group_size
    for index, row in ((2, 4), (4, 5), (3, 6)):
        size = sizes[index]
        total = 0.0
        for owner in range(fsdp_size):
            member, part = divmod(owner, per_member)
            total = total + chosen(
                place == owner, bias_rows[member, row : row + 1, part * size : (part + 1) * size]
            )
        final[:, starts[index] : starts[index] + size] = total


def forward_kernel(
    sizes,
    tokens,
    upstream,
    conditions,
    segments,
    cond_weight,
    bias_vector,
    lengths,
    input_weight,
    attend_weight,
    weight_one,
    weight_two,
    mod_out,
    bias_out,
    one_out,
    heads_out,
    log_out,
    mixed_out,
    branch_out,
    middle_out,
    two_out,
    upper_out,
    input_out,
    attend_out,
    expand_out,
    reduce_out,
    act_out,
    act_send,
    bias_table,
    weight_zero,
    act_got,
    bias_rows,
    bias_got,
    mod_parts,
    mod_got,
    mod_row,
    group_got,
    weights,
    normed,
    lent,
    got,
    crossing,
    crossed,
    total,
    one,
    two,
    upper,
    heads,
    mixed,
    input_pad,
    attend_pad,
    send_sems,
    recv_sems,
    local_sems,
):
    fsdp_size, group_size, quarter, width, own_width, shard = sizes
    links = Links(fsdp_size, group_size)
    sends = Sends(send_sems, recv_sems)
    blocks = (weight_zero, weight_one, weight_two)
    local_heads = own_width // HEAD_DIM
    head_span = local_heads * HEAD_PAD
    chunk = 32
    chunks = quarter // chunk

    act_slots = [sends.slot() for _ in range(fsdp_size)]
    mod_slots = [sends.slot() for _ in range(fsdp_size)]
    group_slots = [sends.slot() for _ in range(group_size)]
    bias_slots = [sends.slot() for _ in range(fsdp_size)]
    level_slots = [[sends.slot() for _ in range(links.depth)] for _ in blocks]
    side_slots = [[sends.slot() for _ in range(links.depth)] for _ in blocks]
    onward_slots = [sends.slot() for _ in blocks]
    gather_one = GroupGather(links, sends, one, quarter)
    gather_two = GroupGather(links, sends, two, quarter)
    gather_upper = GroupGather(links, sends, upper, quarter)
    branch_sum = GroupSum(links, sends, lent, got, crossing, crossed, total)
    opened = []

    def shard_rows(block, place):
        return weights.at[block, aligned(place, shard), :]

    inner = links.level * (links.depth - 1 - links.level) > 0
    near = jnp.where(links.level < 2, 3, 1)
    order = (2, near, 4 - near)

    def level_copy(block, shift):
        own = shard_rows(block, links.place)
        target = links.level_at(shift) * 2 + links.side
        return sends.copy(
            level_slots[block][0] + shift, blocks[block], own, links.to_place(target)
        )

    def offer_levels(block):
        level_copy(block, 2).start()
        level_copy(block, 4 - near).start()

        @pl.when(inner)
        def _():
            level_copy(block, near).start()

    def offer_side(block):
        own = shard_rows(block, links.place)
        sends.start(side_slots[block][0], blocks[block], own, links.to_place(links.side_mate))

    def keep_own(block):
        kept = pltpu.make_async_copy(
            blocks[block], shard_rows(block, links.place), local_sems.at[block]
        )
        kept.start()
        return kept

    def forward_copy(block):
        rows = shard_rows(block, links.level_at(2) * 2 + links.side)
        return pltpu.make_async_remote_copy(
            src_ref=rows,
            dst_ref=rows,
            send_sem=send_sems.at[onward_slots[block]],
            recv_sem=recv_sems.at[level_slots[block][0] + 2 * links.level - 1],
            device_id=links.to_place((3 * links.level - 3) * 2 + links.side),
            device_id_type=MESH,
        )

    def side_copy(block, shift):
        rows = shard_rows(block, links.level_at(-shift) * 2 + links.side)
        return sends.copy(
            side_slots[block][0] + shift, rows, rows, links.to_place(links.side_mate)
        )

    def relay(block, index):
        shift = order[index]
        source = links.level_at(-shift) * 2 + links.side
        rows = shard_rows(block, source)
        sends.arrived(level_slots[block][0] + shift, rows, links.to_place(source))
        if index == 0:

            @pl.when(inner)
            def _():
                forward_copy(block).start()

        side_copy(block, shift).start()
        return source

    def side_arrived(block, index):
        shift = order[index - 1] if index else 0
        source = links.level_at(-shift) * 2 + 1 - links.side
        sends.arrived(
            side_slots[block][0] + shift, shard_rows(block, source), links.to_place(links.side_mate)
        )
        return source

    def finish_weights(block):
        level_copy(block, 2).wait_send()
        level_copy(block, 4 - near).wait_send()

        @pl.when(inner)
        def _():
            level_copy(block, near).wait_send()
            forward_copy(block).wait_send()

        for shift in order:
            side_copy(block, shift).wait_send()

    def keep(index, source, target):
        made = pltpu.make_async_copy(source, target, local_sems.at[index])
        made.start()
        opened.append(made)

    greeted = links.greet()
    raw = conditions[...].astype(float_type)
    activated = (raw / (1.0 + jnp.exp(-raw))).astype(brain_type).astype(float_type)
    act_send[...] = jnp.zeros_like(act_send)
    for place in range(fsdp_size):
        act_send[place, 0:4, :] = activated[:, place * shard : (place + 1) * shard]
    for index in range(3):
        weight_zero[:, index * own_width : (index + 1) * own_width] = input_weight[index]
    weight_zero[:, 3 * own_width : 4 * own_width] = attend_weight[...]
    links.await_all(greeted)
    for shift in range(1, fsdp_size):
        target = lax.rem(links.place + shift, fsdp_size)
        sends.start(
            act_slots[shift], act_send.at[target], act_got.at[links.place], links.to_place(target)
        )
    act_got[pl.ds(links.place, 1)] = act_send[pl.ds(links.place, 1)]
    kept_zero, kept_one, kept_two = [keep_own(block) for block in range(3)]
    hidden_total = weight_one.shape[1] * group_size
    own_biases(links, bias_vector, bias_table, own_width, bias_sizes(fsdp_size, width, hidden_total))

    def norm_tokens(index, carry):
        rows = aligned(index, chunk)
        normed[rows, :] = normed_rows(tokens[rows, :].astype(float_type))[0]
        return carry

    for shift in range(1, fsdp_size):
        source = lax.rem(links.place + fsdp_size - shift, fsdp_size)
        sends.arrived(act_slots[shift], act_got.at[source], links.to_place(source))
    activated = act_got[...].reshape(fsdp_size * 8, shard).astype(brain_type)
    for index in range(6):
        to = slice(index * own_width, (index + 1) * own_width)
        mod_parts[:, :, to] = (
            jnp.dot(activated, cond_weight[index], preferred_element_type=float_type).reshape(
                fsdp_size, 8, own_width
            )
            + bias_table[:, to][None]
        )
    act_out[...] = act_got[...]
    for shift in range(1, fsdp_size):
        target = lax.rem(links.place + shift, fsdp_size)
        sends.start(
            mod_slots[shift],
            mod_parts.at[target, 0:4, :],
            mod_got.at[links.place, 0:4, :],
            links.to_place(target),
        )
    offer_levels(0)
    offer_side(0)
    bias_rows[...] = bias_table[4:8, :].astype(brain_type)
    for shift in range(1, fsdp_size):
        target = lax.rem(links.place + shift, fsdp_size)
        sends.start(
            bias_slots[shift], bias_rows, bias_got.at[links.place], links.to_place(target)
        )
    bias_got[pl.ds(links.place, 1)] = bias_rows[...][None]
    offer_levels(1)
    offer_levels(2)
    offer_side(1)
    mod_got[pl.ds(links.place, 1)] = mod_parts[pl.ds(links.place, 1)]
    lax.fori_loop(0, chunks, norm_tokens, 0)
    input_pad[...] = jnp.zeros_like(input_pad)
    attend_pad[...] = jnp.zeros_like(attend_pad)
    kept_zero.wait()

    def spread_shard(place):
        rows = aligned(place, shard)
        spread_heads(weights.at[0], input_pad, rows, 0, 3 * local_heads, 0)
        spread_heads(weights.at[0], attend_pad, rows, 3 * local_heads, local_heads, 0)

    spread_shard(links.place)
    for shift in range(1, fsdp_size):
        source = lax.rem(links.place + fsdp_size - shift, fsdp_size)
        sends.arrived(
            mod_slots[shift], mod_got.at[source, 0:4, :], links.to_place(source)
        )
    summed = mod_got[0, 0:4, :]
    for index in range(1, fsdp_size):
        summed = summed + mod_got[index, 0:4, :]
    mod_row[...] = summed
    for shift in range(1, group_size):
        target = lax.rem(links.member + shift, group_size)
        sends.start(group_slots[shift], mod_row, group_got.at[links.member], links.to_member(target))
    group_got[pl.ds(links.member, 1)] = mod_row[...][None]
    for shift in range(1, group_size):
        source = lax.rem(links.member + group_size - shift, group_size)
        sends.arrived(group_slots[shift], group_got.at[source], links.to_member(source))
    slot = slot_column(segments)[0:4, 0:1]
    for index in range(6):
        full = jnp.concatenate(
            [
                group_got[member, :, index * own_width : (index + 1) * own_width]
                for member in range(group_size)
            ],
            axis=1,
        )
        mod_out[index : index + 1, :] = jnp.sum(full * slot, axis=0, keepdims=True)
    mod_out[6:8, :] = jnp.zeros((2, width), float_type)

    own_rows = links.member * quarter

    def first_norm(index, carry):
        rows = aligned(index, chunk)
        to = pl.ds(pl.multiple_of(own_rows + index * chunk, chunk), chunk)
        one[to, :] = (normed[rows, :] * (1.0 + mod_out[1:2, :]) + mod_out[0:1, :]).astype(brain_type)
        return carry

    lax.fori_loop(0, chunks, first_norm, 0)
    gather_one.start_half()
    gather_one.start_core()
    first_sources = [relay(0, index) for index in range(links.depth - 1)]
    offer_side(2)

    def upper_rows(index, carry):
        rows = aligned(index, chunk)
        to = pl.ds(pl.multiple_of(own_rows + index * chunk, chunk), chunk)
        upper[to, :] = (mod_out[5:6, :] * upstream[rows, :].astype(float_type)).astype(brain_type)
        return carry

    lax.fori_loop(0, chunks, upper_rows, 0)

    for source in first_sources:
        spread_shard(source)
    gather_one.pass_on()
    gather_upper.start_half()
    gather_upper.start_core()
    gather_one.await_core()
    for shift in range(links.depth):
        spread_shard(side_arrived(0, shift))
    gather_one.await_far()
    keep(3, one, one_out)
    keep(4, input_pad, input_out)
    keep(5, attend_pad, attend_out)

    for shift in range(1, fsdp_size):
        source = lax.rem(links.place + fsdp_size - shift, fsdp_size)
        sends.arrived(bias_slots[shift], bias_got.at[source], links.to_place(source))
    bias_sum = bias_got[0].astype(float_type)
    for index in range(1, fsdp_size):
        bias_sum = bias_sum + bias_got[index].astype(float_type)
    bias_out[0:4, :] = jnp.zeros_like(bias_sum)
    bias_out[4:8, :] = bias_sum
    bias_pad = bias_out[7:8, 0 : 2 * head_span]

    def project(index, carry):
        rows = aligned(index, quarter)
        values = jnp.dot(one[rows, :], input_pad[...], preferred_element_type=float_type)
        heads[rows, 0:head_span] = (values[:, 0:head_span] + bias_pad[:, 0:head_span]).astype(
            brain_type
        )
        heads[rows, head_span : 2 * head_span] = values[:, head_span : 2 * head_span].astype(
            brain_type
        )
        heads[rows, 2 * head_span :] = (
            values[:, 2 * head_span :] + bias_pad[:, head_span:]
        ).astype(brain_type)
        return carry

    lax.fori_loop(0, group_size, project, 0)
    keep(6, heads, heads_out)

    power_scale = math.log2(math.e) / math.sqrt(HEAD_DIM)

    def attend(head, turn):
        part = branch_sum.member_of(turn)
        step = turn * local_heads + head
        rows = aligned(part, quarter)

        def columns(base):
            return aligned(base * local_heads + head, HEAD_PAD)

        raw = lax.dot_general(
            heads[rows, columns(0)],
            heads[:, columns(1)],
            (((1,), (1,)), ((), ())),
            preferred_element_type=float_type,
        )
        scores = jnp.concatenate(
            [
                raw[:, other * quarter : (other + 1) * quarter]
                + pair_mask(lengths, part * quarter, other * quarter)
                for other in range(group_size)
            ],
            axis=1,
        )
        top = jnp.max(scores, axis=1, keepdims=True)
        powers = jnp.exp2(scores * power_scale - top * power_scale)
        totals = jnp.sum(powers, axis=1, keepdims=True)
        value = jnp.dot(
            powers.astype(brain_type), heads[:, columns(2)], preferred_element_type=float_type
        )
        mixed[rows, aligned(head, HEAD_PAD)] = (value / totals).astype(brain_type)
        turned = jnp.transpose(
            jnp.broadcast_to(top * power_scale + jnp.log2(totals), (quarter, HEAD_PAD))
        )
        log_out[head, :, rows] = turned[0:8, :]
        for index, late in enumerate((1, 6, 11)):

            @pl.when(step == late)
            def _():
                relay(1, index)

        @pl.when(step == 4)
        def _():
            gather_upper_in_loop()

        return turn

    def gather_upper_in_loop():
        mate = links.half_mate
        passed = gather_upper.rows(mate)
        sends.arrived(gather_upper.slots[1], passed, links.to_member(mate))
        sends.copy(
            gather_upper.slots[2], passed, passed, links.to_member(links.core_mate)
        ).start()

    def branch_part(member):
        return lax.dot_general(
            mixed[aligned(member, quarter), :],
            attend_pad[...],
            (((1,), (1,)), ((), ())),
            preferred_element_type=float_type,
        )

    def attend_turn(turn, carry):
        lax.fori_loop(0, local_heads, attend, turn)
        branch_sum.step(turn, branch_part(branch_sum.member_of(turn)), True)
        return carry

    lax.fori_loop(0, group_size, attend_turn, 0)
    passed = gather_upper.rows(links.half_mate)
    sends.open.append(
        sends.copy(gather_upper.slots[2], passed, passed, links.to_member(links.core_mate))
    )
    keep(7, mixed, mixed_out)
    branch_sum.note(True)
    gather_upper.await_core()
    gather_upper.await_far()
    keep(8, upper, upper_out)
    relay(2, 0)
    branch_sum.await_cross()

    def second_norm(index, carry):
        rows = aligned(index, chunk)
        to = pl.ds(pl.multiple_of(own_rows + index * chunk, chunk), chunk)
        branch = branch_sum.rows(rows) + bias_out[5:6, 0:width]
        branch_out[rows, :] = branch
        middle = tokens[rows, :].astype(float_type) + mod_out[2:3, :] * branch
        middle_out[rows, :] = middle
        two[to, :] = (normed_rows(middle)[0] * (1.0 + mod_out[4:5, :]) + mod_out[3:4, :]).astype(
            brain_type
        )
        return carry

    lax.fori_loop(0, chunks, second_norm, 0)
    gather_two.start_half()
    gather_two.start_core()
    relay(2, 1)
    relay(2, 2)
    gather_two.pass_on()
    kept_one.wait()
    for shift in range(links.depth):
        side_arrived(1, shift)
    keep(9, weights.at[1], expand_out)
    gather_two.await_core()
    gather_two.await_far()
    keep(10, two, two_out)
    kept_two.wait()
    for shift in range(links.depth):
        side_arrived(2, shift)
    keep(11, weights.at[2], reduce_out)
    for made in opened:
        made.wait()
    for block in range(3):
        finish_weights(block)
    sends.finish()


def run_forward(
    sizes, tokens, upstream, conditions, segments, cond_weight, bias_vector, lengths, weights
):
    fsdp_size, group_size, quarter, width, own_width, shard = sizes
    row_length = quarter * group_size
    local_heads = own_width // HEAD_DIM
    span = local_heads * HEAD_PAD
    hidden = weights[2].shape[1]
    in_vmem = pl.BlockSpec(memory_space=pltpu.VMEM)
    anywhere = pl.BlockSpec(memory_space=pl.ANY)
    shape = jax.ShapeDtypeStruct
    out_shape = (
        shape((8, width), float_type),
        shape((8, 6 * own_width), float_type),
        shape((row_length, width), brain_type),
        shape((row_length, 3 * span), brain_type),
        shape((local_heads, 8, row_length), float_type),
        shape((row_length, span), brain_type),
        shape((quarter, width), float_type),
        shape((quarter, width), float_type),
        shape((row_length, width), brain_type),
        shape((row_length, width), brain_type),
        shape((width, 3 * span), brain_type),
        shape((width, span), brain_type),
        shape((width, hidden), brain_type),
        shape((width, hidden), brain_type),
        shape((fsdp_size, 8, shard), float_type),
    )
    out_specs = (
        in_vmem,
        in_vmem,
        anywhere,
        anywhere,
        in_vmem,
        anywhere,
        in_vmem,
        in_vmem,
        anywhere,
        anywhere,
        anywhere,
        anywhere,
        anywhere,
        anywhere,
        in_vmem,
    )
    copies = 3 * fsdp_size + group_size + 6 * (fsdp_size // 2) + 3 * 3 + 6
    vmem = pltpu.VMEM
    scratch = [
        vmem((fsdp_size, 8, shard), float_type),
        vmem((8, 6 * own_width), float_type),
        vmem((shard, 4 * own_width), brain_type),
        vmem((fsdp_size, 8, shard), float_type),
        vmem((4, 6 * own_width), brain_type),
        vmem((fsdp_size, 4, 6 * own_width), brain_type),
        vmem((fsdp_size, 8, 6 * own_width), float_type),
        vmem((fsdp_size, 8, 6 * own_width), float_type),
        vmem((4, 6 * own_width), float_type),
        vmem((group_size, 4, 6 * own_width), float_type),
        vmem((3, width, hidden), brain_type),
        vmem((quarter, width), float_type),
        vmem((2, quarter, width), brain_type),
        vmem((2, quarter, width), brain_type),
        vmem((quarter, width), brain_type),
        vmem((quarter, width), brain_type),
        vmem((quarter, width), float_type),
        vmem((row_length, width), brain_type),
        vmem((row_length, width), brain_type),
        vmem((row_length, width), brain_type),
        vmem((row_length, 3 * span), brain_type),
        vmem((row_length, span), brain_type),
        vmem((width, 3 * span), brain_type),
        vmem((width, span), brain_type),
        pltpu.SemaphoreType.DMA((copies,)),
        pltpu.SemaphoreType.DMA((copies,)),
        pltpu.SemaphoreType.DMA((12,)),
    ]
    return pl.pallas_call(
        functools.partial(forward_kernel, sizes),
        out_shape=out_shape,
        in_specs=[in_vmem] * 6 + [pl.BlockSpec(memory_space=pltpu.SMEM)] + [in_vmem] * 4,
        out_specs=out_specs,
        scratch_shapes=scratch,
        compiler_params=pltpu.CompilerParams(
            collective_id=0, has_side_effects=True, vmem_limit_bytes=TOP_VMEM
        ),
        name="forward_row",
    )(tokens, upstream, conditions, segments, cond_weight, bias_vector, lengths, *weights)


class ShardSum:
    def __init__(self, links, sends, block, side_got, level_got, shard, first=None):
        self.links, self.sends, self.block = links, sends, block
        self.side_got, self.level_got, self.shard = side_got, level_got, shard
        if first is None:
            first = sends.used
            sends.used += 2 * links.depth
        self.first = first

    def order(self):
        return list(range(1, self.links.depth)) + [0]

    def rows(self, place):
        return aligned(place, self.shard)

    def side(self, shift):
        links = self.links
        level = links.level_at(shift)
        return self.sends.copy(
            self.first + shift,
            self.block.at[self.rows(level * 2 + 1 - links.side), :],
            self.side_got.at[shift],
            links.to_place(links.side_mate),
        )

    def start(self, note=True):
        for shift in self.order():
            self.side(shift).start()
        if note:
            self.note_sides()

    def note_sides(self):
        self.sends.open += [self.side(shift) for shift in self.order()]

    def fold(self, shift, note=True):
        links = self.links
        self.sends.arrived(
            self.first + shift, self.side_got.at[shift], links.to_place(links.side_mate)
        )
        if shift:
            target = links.level_at(shift) * 2 + links.side
            rows = self.rows(target)
            self.block[rows, :] = (
                self.block[rows, :].astype(float_type) + self.side_got[shift].astype(float_type)
            ).astype(brain_type)
            self.push(shift).start()
            if note:
                self.sends.open.append(self.push(shift))

    def push(self, shift):
        links = self.links
        target = links.level_at(shift) * 2 + links.side
        return self.sends.copy(
            self.first + links.depth + shift,
            self.block.at[self.rows(target), :],
            self.level_got.at[shift],
            links.to_place(target),
        )

    def total(self):
        links = self.links
        summed = self.block[self.rows(links.place), :].astype(float_type) + self.side_got[0].astype(
            float_type
        )
        for shift in range(1, links.depth):
            source = links.level_at(-shift) * 2 + links.side
            self.sends.arrived(
                self.first + links.depth + shift, self.level_got.at[shift], links.to_place(source)
            )
            summed = summed + self.level_got[shift].astype(float_type)
        return summed


def with_late(kernel, late):
    count = len(late)

    def wrapped(*refs):
        refs, buffers, sems = list(refs[: -count - 1]), refs[-count - 1 : -1], refs[-1]
        copies = []
        for index, place in enumerate(late):
            made = pltpu.make_async_copy(refs[place], buffers[index], sems.at[index])
            made.start()
            copies.append(made)
            refs[place] = buffers[index]
        kernel(copies, *refs)

    return wrapped


def late_scratch(late, arrays):
    buffers = [pltpu.VMEM(arrays[place].shape, arrays[place].dtype) for place in late]
    return buffers + [pltpu.SemaphoreType.DMA((len(late),))]


def fold_rows(values):
    count, width = values.shape
    return jnp.sum(values.reshape(count // 8, 8, width), axis=0)


def gelu_pair(values):
    root = math.sqrt(2.0 / math.pi)
    square = values * values
    bend = jnp.tanh(values * (root + root * 0.044715 * square))
    half = 0.5 * (1.0 + bend)
    slope = half + (0.5 * values) * (1.0 - bend * bend) * (root + root * 3 * 0.044715 * square)
    return values * half, slope


def across_rows(left, right):
    return lax.dot_general(left, right, (((0,), (0,)), ((), ())), preferred_element_type=float_type)


def middle_kernel(
    sizes,
    fetched,
    two,
    upper,
    expand,
    reduce,
    mods,
    biases,
    middle,
    branch,
    upstream,
    attend_pad,
    mixed,
    far_out,
    near_out,
    grads_out,
    attend_out,
    late_out,
    expand_out,
    reduce_out,
    slope_out,
    sums_out,
    active,
    inner_grad,
    lent_t,
    got_t,
    crossing_t,
    crossed_t,
    total_t,
    lent_o,
    got_o,
    branch_whole,
    pair_blocks,
    side_got,
    level_got,
    last_block,
    side_last,
    level_last,
    sums,
    send_sems,
    recv_sems,
):
    fsdp_size, group_size, quarter, width, own_width, shard = sizes
    links = Links(fsdp_size, group_size)
    sends = Sends(send_sems, recv_sems)
    local_heads = own_width // HEAD_DIM
    chunk = 32
    chunks = quarter // chunk
    two_sum = GroupSum(links, sends, lent_t, got_t, crossing_t, crossed_t, total_t)
    outer_sum = GroupSum(links, sends, lent_o, got_o, far_out, None, near_out)
    gather = GroupGather(links, sends, branch_whole, quarter)
    hidden = expand.shape[1]
    part = 384
    first_slot = sends.used
    pairs = hidden // part - 1
    sends.used += 2 * links.depth * pairs

    def pair_sum(index):
        return ShardSum(
            links,
            sends,
            pair_blocks.at[index],
            side_got.at[index],
            level_got.at[index],
            shard,
            first_slot + 2 * links.depth * index,
        )

    pair_totals = [pair_sum(index) for index in range(pairs)]
    pair_totals.append(ShardSum(links, sends, last_block, side_last, level_last, shard))
    links.meet()
    sums[...] = jnp.zeros_like(sums)

    def feed_part(picked, reduce_target, expand_target):
        def feed_rows(step, carry):
            rows = aligned(step, quarter)
            inner = (
                jnp.dot(two[rows, :], expand[:, picked], preferred_element_type=float_type)
                + biases[4:5, picked]
            )
            active_grad = jnp.dot(
                upper[rows, :], reduce[:, picked], preferred_element_type=float_type
            )
            value, slope = gelu_pair(inner)
            active[rows, picked] = value.astype(brain_type)
            low = (active_grad * slope).astype(brain_type)
            inner_grad[rows, picked] = low
            sums[4, :, picked] = sums[4, :, picked] + fold_rows(low.astype(float_type))
            return carry

        lax.fori_loop(0, group_size, feed_rows, 0)

        def grad_rows(step, carry):
            rows = aligned(step, part)
            reduce_target[rows, :] = across_rows(upper[:, rows], active[:, picked]).astype(
                brain_type
            )
            expand_target[rows, :] = across_rows(two[:, rows], inner_grad[:, picked]).astype(
                brain_type
            )
            return carry

        lax.fori_loop(0, width // part, grad_rows, 0)

    def feed(index, carry):
        feed_part(
            aligned(index, part),
            pair_blocks.at[index, :, 0:part],
            pair_blocks.at[index, :, part : 2 * part],
        )
        pair_sum(index).start(False)
        return carry

    lax.fori_loop(0, pairs, feed, 0)
    for item in pair_totals[:-1]:
        item.note_sides()
    pair_totals[0].fold(1)
    pair_totals[0].fold(2)
    feed_part(pl.ds(pairs * part, part), last_block, late_out)
    pair_totals[2].start()
    pair_totals[0].fold(3)

    def give(step, carry):
        rows = aligned(two_sum.member_of(step), quarter)
        two_sum.step(step, against(inner_grad[rows, :], expand[...]), True)
        outer_sum.step(step, against(active[rows, :], reduce[...]), False)

        @pl.when(step == 1)
        def _():
            pair_totals[0].fold(0)

        @pl.when(step == group_size - 1)
        def _():
            pair_totals[1].fold(1, False)

        return carry

    lax.fori_loop(0, group_size, give, 0)
    sends.open.append(pair_totals[1].push(1))
    two_sum.note(True)
    outer_sum.note(False)

    def near_rows(index, carry):
        rows = aligned(index, chunk)
        near_out[rows, :] = near_out[rows, :] + got_o[1, rows, :].astype(float_type)
        return carry

    lax.fori_loop(0, chunks, near_rows, 0)

    for shift in (2, 3):
        pair_totals[1].fold(shift)
    for made in fetched:
        made.wait()
    two_sum.await_cross()
    own_rows = links.member * quarter

    def second_back(index, carry):
        rows = aligned(index, chunk)
        to = pl.ds(pl.multiple_of(own_rows + index * chunk, chunk), chunk)
        two_grad = two_sum.rows(rows)
        normed, root = normed_rows(middle[rows, :])
        scaled = two_grad * (1.0 + mods[4:5, :])
        centered = (
            scaled
            - jnp.mean(scaled, axis=-1, keepdims=True)
            - normed * jnp.mean(scaled * normed, axis=-1, keepdims=True)
        )
        slope = upstream[rows, :].astype(float_type) + root * centered
        slope_out[rows, :] = slope
        low = (mods[2:3, :] * slope).astype(brain_type)
        branch_whole[to, :] = low
        sums[0] = sums[0] + fold_rows(slope * branch[rows, :])
        sums[1] = sums[1] + fold_rows(two_grad)
        sums[2] = sums[2] + fold_rows(two_grad * normed)
        sums[3] = sums[3] + fold_rows(low.astype(float_type))
        sums[5] = sums[5] + fold_rows(upper[to, :].astype(float_type))
        return carry

    lax.fori_loop(0, chunks, second_back, 0)
    gather.start_half()
    gather.start_core()

    for index in range(6):
        sums_out[index : index + 1, :] = jnp.sum(sums[index], axis=0, keepdims=True)
    sums_out[6:8, :] = jnp.zeros((2, width), float_type)
    pair_totals[1].fold(0)
    pair_totals[2].fold(1)
    pair_totals[2].fold(2)
    gather.pass_on()
    pair_totals[2].fold(3)
    gather.await_core()
    gather.await_far()

    def head_grads(index, carry):
        rows = aligned(index, quarter)
        grads_out[rows, :] = jnp.dot(
            branch_whole[rows, :], attend_pad[...], preferred_element_type=float_type
        ).astype(brain_type)
        return carry

    lax.fori_loop(0, group_size, head_grads, 0)

    def attend_part(index, carry):
        columns = aligned(index, part)
        value = across_rows(branch_whole[:, columns], mixed[...])
        for head in range(local_heads):
            attend_out[columns, head * HEAD_DIM : (head + 1) * HEAD_DIM] = value[
                :, head * HEAD_PAD : head * HEAD_PAD + HEAD_DIM
            ].astype(brain_type)
        return carry

    lax.fori_loop(0, width // part, attend_part, 0)
    pair_totals[2].fold(0)
    for index, item in enumerate(pair_totals[:-1]):
        pair = item.total()
        reduce_out[:, index * part : (index + 1) * part] = pair[:, 0:part]
        expand_out[:, index * part : (index + 1) * part] = pair[:, part:]
    reduce_out[:, pairs * part :] = pair_totals[-1].total()
    sends.finish()


def run_middle(sizes, *arrays):
    fsdp_size, group_size, quarter, width, own_width, shard = sizes
    row_length = quarter * group_size
    span = own_width // HEAD_DIM * HEAD_PAD
    hidden = arrays[2].shape[1]
    depth = fsdp_size // 2
    in_vmem = pl.BlockSpec(memory_space=pltpu.VMEM)
    shape = jax.ShapeDtypeStruct
    vmem = pltpu.VMEM
    copies = 3 + 3 + 3 + 2 * depth * (hidden // 384)
    late = (6, 7, 8, 9, 10)
    in_specs = [in_vmem] * len(arrays)
    for place in late:
        in_specs[place] = pl.BlockSpec(memory_space=pl.ANY)
    return pl.pallas_call(
        with_late(functools.partial(middle_kernel, sizes), late),
        out_shape=(
            shape((quarter, width), brain_type),
            shape((quarter, width), float_type),
            shape((row_length, span), brain_type),
            shape((width, own_width), brain_type),
            shape((width, 384), brain_type),
            shape((shard, hidden - 384), float_type),
            shape((shard, hidden), float_type),
            shape((quarter, width), float_type),
            shape((8, width), float_type),
        ),
        in_specs=in_specs,
        out_specs=(in_vmem,) * 9,
        scratch_shapes=[
            vmem((row_length, hidden), brain_type),
            vmem((row_length, hidden), brain_type),
            vmem((2, quarter, width), brain_type),
            vmem((2, quarter, width), brain_type),
            vmem((quarter, width), brain_type),
            vmem((quarter, width), brain_type),
            vmem((quarter, width), float_type),
            vmem((2, quarter, width), brain_type),
            vmem((2, quarter, width), brain_type),
            vmem((row_length, width), brain_type),
            vmem((hidden // 384 - 1, width, 768), brain_type),
            vmem((hidden // 384 - 1, depth, shard, 768), brain_type),
            vmem((hidden // 384 - 1, depth, shard, 768), brain_type),
            vmem((width, 384), brain_type),
            vmem((depth, shard, 384), brain_type),
            vmem((depth, shard, 384), brain_type),
            vmem((6, 8, width), float_type),
            pltpu.SemaphoreType.DMA((copies,)),
            pltpu.SemaphoreType.DMA((copies,)),
        ]
        + late_scratch(late, arrays),
        compiler_params=pltpu.CompilerParams(
            collective_id=1, has_side_effects=True, vmem_limit_bytes=TOP_VMEM
        ),
        name="middle_row",
    )(*arrays)


def backward_kernel(
    sizes,
    hidden,
    fetched,
    heads,
    logs,
    head_grads,
    mixed,
    one,
    input_pad,
    tokens,
    mods,
    biases,
    slope,
    upstream,
    middle,
    far_sum,
    near_sum,
    late_grad,
    expand_part,
    attend_grad,
    sums_in,
    cond_weight,
    act_all,
    conditions,
    segments,
    lengths,
    output_out,
    token_out,
    act_out,
    cond_out,
    bias_final,
    expand_out,
    input_out,
    attend_out,
    crossed_o,
    joined,
    query_sum,
    delta_rows,
    lent,
    got,
    crossing,
    crossed,
    total,
    attend_block,
    head_blocks,
    compact,
    side_zero,
    level_zero,
    side_heads,
    level_heads,
    sums,
    slabs,
    slab_got,
    place_slab,
    place_got,
    act_part,
    act_got,
    act_group,
    bias_row,
    bias_out,
    send_sems,
    recv_sems,
):
    fsdp_size, group_size, quarter, width, own_width, shard = sizes
    links = Links(fsdp_size, group_size)
    sends = Sends(send_sems, recv_sems)
    local_heads = own_width // HEAD_DIM
    span = local_heads * HEAD_PAD
    row_length = quarter * group_size
    chunk = 32
    chunks = quarter // chunk
    one_sum = GroupSum(links, sends, lent, got, crossing, crossed, total)
    attend_sum = ShardSum(links, sends, attend_block, side_zero, level_zero, shard)
    head_slot = sends.used
    sends.used += 2 * links.depth * local_heads

    def head_sum(head):
        return ShardSum(
            links,
            sends,
            head_blocks.at[head],
            side_heads.at[head],
            level_heads.at[head],
            shard,
            head_slot + 2 * links.depth * head,
        )

    head_sums = [head_sum(head) for head in range(local_heads)]
    outer_slot = sends.slot()
    slab_slots = [sends.slot() for _ in range(group_size)]
    place_slots = [sends.slot() for _ in range(fsdp_size)]
    part_slots = [sends.slot() for _ in range(fsdp_size)]
    row_slots = [sends.slot() for _ in range(group_size)]
    bias_slots = [sends.slot() for _ in range(group_size)]

    def to_places(slots, source_of, target):
        for shift in range(1, fsdp_size):
            place = lax.rem(links.place + shift, fsdp_size)
            sends.start(
                slots[shift], source_of(place), target.at[links.place], links.to_place(place)
            )

    def from_places(slots, target):
        for shift in range(1, fsdp_size):
            place = lax.rem(links.place + fsdp_size - shift, fsdp_size)
            sends.arrived(slots[shift], target.at[place], links.to_place(place))

    def to_members(slots, source_of, target):
        for shift in range(1, group_size):
            member = lax.rem(links.member + shift, group_size)
            sends.start(
                slots[shift], source_of(member), target.at[links.member], links.to_member(member)
            )

    def from_members(slots, target):
        for shift in range(1, group_size):
            member = lax.rem(links.member + group_size - shift, group_size)
            sends.arrived(slots[shift], target.at[member], links.to_member(member))

    links.meet()
    sends.start(outer_slot, far_sum, crossed_o, links.to_member(links.half_mate))
    sums[...] = jnp.zeros_like(sums)
    late = late_grad.shape[1]
    attend_block[:, 0:late] = late_grad[...]
    attend_block[:, late + own_width :] = jnp.zeros_like(attend_block[:, late + own_width :])
    attend_block[:, late : late + own_width] = attend_grad[...]
    attend_sum.start()
    compact[...] = jnp.zeros_like(compact)

    power_scale = math.log2(math.e) / math.sqrt(HEAD_DIM)
    score_scale = 1.0 / math.sqrt(HEAD_DIM)

    def columns(base, head):
        return aligned(base * local_heads + head, HEAD_PAD)

    def head_deltas(head, carry):
        product = head_grads[:, columns(0, head)].astype(float_type) * mixed[
            :, columns(0, head)
        ].astype(float_type)
        delta = jnp.sum(product, axis=1, keepdims=True)
        turned = jnp.transpose(jnp.broadcast_to(delta, (row_length, HEAD_PAD)))
        delta_rows[head] = turned[0:8, :]
        return carry

    lax.fori_loop(0, local_heads, head_deltas, 0)

    def attend_back(part, head):
        rows = aligned(part, quarter)
        query = heads[:, columns(0, head)]
        key = heads[rows, columns(1, head)]
        value = heads[rows, columns(2, head)]
        grad = head_grads[:, columns(0, head)]
        shift = jnp.concatenate(
            [
                pair_mask(lengths, part * quarter, other * quarter)
                - logs[head, 0:1, other * quarter : (other + 1) * quarter]
                for other in range(group_size)
            ],
            axis=1,
        )
        probable = jnp.exp2(against(key, query) * power_scale + shift)
        value_grad = jnp.dot(probable.astype(brain_type), grad, preferred_element_type=float_type)
        score_grad = (probable * (against(value, grad) - delta_rows[head, 0:1, :])).astype(
            brain_type
        )
        key_grad = jnp.dot(score_grad, query, preferred_element_type=float_type)
        joined[rows, columns(1, head)] = (key_grad * score_scale).astype(brain_type)
        joined[rows, columns(2, head)] = value_grad.astype(brain_type)
        query_grad = across_rows(score_grad, key)

        @pl.when(part == 0)
        def _():
            query_sum[...] = query_grad

        @pl.when(part > 0)
        def _():
            query_sum[...] = query_sum[...] + query_grad

        @pl.when(part == group_size - 1)
        def _():
            joined[:, columns(0, head)] = (query_sum[...] * score_scale).astype(brain_type)

        step = head * group_size + part
        for shift, at in ((1, 3), (2, 5), (3, 8)):

            @pl.when(step == at)
            def _():
                attend_sum.fold(shift, False)

        for shift in range(1, links.depth):

            @pl.when((part == shift) & (head > 2))
            def _():
                head_sum(head - 3).fold(shift, False)

        return head

    block_rows = 384

    def head_back(head, carry):
        lax.fori_loop(0, group_size, attend_back, head)
        for base in range(3):
            compact[:, base * HEAD_DIM : (base + 1) * HEAD_DIM] = joined[:, columns(base, head)][
                :, 0:HEAD_DIM
            ]

        def input_part(index, inner):
            picked = aligned(index, block_rows)
            head_blocks[head, picked, :] = across_rows(one[:, picked], compact[...]).astype(
                brain_type
            )
            return inner

        lax.fori_loop(0, width // block_rows, input_part, 0)
        head_sum(head).start(False)
        return carry

    fetched[0].wait()
    lax.fori_loop(0, local_heads, head_back, 0)
    for made in fetched[1:]:
        made.wait()
    for item in head_sums:
        item.note_sides()
    for item in [attend_sum] + head_sums:
        for shift in range(1, links.depth):
            sends.open.append(item.push(shift))

    def one_step(step, carry):
        rows = aligned(one_sum.member_of(step), quarter)
        one_sum.step(step, against(joined[rows, :], input_pad[...]), True)
        for shift in range(1, links.depth):

            @pl.when(step == shift)
            def _():
                head_sums[1].fold(shift, False)

        return carry

    lax.fori_loop(0, group_size, one_step, 0)
    one_sum.note(True)
    for shift in range(1, links.depth):
        head_sums[2].fold(shift, False)

    sends.arrived(outer_slot, crossed_o, links.to_member(links.half_mate))

    def finish_rows(index, carry):
        rows = aligned(index, chunk)
        outer = (
            near_sum[rows, :] + crossed_o[rows, :].astype(float_type) + biases[6:7, 0:width]
        )
        output_out[rows, :] = (middle[rows, :] + mods[5:6, :] * outer).astype(brain_type)
        sums[2] = sums[2] + fold_rows(upstream[rows, :].astype(float_type) * outer)
        return carry

    lax.fori_loop(0, chunks, finish_rows, 0)

    def pair_sums(index, carry):
        rows = aligned(index, 128)
        sums[3, :, 0:span] = sums[3, :, 0:span] + fold_rows(
            joined[rows, 0:span].astype(float_type)
        )
        sums[4, :, 0:span] = sums[4, :, 0:span] + fold_rows(
            joined[rows, 2 * span : 3 * span].astype(float_type)
        )
        return carry

    lax.fori_loop(0, row_length // 128, pair_sums, 0)
    for shift in range(1, links.depth):
        head_sums[3].fold(shift, False)
    one_sum.await_cross()

    def first_back(index, carry):
        rows = aligned(index, chunk)
        one_grad = one_sum.rows(rows)
        normed, root = normed_rows(tokens[rows, :].astype(float_type))
        scaled = one_grad * (1.0 + mods[1:2, :])
        centered = (
            scaled
            - jnp.mean(scaled, axis=-1, keepdims=True)
            - normed * jnp.mean(scaled * normed, axis=-1, keepdims=True)
        )
        token_out[rows, :] = slope[rows, :] + root * centered
        sums[0] = sums[0] + fold_rows(one_grad)
        sums[1] = sums[1] + fold_rows(one_grad * normed)
        return carry

    lax.fori_loop(0, chunks, first_back, 0)

    def summed(index):
        return jnp.sum(sums[index], axis=0, keepdims=True)

    six = (
        summed(0),
        summed(1),
        sums_in[0:1, :],
        sums_in[1:2, :],
        sums_in[2:3, :],
        summed(2),
    )
    slabs[...] = jnp.zeros_like(slabs)
    slots = slot_column(segments)[0:4, 0:1]
    for member in range(group_size):
        low, high = member * own_width, (member + 1) * own_width
        for index in range(6):
            to = slice(index * own_width, (index + 1) * own_width)
            slabs[member, 0:4, to] = slots * six[index][:, low:high]
        slabs[member, 4:5, 0:own_width] = sums_in[3:4, low:high]
        slabs[member, 5:6, 0:own_width] = sums_in[5:6, low:high]
    to_members(slab_slots, lambda member: slabs.at[member], slab_got)
    slab_got[pl.ds(links.member, 1)] = slabs[pl.ds(links.member, 1)]
    from_members(slab_slots, slab_got)
    row = slab_got[0]
    for member in range(1, group_size):
        row = row + slab_got[member]
    bias_row[...] = row
    bias_row[6:7, 0:width] = sums_in[4:5, :]
    bias_row[7:8, 0:span] = summed(3)[:, 0:span]
    bias_row[7:8, span : 2 * span] = summed(4)[:, 0:span]
    place_slab[...] = bias_row[...].astype(brain_type)
    to_places(place_slots, lambda place: place_slab, place_got)
    place_got[pl.ds(links.place, 1)] = place_slab[...][None]
    from_places(place_slots, place_got)
    low_rows = (
        place_got[...]
        .astype(float_type)
        .reshape(fsdp_size * 8, 6 * own_width)
        .astype(brain_type)
    )
    parts = [low_rows[:, index * own_width : (index + 1) * own_width] for index in range(6)]
    act_part[...] = sum(
        against(values, cond_weight[index]) for index, values in enumerate(parts)
    ).reshape(fsdp_size, 8, shard)
    to_places(part_slots, lambda place: act_part.at[place], act_got)
    act_got[pl.ds(links.place, 1)] = act_part[pl.ds(links.place, 1)]
    bias_sum = place_got[0].astype(float_type)
    for place in range(1, fsdp_size):
        bias_sum = bias_sum + place_got[place].astype(float_type)
    bias_row[...] = bias_sum
    bias_row[0:1, :] = jnp.sum(bias_sum[0:4, :], axis=0, keepdims=True)
    to_members(bias_slots, lambda member: bias_row, bias_out)
    bias_out[pl.ds(links.member, 1)] = bias_row[...][None]
    activated = act_all[...].reshape(fsdp_size * 8, shard).astype(brain_type)
    for index, values in enumerate(parts):
        cond_out[index] = across_rows(activated, values)
    from_places(part_slots, act_got)
    to_members(row_slots, lambda member: act_got, act_group)
    act_group[pl.ds(links.member, 1)] = act_got[...][None]
    from_members(row_slots, act_group)
    from_members(bias_slots, bias_out)
    act_sum = act_group[0]
    for member in range(1, group_size):
        act_sum = act_sum + act_group[member]
    raw = conditions[...].astype(float_type)
    gate = 1.0 / (1.0 + jnp.exp(-raw))
    slope_silu = gate * (1.0 + raw * (1.0 - gate))
    for place in range(fsdp_size):
        to = slice(place * shard, (place + 1) * shard)
        act_out[:, to] = act_sum[place, 0:4, :] * slope_silu[:, to]
    sizes_all = bias_sizes(fsdp_size, width, hidden * group_size)
    owned_biases(links, bias_out, bias_final, own_width, sizes_all, bias_starts(sizes_all))
    for item in [attend_sum] + head_sums:
        item.fold(0)
    joint = attend_sum.total()
    expand_out[:, 0 : hidden - late] = expand_part[...]
    expand_out[:, hidden - late :] = joint[:, 0:late]
    attend_out[...] = joint[:, late : late + own_width]
    for head, item in enumerate(head_sums):
        joint = item.total()
        for index in range(3):
            input_out[index, :, head * HEAD_DIM : (head + 1) * HEAD_DIM] = joint[
                :, index * HEAD_DIM : (index + 1) * HEAD_DIM
            ]
    sends.finish()


def bias_starts(sizes):
    starts = [0]
    for size in sizes:
        starts.append(starts[-1] + (size + HEAD_PAD - 1) // HEAD_PAD * HEAD_PAD)
    return starts


def run_backward(sizes, hidden, *arrays):
    fsdp_size, group_size, quarter, width, own_width, shard = sizes
    row_length = quarter * group_size
    local_heads = own_width // HEAD_DIM
    span = local_heads * HEAD_PAD
    depth = fsdp_size // 2
    six = 6 * own_width
    in_vmem = pl.BlockSpec(memory_space=pltpu.VMEM)
    shape = jax.ShapeDtypeStruct
    vmem = pltpu.VMEM
    copies = 3 + 4 * depth + 1 + 2 * fsdp_size + 3 * group_size + 2 * depth * local_heads
    head_span = (3 * HEAD_DIM + HEAD_PAD - 1) // HEAD_PAD * HEAD_PAD
    attend_span = (own_width + 384 + HEAD_PAD - 1) // HEAD_PAD * HEAD_PAD
    bias_span = bias_starts(bias_sizes(fsdp_size, width, hidden * group_size))[-1]
    in_specs = [in_vmem] * len(arrays)
    in_specs[-1] = pl.BlockSpec(memory_space=pltpu.SMEM)
    late = (4, 5, 6, 9, 10, 11, 13)
    for place in late:
        in_specs[place] = pl.BlockSpec(memory_space=pl.ANY)
    return pl.pallas_call(
        with_late(functools.partial(backward_kernel, sizes, hidden), late),
        out_shape=(
            shape((quarter, width), brain_type),
            shape((quarter, width), float_type),
            shape((4, width), float_type),
            shape((6, shard, own_width), float_type),
            shape((1, bias_span), float_type),
            shape((shard, hidden), float_type),
            shape((3, shard, own_width), float_type),
            shape((shard, own_width), float_type),
        ),
        in_specs=in_specs,
        out_specs=(in_vmem,) * 8,
        scratch_shapes=[
            vmem((quarter, width), brain_type),
            vmem((row_length, 3 * span), brain_type),
            vmem((row_length, HEAD_PAD), float_type),
            vmem((local_heads, 8, row_length), float_type),
            vmem((2, quarter, width), brain_type),
            vmem((2, quarter, width), brain_type),
            vmem((quarter, width), brain_type),
            vmem((quarter, width), brain_type),
            vmem((quarter, width), float_type),
            vmem((width, attend_span), brain_type),
            vmem((local_heads, width, head_span), brain_type),
            vmem((row_length, head_span), brain_type),
            vmem((depth, shard, attend_span), brain_type),
            vmem((depth, shard, attend_span), brain_type),
            vmem((local_heads, depth, shard, head_span), brain_type),
            vmem((local_heads, depth, shard, head_span), brain_type),
            vmem((5, 8, width), float_type),
            vmem((group_size, 8, six), float_type),
            vmem((group_size, 8, six), float_type),
            vmem((8, six), brain_type),
            vmem((fsdp_size, 8, six), brain_type),
            vmem((fsdp_size, 8, shard), float_type),
            vmem((fsdp_size, 8, shard), float_type),
            vmem((group_size, fsdp_size, 8, shard), float_type),
            vmem((8, six), float_type),
            vmem((group_size, 8, six), float_type),
            pltpu.SemaphoreType.DMA((copies,)),
            pltpu.SemaphoreType.DMA((copies,)),
        ]
        + late_scratch(late, arrays),
        compiler_params=pltpu.CompilerParams(
            collective_id=2, has_side_effects=True, vmem_limit_bytes=TOP_VMEM
        ),
        name="backward_row",
    )(*arrays)


def deliver_kernel(sizes, count, bias_row, *refs):
    sources, targets = refs[:count], refs[count : 2 * count]
    shares = refs[2 * count : 2 * count + len(sizes)]
    buffers = refs[2 * count + len(sizes) : 3 * count + len(sizes)]
    sems = refs[-1]

    def taken(index):
        return pltpu.make_async_copy(sources[index], buffers[index], sems.at[index])

    def given(index):
        return pltpu.make_async_copy(buffers[index], targets[index], sems.at[count + index])

    for index in range(count):
        taken(index).start()
    for start, size, share in zip(bias_starts(sizes), sizes, shares):
        share[...] = bias_row[0, start : start + size]
    for index in range(count):
        taken(index).wait()
        given(index).start()
    for index in range(count):
        given(index).wait()


def deliver(bias_row, sizes, *arrays):
    count = len(arrays)
    in_vmem = pl.BlockSpec(memory_space=pltpu.VMEM)
    anywhere = pl.BlockSpec(memory_space=pl.ANY)
    shape = jax.ShapeDtypeStruct
    return pl.pallas_call(
        functools.partial(deliver_kernel, sizes, count),
        out_shape=[shape(item.shape, item.dtype) for item in arrays]
        + [shape((size,), float_type) for size in sizes],
        in_specs=[in_vmem] + [anywhere] * count,
        out_specs=[anywhere] * count + [in_vmem] * len(sizes),
        scratch_shapes=[pltpu.VMEM(item.shape, item.dtype) for item in arrays]
        + [pltpu.SemaphoreType.DMA((2 * count,))],
        compiler_params=pltpu.CompilerParams(vmem_limit_bytes=TOP_VMEM),
        name="deliver_row",
    )(bias_row, *arrays)


def fast_local(
    tokens,
    conditions,
    lengths,
    segments,
    condition_weight,
    condition_bias,
    input_weight,
    input_bias,
    attend_weight,
    attend_bias,
    expand_weight,
    expand_bias,
    reduce_weight,
    reduce_bias,
    cotangent,
):
    _, quarter, width = tokens.shape
    group_size, fsdp_size = lax.axis_size("rep"), lax.axis_size("fsdp")
    shard, _, own_width = condition_weight.shape
    hidden = expand_weight.shape[1]
    sizes = (fsdp_size, group_size, quarter, width, own_width, shard)
    biases = (condition_bias, input_bias, attend_bias, expand_bias, reduce_bias)
    bias_total = sum(item.shape[0] for item in biases)
    bias_end = (bias_total + 1023) // 1024 * 1024
    bias_vector, start = 0.0, 0
    for item in biases:
        end = start + item.shape[0]
        bias_vector = bias_vector + jnp.pad(item.astype(float_type), (start, bias_end - end))
        start = end
    bias_vector = bias_vector[None]
    cond_blocks = condition_weight.transpose(1, 0, 2)
    condition_rows = conditions[0]
    token_rows = tokens.reshape(quarter, width)
    upstream = cotangent.reshape(quarter, width)
    (
        mods,
        biases,
        one,
        heads,
        logs,
        mixed,
        branch,
        middle,
        two,
        upper,
        input_pad,
        attend_pad,
        expand_all,
        reduce_all,
        act_all,
    ) = run_forward(
        sizes,
        token_rows,
        upstream,
        condition_rows,
        segments,
        cond_blocks,
        bias_vector,
        lengths,
        (input_weight.transpose(1, 0, 2), attend_weight, expand_weight, reduce_weight),
    )
    (
        far_sum,
        near_sum,
        head_grads,
        attend_grad,
        late_grad,
        expand_part,
        reduce_final,
        slope,
        sums,
    ) = (
        run_middle(
            sizes,
            two,
            upper,
            expand_all,
            reduce_all,
            mods,
            biases,
            middle,
            branch,
            upstream,
            attend_pad,
            mixed,
        )
    )
    (
        output,
        token_grad,
        condition_grad,
        cond_grad,
        bias_final,
        expand_final,
        input_final,
        attend_final,
    ) = run_backward(
        sizes,
        hidden,
        heads,
        logs,
        head_grads,
        mixed,
        one,
        input_pad,
        token_rows,
        mods,
        biases,
        slope,
        upstream,
        middle,
        far_sum,
        near_sum,
        late_grad,
        expand_part,
        attend_grad,
        sums,
        cond_blocks,
        act_all,
        condition_rows,
        segments,
        lengths,
    )

    (
        output,
        token_grad,
        condition_grad,
        cond_grad,
        input_final,
        attend_final,
        expand_final,
        reduce_final,
        condition_bias_final,
        input_bias_final,
        attend_bias_final,
        expand_bias_final,
        reduce_bias_final,
    ) = deliver(
        bias_final,
        bias_sizes(fsdp_size, width, hidden * group_size),
        output,
        token_grad,
        condition_grad,
        cond_grad,
        input_final,
        attend_final,
        expand_final,
        reduce_final,
    )
    return (
        output[None],
        token_grad[None],
        condition_grad[None],
        cond_grad.transpose(1, 0, 2),
        condition_bias_final,
        input_final.transpose(1, 0, 2),
        input_bias_final,
        attend_final,
        attend_bias_final,
        expand_final,
        expand_bias_final,
        reduce_final,
        reduce_bias_final,
    )


def solution(mesh):
    in_specs = (
        P("fsdp", "rep", None),
        P("fsdp", None, None),
        P("fsdp", None),
        P("fsdp", "rep"),
        P("fsdp", None, "rep"),
        P("fsdp"),
        P("fsdp", None, "rep"),
        P("fsdp"),
        P("fsdp", "rep"),
        P("fsdp"),
        P("fsdp", "rep"),
        P("fsdp"),
        P("fsdp", "rep"),
        P("fsdp"),
        P("fsdp", "rep", None),
    )
    out_specs = (
        P("fsdp", "rep", None),
        P("fsdp", "rep", None),
        P("fsdp", None, None),
        P("fsdp", None, "rep"),
        P("fsdp"),
        P("fsdp", None, "rep"),
        P("fsdp"),
        P("fsdp", "rep"),
        P("fsdp"),
        P("fsdp", "rep"),
        P("fsdp"),
        P("fsdp", "rep"),
        P("fsdp"),
    )
    local = fast_local if mesh.shape["fsdp"] == 8 else plain_local
    return jax.shard_map(local, mesh=mesh, in_specs=in_specs, out_specs=out_specs, check_vma=False)
```

```python
import functools
import math

import jax
import jax.numpy as jnp
from jax import lax
from jax.experimental import pallas as pl
from jax.experimental.pallas import tpu as pltpu
from jax.sharding import PartitionSpec as P

HEAD_DIM = 72


epsilon = 1e-06
highest = lax.Precision.HIGHEST
float_type = jnp.float32
brain_type = jnp.bfloat16


def layer_normed(values):
    center = jnp.mean(values, axis=-1, keepdims=True)
    shifted = values - center
    spread = jnp.mean(shifted * shifted, axis=-1, keepdims=True)
    return shifted * lax.rsqrt(spread + epsilon)


def modulated(values, shift_term, scale_term):
    return layer_normed(values) * (1.0 + scale_term) + shift_term


def gelu_tanh(values):
    return jax.nn.gelu(values, approximate=True)


def image_index(row_ends, positions):
    return jnp.sum((positions[..., :, None] >= row_ends[..., None, :-1]).astype(jnp.int32), axis=-1)


def across(left, right):
    return lax.dot_general(left, right, (((0,), (0,)), ((), ())), preferred_element_type=float_type)


def against(left, right):
    return lax.dot_general(left, right, (((1,), (1,)), ((), ())), preferred_element_type=float_type)


def column_sums(values):
    return jnp.sum(values.astype(float_type), axis=0)


def spread_columns(own_part, total, start):
    empty = jnp.zeros(own_part.shape[:-1] + (total,), float_type)
    return lax.dynamic_update_slice_in_dim(empty, own_part, start, own_part.ndim - 1)


def gather_block(*weights):
    return tuple(lax.all_gather(item, "fsdp", axis=0, tiled=True) for item in weights)


def plain_local(
    tokens,
    conditions,
    lengths,
    segments,
    condition_weight,
    condition_bias,
    input_weight,
    input_bias,
    attend_weight,
    attend_bias,
    expand_weight,
    expand_bias,
    reduce_weight,
    reduce_bias,
    cotangent,
):
    row_count, quarter, model_width = tokens.shape
    slot_count = conditions.shape[1]
    group_size = lax.axis_size("rep")
    group_place = lax.axis_index("rep")
    row_length = quarter * group_size
    own_width = condition_weight.shape[2]
    column_start = group_place * own_width
    hidden_width = expand_weight.shape[1]
    hidden_start = group_place * hidden_width
    local_heads = own_width // HEAD_DIM
    score_scale = 1.0 / math.sqrt(HEAD_DIM)
    patch_count = row_count * quarter
    image_count = row_count * slot_count
    key_place = jnp.arange(row_length, dtype=jnp.int32)
    row_ends = jnp.cumsum(lengths, axis=1, dtype=jnp.int32)
    row_images = image_index(row_ends, key_place)
    allowed = row_images[:, :, None] == row_images[:, None, :]

    def whole_rows(values):
        joined_rows = lax.all_gather(
            values.reshape(row_count, quarter, -1), "rep", axis=1, tiled=True
        )
        return joined_rows.reshape(row_count * row_length, -1)

    def own_rows(values):
        summed = lax.psum_scatter(
            values.reshape(row_count, row_length, -1), "rep", scatter_dimension=1, tiled=True
        )
        return summed.reshape(patch_count, -1)

    fsdp_size = lax.axis_size("fsdp")
    fsdp_place = lax.axis_index("fsdp")
    own_depth = condition_weight.shape[0]
    condition_values = conditions.astype(float_type)
    activated_own = jax.nn.silu(condition_values).reshape(image_count, model_width).astype(brain_type)
    activated_all = lax.all_gather(activated_own, "fsdp", axis=0, tiled=True)
    activated = lax.dynamic_slice_in_dim(activated_all, fsdp_place * own_depth, own_depth, 1)
    local_biases = (condition_bias, input_bias, attend_bias, expand_bias, reduce_bias)
    share_sizes = [item.shape[0] for item in local_biases]
    bias_ends = [sum(share_sizes[:k]) for k in range(len(share_sizes) + 1)]
    bias_table = lax.all_gather(jnp.concatenate(local_biases), "fsdp", axis=0, tiled=False)
    condition_bias_all, input_bias_all, attend_bias_all, expand_bias_all, reduce_bias_all = [
        bias_table[:, low:high].reshape(-1) for low, high in zip(bias_ends[:-1], bias_ends[1:])
    ]
    condition_bias_own = lax.dynamic_slice_in_dim(
        condition_bias_all.reshape(6, model_width), column_start, own_width, 1
    )
    modulation_parts = jnp.einsum(
        "id,dkm->ikm", activated, condition_weight, preferred_element_type=float_type
    )
    modulation_own = (
        lax.psum_scatter(modulation_parts, "fsdp", scatter_dimension=0, tiled=True)
        + condition_bias_own[None]
    )
    modulation = lax.all_gather(modulation_own, "rep", axis=2, tiled=True).reshape(
        row_count, slot_count, -1
    )
    slot_table = (
        segments[:, :, None] == jnp.arange(slot_count, dtype=jnp.int32)[None, None, :]
    ).astype(float_type)
    per_token = jnp.einsum("rqs,rsm->rqm", slot_table, modulation, precision=highest).reshape(
        patch_count, -1
    )
    shift_one, scale_one, gate_one, shift_two, scale_two, gate_two = jnp.split(per_token, 6, axis=1)
    token_values = tokens.reshape(patch_count, model_width).astype(float_type)

    def split_heads(values):
        return values.reshape(row_count, row_length, local_heads, HEAD_DIM).transpose(2, 0, 1, 3)

    def merge_heads(values):
        return values.transpose(1, 2, 0, 3).reshape(row_count * row_length, own_width)

    def allowed_scores(query_head, key_head):
        scores = (
            jnp.einsum("rqd,rkd->rqk", query_head, key_head, preferred_element_type=float_type)
            * score_scale
        )
        return jnp.where(allowed, scores, -1e30)

    def head_forward(parts):
        query_head, key_head, value_head = parts
        scores = allowed_scores(query_head, key_head)
        row_max = jnp.max(scores, axis=-1, keepdims=True)
        powers = jnp.exp(scores - row_max)
        totals = jnp.sum(powers, axis=-1, keepdims=True)
        weights_low = (powers / totals).astype(brain_type)
        mixed = jnp.einsum(
            "rqk,rkd->rqd", weights_low, value_head, preferred_element_type=float_type
        )
        return (mixed, row_max + jnp.log(totals))

    def head_backward(parts):
        query_head, key_head, value_head, grad_head, log_head = parts
        scores = allowed_scores(query_head, key_head)
        probable = jnp.exp(scores - log_head)
        prob_grad = jnp.einsum(
            "rqd,rkd->rqk", grad_head, value_head, preferred_element_type=float_type
        )
        score_grad = (
            probable * (prob_grad - jnp.sum(probable * prob_grad, axis=-1, keepdims=True))
        ).astype(brain_type)
        query_part = (
            jnp.einsum("rqk,rkd->rqd", score_grad, key_head, preferred_element_type=float_type)
            * score_scale
        )
        key_part = (
            jnp.einsum("rqk,rqd->rkd", score_grad, query_head, preferred_element_type=float_type)
            * score_scale
        )
        value_part = jnp.einsum(
            "rqk,rqd->rkd",
            probable.astype(brain_type),
            grad_head,
            preferred_element_type=float_type,
        )
        return (query_part, key_part, value_part)

    def trunk(gathered):
        (
            input_all,
            input_bias_all,
            attend_all,
            attend_bias_all,
            expand_all,
            expand_bias_all,
            reduce_all,
            reduce_bias_all,
        ) = gathered
        bias_pair = lax.dynamic_slice_in_dim(
            input_bias_all.reshape(2, model_width), column_start, own_width, 1
        )
        expand_bias_own = lax.dynamic_slice_in_dim(expand_bias_all, hidden_start, hidden_width, 0)
        normed_one = modulated(token_values, shift_one, scale_one).astype(brain_type)
        whole_one = whole_rows(normed_one)
        joined = jnp.einsum("nd,dkm->nkm", whole_one, input_all, preferred_element_type=float_type)
        queries = (joined[:, 0] + bias_pair[0]).astype(brain_type)
        keys_row = joined[:, 1].astype(brain_type)
        values_row = (joined[:, 2] + bias_pair[1]).astype(brain_type)
        query_heads = split_heads(queries)
        key_heads = split_heads(keys_row)
        value_heads = split_heads(values_row)
        mixed, log_totals = lax.map(head_forward, (query_heads, key_heads, value_heads))
        attended = merge_heads(mixed).astype(brain_type)
        branch = own_rows(against(attended, attend_all)) + attend_bias_all
        middle = token_values + gate_one * branch
        normed_two = modulated(middle, shift_two, scale_two).astype(brain_type)
        whole_two = whole_rows(normed_two)
        inner = jnp.dot(whole_two, expand_all, preferred_element_type=float_type) + expand_bias_own
        active = gelu_tanh(inner).astype(brain_type)
        outer = own_rows(against(active, reduce_all)) + reduce_bias_all
        result = middle + gate_two * outer
        return (
            result,
            gathered,
            whole_one,
            query_heads,
            key_heads,
            value_heads,
            log_totals,
            attended,
            branch,
            middle,
            whole_two,
            inner,
            active,
            outer,
        )

    input_all, attend_all, expand_all, reduce_all = gather_block(
        input_weight, attend_weight, expand_weight, reduce_weight
    )
    state = trunk(
        (
            input_all,
            input_bias_all,
            attend_all,
            attend_bias_all,
            expand_all,
            expand_bias_all,
            reduce_all,
            reduce_bias_all,
        )
    )
    output = state[0].astype(brain_type).reshape(row_count, quarter, model_width)
    (
        _,
        gathered,
        whole_one,
        query_heads,
        key_heads,
        value_heads,
        log_totals,
        attended,
        branch,
        middle,
        whole_two,
        inner,
        active,
        outer,
    ) = state
    upstream = cotangent.reshape(patch_count, model_width).astype(float_type)
    outer_grad = (gate_two * upstream).astype(brain_type)
    gate_two_grad = upstream * outer
    outer_whole = whole_rows(outer_grad)
    reduce_grad = across(outer_whole, active)
    reduce_bias_grad = column_sums(outer_grad)
    active_grad = jnp.dot(outer_whole, reduce_all, preferred_element_type=float_type)
    _, gelu_back = jax.vjp(gelu_tanh, inner)
    inner_grad = gelu_back(active_grad)[0].astype(brain_type)
    expand_grad = across(whole_two, inner_grad)
    expand_bias_full = spread_columns(
        column_sums(inner_grad), hidden_width * group_size, hidden_start
    )
    two_grad = own_rows(against(inner_grad, expand_all))
    _, second_back = jax.vjp(modulated, middle, shift_two, scale_two)
    middle_norm_grad, shift_two_grad, scale_two_grad = second_back(two_grad)
    middle_grad = upstream + middle_norm_grad
    gate_one_grad = middle_grad * branch
    branch_grad = (gate_one * middle_grad).astype(brain_type)
    branch_whole = whole_rows(branch_grad)
    attend_grad = across(branch_whole, attended)
    attend_bias_grad = column_sums(branch_grad)
    attended_grad = jnp.dot(branch_whole, attend_all, preferred_element_type=float_type).astype(
        brain_type
    )
    grad_heads = split_heads(attended_grad)
    query_parts, key_parts, value_parts = lax.map(
        head_backward, (query_heads, key_heads, value_heads, grad_heads, log_totals)
    )
    query_low = merge_heads(query_parts).astype(brain_type)
    key_low = merge_heads(key_parts).astype(brain_type)
    value_low = merge_heads(value_parts).astype(brain_type)
    joined_grad = jnp.stack([query_low, key_low, value_low], axis=1)
    input_grad = jnp.einsum(
        "nd,nkm->dkm", whole_one, joined_grad, preferred_element_type=float_type
    )
    input_bias_pair = jnp.stack([column_sums(query_low), column_sums(value_low)])
    input_bias_full = spread_columns(input_bias_pair, model_width, column_start).reshape(-1)
    one_grad = own_rows(
        jnp.einsum("nkm,dkm->nd", joined_grad, input_all, preferred_element_type=float_type)
    )
    _, first_back = jax.vjp(modulated, token_values, shift_one, scale_one)
    token_norm_grad, shift_one_grad, scale_one_grad = first_back(one_grad)
    token_grad = (middle_grad + token_norm_grad).reshape(row_count, quarter, model_width)
    six_grads = jnp.stack(
        [
            shift_one_grad,
            scale_one_grad,
            gate_one_grad,
            shift_two_grad,
            scale_two_grad,
            gate_two_grad,
        ],
        axis=1,
    ).reshape(row_count, quarter, 6, model_width)
    modulation_part = jnp.einsum("rqs,rqkm->rskm", slot_table, six_grads, precision=highest)
    modulation_grad = lax.psum_scatter(modulation_part, "rep", scatter_dimension=3, tiled=True)
    modulation_low = lax.all_gather(
        modulation_grad.reshape(image_count, 6, own_width).astype(brain_type),
        "fsdp",
        axis=0,
        tiled=True,
    )
    condition_weight_final = jnp.einsum(
        "id,ikm->dkm", activated, modulation_low, preferred_element_type=float_type
    )
    condition_bias_full = lax.all_gather(
        column_sums(modulation_low), "rep", axis=1, tiled=True
    ).reshape(-1)
    bias_depth = condition_bias.shape[0]
    condition_bias_final = lax.dynamic_slice_in_dim(
        condition_bias_full, fsdp_place * bias_depth, bias_depth, 0
    )
    activated_part = jnp.einsum(
        "ikm,dkm->id", modulation_low, condition_weight, preferred_element_type=float_type
    )
    activated_wide = lax.all_to_all(
        activated_part.reshape(fsdp_size, image_count, own_depth), "fsdp", 0, 0
    )
    activated_row = jnp.transpose(activated_wide, (1, 0, 2)).reshape(image_count, model_width)
    bias_rows = jnp.concatenate(
        [
            item.reshape(fsdp_size, -1)
            for item in (input_bias_full, attend_bias_grad, expand_bias_full, reduce_bias_grad)
        ],
        axis=1,
    )
    bias_own = lax.psum_scatter(bias_rows, "fsdp", scatter_dimension=0, tiled=True).reshape(-1)
    activated_grad, bias_sum = lax.psum((activated_row, bias_own), "rep")
    input_bias_final, attend_bias_final, expand_bias_final, reduce_bias_final = jnp.split(
        bias_sum, [end - share_sizes[0] for end in bias_ends[2:-1]]
    )
    input_final, attend_final, expand_final, reduce_final = [
        lax.psum_scatter(item.astype(brain_type), "fsdp", scatter_dimension=0, tiled=True).astype(
            float_type
        )
        for item in (input_grad, attend_grad, expand_grad, reduce_grad)
    ]
    _, silu_back = jax.vjp(jax.nn.silu, condition_values)
    condition_grad = silu_back(activated_grad.reshape(row_count, slot_count, model_width))[0]
    return (
        output,
        token_grad,
        condition_grad,
        condition_weight_final,
        condition_bias_final,
        input_final,
        input_bias_final,
        attend_final,
        attend_bias_final,
        expand_final,
        expand_bias_final,
        reduce_final,
        reduce_bias_final,
    )


MESH = pl.DeviceIdType.MESH
HEAD_PAD = 128
TOP_VMEM = 60 * 1024 * 1024


def aligned(index, step):
    return pl.ds(pl.multiple_of(index * step, step), step)


class Links:
    def __init__(self, fsdp_size, group_size):
        self.fsdp_size = fsdp_size
        self.group_size = group_size
        self.depth = fsdp_size // 2
        self.place = lax.axis_index("fsdp")
        self.member = lax.axis_index("rep")
        self.level = self.place // 2
        self.side = self.place % 2
        self.core = self.member % 2
        self.half = self.member // 2

    def to_place(self, place):
        return (place, self.member)

    def to_member(self, member):
        return (self.place, member)

    @property
    def core_mate(self):
        return self.half * 2 + 1 - self.core

    @property
    def half_mate(self):
        return (1 - self.half) * 2 + self.core

    @property
    def far_mate(self):
        return (1 - self.half) * 2 + 1 - self.core

    @property
    def side_mate(self):
        return self.level * 2 + 1 - self.side

    def level_at(self, shift):
        return lax.rem(self.level + shift + self.depth, self.depth)

    def meet(self):
        self.await_all(self.greet())

    def await_all(self, count):
        pl.semaphore_wait(pltpu.get_barrier_semaphore(), count)

    def greet(self):
        barrier = pltpu.get_barrier_semaphore()
        count = 0
        for shift in range(1, self.fsdp_size):
            target = lax.rem(self.place + shift, self.fsdp_size)
            pl.semaphore_signal(barrier, inc=1, device_id=self.to_place(target), device_id_type=MESH)
            count += 1
        for shift in range(1, self.group_size):
            target = lax.rem(self.member + shift, self.group_size)
            pl.semaphore_signal(barrier, inc=1, device_id=self.to_member(target), device_id_type=MESH)
            count += 1
        return count


class Sends:
    def __init__(self, send_sems, recv_sems):
        self.send_sems = send_sems
        self.recv_sems = recv_sems
        self.used = 0
        self.open = []

    def slot(self):
        self.used += 1
        return self.used - 1

    def copy(self, slot, source, target, device):
        return pltpu.make_async_remote_copy(
            src_ref=source,
            dst_ref=target,
            send_sem=self.send_sems.at[slot],
            recv_sem=self.recv_sems.at[slot],
            device_id=device,
            device_id_type=MESH,
        )

    def start(self, slot, source, target, device):
        made = self.copy(slot, source, target, device)
        made.start()
        self.open.append(made)

    def arrived(self, slot, target, device):
        self.copy(slot, target, target, device).wait_recv()

    def finish(self):
        for made in self.open:
            made.wait_send()


class GroupGather:
    def __init__(self, links, sends, buffer, quarter):
        self.links, self.sends, self.buffer, self.quarter = links, sends, buffer, quarter
        self.slots = [sends.slot() for _ in range(3)]

    def rows(self, member):
        return self.buffer.at[aligned(member, self.quarter), :]

    def start_core(self):
        own = self.rows(self.links.member)
        mate = self.links.to_member(self.links.core_mate)
        self.sends.start(self.slots[0], own, own, mate)

    def start_half(self):
        own = self.rows(self.links.member)
        self.sends.start(self.slots[1], own, own, self.links.to_member(self.links.half_mate))

    def await_core(self):
        mate = self.links.core_mate
        self.sends.arrived(self.slots[0], self.rows(mate), self.links.to_member(mate))

    def pass_on(self):
        mate = self.links.half_mate
        self.sends.arrived(self.slots[1], self.rows(mate), self.links.to_member(mate))
        passed = self.rows(mate)
        self.sends.start(
            self.slots[2], passed, passed, self.links.to_member(self.links.core_mate)
        )

    def await_far(self):
        mate = self.links.core_mate
        self.sends.arrived(self.slots[2], self.rows(self.links.far_mate), self.links.to_member(mate))


class GroupSum:
    def __init__(self, links, sends, lent, got, crossing, crossed, total):
        self.links, self.sends = links, sends
        self.lent, self.got, self.crossing, self.crossed, self.total = (
            lent,
            got,
            crossing,
            crossed,
            total,
        )
        self.slots = [sends.slot() for _ in range(3)]

    def member_of(self, step):
        half = lax.rem(self.links.half + 1 - step // 2 + 2, 2)
        core = lax.rem(self.links.core + 1 - step % 2 + 2, 2)
        return half * 2 + core

    def lend(self, index):
        mate = self.links.to_member(self.links.core_mate)
        return self.sends.copy(
            self.slots[0] + index, self.lent.at[index], self.got.at[index], mate
        )

    def cross(self):
        mate = self.links.to_member(self.links.half_mate)
        return self.sends.copy(self.slots[2], self.crossing, self.crossed, mate)

    def step(self, step, value, crosses):
        index = step // 2
        self.total[...] = value

        @pl.when(step % 2 == 0)
        def _():
            self.lent[index] = self.total[...].astype(brain_type)
            self.lend(index).start()

        @pl.when(step % 2 == 1)
        def _():
            self.lend(index).wait_recv()

        @pl.when(step == 1)
        def _():
            self.crossing[...] = (self.total[...] + self.got[0].astype(float_type)).astype(
                brain_type
            )
            if crosses:
                self.cross().start()

    def note(self, crosses):
        self.sends.open += [self.lend(0), self.lend(1)]
        if crosses:
            self.sends.open.append(self.cross())

    def await_cross(self):
        self.sends.arrived(
            self.slots[2], self.crossed, self.links.to_member(self.links.half_mate)
        )

    def rows(self, rows):
        return (
            self.total[rows, :]
            + self.got[1, rows, :].astype(float_type)
            + self.crossed[rows, :].astype(float_type)
        )


def normed_rows(values):
    center = jnp.mean(values, axis=-1, keepdims=True)
    shifted = values - center
    spread = jnp.mean(shifted * shifted, axis=-1, keepdims=True)
    root = lax.rsqrt(spread + epsilon)
    return shifted * root, root


def spread_heads(source, target, rows, first, heads, target_first):
    for head in range(heads):
        low, to = HEAD_DIM * (first + head), HEAD_PAD * (target_first + head)
        target[rows, to : to + HEAD_DIM] = source[rows, low : low + HEAD_DIM]


def slot_column(segments):
    slots = lax.broadcasted_iota(jnp.int32, (8, HEAD_PAD), 0)
    return jnp.where(slots == segments[0:1, 0:HEAD_PAD], 1.0, 0.0)


def image_at(lengths, start):
    end, image = 0, 0
    for slot in range(lengths.shape[1] - 1):
        end = end + lengths[0, slot]
        image = image + jnp.where(start >= end, 1, 0)
    return image


def pair_mask(lengths, first, second):
    return jnp.where(image_at(lengths, first) == image_at(lengths, second), 0.0, -1e30)


def chosen(flag, values):
    return values * jnp.where(flag, 1.0, 0.0)


def bias_sizes(fsdp_size, width, hidden_total):
    return [size // fsdp_size for size in (6 * width, 2 * width, width, hidden_total, width)]


def own_biases(links, bias_vector, bias_table, own_width, sizes):
    place, member = links.place, links.member
    group_size = links.group_size
    starts = [sum(sizes[:index]) for index in range(6)]

    def piece(index, low, size):
        return bias_vector[0:1, starts[index] + low : starts[index] + low + size]

    bias_table[...] = jnp.zeros_like(bias_table)
    blocks = sizes[0] // own_width
    for kind in range(6):
        row = sum(
            chosen(
                place * blocks + index == kind * group_size + member,
                piece(0, index * own_width, own_width),
            )
            for index in range(blocks)
        )
        bias_table[0:4, kind * own_width : (kind + 1) * own_width] = jnp.broadcast_to(
            row, (4, own_width)
        )
    per_member = links.fsdp_size // group_size
    for part in range(per_member):
        bias_table[4:5, part * sizes[3] : (part + 1) * sizes[3]] = chosen(
            place == member * per_member + part, piece(3, 0, sizes[3])
        )
    for row, index in ((5, 2), (6, 4)):
        for other in range(links.fsdp_size):
            bias_table[row : row + 1, other * sizes[index] : (other + 1) * sizes[index]] = chosen(
                place == other, piece(index, 0, sizes[index])
            )
    local_heads = own_width // HEAD_DIM
    for pair in range(2):
        for head in range(local_heads):
            to = (pair * local_heads + head) * HEAD_PAD
            bias_table[7:8, to : to + HEAD_DIM] = chosen(
                place == pair * group_size + member, piece(1, head * HEAD_DIM, HEAD_DIM)
            )


def owned_biases(links, bias_rows, final, own_width, sizes, starts):
    place = links.place
    group_size, fsdp_size = links.group_size, links.fsdp_size
    blocks = sizes[0] // own_width
    final[...] = jnp.zeros_like(final)
    for index in range(blocks):
        total = 0.0
        for owner in range(fsdp_size):
            kind, member = divmod(owner * blocks + index, group_size)
            total = total + chosen(
                place == owner,
                bias_rows[member, 0:1, kind * own_width : (kind + 1) * own_width],
            )
        to = starts[0] + index * own_width
        final[:, to : to + own_width] = total
    local_heads = own_width // HEAD_DIM
    for head in range(local_heads):
        total = 0.0
        for owner in range(fsdp_size):
            pair, member = divmod(owner, group_size)
            low = (pair * local_heads + head) * HEAD_PAD
            total = total + chosen(place == owner, bias_rows[member, 7:8, low : low + HEAD_DIM])
        to = starts[1] + head * HEAD_DIM
        final[:, to : to + HEAD_DIM] = total
    per_member = fsdp_size // group_size
    for index, row in ((2, 4), (4, 5), (3, 6)):
        size = sizes[index]
        total = 0.0
        for owner in range(fsdp_size):
            member, part = divmod(owner, per_member)
            total = total + chosen(
                place == owner, bias_rows[member, row : row + 1, part * size : (part + 1) * size]
            )
        final[:, starts[index] : starts[index] + size] = total


def forward_kernel(
    sizes,
    tokens,
    upstream,
    conditions,
    segments,
    cond_weight,
    bias_vector,
    lengths,
    input_weight,
    attend_weight,
    weight_one,
    weight_two,
    mod_out,
    bias_out,
    one_out,
    heads_out,
    log_out,
    mixed_out,
    branch_out,
    middle_out,
    two_out,
    upper_out,
    input_out,
    attend_out,
    expand_out,
    reduce_out,
    act_out,
    act_send,
    bias_table,
    weight_zero,
    act_got,
    bias_rows,
    bias_got,
    mod_parts,
    mod_got,
    mod_row,
    group_got,
    weights,
    normed,
    lent,
    got,
    crossing,
    crossed,
    total,
    one,
    two,
    upper,
    heads,
    mixed,
    input_pad,
    attend_pad,
    send_sems,
    recv_sems,
    local_sems,
):
    fsdp_size, group_size, quarter, width, own_width, shard = sizes
    links = Links(fsdp_size, group_size)
    sends = Sends(send_sems, recv_sems)
    blocks = (weight_zero, weight_one, weight_two)
    local_heads = own_width // HEAD_DIM
    head_span = local_heads * HEAD_PAD
    chunk = 32
    chunks = quarter // chunk

    act_slots = [sends.slot() for _ in range(fsdp_size)]
    mod_slots = [sends.slot() for _ in range(fsdp_size)]
    group_slots = [sends.slot() for _ in range(group_size)]
    bias_slots = [sends.slot() for _ in range(fsdp_size)]
    level_slots = [[sends.slot() for _ in range(links.depth)] for _ in blocks]
    side_slots = [[sends.slot() for _ in range(links.depth)] for _ in blocks]
    onward_slots = [sends.slot() for _ in blocks]
    gather_one = GroupGather(links, sends, one, quarter)
    gather_two = GroupGather(links, sends, two, quarter)
    gather_upper = GroupGather(links, sends, upper, quarter)
    branch_sum = GroupSum(links, sends, lent, got, crossing, crossed, total)
    opened = []

    def shard_rows(block, place):
        return weights.at[block, aligned(place, shard), :]

    inner = links.level * (links.depth - 1 - links.level) > 0
    near = jnp.where(links.level < 2, 3, 1)
    order = (2, near, 4 - near)

    def level_copy(block, shift):
        own = shard_rows(block, links.place)
        target = links.level_at(shift) * 2 + links.side
        return sends.copy(
            level_slots[block][0] + shift, blocks[block], own, links.to_place(target)
        )

    def offer_levels(block):
        level_copy(block, 2).start()
        level_copy(block, 4 - near).start()

        @pl.when(inner)
        def _():
            level_copy(block, near).start()

    def offer_side(block):
        own = shard_rows(block, links.place)
        sends.start(side_slots[block][0], blocks[block], own, links.to_place(links.side_mate))

    def keep_own(block):
        kept = pltpu.make_async_copy(
            blocks[block], shard_rows(block, links.place), local_sems.at[block]
        )
        kept.start()
        return kept

    def forward_copy(block):
        rows = shard_rows(block, links.level_at(2) * 2 + links.side)
        return pltpu.make_async_remote_copy(
            src_ref=rows,
            dst_ref=rows,
            send_sem=send_sems.at[onward_slots[block]],
            recv_sem=recv_sems.at[level_slots[block][0] + 2 * links.level - 1],
            device_id=links.to_place((3 * links.level - 3) * 2 + links.side),
            device_id_type=MESH,
        )

    def side_copy(block, shift):
        rows = shard_rows(block, links.level_at(-shift) * 2 + links.side)
        return sends.copy(
            side_slots[block][0] + shift, rows, rows, links.to_place(links.side_mate)
        )

    def relay(block, index):
        shift = order[index]
        source = links.level_at(-shift) * 2 + links.side
        rows = shard_rows(block, source)
        sends.arrived(level_slots[block][0] + shift, rows, links.to_place(source))
        if index == 0:

            @pl.when(inner)
            def _():
                forward_copy(block).start()

        side_copy(block, shift).start()
        return source

    def side_arrived(block, index):
        shift = order[index - 1] if index else 0
        source = links.level_at(-shift) * 2 + 1 - links.side
        sends.arrived(
            side_slots[block][0] + shift, shard_rows(block, source), links.to_place(links.side_mate)
        )
        return source

    def finish_weights(block):
        level_copy(block, 2).wait_send()
        level_copy(block, 4 - near).wait_send()

        @pl.when(inner)
        def _():
            level_copy(block, near).wait_send()
            forward_copy(block).wait_send()

        for shift in order:
            side_copy(block, shift).wait_send()

    def keep(index, source, target):
        made = pltpu.make_async_copy(source, target, local_sems.at[index])
        made.start()
        opened.append(made)

    greeted = links.greet()
    raw = conditions[...].astype(float_type)
    activated = (raw / (1.0 + jnp.exp(-raw))).astype(brain_type).astype(float_type)
    act_send[...] = jnp.zeros_like(act_send)
    for place in range(fsdp_size):
        act_send[place, 0:4, :] = activated[:, place * shard : (place + 1) * shard]
    for index in range(3):
        weight_zero[:, index * own_width : (index + 1) * own_width] = input_weight[index]
    weight_zero[:, 3 * own_width : 4 * own_width] = attend_weight[...]
    links.await_all(greeted)
    for shift in range(1, fsdp_size):
        target = lax.rem(links.place + shift, fsdp_size)
        sends.start(
            act_slots[shift], act_send.at[target], act_got.at[links.place], links.to_place(target)
        )
    act_got[pl.ds(links.place, 1)] = act_send[pl.ds(links.place, 1)]
    kept_zero, kept_one, kept_two = [keep_own(block) for block in range(3)]
    hidden_total = weight_one.shape[1] * group_size
    own_biases(links, bias_vector, bias_table, own_width, bias_sizes(fsdp_size, width, hidden_total))

    def norm_tokens(index, carry):
        rows = aligned(index, chunk)
        normed[rows, :] = normed_rows(tokens[rows, :].astype(float_type))[0]
        return carry

    for shift in range(1, fsdp_size):
        source = lax.rem(links.place + fsdp_size - shift, fsdp_size)
        sends.arrived(act_slots[shift], act_got.at[source], links.to_place(source))
    activated = act_got[...].reshape(fsdp_size * 8, shard).astype(brain_type)
    for index in range(6):
        to = slice(index * own_width, (index + 1) * own_width)
        mod_parts[:, :, to] = (
            jnp.dot(activated, cond_weight[index], preferred_element_type=float_type).reshape(
                fsdp_size, 8, own_width
            )
            + bias_table[:, to][None]
        )
    act_out[...] = act_got[...]
    for shift in range(1, fsdp_size):
        target = lax.rem(links.place + shift, fsdp_size)
        sends.start(
            mod_slots[shift],
            mod_parts.at[target, 0:4, :],
            mod_got.at[links.place, 0:4, :],
            links.to_place(target),
        )
    offer_levels(0)
    offer_side(0)
    bias_rows[...] = bias_table[4:8, :].astype(brain_type)
    for shift in range(1, fsdp_size):
        target = lax.rem(links.place + shift, fsdp_size)
        sends.start(
            bias_slots[shift], bias_rows, bias_got.at[links.place], links.to_place(target)
        )
    bias_got[pl.ds(links.place, 1)] = bias_rows[...][None]
    offer_levels(1)
    offer_levels(2)
    offer_side(1)
    offer_side(2)
    mod_got[pl.ds(links.place, 1)] = mod_parts[pl.ds(links.place, 1)]
    lax.fori_loop(0, chunks, norm_tokens, 0)
    input_pad[...] = jnp.zeros_like(input_pad)
    attend_pad[...] = jnp.zeros_like(attend_pad)
    kept_zero.wait()

    def spread_shard(place):
        rows = aligned(place, shard)
        spread_heads(weights.at[0], input_pad, rows, 0, 3 * local_heads, 0)
        spread_heads(weights.at[0], attend_pad, rows, 3 * local_heads, local_heads, 0)

    spread_shard(links.place)
    for shift in range(1, fsdp_size):
        source = lax.rem(links.place + fsdp_size - shift, fsdp_size)
        sends.arrived(
            mod_slots[shift], mod_got.at[source, 0:4, :], links.to_place(source)
        )
    summed = mod_got[0, 0:4, :]
    for index in range(1, fsdp_size):
        summed = summed + mod_got[index, 0:4, :]
    mod_row[...] = summed
    for shift in range(1, group_size):
        target = lax.rem(links.member + shift, group_size)
        sends.start(group_slots[shift], mod_row, group_got.at[links.member], links.to_member(target))
    group_got[pl.ds(links.member, 1)] = mod_row[...][None]
    for shift in range(1, group_size):
        source = lax.rem(links.member + group_size - shift, group_size)
        sends.arrived(group_slots[shift], group_got.at[source], links.to_member(source))
    slot = slot_column(segments)[0:4, 0:1]
    for index in range(6):
        full = jnp.concatenate(
            [
                group_got[member, :, index * own_width : (index + 1) * own_width]
                for member in range(group_size)
            ],
            axis=1,
        )
        mod_out[index : index + 1, :] = jnp.sum(full * slot, axis=0, keepdims=True)
    mod_out[6:8, :] = jnp.zeros((2, width), float_type)

    own_rows = links.member * quarter

    def first_norm(index, carry):
        rows = aligned(index, chunk)
        to = pl.ds(pl.multiple_of(own_rows + index * chunk, chunk), chunk)
        one[to, :] = (normed[rows, :] * (1.0 + mod_out[1:2, :]) + mod_out[0:1, :]).astype(brain_type)
        return carry

    lax.fori_loop(0, chunks, first_norm, 0)
    gather_one.start_half()
    gather_one.start_core()
    first_sources = [relay(0, index) for index in range(links.depth - 1)]

    def upper_rows(index, carry):
        rows = aligned(index, chunk)
        to = pl.ds(pl.multiple_of(own_rows + index * chunk, chunk), chunk)
        upper[to, :] = (mod_out[5:6, :] * upstream[rows, :].astype(float_type)).astype(brain_type)
        return carry

    lax.fori_loop(0, chunks, upper_rows, 0)

    for source in first_sources:
        spread_shard(source)
    gather_one.pass_on()
    gather_upper.start_half()
    gather_upper.start_core()
    gather_one.await_core()
    for shift in range(links.depth):
        spread_shard(side_arrived(0, shift))
    gather_one.await_far()
    keep(3, one, one_out)
    keep(4, input_pad, input_out)
    keep(5, attend_pad, attend_out)

    for shift in range(1, fsdp_size):
        source = lax.rem(links.place + fsdp_size - shift, fsdp_size)
        sends.arrived(bias_slots[shift], bias_got.at[source], links.to_place(source))
    bias_sum = bias_got[0].astype(float_type)
    for index in range(1, fsdp_size):
        bias_sum = bias_sum + bias_got[index].astype(float_type)
    bias_out[0:4, :] = jnp.zeros_like(bias_sum)
    bias_out[4:8, :] = bias_sum
    bias_pad = bias_out[7:8, 0 : 2 * head_span]

    def project(index, carry):
        rows = aligned(index, quarter)
        values = jnp.dot(one[rows, :], input_pad[...], preferred_element_type=float_type)
        heads[rows, 0:head_span] = (values[:, 0:head_span] + bias_pad[:, 0:head_span]).astype(
            brain_type
        )
        heads[rows, head_span : 2 * head_span] = values[:, head_span : 2 * head_span].astype(
            brain_type
        )
        heads[rows, 2 * head_span :] = (
            values[:, 2 * head_span :] + bias_pad[:, head_span:]
        ).astype(brain_type)
        return carry

    lax.fori_loop(0, group_size, project, 0)
    keep(6, heads, heads_out)

    power_scale = math.log2(math.e) / math.sqrt(HEAD_DIM)

    def attend(head, turn):
        part = branch_sum.member_of(turn)
        step = turn * local_heads + head
        rows = aligned(part, quarter)

        def columns(base):
            return aligned(base * local_heads + head, HEAD_PAD)

        raw = lax.dot_general(
            heads[rows, columns(0)],
            heads[:, columns(1)],
            (((1,), (1,)), ((), ())),
            preferred_element_type=float_type,
        )
        scores = jnp.concatenate(
            [
                raw[:, other * quarter : (other + 1) * quarter]
                + pair_mask(lengths, part * quarter, other * quarter)
                for other in range(group_size)
            ],
            axis=1,
        )
        top = jnp.max(scores, axis=1, keepdims=True)
        powers = jnp.exp2(scores * power_scale - top * power_scale)
        totals = jnp.sum(powers, axis=1, keepdims=True)
        value = jnp.dot(
            powers.astype(brain_type), heads[:, columns(2)], preferred_element_type=float_type
        )
        mixed[rows, aligned(head, HEAD_PAD)] = (value / totals).astype(brain_type)
        turned = jnp.transpose(
            jnp.broadcast_to(top * power_scale + jnp.log2(totals), (quarter, HEAD_PAD))
        )
        log_out[head, :, rows] = turned[0:8, :]
        for index, late in enumerate((1, 6, 11)):

            @pl.when(step == late)
            def _():
                relay(1, index)

        @pl.when(step == 4)
        def _():
            gather_upper_in_loop()

        return turn

    def gather_upper_in_loop():
        mate = links.half_mate
        passed = gather_upper.rows(mate)
        sends.arrived(gather_upper.slots[1], passed, links.to_member(mate))
        sends.copy(
            gather_upper.slots[2], passed, passed, links.to_member(links.core_mate)
        ).start()

    def branch_part(member):
        return lax.dot_general(
            mixed[aligned(member, quarter), :],
            attend_pad[...],
            (((1,), (1,)), ((), ())),
            preferred_element_type=float_type,
        )

    def attend_turn(turn, carry):
        lax.fori_loop(0, local_heads, attend, turn)
        branch_sum.step(turn, branch_part(branch_sum.member_of(turn)), True)
        return carry

    lax.fori_loop(0, group_size, attend_turn, 0)
    passed = gather_upper.rows(links.half_mate)
    sends.open.append(
        sends.copy(gather_upper.slots[2], passed, passed, links.to_member(links.core_mate))
    )
    keep(7, mixed, mixed_out)
    branch_sum.note(True)
    gather_upper.await_core()
    gather_upper.await_far()
    keep(8, upper, upper_out)
    relay(2, 0)
    branch_sum.await_cross()

    def second_norm(index, carry):
        rows = aligned(index, chunk)
        to = pl.ds(pl.multiple_of(own_rows + index * chunk, chunk), chunk)
        branch = branch_sum.rows(rows) + bias_out[5:6, 0:width]
        branch_out[rows, :] = branch
        middle = tokens[rows, :].astype(float_type) + mod_out[2:3, :] * branch
        middle_out[rows, :] = middle
        two[to, :] = (normed_rows(middle)[0] * (1.0 + mod_out[4:5, :]) + mod_out[3:4, :]).astype(
            brain_type
        )
        return carry

    lax.fori_loop(0, chunks, second_norm, 0)
    gather_two.start_half()
    gather_two.start_core()
    relay(2, 1)
    relay(2, 2)
    gather_two.pass_on()
    kept_one.wait()
    for shift in range(links.depth):
        side_arrived(1, shift)
    keep(9, weights.at[1], expand_out)
    gather_two.await_core()
    gather_two.await_far()
    keep(10, two, two_out)
    kept_two.wait()
    for shift in range(links.depth):
        side_arrived(2, shift)
    keep(11, weights.at[2], reduce_out)
    for made in opened:
        made.wait()
    for block in range(3):
        finish_weights(block)
    sends.finish()


def run_forward(
    sizes, tokens, upstream, conditions, segments, cond_weight, bias_vector, lengths, weights
):
    fsdp_size, group_size, quarter, width, own_width, shard = sizes
    row_length = quarter * group_size
    local_heads = own_width // HEAD_DIM
    span = local_heads * HEAD_PAD
    hidden = weights[2].shape[1]
    in_vmem = pl.BlockSpec(memory_space=pltpu.VMEM)
    anywhere = pl.BlockSpec(memory_space=pl.ANY)
    shape = jax.ShapeDtypeStruct
    out_shape = (
        shape((8, width), float_type),
        shape((8, 6 * own_width), float_type),
        shape((row_length, width), brain_type),
        shape((row_length, 3 * span), brain_type),
        shape((local_heads, 8, row_length), float_type),
        shape((row_length, span), brain_type),
        shape((quarter, width), float_type),
        shape((quarter, width), float_type),
        shape((row_length, width), brain_type),
        shape((row_length, width), brain_type),
        shape((width, 3 * span), brain_type),
        shape((width, span), brain_type),
        shape((width, hidden), brain_type),
        shape((width, hidden), brain_type),
        shape((fsdp_size, 8, shard), float_type),
    )
    out_specs = (
        in_vmem,
        in_vmem,
        anywhere,
        anywhere,
        in_vmem,
        anywhere,
        in_vmem,
        in_vmem,
        anywhere,
        anywhere,
        anywhere,
        anywhere,
        anywhere,
        anywhere,
        in_vmem,
    )
    copies = 3 * fsdp_size + group_size + 6 * (fsdp_size // 2) + 3 * 3 + 6
    vmem = pltpu.VMEM
    scratch = [
        vmem((fsdp_size, 8, shard), float_type),
        vmem((8, 6 * own_width), float_type),
        vmem((shard, 4 * own_width), brain_type),
        vmem((fsdp_size, 8, shard), float_type),
        vmem((4, 6 * own_width), brain_type),
        vmem((fsdp_size, 4, 6 * own_width), brain_type),
        vmem((fsdp_size, 8, 6 * own_width), float_type),
        vmem((fsdp_size, 8, 6 * own_width), float_type),
        vmem((4, 6 * own_width), float_type),
        vmem((group_size, 4, 6 * own_width), float_type),
        vmem((3, width, hidden), brain_type),
        vmem((quarter, width), float_type),
        vmem((2, quarter, width), brain_type),
        vmem((2, quarter, width), brain_type),
        vmem((quarter, width), brain_type),
        vmem((quarter, width), brain_type),
        vmem((quarter, width), float_type),
        vmem((row_length, width), brain_type),
        vmem((row_length, width), brain_type),
        vmem((row_length, width), brain_type),
        vmem((row_length, 3 * span), brain_type),
        vmem((row_length, span), brain_type),
        vmem((width, 3 * span), brain_type),
        vmem((width, span), brain_type),
        pltpu.SemaphoreType.DMA((copies,)),
        pltpu.SemaphoreType.DMA((copies,)),
        pltpu.SemaphoreType.DMA((12,)),
    ]
    return pl.pallas_call(
        functools.partial(forward_kernel, sizes),
        out_shape=out_shape,
        in_specs=[in_vmem] * 6 + [pl.BlockSpec(memory_space=pltpu.SMEM)] + [in_vmem] * 4,
        out_specs=out_specs,
        scratch_shapes=scratch,
        compiler_params=pltpu.CompilerParams(
            collective_id=0, has_side_effects=True, vmem_limit_bytes=TOP_VMEM
        ),
        name="forward_row",
    )(tokens, upstream, conditions, segments, cond_weight, bias_vector, lengths, *weights)


class ShardSum:
    def __init__(self, links, sends, block, side_got, level_got, shard, first=None):
        self.links, self.sends, self.block = links, sends, block
        self.side_got, self.level_got, self.shard = side_got, level_got, shard
        if first is None:
            first = sends.used
            sends.used += 2 * links.depth
        self.first = first

    def order(self):
        return list(range(1, self.links.depth)) + [0]

    def rows(self, place):
        return aligned(place, self.shard)

    def side(self, shift):
        links = self.links
        level = links.level_at(shift)
        return self.sends.copy(
            self.first + shift,
            self.block.at[self.rows(level * 2 + 1 - links.side), :],
            self.side_got.at[shift],
            links.to_place(links.side_mate),
        )

    def start(self, note=True):
        for shift in self.order():
            self.side(shift).start()
        if note:
            self.note_sides()

    def note_sides(self):
        self.sends.open += [self.side(shift) for shift in self.order()]

    def fold(self, shift, note=True):
        links = self.links
        self.sends.arrived(
            self.first + shift, self.side_got.at[shift], links.to_place(links.side_mate)
        )
        if shift:
            target = links.level_at(shift) * 2 + links.side
            rows = self.rows(target)
            self.block[rows, :] = (
                self.block[rows, :].astype(float_type) + self.side_got[shift].astype(float_type)
            ).astype(brain_type)
            self.push(shift).start()
            if note:
                self.sends.open.append(self.push(shift))

    def push(self, shift):
        links = self.links
        target = links.level_at(shift) * 2 + links.side
        return self.sends.copy(
            self.first + links.depth + shift,
            self.block.at[self.rows(target), :],
            self.level_got.at[shift],
            links.to_place(target),
        )

    def total(self):
        links = self.links
        summed = self.block[self.rows(links.place), :].astype(float_type) + self.side_got[0].astype(
            float_type
        )
        for shift in range(1, links.depth):
            source = links.level_at(-shift) * 2 + links.side
            self.sends.arrived(
                self.first + links.depth + shift, self.level_got.at[shift], links.to_place(source)
            )
            summed = summed + self.level_got[shift].astype(float_type)
        return summed


def with_late(kernel, late):
    count = len(late)

    def wrapped(*refs):
        refs, buffers, sems = list(refs[: -count - 1]), refs[-count - 1 : -1], refs[-1]
        copies = []
        for index, place in enumerate(late):
            made = pltpu.make_async_copy(refs[place], buffers[index], sems.at[index])
            made.start()
            copies.append(made)
            refs[place] = buffers[index]
        kernel(copies, *refs)

    return wrapped


def late_scratch(late, arrays):
    buffers = [pltpu.VMEM(arrays[place].shape, arrays[place].dtype) for place in late]
    return buffers + [pltpu.SemaphoreType.DMA((len(late),))]


def fold_rows(values):
    count, width = values.shape
    return jnp.sum(values.reshape(count // 8, 8, width), axis=0)


def gelu_pair(values):
    root = math.sqrt(2.0 / math.pi)
    square = values * values
    bend = jnp.tanh(values * (root + root * 0.044715 * square))
    half = 0.5 * (1.0 + bend)
    slope = half + (0.5 * values) * (1.0 - bend * bend) * (root + root * 3 * 0.044715 * square)
    return values * half, slope


def across_rows(left, right):
    return lax.dot_general(left, right, (((0,), (0,)), ((), ())), preferred_element_type=float_type)


def middle_kernel(
    sizes,
    fetched,
    two,
    upper,
    expand,
    reduce,
    mods,
    biases,
    middle,
    branch,
    upstream,
    attend_pad,
    mixed,
    far_out,
    near_out,
    grads_out,
    attend_out,
    late_out,
    expand_out,
    reduce_out,
    slope_out,
    sums_out,
    active,
    inner_grad,
    lent_t,
    got_t,
    crossing_t,
    crossed_t,
    total_t,
    lent_o,
    got_o,
    branch_whole,
    pair_blocks,
    side_got,
    level_got,
    last_block,
    side_last,
    level_last,
    sums,
    send_sems,
    recv_sems,
):
    fsdp_size, group_size, quarter, width, own_width, shard = sizes
    links = Links(fsdp_size, group_size)
    sends = Sends(send_sems, recv_sems)
    local_heads = own_width // HEAD_DIM
    chunk = 32
    chunks = quarter // chunk
    two_sum = GroupSum(links, sends, lent_t, got_t, crossing_t, crossed_t, total_t)
    outer_sum = GroupSum(links, sends, lent_o, got_o, far_out, None, near_out)
    gather = GroupGather(links, sends, branch_whole, quarter)
    hidden = expand.shape[1]
    part = 384
    first_slot = sends.used
    pairs = hidden // part - 1
    sends.used += 2 * links.depth * pairs

    def pair_sum(index):
        return ShardSum(
            links,
            sends,
            pair_blocks.at[index],
            side_got.at[index],
            level_got.at[index],
            shard,
            first_slot + 2 * links.depth * index,
        )

    pair_totals = [pair_sum(index) for index in range(pairs)]
    pair_totals.append(ShardSum(links, sends, last_block, side_last, level_last, shard))
    links.meet()
    sums[...] = jnp.zeros_like(sums)

    def feed_part(picked, reduce_target, expand_target):
        def feed_rows(step, carry):
            rows = aligned(step, quarter)
            inner = (
                jnp.dot(two[rows, :], expand[:, picked], preferred_element_type=float_type)
                + biases[4:5, picked]
            )
            active_grad = jnp.dot(
                upper[rows, :], reduce[:, picked], preferred_element_type=float_type
            )
            value, slope = gelu_pair(inner)
            active[rows, picked] = value.astype(brain_type)
            low = (active_grad * slope).astype(brain_type)
            inner_grad[rows, picked] = low
            sums[4, :, picked] = sums[4, :, picked] + fold_rows(low.astype(float_type))
            return carry

        lax.fori_loop(0, group_size, feed_rows, 0)

        def grad_rows(step, carry):
            rows = aligned(step, part)
            reduce_target[rows, :] = across_rows(upper[:, rows], active[:, picked]).astype(
                brain_type
            )
            expand_target[rows, :] = across_rows(two[:, rows], inner_grad[:, picked]).astype(
                brain_type
            )
            return carry

        lax.fori_loop(0, width // part, grad_rows, 0)

    def feed(index, carry):
        feed_part(
            aligned(index, part),
            pair_blocks.at[index, :, 0:part],
            pair_blocks.at[index, :, part : 2 * part],
        )
        pair_sum(index).start(False)
        return carry

    lax.fori_loop(0, pairs, feed, 0)
    for item in pair_totals[:-1]:
        item.note_sides()
    pair_totals[0].fold(1)
    pair_totals[0].fold(2)
    feed_part(pl.ds(pairs * part, part), last_block, late_out)
    pair_totals[2].start()
    pair_totals[0].fold(3)

    def give(step, carry):
        rows = aligned(two_sum.member_of(step), quarter)
        two_sum.step(step, against(inner_grad[rows, :], expand[...]), True)
        outer_sum.step(step, against(active[rows, :], reduce[...]), False)

        @pl.when(step == 1)
        def _():
            pair_totals[0].fold(0)

        @pl.when(step == group_size - 1)
        def _():
            pair_totals[1].fold(1, False)

        return carry

    lax.fori_loop(0, group_size, give, 0)
    sends.open.append(pair_totals[1].push(1))
    two_sum.note(True)
    outer_sum.note(False)

    def near_rows(index, carry):
        rows = aligned(index, chunk)
        near_out[rows, :] = near_out[rows, :] + got_o[1, rows, :].astype(float_type)
        return carry

    lax.fori_loop(0, chunks, near_rows, 0)

    for shift in (2, 3):
        pair_totals[1].fold(shift)
    for made in fetched:
        made.wait()
    two_sum.await_cross()
    own_rows = links.member * quarter

    def second_back(index, carry):
        rows = aligned(index, chunk)
        to = pl.ds(pl.multiple_of(own_rows + index * chunk, chunk), chunk)
        two_grad = two_sum.rows(rows)
        normed, root = normed_rows(middle[rows, :])
        scaled = two_grad * (1.0 + mods[4:5, :])
        centered = (
            scaled
            - jnp.mean(scaled, axis=-1, keepdims=True)
            - normed * jnp.mean(scaled * normed, axis=-1, keepdims=True)
        )
        slope = upstream[rows, :].astype(float_type) + root * centered
        slope_out[rows, :] = slope
        low = (mods[2:3, :] * slope).astype(brain_type)
        branch_whole[to, :] = low
        sums[0] = sums[0] + fold_rows(slope * branch[rows, :])
        sums[1] = sums[1] + fold_rows(two_grad)
        sums[2] = sums[2] + fold_rows(two_grad * normed)
        sums[3] = sums[3] + fold_rows(low.astype(float_type))
        sums[5] = sums[5] + fold_rows(upper[to, :].astype(float_type))
        return carry

    lax.fori_loop(0, chunks, second_back, 0)
    gather.start_half()
    gather.start_core()

    for index in range(6):
        sums_out[index : index + 1, :] = jnp.sum(sums[index], axis=0, keepdims=True)
    sums_out[6:8, :] = jnp.zeros((2, width), float_type)
    pair_totals[1].fold(0)
    pair_totals[2].fold(1)
    pair_totals[2].fold(2)
    gather.pass_on()
    pair_totals[2].fold(3)
    gather.await_core()
    gather.await_far()

    def head_grads(index, carry):
        rows = aligned(index, quarter)
        grads_out[rows, :] = jnp.dot(
            branch_whole[rows, :], attend_pad[...], preferred_element_type=float_type
        ).astype(brain_type)
        return carry

    lax.fori_loop(0, group_size, head_grads, 0)

    def attend_part(index, carry):
        columns = aligned(index, part)
        value = across_rows(branch_whole[:, columns], mixed[...])
        for head in range(local_heads):
            attend_out[columns, head * HEAD_DIM : (head + 1) * HEAD_DIM] = value[
                :, head * HEAD_PAD : head * HEAD_PAD + HEAD_DIM
            ].astype(brain_type)
        return carry

    lax.fori_loop(0, width // part, attend_part, 0)
    pair_totals[2].fold(0)
    for index, item in enumerate(pair_totals[:-1]):
        pair = item.total()
        reduce_out[:, index * part : (index + 1) * part] = pair[:, 0:part]
        expand_out[:, index * part : (index + 1) * part] = pair[:, part:]
    reduce_out[:, pairs * part :] = pair_totals[-1].total()
    sends.finish()


def run_middle(sizes, *arrays):
    fsdp_size, group_size, quarter, width, own_width, shard = sizes
    row_length = quarter * group_size
    span = own_width // HEAD_DIM * HEAD_PAD
    hidden = arrays[2].shape[1]
    depth = fsdp_size // 2
    in_vmem = pl.BlockSpec(memory_space=pltpu.VMEM)
    shape = jax.ShapeDtypeStruct
    vmem = pltpu.VMEM
    copies = 3 + 3 + 3 + 2 * depth * (hidden // 384)
    late = (6, 7, 8, 9, 10)
    in_specs = [in_vmem] * len(arrays)
    for place in late:
        in_specs[place] = pl.BlockSpec(memory_space=pl.ANY)
    return pl.pallas_call(
        with_late(functools.partial(middle_kernel, sizes), late),
        out_shape=(
            shape((quarter, width), brain_type),
            shape((quarter, width), float_type),
            shape((row_length, span), brain_type),
            shape((width, own_width), brain_type),
            shape((width, 384), brain_type),
            shape((shard, hidden - 384), float_type),
            shape((shard, hidden), float_type),
            shape((quarter, width), float_type),
            shape((8, width), float_type),
        ),
        in_specs=in_specs,
        out_specs=(in_vmem,) * 9,
        scratch_shapes=[
            vmem((row_length, hidden), brain_type),
            vmem((row_length, hidden), brain_type),
            vmem((2, quarter, width), brain_type),
            vmem((2, quarter, width), brain_type),
            vmem((quarter, width), brain_type),
            vmem((quarter, width), brain_type),
            vmem((quarter, width), float_type),
            vmem((2, quarter, width), brain_type),
            vmem((2, quarter, width), brain_type),
            vmem((row_length, width), brain_type),
            vmem((hidden // 384 - 1, width, 768), brain_type),
            vmem((hidden // 384 - 1, depth, shard, 768), brain_type),
            vmem((hidden // 384 - 1, depth, shard, 768), brain_type),
            vmem((width, 384), brain_type),
            vmem((depth, shard, 384), brain_type),
            vmem((depth, shard, 384), brain_type),
            vmem((6, 8, width), float_type),
            pltpu.SemaphoreType.DMA((copies,)),
            pltpu.SemaphoreType.DMA((copies,)),
        ]
        + late_scratch(late, arrays),
        compiler_params=pltpu.CompilerParams(
            collective_id=1, has_side_effects=True, vmem_limit_bytes=TOP_VMEM
        ),
        name="middle_row",
    )(*arrays)


def backward_kernel(
    sizes,
    hidden,
    fetched,
    heads,
    logs,
    head_grads,
    mixed,
    one,
    input_pad,
    tokens,
    mods,
    biases,
    slope,
    upstream,
    middle,
    far_sum,
    near_sum,
    late_grad,
    expand_part,
    attend_grad,
    sums_in,
    cond_weight,
    act_all,
    conditions,
    segments,
    lengths,
    output_out,
    token_out,
    act_out,
    cond_out,
    bias_final,
    expand_out,
    input_out,
    attend_out,
    crossed_o,
    joined,
    query_sum,
    delta_rows,
    lent,
    got,
    crossing,
    crossed,
    total,
    attend_block,
    head_blocks,
    compact,
    side_zero,
    level_zero,
    side_heads,
    level_heads,
    sums,
    slabs,
    slab_got,
    place_slab,
    place_got,
    act_part,
    act_got,
    act_group,
    bias_row,
    bias_out,
    send_sems,
    recv_sems,
):
    fsdp_size, group_size, quarter, width, own_width, shard = sizes
    links = Links(fsdp_size, group_size)
    sends = Sends(send_sems, recv_sems)
    local_heads = own_width // HEAD_DIM
    span = local_heads * HEAD_PAD
    row_length = quarter * group_size
    chunk = 32
    chunks = quarter // chunk
    one_sum = GroupSum(links, sends, lent, got, crossing, crossed, total)
    attend_sum = ShardSum(links, sends, attend_block, side_zero, level_zero, shard)
    head_slot = sends.used
    sends.used += 2 * links.depth * local_heads

    def head_sum(head):
        return ShardSum(
            links,
            sends,
            head_blocks.at[head],
            side_heads.at[head],
            level_heads.at[head],
            shard,
            head_slot + 2 * links.depth * head,
        )

    head_sums = [head_sum(head) for head in range(local_heads)]
    outer_slot = sends.slot()
    slab_slots = [sends.slot() for _ in range(group_size)]
    place_slots = [sends.slot() for _ in range(fsdp_size)]
    part_slots = [sends.slot() for _ in range(fsdp_size)]
    row_slots = [sends.slot() for _ in range(group_size)]
    bias_slots = [sends.slot() for _ in range(group_size)]

    def to_places(slots, source_of, target):
        for shift in range(1, fsdp_size):
            place = lax.rem(links.place + shift, fsdp_size)
            sends.start(
                slots[shift], source_of(place), target.at[links.place], links.to_place(place)
            )

    def from_places(slots, target):
        for shift in range(1, fsdp_size):
            place = lax.rem(links.place + fsdp_size - shift, fsdp_size)
            sends.arrived(slots[shift], target.at[place], links.to_place(place))

    def to_members(slots, source_of, target):
        for shift in range(1, group_size):
            member = lax.rem(links.member + shift, group_size)
            sends.start(
                slots[shift], source_of(member), target.at[links.member], links.to_member(member)
            )

    def from_members(slots, target):
        for shift in range(1, group_size):
            member = lax.rem(links.member + group_size - shift, group_size)
            sends.arrived(slots[shift], target.at[member], links.to_member(member))

    links.meet()
    sends.start(outer_slot, far_sum, crossed_o, links.to_member(links.half_mate))
    sums[...] = jnp.zeros_like(sums)
    late = late_grad.shape[1]
    attend_block[:, 0:late] = late_grad[...]
    attend_block[:, late + own_width :] = jnp.zeros_like(attend_block[:, late + own_width :])
    attend_block[:, late : late + own_width] = attend_grad[...]
    attend_sum.start()
    compact[...] = jnp.zeros_like(compact)

    power_scale = math.log2(math.e) / math.sqrt(HEAD_DIM)
    score_scale = 1.0 / math.sqrt(HEAD_DIM)

    def columns(base, head):
        return aligned(base * local_heads + head, HEAD_PAD)

    def head_deltas(head, carry):
        product = head_grads[:, columns(0, head)].astype(float_type) * mixed[
            :, columns(0, head)
        ].astype(float_type)
        delta = jnp.sum(product, axis=1, keepdims=True)
        turned = jnp.transpose(jnp.broadcast_to(delta, (row_length, HEAD_PAD)))
        delta_rows[head] = turned[0:8, :]
        return carry

    lax.fori_loop(0, local_heads, head_deltas, 0)

    def attend_back(part, head):
        rows = aligned(part, quarter)
        query = heads[:, columns(0, head)]
        key = heads[rows, columns(1, head)]
        value = heads[rows, columns(2, head)]
        grad = head_grads[:, columns(0, head)]
        shift = jnp.concatenate(
            [
                pair_mask(lengths, part * quarter, other * quarter)
                - logs[head, 0:1, other * quarter : (other + 1) * quarter]
                for other in range(group_size)
            ],
            axis=1,
        )
        probable = jnp.exp2(against(key, query) * power_scale + shift)
        value_grad = jnp.dot(probable.astype(brain_type), grad, preferred_element_type=float_type)
        score_grad = (probable * (against(value, grad) - delta_rows[head, 0:1, :])).astype(
            brain_type
        )
        key_grad = jnp.dot(score_grad, query, preferred_element_type=float_type)
        joined[rows, columns(1, head)] = (key_grad * score_scale).astype(brain_type)
        joined[rows, columns(2, head)] = value_grad.astype(brain_type)
        query_grad = across_rows(score_grad, key)

        @pl.when(part == 0)
        def _():
            query_sum[...] = query_grad

        @pl.when(part > 0)
        def _():
            query_sum[...] = query_sum[...] + query_grad

        @pl.when(part == group_size - 1)
        def _():
            joined[:, columns(0, head)] = (query_sum[...] * score_scale).astype(brain_type)

        step = head * group_size + part
        for shift, at in ((1, 3), (2, 5), (3, 8)):

            @pl.when(step == at)
            def _():
                attend_sum.fold(shift, False)

        for shift in range(1, links.depth):

            @pl.when((part == shift) & (head > 2))
            def _():
                head_sum(head - 3).fold(shift, False)

        return head

    block_rows = 384

    def head_back(head, carry):
        lax.fori_loop(0, group_size, attend_back, head)
        for base in range(3):
            compact[:, base * HEAD_DIM : (base + 1) * HEAD_DIM] = joined[:, columns(base, head)][
                :, 0:HEAD_DIM
            ]

        def input_part(index, inner):
            picked = aligned(index, block_rows)
            head_blocks[head, picked, :] = across_rows(one[:, picked], compact[...]).astype(
                brain_type
            )
            return inner

        lax.fori_loop(0, width // block_rows, input_part, 0)
        head_sum(head).start(False)
        return carry

    fetched[0].wait()
    lax.fori_loop(0, local_heads, head_back, 0)
    for made in fetched[1:]:
        made.wait()
    for item in head_sums:
        item.note_sides()
    for item in [attend_sum] + head_sums:
        for shift in range(1, links.depth):
            sends.open.append(item.push(shift))

    def one_step(step, carry):
        rows = aligned(one_sum.member_of(step), quarter)
        one_sum.step(step, against(joined[rows, :], input_pad[...]), True)
        for shift in range(1, links.depth):

            @pl.when(step == shift)
            def _():
                head_sums[1].fold(shift, False)

        return carry

    lax.fori_loop(0, group_size, one_step, 0)
    one_sum.note(True)

    sends.arrived(outer_slot, crossed_o, links.to_member(links.half_mate))

    def finish_rows(index, carry):
        rows = aligned(index, chunk)
        outer = (
            near_sum[rows, :] + crossed_o[rows, :].astype(float_type) + biases[6:7, 0:width]
        )
        output_out[rows, :] = (middle[rows, :] + mods[5:6, :] * outer).astype(brain_type)
        sums[2] = sums[2] + fold_rows(upstream[rows, :].astype(float_type) * outer)
        return carry

    lax.fori_loop(0, chunks, finish_rows, 0)

    for shift in range(1, links.depth):
        head_sums[2].fold(shift, False)

    def pair_sums(index, carry):
        rows = aligned(index, 128)
        sums[3, :, 0:span] = sums[3, :, 0:span] + fold_rows(
            joined[rows, 0:span].astype(float_type)
        )
        sums[4, :, 0:span] = sums[4, :, 0:span] + fold_rows(
            joined[rows, 2 * span : 3 * span].astype(float_type)
        )
        return carry

    lax.fori_loop(0, row_length // 128, pair_sums, 0)
    for shift in range(1, links.depth):
        head_sums[3].fold(shift, False)
    one_sum.await_cross()

    def first_back(index, carry):
        rows = aligned(index, chunk)
        one_grad = one_sum.rows(rows)
        normed, root = normed_rows(tokens[rows, :].astype(float_type))
        scaled = one_grad * (1.0 + mods[1:2, :])
        centered = (
            scaled
            - jnp.mean(scaled, axis=-1, keepdims=True)
            - normed * jnp.mean(scaled * normed, axis=-1, keepdims=True)
        )
        token_out[rows, :] = slope[rows, :] + root * centered
        sums[0] = sums[0] + fold_rows(one_grad)
        sums[1] = sums[1] + fold_rows(one_grad * normed)
        return carry

    lax.fori_loop(0, chunks, first_back, 0)

    def summed(index):
        return jnp.sum(sums[index], axis=0, keepdims=True)

    six = (
        summed(0),
        summed(1),
        sums_in[0:1, :],
        sums_in[1:2, :],
        sums_in[2:3, :],
        summed(2),
    )
    slabs[...] = jnp.zeros_like(slabs)
    slots = slot_column(segments)[0:4, 0:1]
    for member in range(group_size):
        low, high = member * own_width, (member + 1) * own_width
        for index in range(6):
            to = slice(index * own_width, (index + 1) * own_width)
            slabs[member, 0:4, to] = slots * six[index][:, low:high]
        slabs[member, 4:5, 0:own_width] = sums_in[3:4, low:high]
        slabs[member, 5:6, 0:own_width] = sums_in[5:6, low:high]
    to_members(slab_slots, lambda member: slabs.at[member], slab_got)
    slab_got[pl.ds(links.member, 1)] = slabs[pl.ds(links.member, 1)]
    from_members(slab_slots, slab_got)
    row = slab_got[0]
    for member in range(1, group_size):
        row = row + slab_got[member]
    bias_row[...] = row
    bias_row[6:7, 0:width] = sums_in[4:5, :]
    bias_row[7:8, 0:span] = summed(3)[:, 0:span]
    bias_row[7:8, span : 2 * span] = summed(4)[:, 0:span]
    place_slab[...] = bias_row[...].astype(brain_type)
    to_places(place_slots, lambda place: place_slab, place_got)
    place_got[pl.ds(links.place, 1)] = place_slab[...][None]
    from_places(place_slots, place_got)
    low_rows = (
        place_got[...]
        .astype(float_type)
        .reshape(fsdp_size * 8, 6 * own_width)
        .astype(brain_type)
    )
    parts = [low_rows[:, index * own_width : (index + 1) * own_width] for index in range(6)]
    act_part[...] = sum(
        against(values, cond_weight[index]) for index, values in enumerate(parts)
    ).reshape(fsdp_size, 8, shard)
    to_places(part_slots, lambda place: act_part.at[place], act_got)
    act_got[pl.ds(links.place, 1)] = act_part[pl.ds(links.place, 1)]
    bias_sum = place_got[0].astype(float_type)
    for place in range(1, fsdp_size):
        bias_sum = bias_sum + place_got[place].astype(float_type)
    bias_row[...] = bias_sum
    bias_row[0:1, :] = jnp.sum(bias_sum[0:4, :], axis=0, keepdims=True)
    to_members(bias_slots, lambda member: bias_row, bias_out)
    bias_out[pl.ds(links.member, 1)] = bias_row[...][None]
    activated = act_all[...].reshape(fsdp_size * 8, shard).astype(brain_type)
    for index, values in enumerate(parts):
        cond_out[index] = across_rows(activated, values)
    from_places(part_slots, act_got)
    to_members(row_slots, lambda member: act_got, act_group)
    act_group[pl.ds(links.member, 1)] = act_got[...][None]
    from_members(row_slots, act_group)
    from_members(bias_slots, bias_out)
    act_sum = act_group[0]
    for member in range(1, group_size):
        act_sum = act_sum + act_group[member]
    raw = conditions[...].astype(float_type)
    gate = 1.0 / (1.0 + jnp.exp(-raw))
    slope_silu = gate * (1.0 + raw * (1.0 - gate))
    for place in range(fsdp_size):
        to = slice(place * shard, (place + 1) * shard)
        act_out[:, to] = act_sum[place, 0:4, :] * slope_silu[:, to]
    sizes_all = bias_sizes(fsdp_size, width, hidden * group_size)
    owned_biases(links, bias_out, bias_final, own_width, sizes_all, bias_starts(sizes_all))
    for item in [attend_sum] + head_sums:
        item.fold(0)
    joint = attend_sum.total()
    expand_out[:, 0 : hidden - late] = expand_part[...]
    expand_out[:, hidden - late :] = joint[:, 0:late]
    attend_out[...] = joint[:, late : late + own_width]
    for head, item in enumerate(head_sums):
        joint = item.total()
        for index in range(3):
            input_out[index, :, head * HEAD_DIM : (head + 1) * HEAD_DIM] = joint[
                :, index * HEAD_DIM : (index + 1) * HEAD_DIM
            ]
    sends.finish()


def bias_starts(sizes):
    starts = [0]
    for size in sizes:
        starts.append(starts[-1] + (size + HEAD_PAD - 1) // HEAD_PAD * HEAD_PAD)
    return starts


def run_backward(sizes, hidden, *arrays):
    fsdp_size, group_size, quarter, width, own_width, shard = sizes
    row_length = quarter * group_size
    local_heads = own_width // HEAD_DIM
    span = local_heads * HEAD_PAD
    depth = fsdp_size // 2
    six = 6 * own_width
    in_vmem = pl.BlockSpec(memory_space=pltpu.VMEM)
    shape = jax.ShapeDtypeStruct
    vmem = pltpu.VMEM
    copies = 3 + 4 * depth + 1 + 2 * fsdp_size + 3 * group_size + 2 * depth * local_heads
    head_span = (3 * HEAD_DIM + HEAD_PAD - 1) // HEAD_PAD * HEAD_PAD
    attend_span = (own_width + 384 + HEAD_PAD - 1) // HEAD_PAD * HEAD_PAD
    bias_span = bias_starts(bias_sizes(fsdp_size, width, hidden * group_size))[-1]
    in_specs = [in_vmem] * len(arrays)
    in_specs[-1] = pl.BlockSpec(memory_space=pltpu.SMEM)
    late = (4, 5, 6, 9, 10, 11, 13, 15, 18)
    for place in late:
        in_specs[place] = pl.BlockSpec(memory_space=pl.ANY)
    return pl.pallas_call(
        with_late(functools.partial(backward_kernel, sizes, hidden), late),
        out_shape=(
            shape((quarter, width), brain_type),
            shape((quarter, width), float_type),
            shape((4, width), float_type),
            shape((6, shard, own_width), float_type),
            shape((1, bias_span), float_type),
            shape((shard, hidden), float_type),
            shape((3, shard, own_width), float_type),
            shape((shard, own_width), float_type),
        ),
        in_specs=in_specs,
        out_specs=(in_vmem,) * 8,
        scratch_shapes=[
            vmem((quarter, width), brain_type),
            vmem((row_length, 3 * span), brain_type),
            vmem((row_length, HEAD_PAD), float_type),
            vmem((local_heads, 8, row_length), float_type),
            vmem((2, quarter, width), brain_type),
            vmem((2, quarter, width), brain_type),
            vmem((quarter, width), brain_type),
            vmem((quarter, width), brain_type),
            vmem((quarter, width), float_type),
            vmem((width, attend_span), brain_type),
            vmem((local_heads, width, head_span), brain_type),
            vmem((row_length, head_span), brain_type),
            vmem((depth, shard, attend_span), brain_type),
            vmem((depth, shard, attend_span), brain_type),
            vmem((local_heads, depth, shard, head_span), brain_type),
            vmem((local_heads, depth, shard, head_span), brain_type),
            vmem((5, 8, width), float_type),
            vmem((group_size, 8, six), float_type),
            vmem((group_size, 8, six), float_type),
            vmem((8, six), brain_type),
            vmem((fsdp_size, 8, six), brain_type),
            vmem((fsdp_size, 8, shard), float_type),
            vmem((fsdp_size, 8, shard), float_type),
            vmem((group_size, fsdp_size, 8, shard), float_type),
            vmem((8, six), float_type),
            vmem((group_size, 8, six), float_type),
            pltpu.SemaphoreType.DMA((copies,)),
            pltpu.SemaphoreType.DMA((copies,)),
        ]
        + late_scratch(late, arrays),
        compiler_params=pltpu.CompilerParams(
            collective_id=2, has_side_effects=True, vmem_limit_bytes=TOP_VMEM
        ),
        name="backward_row",
    )(*arrays)


def deliver_kernel(sizes, count, bias_row, *refs):
    sources, targets = refs[:count], refs[count : 2 * count]
    shares = refs[2 * count : 2 * count + len(sizes)]
    buffers = refs[2 * count + len(sizes) : 3 * count + len(sizes)]
    sems = refs[-1]

    def taken(index):
        return pltpu.make_async_copy(sources[index], buffers[index], sems.at[index])

    def given(index):
        return pltpu.make_async_copy(buffers[index], targets[index], sems.at[count + index])

    for index in range(count):
        taken(index).start()
    for start, size, share in zip(bias_starts(sizes), sizes, shares):
        share[...] = bias_row[0, start : start + size]
    for index in range(count):
        taken(index).wait()
        given(index).start()
    for index in range(count):
        given(index).wait()


def deliver(bias_row, sizes, *arrays):
    count = len(arrays)
    in_vmem = pl.BlockSpec(memory_space=pltpu.VMEM)
    anywhere = pl.BlockSpec(memory_space=pl.ANY)
    shape = jax.ShapeDtypeStruct
    return pl.pallas_call(
        functools.partial(deliver_kernel, sizes, count),
        out_shape=[shape(item.shape, item.dtype) for item in arrays]
        + [shape((size,), float_type) for size in sizes],
        in_specs=[in_vmem] + [anywhere] * count,
        out_specs=[anywhere] * count + [in_vmem] * len(sizes),
        scratch_shapes=[pltpu.VMEM(item.shape, item.dtype) for item in arrays]
        + [pltpu.SemaphoreType.DMA((2 * count,))],
        compiler_params=pltpu.CompilerParams(vmem_limit_bytes=TOP_VMEM),
        name="deliver_row",
    )(bias_row, *arrays)


def fast_local(
    tokens,
    conditions,
    lengths,
    segments,
    condition_weight,
    condition_bias,
    input_weight,
    input_bias,
    attend_weight,
    attend_bias,
    expand_weight,
    expand_bias,
    reduce_weight,
    reduce_bias,
    cotangent,
):
    _, quarter, width = tokens.shape
    group_size, fsdp_size = lax.axis_size("rep"), lax.axis_size("fsdp")
    shard, _, own_width = condition_weight.shape
    hidden = expand_weight.shape[1]
    sizes = (fsdp_size, group_size, quarter, width, own_width, shard)
    biases = (condition_bias, input_bias, attend_bias, expand_bias, reduce_bias)
    bias_total = sum(item.shape[0] for item in biases)
    bias_end = (bias_total + 1023) // 1024 * 1024
    bias_vector, start = 0.0, 0
    for item in biases:
        end = start + item.shape[0]
        bias_vector = bias_vector + jnp.pad(item.astype(float_type), (start, bias_end - end))
        start = end
    bias_vector = bias_vector[None]
    cond_blocks = condition_weight.transpose(1, 0, 2)
    condition_rows = conditions[0]
    token_rows = tokens.reshape(quarter, width)
    upstream = cotangent.reshape(quarter, width)
    (
        mods,
        biases,
        one,
        heads,
        logs,
        mixed,
        branch,
        middle,
        two,
        upper,
        input_pad,
        attend_pad,
        expand_all,
        reduce_all,
        act_all,
    ) = run_forward(
        sizes,
        token_rows,
        upstream,
        condition_rows,
        segments,
        cond_blocks,
        bias_vector,
        lengths,
        (input_weight.transpose(1, 0, 2), attend_weight, expand_weight, reduce_weight),
    )
    (
        far_sum,
        near_sum,
        head_grads,
        attend_grad,
        late_grad,
        expand_part,
        reduce_final,
        slope,
        sums,
    ) = (
        run_middle(
            sizes,
            two,
            upper,
            expand_all,
            reduce_all,
            mods,
            biases,
            middle,
            branch,
            upstream,
            attend_pad,
            mixed,
        )
    )
    (
        output,
        token_grad,
        condition_grad,
        cond_grad,
        bias_final,
        expand_final,
        input_final,
        attend_final,
    ) = run_backward(
        sizes,
        hidden,
        heads,
        logs,
        head_grads,
        mixed,
        one,
        input_pad,
        token_rows,
        mods,
        biases,
        slope,
        upstream,
        middle,
        far_sum,
        near_sum,
        late_grad,
        expand_part,
        attend_grad,
        sums,
        cond_blocks,
        act_all,
        condition_rows,
        segments,
        lengths,
    )

    (
        output,
        token_grad,
        condition_grad,
        cond_grad,
        input_final,
        attend_final,
        expand_final,
        reduce_final,
        condition_bias_final,
        input_bias_final,
        attend_bias_final,
        expand_bias_final,
        reduce_bias_final,
    ) = deliver(
        bias_final,
        bias_sizes(fsdp_size, width, hidden * group_size),
        output,
        token_grad,
        condition_grad,
        cond_grad,
        input_final,
        attend_final,
        expand_final,
        reduce_final,
    )
    return (
        output[None],
        token_grad[None],
        condition_grad[None],
        cond_grad.transpose(1, 0, 2),
        condition_bias_final,
        input_final.transpose(1, 0, 2),
        input_bias_final,
        attend_final,
        attend_bias_final,
        expand_final,
        expand_bias_final,
        reduce_final,
        reduce_bias_final,
    )


def solution(mesh):
    in_specs = (
        P("fsdp", "rep", None),
        P("fsdp", None, None),
        P("fsdp", None),
        P("fsdp", "rep"),
        P("fsdp", None, "rep"),
        P("fsdp"),
        P("fsdp", None, "rep"),
        P("fsdp"),
        P("fsdp", "rep"),
        P("fsdp"),
        P("fsdp", "rep"),
        P("fsdp"),
        P("fsdp", "rep"),
        P("fsdp"),
        P("fsdp", "rep", None),
    )
    out_specs = (
        P("fsdp", "rep", None),
        P("fsdp", "rep", None),
        P("fsdp", None, None),
        P("fsdp", None, "rep"),
        P("fsdp"),
        P("fsdp", None, "rep"),
        P("fsdp"),
        P("fsdp", "rep"),
        P("fsdp"),
        P("fsdp", "rep"),
        P("fsdp"),
        P("fsdp", "rep"),
        P("fsdp"),
    )
    local = fast_local if mesh.shape["fsdp"] == 8 else plain_local
    return jax.shard_map(local, mesh=mesh, in_specs=in_specs, out_specs=out_specs, check_vma=False)
```
